32 devices in a mesh: dp: 4 (over z), expert: 8 (over y, x, core).
Axes of the slice: x: 2, y: 2, z: 4, core: 2. Of those that a mesh axis runs over, the one named last changes fastest.
Arguments:
- inputs: bfloat16 [8, 1024, 1024], P('expert', 'dp'), may hold values from -6 to 6
- cotangent: bfloat16 [8, 1024, 1024], P('expert', 'dp'), may hold values from -6 to 6
- gain_attn: bfloat16 [1024], P(('dp', 'expert')), may hold values from 0.5 to 1.5
- w_query: bfloat16 [1024, 1024], P(('dp', 'expert')), may hold values from -0.1875 to 0.1875
- w_key: bfloat16 [1024, 1024], P(('dp', 'expert')), may hold values from -0.1875 to 0.1875
- w_value: bfloat16 [1024, 1024], P(('dp', 'expert')), may hold values from -0.1875 to 0.1875
- w_out: bfloat16 [1024, 1024], P(('dp', 'expert')), may hold values from -3 to 3
- position_bias: bfloat16 [512], P(('dp', 'expert')), may hold values from -4 to 4
- gain_moe: bfloat16 [1024], P(('dp', 'expert')), may hold values from 0.5 to 1.5
- w_gate: bfloat16 [8, 1024, 2816], P('expert', 'dp'), may hold values from -0.1875 to 0.1875
- w_up: bfloat16 [8, 1024, 2816], P('expert', 'dp'), may hold values from -0.1875 to 0.1875
- w_down: bfloat16 [8, 2816, 1024], P('expert', 'dp'), may hold values from -0.21875 to 0.21875
- routes: int32 [8, 1024, 2], P('expert', 'dp'), may hold values from 0 to 7, all different within a row
- gate_fixed: int32 [8, 1024], P('expert', 'dp'), may hold values from 13107 to 52428
Outputs:
- block_out: bfloat16 [8, 1024, 1024], P('expert', 'dp')
- grad_inputs: bfloat16 [8, 1024, 1024], P('expert', 'dp')
- grad_gain_attn: float32 [1024], P(('dp', 'expert'))
- grad_w_query: float32 [1024, 1024], P(('dp', 'expert'))
- grad_w_key: float32 [1024, 1024], P(('dp', 'expert'))
- grad_w_value: float32 [1024, 1024], P(('dp', 'expert'))
- grad_w_out: float32 [1024, 1024], P(('dp', 'expert'))
- grad_position_bias: float32 [512], P(('dp', 'expert'))
- grad_gain_moe: float32 [1024], P(('dp', 'expert'))
- grad_w_gate: float32 [8, 1024, 2816], P('expert', 'dp')
- grad_w_up: float32 [8, 1024, 2816], P('expert', 'dp')
- grad_w_down: float32 [8, 2816, 1024], P('expert', 'dp')
The draws below stay inside these ranges and needn't reach their ends.
Inputs may be any that keep to these rules, and one draw needn't show every extreme that they name: `routes`: each token names two different experts.
All inputs are finite; a program needn't handle non-finite values.
Results may differ from the reference program's by a relative error of at most 0.03.
Values may be sent and summed in bfloat16 or wider, within the bound.
A program may use at most 256 MiB of HBM per device.

```python
import jax
import jax.numpy as jnp
from jax import lax

D = 1024
HEADS = 16
HEAD_DIM = 64
FF = 2816
BUCKETS = 32
SEQ_LEN = 1024
HD = 1024
EXPERTS = 8
SEQS = 8
CAP = 80
N_DP = 4


def place_ends(entries, own_key, smallest, high):
    longest = entries.shape.index(max(entries.shape))
    spots = []
    for shift in (0, 1):
        where = [jax.random.randint(jax.random.fold_in(own_key, axis), (), 0, length) for axis, length in enumerate(entries.shape)]
        where[longest] = (where[longest] + shift) % entries.shape[longest]
        spots.append(tuple(where))
    return entries.at[spots[0]].set(smallest).at[spots[1]].set(high)


def raised(array, stream_key, source, target, parts, factor):
    owner, partner = [(jnp.arange(array.shape[dim]) // (array.shape[dim] // parts)).reshape([-1 if axis == dim else 1 for axis in range(array.ndim)]) for dim in (source, target)]
    chosen = jax.random.permutation(stream_key, parts)[partner]
    strong = (owner == chosen) | (owner == (partner + parts // 2) % parts)
    return jnp.where(strong, factor * array, array)


def level_of(own_key, dims, pieces, low, top_value):
    def one(axis_at, blocks):
        heights = jax.random.uniform(jax.random.fold_in(jax.random.fold_in(own_key, 6), axis_at), (blocks,), jnp.float32, low / len(pieces), top_value / len(pieces))
        return jnp.repeat(jnp.exp(heights), dims[axis_at] // blocks).reshape((-1,) + (1,) * (len(dims) - axis_at - 1))

    loudness = one(*pieces[0])
    for cut in pieces[1:]:
        loudness = loudness * one(*cut)
    return loudness


def picks_of(stream_key, rows, amount, top, lift):
    sequence = jax.random.permutation(jax.random.fold_in(stream_key, 1), amount)
    boost = sequence
    for power in range(3):
        boost = boost * boost // amount
    boost = boost * lift // amount
    lots = jax.random.randint(jax.random.fold_in(stream_key, 2), (rows, amount), 0, 4096) + boost
    fixed_rows = jax.random.permutation(jax.random.fold_in(stream_key, 3), rows)[jnp.arange(amount) % rows]
    lots = jnp.where(jnp.arange(rows)[:, None] == fixed_rows[None, :], 1 << 14, lots)
    score = lots * amount + jnp.arange(amount)
    return lax.top_k(score.astype(jnp.int32), top)[1].astype(jnp.int32)


def noise(own_key, dims, spread, reach, cuts=(), kind=jnp.bfloat16):
    values = jax.random.normal(own_key, dims, jnp.float32) * spread
    if len(cuts) > 0:
        values = level_of(own_key, dims, cuts, -0.22, 0.18) * values
    return jnp.clip(values, min=-reach, max=reach).astype(kind)


def bell_draw_with(own_key, shape, spread, bound, pieces, heavy, kind=jnp.bfloat16):
    values = spread * jax.random.normal(own_key, shape, jnp.float32)
    if pieces:
        values = values * level_of(own_key, shape, pieces, -0.22, 0.18)
    return jnp.clip(raised(values, jax.random.fold_in(own_key, 3), *heavy), -bound, bound).astype(kind)


def setup_inputs(seed: int = 0) -> dict:
    arg_keys = jax.random.split(jax.random.key(seed), 15)
    return {
        "inputs": bell_draw_with(arg_keys[0], (SEQS, SEQ_LEN, D), 1.0, 6.0, ((0, 8), (1, 4)), (0, 2, 8, 2.0)),
        "cotangent": noise(arg_keys[1], (SEQS, SEQ_LEN, D), 1.0, 6.0, ((0, 8), (1, 4))),
        "gain_attn": jnp.clip(1.0 + 0.1 * jax.random.normal(arg_keys[2], (D,), jnp.float32), 0.5, 1.5).astype(jnp.bfloat16),
        "w_query": noise(arg_keys[3], (D, HD), D ** -0.5, 0.1875, ((0, 32),)),
        "w_key": noise(arg_keys[4], (D, HD), D ** -0.5, 0.1875, ((0, 32),)),
        "w_value": noise(arg_keys[5], (D, HD), D ** -0.5, 0.1875, ((0, 32),)),
        "w_out": noise(arg_keys[6], (HD, D), (HD * 4 // SEQ_LEN) ** -0.5, 3.0, ((0, 32),)),
        "position_bias": noise(arg_keys[7], (BUCKETS * HEADS,), 0.8, 4.0, ((0, 32),)),
        "gain_moe": jnp.clip(1.0 + 0.1 * jax.random.normal(arg_keys[8], (D,), jnp.float32), 0.5, 1.5).astype(jnp.bfloat16),
        "w_gate": noise(arg_keys[9], (EXPERTS, D, FF), D ** -0.5, 0.1875, ((0, 8), (1, 4))),
        "w_up": noise(arg_keys[10], (EXPERTS, D, FF), D ** -0.5, 0.1875, ((0, 8), (1, 4))),
        "w_down": noise(arg_keys[11], (EXPERTS, FF, D), (FF // 4) ** -0.5, 0.21875, ((0, 8), (1, 4))),
        "routes": picks_of(arg_keys[12], SEQS * SEQ_LEN, EXPERTS, 2, 2048).reshape((SEQS, SEQ_LEN, 2)),
        "gate_fixed": place_ends(jax.random.randint(arg_keys[13], (SEQS, SEQ_LEN), 13107, 52429), jax.random.fold_in(arg_keys[13], 1), 13107, 52428).astype(jnp.int32),
    }


THRESHOLDS = (12, 16, 23, 32, 46, 64, 91)
EPSILON = 1e-06
HIGHEST = lax.Precision.HIGHEST

@jax.custom_vjp
def low(v):
    return lax.optimization_barrier(v.astype(jnp.bfloat16)).astype(jnp.float32)

@jax.custom_vjp
def low_back(v):
    return v

def low_keep(v):
    return (low(v), None)

def low_pass(kept, grad):
    return (grad,)

def back_keep(v):
    return (v, None)

def back_low(kept, grad):
    return (low(grad),)
low.defvjp(low_keep, low_pass)
low_back.defvjp(back_keep, back_low)

def bucket_table(query_pos, key_pos):
    offset = key_pos[None, :] - query_pos[:, None]
    distance = jnp.abs(offset)
    banded = jnp.full(distance.shape, 8, jnp.int32)
    for cutoff in THRESHOLDS:
        banded = banded + (distance >= cutoff).astype(jnp.int32)
    nearby = jnp.where(distance < 8, distance, banded)
    return nearby + jnp.where(offset > 0, 16, 0).astype(jnp.int32)

def rms_norm(values, gain):
    return values * lax.rsqrt(lax.optimization_barrier(jnp.mean(values * values, axis=-1, keepdims=True)) + EPSILON) * gain

def attend(seq_x, gain_attn, w_query, w_key, w_value, w_out, bias_full):
    length = seq_x.shape[0]
    normed = low(rms_norm(seq_x, gain_attn))
    queries = low_back(low(jnp.dot(normed, w_query, precision=HIGHEST))).reshape(length, HEADS, HEAD_DIM)
    keys_all = low_back(low(jnp.dot(normed, w_key, precision=HIGHEST))).reshape(length, HEADS, HEAD_DIM)
    values_all = low_back(low(jnp.dot(normed, w_value, precision=HIGHEST))).reshape(length, HEADS, HEAD_DIM)
    scale = HEAD_DIM ** (-0.5)
    logits = jnp.einsum('qhd,khd->hqk', queries, keys_all, precision=HIGHEST) * scale + bias_full
    logits = low_back(logits)
    attn_probs = low(jax.nn.softmax(logits, axis=-1))
    mixed_out = jnp.einsum('hqk,khd->qhd', attn_probs, values_all, precision=HIGHEST).reshape(length, HD)
    mixed_out = low_back(low(mixed_out))
    return low_back(jnp.dot(mixed_out, w_out, precision=HIGHEST))

def expert(slot_in, gate_w, up_w, down_w):
    gate_pre = low_back(jnp.dot(slot_in, gate_w, precision=HIGHEST))
    up_pre = low_back(jnp.dot(slot_in, up_w, precision=HIGHEST))
    hidden = low(jax.nn.gelu(gate_pre, approximate=True) * up_pre)
    return low_back(low(jnp.dot(hidden, down_w, precision=HIGHEST)))

def reference(inputs, cotangent, gain_attn, w_query, w_key, w_value, w_out, position_bias, gain_moe, w_gate, w_up, w_down, routes, gate_fixed):

    def forward(xf, g_attn, wq_f, wk_f, wv_f, wo_f, bias_flat, g_moe, wg_f, wu_f, wd_f):
        seqs, length, width = xf.shape
        positions = jnp.arange(length, dtype=jnp.int32)
        buckets = bucket_table(positions, positions)
        table = bias_flat.reshape(BUCKETS, HEADS)
        bias_full = jnp.transpose(table[buckets], (2, 0, 1))
        attend_seq = jax.checkpoint(attend)
        attn_out = lax.map(lambda seq_x: attend_seq(seq_x, g_attn, wq_f, wk_f, wv_f, wo_f, bias_full), xf)
        resid = xf + attn_out
        normed2 = low(rms_norm(resid, g_moe))
        groups = seqs * N_DP
        tok_group = length // N_DP
        grouped = normed2.reshape(groups, tok_group, width)
        pair_expert = routes.reshape(groups, tok_group * 2)
        expert_ids = jnp.arange(EXPERTS, dtype=jnp.int32)
        onehot = (pair_expert[:, :, None] == expert_ids).astype(jnp.int32)
        earlier = jnp.cumsum(onehot, axis=1) - onehot
        slot_idx = lax.optimization_barrier(jnp.sum(earlier * onehot, axis=2))
        kept = slot_idx < CAP
        group_ids = jnp.arange(groups, dtype=jnp.int32)[:, None]
        total_slots = EXPERTS * groups * CAP
        dest = jnp.where(kept, (pair_expert * groups + group_ids) * CAP + slot_idx, total_slots).astype(jnp.int32)
        pair_rows = jnp.repeat(grouped, 2, axis=1).reshape(-1, width)
        buffer = jnp.zeros((total_slots + 1, width), jnp.float32).at[dest.reshape(-1)].add(pair_rows)
        slot_in = low_back(buffer[:total_slots]).reshape(EXPERTS, groups * CAP, width)
        expert_seq = jax.checkpoint(expert)
        expert_out = lax.map(lambda items: expert_seq(items[0], items[1], items[2], items[3]), (slot_in, wg_f, wu_f, wd_f))
        out_rows = jnp.concatenate([expert_out.reshape(total_slots, width), jnp.zeros((1, width), jnp.float32)], axis=0)
        picked = out_rows[dest.reshape(-1)].reshape(groups, tok_group, 2, width)
        first_gate = gate_fixed.reshape(groups, tok_group).astype(jnp.float32) / 65536.0
        gate_pair = jnp.stack([first_gate, 1.0 - first_gate], axis=-1)
        moe_out = lax.optimization_barrier(jnp.sum(picked * gate_pair[..., None], axis=2)).reshape(seqs, length, width)
        return resid + moe_out
    floats = tuple((item.astype(jnp.float32) for item in (inputs, gain_attn, w_query, w_key, w_value, w_out, position_bias, gain_moe, w_gate, w_up, w_down)))
    result, pullback = jax.vjp(forward, *floats)
    grads = pullback(cotangent.astype(jnp.float32))
    return (result.astype(jnp.bfloat16), grads[0].astype(jnp.bfloat16), grads[1], grads[2], grads[3], grads[4], grads[5], grads[6], grads[7], grads[8], grads[9], grads[10])
```

```python
import functools

import jax
import jax.numpy as jnp
from jax import lax
from jax.experimental import pallas as pl
from jax.experimental.pallas import tpu as pltpu
from jax.sharding import PartitionSpec as P

HEADS = 16
HEAD_DIM = 64
BUCKETS = 32
THRESHOLDS = (12, 16, 23, 32, 46, 64, 91)
EPSILON = 1e-06
SCALE = HEAD_DIM ** (-0.5)
BF16 = jnp.bfloat16
F32 = jnp.float32
GELU_C = 0.7978845608028654
GELU_A = 0.044715
VMEM_LIMIT = 56 * 1024 * 1024

NT = (((1,), (1,)), ((), ()))
TN = (((0,), (0,)), ((), ()))
NN = (((1,), (0,)), ((), ()))


def mm(a, b, dims=NN):
    return lax.dot_general(a, b, dims, preferred_element_type=F32)


def bucket_of(offset):
    distance = jnp.abs(offset)
    banded = jnp.full(distance.shape, 8, jnp.int32)
    for cutoff in THRESHOLDS:
        banded = banded + (distance >= cutoff).astype(jnp.int32)
    nearby = jnp.where(distance < 8, distance, banded)
    return nearby + jnp.where(offset > 0, 16, 0).astype(jnp.int32)


def norm_forward(values, gain):
    inverse = lax.rsqrt(jnp.mean(values * values, axis=-1, keepdims=True) + EPSILON)
    return (inverse, (values * inverse * gain).astype(BF16))


def norm_backward(values, inverse, gain, grad_normed):
    scaled = gain * grad_normed
    grad_gain = jnp.sum(grad_normed * values * inverse, axis=0)
    grad_values = inverse * scaled - values * inverse**3 * jnp.mean(
        scaled * values, axis=-1, keepdims=True
    )
    return (grad_gain, grad_values)


def bias_tile(vec_ref, head, tile_ref):
    block, wide = tile_ref.shape
    row = jnp.broadcast_to(vec_ref[pl.ds(head, 1), :], (block, wide))
    tile_ref[...] = pltpu.roll(row, wide - block, 1, stride=1, stride_axis=0)


def tile_offset(dp, n, block, query_block, key_block):
    query_abs = lax.rem(dp - query_block + n, n)
    key_abs = lax.rem(dp - key_block + n, n)
    return pl.multiple_of((key_abs - query_abs + n - 1) * block, 128)


def head_logits(n, block, dp, query_block, q_pair, k_pair, mask, tile_ref):
    masked = jnp.where(mask, q_pair, jnp.zeros_like(q_pair))
    raw = mm(masked, k_pair, NT) * SCALE
    bias = jnp.concatenate(
        [
            tile_ref[:, pl.ds(tile_offset(dp, n, block, query_block, j), block)]
            for j in range(n)
        ],
        axis=1,
    )
    return raw + bias


def attention_forward_kernel(n, block, dp_ref, q_ref, k_ref, v_ref, vec_ref, out_ref, lse_ref, tiles):
    dp = dp_ref[0]
    pair, query_block = pl.program_id(0), pl.program_id(1)

    @pl.when(query_block == 0)
    def _():
        for side in range(2):
            bias_tile(vec_ref, 2 * pair + side, tiles.at[side])

    q_pair, k_pair, v_pair = q_ref[...], k_ref[...], v_ref[...]
    lane = lax.broadcasted_iota(jnp.int32, (block, 128), 1)
    outs, lses = [], []
    for side in range(2):
        mask = (lane >= HEAD_DIM) if side else (lane < HEAD_DIM)
        logits = head_logits(n, block, dp, query_block, q_pair, k_pair, mask, tiles.at[side])
        row_max = jnp.max(logits, axis=-1, keepdims=True)
        exponent = jnp.exp(logits - row_max)
        total = jnp.sum(exponent, axis=-1, keepdims=True)
        low = (exponent * (1.0 / total)).astype(BF16)
        outs.append(mm(low, v_pair))
        lses.append(jnp.broadcast_to(row_max + jnp.log(total), (block, 128)))
    first = lane < HEAD_DIM
    out_ref[...] = jnp.where(first, outs[0], outs[1]).astype(BF16)
    lse_ref[...] = jnp.where(first, lses[0], lses[1])


def attention_forward(dp, n, qkv, vectors):
    rows, triple = qkv.shape
    own = triple // 3
    block = rows // n
    pairs = own // 128
    wide = vectors.shape[1]
    return pl.pallas_call(
        functools.partial(attention_forward_kernel, n, block),
        grid=(pairs, n),
        in_specs=[
            pl.BlockSpec(memory_space=pltpu.SMEM),
            pl.BlockSpec((block, 128), lambda p, i: (i, p)),
            pl.BlockSpec((rows, 128), lambda p, i: (0, pairs + p)),
            pl.BlockSpec((rows, 128), lambda p, i: (0, 2 * pairs + p)),
            pl.BlockSpec((2 * pairs, wide), lambda p, i: (0, 0)),
        ],
        out_specs=[
            pl.BlockSpec((block, 128), lambda p, i: (i, p)),
            pl.BlockSpec((block, 128), lambda p, i: (i, p)),
        ],
        out_shape=[
            jax.ShapeDtypeStruct((rows, own), BF16),
            jax.ShapeDtypeStruct((rows, own), F32),
        ],
        scratch_shapes=[pltpu.VMEM((2, block, wide), F32)],
        compiler_params=pltpu.CompilerParams(vmem_limit_bytes=VMEM_LIMIT),
        cost_estimate=pl.CostEstimate(
            flops=16 * rows * rows * own, bytes_accessed=6 * rows * own, transcendentals=rows * rows * own // 64
        ),
        name="attention_forward",
    )(dp, qkv, qkv, qkv, vectors)


def diagonal_sum(tile):
    rows, wide = tile.shape
    while rows > 1:
        half = rows // 2
        tile = tile[:half] + pltpu.roll(tile[half:], wide - half, 1)
        rows = half
    return tile


def attention_backward_kernel(
    n, block, dp_ref, q_ref, k_ref, v_ref, lse_ref, dm_ref, vec_ref,
    dq_ref, dk_ref, dv_ref, diag_ref, tiles, sums, dk_acc, dv_acc,
):
    dp = dp_ref[0]
    pair, query_block = pl.program_id(0), pl.program_id(1)

    @pl.when(query_block == 0)
    def _():
        for side in range(2):
            bias_tile(vec_ref, 2 * pair + side, tiles.at[side])
        sums[...] = jnp.zeros_like(sums)
        dk_acc[...] = jnp.zeros_like(dk_acc)
        dv_acc[...] = jnp.zeros_like(dv_acc)

    q_pair, k_pair, v_pair, dm_pair = q_ref[...], k_ref[...], v_ref[...], dm_ref[...]
    rows = k_pair.shape[0]
    lane = lax.broadcasted_iota(jnp.int32, (block, 128), 1)
    dqs, dks, dvs = [], [], []
    for side in range(2):
        mask = (lane >= HEAD_DIM) if side else (lane < HEAD_DIM)
        logits = head_logits(n, block, dp, query_block, q_pair, k_pair, mask, tiles.at[side])
        probs = jnp.exp(logits - lse_ref[:, side * HEAD_DIM : side * HEAD_DIM + 1])
        masked = jnp.where(mask, dm_pair, jnp.zeros_like(dm_pair))
        d_probs = mm(masked, v_pair, NT)
        inner = jnp.sum(probs * d_probs, axis=-1, keepdims=True)
        d_logits = (probs * (d_probs - inner)).astype(BF16)
        dvs.append(mm(probs.astype(BF16), dm_pair, TN))
        dqs.append(mm(d_logits, k_pair))
        dks.append(mm(d_logits, q_pair, TN))
        wide = d_logits.astype(F32)
        for j in range(n):
            here = pl.ds(tile_offset(dp, n, block, query_block, j), block)
            sums[side, :, here] += wide[:, j * block : (j + 1) * block]
    dq_ref[...] = (jnp.where(lane < HEAD_DIM, dqs[0], dqs[1]) * SCALE).astype(BF16)
    key_lane = lax.broadcasted_iota(jnp.int32, (rows, 128), 1)
    dk_acc[...] += jnp.where(key_lane < HEAD_DIM, dks[0], dks[1])
    dv_acc[...] += jnp.where(key_lane < HEAD_DIM, dvs[0], dvs[1])

    @pl.when(query_block == n - 1)
    def _():
        dk_ref[...] = (dk_acc[...] * SCALE).astype(BF16)
        dv_ref[...] = dv_acc[...].astype(BF16)
        for side in range(2):
            diag_ref[0, pl.ds(side, 1), :] = diagonal_sum(sums[side])


def attention_backward(dp, n, qkv, lse, d_mixed, vectors):
    rows, triple = qkv.shape
    own = triple // 3
    block = rows // n
    pairs = own // 128
    wide = vectors.shape[1]
    return pl.pallas_call(
        functools.partial(attention_backward_kernel, n, block),
        grid=(pairs, n),
        in_specs=[
            pl.BlockSpec(memory_space=pltpu.SMEM),
            pl.BlockSpec((block, 128), lambda p, i: (i, p)),
            pl.BlockSpec((rows, 128), lambda p, i: (0, pairs + p)),
            pl.BlockSpec((rows, 128), lambda p, i: (0, 2 * pairs + p)),
            pl.BlockSpec((block, 128), lambda p, i: (i, p)),
            pl.BlockSpec((block, 128), lambda p, i: (i, p)),
            pl.BlockSpec((2 * pairs, wide), lambda p, i: (0, 0)),
        ],
        out_specs=[
            pl.BlockSpec((block, 128), lambda p, i: (i, p)),
            pl.BlockSpec((rows, 128), lambda p, i: (0, p)),
            pl.BlockSpec((rows, 128), lambda p, i: (0, p)),
            pl.BlockSpec((1, 2, wide), lambda p, i: (p, 0, 0)),
        ],
        out_shape=[
            jax.ShapeDtypeStruct((rows, own), BF16),
            jax.ShapeDtypeStruct((rows, own), BF16),
            jax.ShapeDtypeStruct((rows, own), BF16),
            jax.ShapeDtypeStruct((pairs, 2, wide), F32),
        ],
        scratch_shapes=[
            pltpu.VMEM((2, block, wide), F32),
            pltpu.VMEM((2, block, wide), F32),
            pltpu.VMEM((rows, 128), F32),
            pltpu.VMEM((rows, 128), F32),
        ],
        compiler_params=pltpu.CompilerParams(vmem_limit_bytes=VMEM_LIMIT),
        cost_estimate=pl.CostEstimate(
            flops=40 * rows * rows * own, bytes_accessed=14 * rows * own, transcendentals=rows * rows * own // 64
        ),
        name="attention_backward",
    )(dp, qkv, qkv, qkv, lse, d_mixed, vectors)


def gelu_pair(v):
    square = v * v
    t = jnp.tanh(GELU_C * (v + GELU_A * v * square))
    half = 0.5 * (1.0 + t)
    slope = half + (0.5 * GELU_C) * v * (1.0 - t * t) * (1.0 + (3.0 * GELU_A) * square)
    return v * half, slope


def expert_kernel(
    main, slots_a, slots_b, dout_a, dout_b, wgu_ref, wd_ref,
    out_ref, dslot_ref, gwgu_ref, gwd_ref, gwgu_acc, gwd_acc,
):
    step = pl.program_id(0)

    @pl.when(step == 0)
    def _():
        gwgu_acc[...] = jnp.zeros_like(gwgu_acc)
        gwd_acc[...] = jnp.zeros_like(gwd_acc)

    slots = jnp.concatenate([slots_a[0], slots_b[0]], axis=0)
    d_out = jnp.concatenate([dout_a[0], dout_b[0]], axis=0)
    rows = slots.shape[0]
    wgu, wd = wgu_ref[...], wd_ref[...]
    pre = mm(slots, wgu)
    d_hidden = mm(d_out, wd, NT)
    low_lane = lax.broadcasted_iota(jnp.int32, (rows, 128), 1) < 64
    gate, up = pre[:, :main], pre[:, main : 2 * main]
    tail = pre[:, 2 * main :]
    tail_up = pltpu.roll(tail, 64, 1)
    act, slope = gelu_pair(gate)
    act_t, slope_t = gelu_pair(tail)
    hidden_t = jnp.where(low_lane, act_t * tail_up, 0.0)
    hidden = jnp.concatenate([(act * up).astype(BF16), hidden_t.astype(BF16)], axis=1)
    out_ref[0] = mm(hidden, wd).astype(BF16)
    gwd_acc[...] += mm(hidden, d_out, TN)
    dh, dh_t = d_hidden[:, :main], d_hidden[:, main:]
    d_gate = dh * up * slope
    d_up = dh * act
    d_tail = jnp.where(low_lane, dh_t * tail_up * slope_t, pltpu.roll(dh_t * act_t, 64, 1))
    d_pre = jnp.concatenate([d_gate.astype(BF16), d_up.astype(BF16), d_tail.astype(BF16)], axis=1)
    dslot_ref[0] = mm(d_pre, wgu, NT).astype(BF16)
    gwgu_acc[...] += mm(slots, d_pre, TN)

    @pl.when(step == pl.num_programs(0) - 1)
    def _():
        gwgu_ref[...] = gwgu_acc[...].astype(BF16)
        gwd_ref[...] = gwd_acc[...]


def experts(slots, d_outs, wgu, wd, steps):
    width, columns = wgu.shape
    deep = wd.shape[0]
    main = (columns - 128) // 2
    slots = [s.reshape(steps, -1, width) for s in slots]
    d_outs = [s.reshape(steps, -1, width) for s in d_outs]
    half = slots[0].shape[1]
    rows = 2 * half * steps
    part = pl.BlockSpec((1, half, width), lambda i: (i, 0, 0))
    whole = pl.BlockSpec((1, 2 * half, width), lambda i: (i, 0, 0))
    return pl.pallas_call(
        functools.partial(expert_kernel, main),
        grid=(steps,),
        in_specs=[
            part, part, part, part,
            pl.BlockSpec((width, columns), lambda i: (0, 0)),
            pl.BlockSpec((deep, width), lambda i: (0, 0)),
        ],
        out_specs=[
            whole, whole,
            pl.BlockSpec((width, columns), lambda i: (0, 0)),
            pl.BlockSpec((deep, width), lambda i: (0, 0)),
        ],
        out_shape=[
            jax.ShapeDtypeStruct((steps, 2 * half, width), BF16),
            jax.ShapeDtypeStruct((steps, 2 * half, width), BF16),
            jax.ShapeDtypeStruct((width, columns), BF16),
            jax.ShapeDtypeStruct((deep, width), F32),
        ],
        scratch_shapes=[
            pltpu.VMEM((width, columns), F32),
            pltpu.VMEM((deep, width), F32),
        ],
        compiler_params=pltpu.CompilerParams(vmem_limit_bytes=VMEM_LIMIT),
        cost_estimate=pl.CostEstimate(
            flops=6 * rows * width * (columns + deep),
            bytes_accessed=8 * rows * width + 8 * width * columns,
            transcendentals=rows * deep,
        ),
        name="experts",
    )(*slots, *d_outs, wgu, wd)


def pack_kernel(n, piece, gate_ref, up_ref, out_ref):
    main = piece // 128 * 128
    gate, up = gate_ref[...], up_ref[...]
    for j in range(n):
        g = gate[:, j * piece : (j + 1) * piece]
        u = up[:, j * piece : (j + 1) * piece]
        out_ref[j] = jnp.concatenate([g[:, :main], u[:, :main], g[:, main:], u[:, main:]], axis=1)


def pack_columns(n, gate, up):
    rows, total = gate.shape
    piece = total // n
    step = min(rows, 64)
    return pl.pallas_call(
        functools.partial(pack_kernel, n, piece),
        grid=(rows // step,),
        in_specs=[pl.BlockSpec((step, total), lambda i: (i, 0))] * 2,
        out_specs=pl.BlockSpec((n, step, 2 * piece), lambda i: (0, i, 0)),
        out_shape=jax.ShapeDtypeStruct((n, rows, 2 * piece), gate.dtype),
        compiler_params=pltpu.CompilerParams(vmem_limit_bytes=VMEM_LIMIT),
        cost_estimate=pl.CostEstimate(flops=0, bytes_accessed=8 * rows * total, transcendentals=0),
        name="pack_columns",
    )(gate, up)


def unpack_kernel(n, piece, in_ref, gate_ref, up_ref):
    main = piece // 128 * 128
    rest = piece - main
    gates, ups = [], []
    for j in range(n):
        block = in_ref[j].astype(F32)
        gates += [block[:, :main], block[:, 2 * main : 2 * main + rest]]
        ups += [block[:, main : 2 * main], block[:, 2 * main + rest :]]
    gate_ref[...] = jnp.concatenate(gates, axis=1)
    up_ref[...] = jnp.concatenate(ups, axis=1)


def unpack_columns(blocks):
    n, rows, both = blocks.shape
    piece = both // 2
    step = min(rows, 64)
    total = n * piece
    return pl.pallas_call(
        functools.partial(unpack_kernel, n, piece),
        grid=(rows // step,),
        in_specs=[pl.BlockSpec((n, step, both), lambda i: (0, i, 0))],
        out_specs=[pl.BlockSpec((step, total), lambda i: (i, 0))] * 2,
        out_shape=[jax.ShapeDtypeStruct((rows, total), F32)] * 2,
        compiler_params=pltpu.CompilerParams(vmem_limit_bytes=VMEM_LIMIT),
        cost_estimate=pl.CostEstimate(flops=0, bytes_accessed=12 * rows * total, transcendentals=0),
        name="unpack_columns",
    )(blocks)


def shift(value, distance, n):
    return lax.ppermute(value, "dp", [(i, (i + distance) % n) for i in range(n)])


def gather_dp(value, n):
    return [value] + [shift(value, d, n) for d in range(1, n)]


def pick(stacked, index):
    return lax.dynamic_index_in_dim(stacked, index, 0, keepdims=False)


def exchange(value):
    return lax.all_to_all(value, "expert", split_axis=0, concat_axis=0, tiled=True)


def local(
    inputs, cotangent, gain_attn, w_query, w_key, w_value, w_out, position_bias,
    gain_moe, w_gate, w_up, w_down, routes, gate_fixed,
):
    n = lax.axis_size("dp")
    experts_n = lax.axis_size("expert")
    dp = lax.axis_index("dp")
    ex = lax.axis_index("expert")
    tok, width = inputs.shape[1:]
    length = n * tok
    own = HEADS * HEAD_DIM // n
    heads_own = HEADS // n
    wrows = w_query.shape[0]
    capacity = 5 * tok // (2 * experts_n)
    slots_n = experts_n * capacity
    order = [lax.rem(dp - j + n, n) for j in range(n)]

    x_blocks = gather_dp(inputs[0], n)
    n_gain, n_bias = gain_attn.shape[0], position_bias.shape[0]
    extra = jnp.concatenate([gain_attn, gain_moe, position_bias])
    extra = jnp.zeros((16, own), BF16).at[0, : 2 * n_gain + n_bias].set(extra)
    columns = jnp.concatenate([w_query, w_key, w_value], axis=0).reshape(3 * wrows, n, own)
    columns = jnp.concatenate(
        [jnp.swapaxes(columns, 0, 1), jnp.broadcast_to(extra, (n, 16, own))], axis=1
    )
    shares = [pick(columns, dp)] + [
        shift(pick(columns, lax.rem(dp + d, n)), d, n) for d in range(1, n)
    ]
    plane = jnp.concatenate(shares, axis=1)
    plane_all = jnp.stack(
        [plane]
        + [
            lax.ppermute(plane, "expert", [(i, i ^ k) for i in range(experts_n)])
            for k in range(1, experts_n)
        ]
    )
    plane_all = jnp.stack([pick(plane_all, ex ^ j) for j in range(experts_n)])
    by_block = plane_all.reshape(experts_n, 3 * wrows + 16, n, own)
    by_block = jnp.stack([lax.dynamic_index_in_dim(by_block, order[j], 2, keepdims=False) for j in range(n)])
    wqkv = (
        by_block[:, :, : 3 * wrows]
        .reshape(n, experts_n, 3, wrows, own)
        .transpose(0, 1, 3, 2, 4)
        .reshape(width, 3 * own)
    )
    extras = by_block[:, :, 3 * wrows]
    gain_one = extras[:, :, :n_gain].reshape(-1).astype(F32)
    gain_two = extras[:, :, n_gain : 2 * n_gain].reshape(-1).astype(F32)
    table = extras[:, :, 2 * n_gain : 2 * n_gain + n_bias].reshape(BUCKETS, HEADS)
    table = lax.dynamic_slice_in_dim(table, dp * heads_own, heads_own, 1)

    outs = jnp.stack(gather_dp(w_out, n))
    outs_all = jnp.stack(
        [outs]
        + [
            lax.ppermute(outs, "expert", [(i, i ^ k) for i in range(experts_n)])
            for k in range(1, experts_n)
        ]
    )
    outs_all = jnp.stack([pick(outs_all, ex ^ j) for j in range(experts_n)])
    w_out_all = jnp.swapaxes(outs_all, 0, 1).reshape(width, width)

    meta = jnp.concatenate([routes[0].T, gate_fixed], axis=0)
    meta_all = jnp.stack(gather_dp(meta, n))
    cot_blocks = gather_dp(cotangent[0], n)

    packed = pack_columns(n, w_gate[0], w_up[0])
    halves = [pick(packed, dp)] + [
        shift(pick(packed, lax.rem(dp + d, n)), d, n) for d in range(1, n)
    ]
    halves = jnp.stack(halves)
    wgu = jnp.concatenate([pick(halves, order[j]) for j in range(n)], axis=0)
    deep = w_down.shape[1]
    padded = -(-deep // 128) * 128
    wd = jnp.pad(w_down[0], ((0, padded - deep), (0, 0)))

    x_all = jnp.concatenate(x_blocks, axis=0).astype(F32)
    _, normed = norm_forward(x_all, gain_one)
    qkv = mm(normed, wqkv).astype(BF16)
    wide = 2 * length
    offsets = jnp.arange(wide, dtype=jnp.int32) - length
    in_bucket = (bucket_of(offsets)[:, None] == jnp.arange(BUCKETS, dtype=jnp.int32)).astype(BF16)
    in_bucket = jnp.where(jnp.abs(offsets)[:, None] < length, in_bucket, jnp.zeros_like(in_bucket))
    vectors = mm(table, in_bucket, (((0,), (1,)), ((), ())))
    place = jnp.reshape(dp, (1,)).astype(jnp.int32)
    mixed_heads, lse = attention_forward(place, n, qkv, vectors)
    mixed_blocks = [mixed_heads[:tok]] + [None] * (n - 1)
    for d in range(1, n):
        mixed_blocks[n - d] = shift(mixed_heads[d * tok : (d + 1) * tok], n - d, n)
    mixed = jnp.concatenate(mixed_blocks, axis=1)
    tokens = inputs[0].astype(F32)
    resid = tokens + mm(mixed, w_out_all)
    inverse_two, normed_two = norm_forward(resid, gain_two)
    normed_two_blocks = gather_dp(normed_two, n)

    ids = jnp.arange(experts_n, dtype=jnp.int32)
    pair = meta_all[:, :2]
    hot = (pair[..., None] == ids).astype(F32)
    earlier_tokens = jnp.tril(jnp.ones((tok, tok), BF16), -1)
    counts = jnp.einsum(
        "ts,gse->gte", earlier_tokens, jnp.sum(hot, axis=1).astype(BF16), preferred_element_type=F32
    )
    slot = jnp.sum(counts[:, None] * hot, axis=-1)
    slot = slot + jnp.stack([jnp.zeros_like(slot[:, 0]), (pair[:, 0] == pair[:, 1]).astype(F32)], axis=1)
    slot = slot.astype(jnp.int32)
    dest = jnp.where(slot < capacity, pair * capacity + slot, -1)
    select = (dest[..., None] == jnp.arange(slots_n, dtype=jnp.int32)).astype(BF16)
    both = select[:, 0] + select[:, 1]
    first_gate = meta_all[:, 2].astype(F32) / 65536.0
    gates = jnp.stack([first_gate, 1.0 - first_gate], axis=1)
    slot_gate = jnp.sum(select.astype(F32) * gates[..., None], axis=(1, 2))

    def to_experts(groups, rows):
        sent = jnp.swapaxes(rows.reshape(groups, experts_n, capacity, width), 0, 1)
        return exchange(sent.reshape(experts_n, groups * capacity, width))

    def dispatch(maps, blocks, factor):
        rows = jnp.einsum("gts,gtd->gsd", maps, blocks, preferred_element_type=F32)
        if factor is not None:
            rows = rows * factor[..., None]
        return to_experts(maps.shape[0], rows.astype(BF16))

    cut = n // 2
    cot_all = jnp.stack(cot_blocks)
    two_all = jnp.stack(normed_two_blocks)
    d_outs = [
        dispatch(both[:cut], cot_all[:cut], slot_gate[:cut]),
        dispatch(both[cut:], cot_all[cut:], slot_gate[cut:]),
    ]
    slots = [dispatch(both[:cut], two_all[:cut], None), dispatch(both[cut:], two_all[cut:], None)]

    steps = 8
    out_rows, dslot_rows, gwgu, gwd = experts(slots, d_outs, wgu, wd, steps)
    grad_w_down = gwd[:deep]

    def from_experts(rows):
        sides = []
        for side in range(2):
            part = rows.reshape(steps, 2, -1, width)[:, side].reshape(experts_n, cut * capacity, width)
            back = exchange(part).reshape(experts_n, cut, capacity, width)
            sides.append(jnp.swapaxes(back, 0, 1).reshape(cut, slots_n, width))
        return sides

    def to_owners(blocks):
        total = blocks[0].astype(F32)
        for d in range(1, n):
            total = total + shift(blocks[d].astype(BF16), n - d, n).astype(F32)
        return total

    dslot_back = from_experts(dslot_rows)
    partial = [
        jnp.einsum("gts,gsd->gtd", both[:cut], dslot_back[0], preferred_element_type=F32),
        jnp.einsum("gts,gsd->gtd", both[cut:], dslot_back[1], preferred_element_type=F32),
    ]
    grad_normed_two = to_owners([partial[d // cut][d % cut] for d in range(n)])
    grad_top = cotangent[0].astype(F32)
    grad_gain_two, grad_resid_norm = norm_backward(resid, inverse_two, gain_two, grad_normed_two)
    grad_resid = grad_top + grad_resid_norm
    grad_attn_low = grad_resid.astype(BF16)
    d_mixed = mm(grad_attn_low, w_out_all, NT).astype(BF16)
    d_mixed_heads = jnp.concatenate(
        [d_mixed[:, :own]]
        + [None] * 0
        + [
            part
            for _, part in sorted(
                (n - d, shift(d_mixed[:, d * own : (d + 1) * own], n - d, n)) for d in range(1, n)
            )
        ],
        axis=0,
    )
    grad_w_out_part = mm(mixed, grad_attn_low, TN)

    dq, dk, dv, diagonals = attention_backward(place, n, qkv, lse, d_mixed_heads, vectors)
    d_qkv = jnp.concatenate([dq, dk, dv], axis=1)
    d_normed_part = mm(d_qkv, wqkv, NT)
    grad_normed = to_owners([d_normed_part[d * tok : (d + 1) * tok] for d in range(n)])
    grad_wqkv_part = mm(normed, d_qkv, TN)
    inverse_one = lax.rsqrt(jnp.mean(tokens * tokens, axis=-1, keepdims=True) + EPSILON)
    grad_gain_one, grad_tok_norm = norm_backward(tokens, inverse_one, gain_one, grad_normed)
    grad_inputs = (grad_resid + grad_tok_norm).astype(BF16)

    out_back = from_experts(out_rows)
    moe = []
    for side in range(2):
        part = select[side * cut : (side + 1) * cut]
        picked = jnp.einsum("gcts,gsd->gctd", part, out_back[side], preferred_element_type=F32)
        moe.append(jnp.sum(picked * gates[side * cut : (side + 1) * cut, :, :, None], axis=1))
    block_out = (resid + to_owners([moe[d // cut][d % cut] for d in range(n)])).astype(BF16)

    pieces = gwgu.reshape(n, tok * 0 + width // n, gwgu.shape[1])
    got = [pick(pieces, dp)] + [
        shift(pick(pieces, lax.rem(dp + d, n)), d, n) for d in range(1, n)
    ]
    got = jnp.stack(got)
    grad_w_gate, grad_w_up = unpack_columns(jnp.stack([pick(got, order[j]) for j in range(n)]))

    def plane_sum(parts):
        return jnp.sum(exchange(parts.astype(BF16)).astype(F32), axis=0)

    go = grad_w_out_part.reshape(n, experts_n, wrows, width)
    go = plane_sum(jnp.swapaxes(go, 0, 1))
    grad_w_out = to_owners([go[d] for d in range(n)])

    gq = grad_wqkv_part.reshape(n, experts_n, wrows, 3 * own)
    gq = plane_sum(jnp.swapaxes(gq, 0, 1)).astype(BF16)
    gq_parts = [pick(gq, dp)] + [shift(pick(gq, lax.rem(dp + d, n)), d, n) for d in range(1, n)]
    gq_parts = jnp.stack(gq_parts)
    gq_all = jnp.stack([pick(gq_parts, order[j]) for j in range(n)]).astype(F32)
    gq_all = gq_all.reshape(n, wrows, 3, own).transpose(2, 1, 0, 3).reshape(3, wrows, width)

    diag_rows = jnp.roll(diagonals.reshape(heads_own, wide), tok, axis=1)
    grad_table = lax.dot_general(
        in_bucket.astype(F32), diag_rows, (((0,), (1,)), ((), ())), precision=lax.Precision.HIGHEST,
        preferred_element_type=F32,
    )
    grad_table = lax.dynamic_update_slice_in_dim(
        jnp.zeros((BUCKETS, HEADS), F32), grad_table, dp * heads_own, 1
    )
    small = jnp.concatenate([grad_gain_one, grad_gain_two, grad_table.reshape(-1)]).reshape(-1, 128)
    step = 1
    while step < experts_n:
        small = small + lax.ppermute(small, "expert", [(i, i ^ step) for i in range(experts_n)])
        step *= 2
    small = sum(gather_dp(small, n)[1:], small).reshape(-1)
    me = dp * experts_n + ex
    grad_gain_attn = lax.dynamic_slice_in_dim(small, me * n_gain, n_gain)
    grad_gain_moe = lax.dynamic_slice_in_dim(small, width + me * n_gain, n_gain)
    grad_bias = lax.dynamic_slice_in_dim(small, 2 * width + me * n_bias, n_bias)

    return (
        block_out[None],
        grad_inputs[None],
        grad_gain_attn,
        gq_all[0],
        gq_all[1],
        gq_all[2],
        grad_w_out,
        grad_bias,
        grad_gain_moe,
        grad_w_gate[None],
        grad_w_up[None],
        grad_w_down[None],
    )


def solution(mesh):
    vector = P(("dp", "expert"))
    matrix = P(("dp", "expert"), None)
    split = P("expert", "dp", None)
    return jax.shard_map(
        local,
        mesh=mesh,
        in_specs=(
            split, split, vector, matrix, matrix, matrix, matrix, vector, vector,
            split, split, split, split, P("expert", "dp"),
        ),
        out_specs=(
            split, split, vector, matrix, matrix, matrix, matrix, vector, vector,
            split, split, split,
        ),
        check_vma=False,
    )
```

```python
import functools

import jax
import jax.numpy as jnp
from jax import lax
from jax.experimental import pallas as pl
from jax.experimental.pallas import tpu as pltpu
from jax.sharding import PartitionSpec as P

HEADS = 16
HEAD_DIM = 64
BUCKETS = 32
THRESHOLDS = (12, 16, 23, 32, 46, 64, 91)
EPSILON = 1e-06
SCALE = HEAD_DIM ** (-0.5)
BF16 = jnp.bfloat16
F32 = jnp.float32
GELU_C = 0.7978845608028654
GELU_A = 0.044715
VMEM_LIMIT = 56 * 1024 * 1024

NT = (((1,), (1,)), ((), ()))
TN = (((0,), (0,)), ((), ()))
NN = (((1,), (0,)), ((), ()))


def mm(a, b, dims=NN):
    return lax.dot_general(a, b, dims, preferred_element_type=F32)


def bucket_of(offset):
    distance = jnp.abs(offset)
    banded = jnp.full(distance.shape, 8, jnp.int32)
    for cutoff in THRESHOLDS:
        banded = banded + (distance >= cutoff).astype(jnp.int32)
    nearby = jnp.where(distance < 8, distance, banded)
    return nearby + jnp.where(offset > 0, 16, 0).astype(jnp.int32)


def norm_forward(values, gain):
    inverse = lax.rsqrt(jnp.mean(values * values, axis=-1, keepdims=True) + EPSILON)
    return (inverse, (values * inverse * gain).astype(BF16))


def norm_backward(values, inverse, gain, grad_normed):
    scaled = gain * grad_normed
    grad_gain = jnp.sum(grad_normed * values * inverse, axis=0)
    grad_values = inverse * scaled - values * inverse**3 * jnp.mean(
        scaled * values, axis=-1, keepdims=True
    )
    return (grad_gain, grad_values)


def bias_tile(vec_ref, head, tile_ref):
    block, wide = tile_ref.shape
    row = jnp.broadcast_to(vec_ref[pl.ds(head, 1), :], (block, wide))
    tile_ref[...] = pltpu.roll(row, wide - block, 1, stride=1, stride_axis=0)


def tile_offset(n, block, query_block, key_block):
    return pl.multiple_of((key_block - query_block + n - 1) * block, 128)


def logits_of(n, block, query_block, q_pair, k_pair, mask, tile_ref):
    masked = jnp.where(mask, q_pair, jnp.zeros_like(q_pair))
    raw = mm(masked, k_pair, NT) * SCALE
    bias = jnp.concatenate(
        [tile_ref[:, pl.ds(tile_offset(n, block, query_block, j), block)] for j in range(n)], axis=1
    )
    return raw + bias


def diagonal_sum(tile):
    rows, wide = tile.shape
    while rows > 1:
        half = rows // 2
        tile = tile[:half] + pltpu.roll(tile[half:], wide - half, 1)
        rows = half
    return tile


def attention_backward_kernel(
    n, block, q_ref, k_ref, v_ref, lse_ref, dm_ref, vec_ref,
    dq_ref, dk_ref, dv_ref, diag_ref, tiles, sums, dk_acc, dv_acc,
):
    pair, query_block = pl.program_id(0), pl.program_id(1)

    @pl.when(query_block == 0)
    def _():
        for side in range(2):
            bias_tile(vec_ref, 2 * pair + side, tiles.at[side])
        sums[...] = jnp.zeros_like(sums)
        dk_acc[...] = jnp.zeros_like(dk_acc)
        dv_acc[...] = jnp.zeros_like(dv_acc)

    q_pair, k_pair, v_pair, dm_pair = q_ref[...], k_ref[...], v_ref[...], dm_ref[...]
    rows = k_pair.shape[0]
    lane = lax.broadcasted_iota(jnp.int32, (block, 128), 1)
    dqs, dks, dvs = [], [], []
    for side in range(2):
        mask = (lane >= HEAD_DIM) if side else (lane < HEAD_DIM)
        logits = logits_of(n, block, query_block, q_pair, k_pair, mask, tiles.at[side])
        probs = jnp.exp(logits - lse_ref[:, side * HEAD_DIM : side * HEAD_DIM + 1])
        masked = jnp.where(mask, dm_pair, jnp.zeros_like(dm_pair))
        d_probs = mm(masked, v_pair, NT)
        inner = jnp.sum(probs * d_probs, axis=-1, keepdims=True)
        d_logits = (probs * (d_probs - inner)).astype(BF16)
        dvs.append(mm(probs.astype(BF16), dm_pair, TN))
        dqs.append(mm(d_logits, k_pair))
        dks.append(mm(d_logits, q_pair, TN))
        wide = d_logits.astype(F32)
        for j in range(n):
            here = pl.ds(tile_offset(n, block, query_block, j), block)
            sums[side, :, here] += wide[:, j * block : (j + 1) * block]
    dq_ref[...] = (jnp.where(lane < HEAD_DIM, dqs[0], dqs[1]) * SCALE).astype(BF16)
    key_lane = lax.broadcasted_iota(jnp.int32, (rows, 128), 1)
    dk_acc[...] += jnp.where(key_lane < HEAD_DIM, dks[0], dks[1])
    dv_acc[...] += jnp.where(key_lane < HEAD_DIM, dvs[0], dvs[1])

    @pl.when(query_block == n - 1)
    def _():
        dk_ref[...] = (dk_acc[...] * SCALE).astype(BF16)
        dv_ref[...] = dv_acc[...].astype(BF16)
        for side in range(2):
            diag_ref[0, pl.ds(side, 1), :] = diagonal_sum(sums[side])


def attention_backward(n, qkv, lse, d_mixed, vectors):
    rows, triple = qkv.shape
    own = triple // 3
    block = rows // n
    pairs = own // 128
    wide = vectors.shape[1]
    return pl.pallas_call(
        functools.partial(attention_backward_kernel, n, block),
        grid=(pairs, n),
        in_specs=[
            pl.BlockSpec((block, 128), lambda p, i: (i, p)),
            pl.BlockSpec((rows, 128), lambda p, i: (0, pairs + p)),
            pl.BlockSpec((rows, 128), lambda p, i: (0, 2 * pairs + p)),
            pl.BlockSpec((block, 128), lambda p, i: (i, p)),
            pl.BlockSpec((block, 128), lambda p, i: (i, p)),
            pl.BlockSpec((2 * pairs, wide), lambda p, i: (0, 0)),
        ],
        out_specs=[
            pl.BlockSpec((block, 128), lambda p, i: (i, p)),
            pl.BlockSpec((rows, 128), lambda p, i: (0, p)),
            pl.BlockSpec((rows, 128), lambda p, i: (0, p)),
            pl.BlockSpec((1, 2, wide), lambda p, i: (p, 0, 0)),
        ],
        out_shape=[
            jax.ShapeDtypeStruct((rows, own), BF16),
            jax.ShapeDtypeStruct((rows, own), BF16),
            jax.ShapeDtypeStruct((rows, own), BF16),
            jax.ShapeDtypeStruct((pairs, 2, wide), F32),
        ],
        scratch_shapes=[
            pltpu.VMEM((2, block, wide), F32),
            pltpu.VMEM((2, block, wide), F32),
            pltpu.VMEM((rows, 128), F32),
            pltpu.VMEM((rows, 128), F32),
        ],
        compiler_params=pltpu.CompilerParams(vmem_limit_bytes=VMEM_LIMIT),
        cost_estimate=pl.CostEstimate(
            flops=40 * rows * rows * own, bytes_accessed=14 * rows * own, transcendentals=rows * rows * own // 64
        ),
        name="attention_backward",
    )(qkv, qkv, qkv, lse, d_mixed, vectors)


def gelu_pair(v):
    square = v * v
    t = jnp.tanh(GELU_C * (v + GELU_A * v * square))
    half = 0.5 * (1.0 + t)
    slope = half + (0.5 * GELU_C) * v * (1.0 - t * t) * (1.0 + (3.0 * GELU_A) * square)
    return v * half, slope


def expert_kernel(
    main, slots_ref, dout_ref, wgu_ref, wd_ref,
    out_ref, dslot_ref, gwgu_ref, gwd_ref, gwgu_acc, gwd_acc,
):
    step = pl.program_id(0)

    @pl.when(step == 0)
    def _():
        gwgu_acc[...] = jnp.zeros_like(gwgu_acc)
        gwd_acc[...] = jnp.zeros_like(gwd_acc)

    slots, d_out = slots_ref[0], dout_ref[0]
    rows = slots.shape[0]
    wgu, wd = wgu_ref[...], wd_ref[...]
    pre = mm(slots, wgu)
    d_hidden = mm(d_out, wd, NT)
    low_lane = lax.broadcasted_iota(jnp.int32, (rows, 128), 1) < 64
    gate, up = pre[:, :main], pre[:, main : 2 * main]
    tail = pre[:, 2 * main :]
    tail_up = pltpu.roll(tail, 64, 1)
    act, slope = gelu_pair(gate)
    act_t, slope_t = gelu_pair(tail)
    hidden_t = jnp.where(low_lane, act_t * tail_up, 0.0)
    hidden = jnp.concatenate([(act * up).astype(BF16), hidden_t.astype(BF16)], axis=1)
    out_ref[0] = mm(hidden, wd).astype(BF16)
    gwd_acc[...] += mm(hidden, d_out, TN)
    dh, dh_t = d_hidden[:, :main], d_hidden[:, main:]
    d_gate = dh * up * slope
    d_up = dh * act
    d_tail = jnp.where(low_lane, dh_t * tail_up * slope_t, pltpu.roll(dh_t * act_t, 64, 1))
    d_pre = jnp.concatenate([d_gate.astype(BF16), d_up.astype(BF16), d_tail.astype(BF16)], axis=1)
    dslot_ref[0] = mm(d_pre, wgu, NT).astype(BF16)
    gwgu_acc[...] += mm(slots, d_pre, TN)

    @pl.when(step == pl.num_programs(0) - 1)
    def _():
        gwgu_ref[...] = gwgu_acc[...].astype(BF16)
        gwd_ref[...] = gwd_acc[...]


def experts(slots, d_outs, wgu, wd, steps):
    width, columns = wgu.shape
    deep = wd.shape[0]
    main = (columns - 128) // 2
    slots = slots.reshape(steps, -1, width)
    d_outs = d_outs.reshape(steps, -1, width)
    half = slots.shape[1]
    rows = half * steps
    part = pl.BlockSpec((1, half, width), lambda i: (i, 0, 0))
    return pl.pallas_call(
        functools.partial(expert_kernel, main),
        grid=(steps,),
        in_specs=[
            part, part,
            pl.BlockSpec((width, columns), lambda i: (0, 0)),
            pl.BlockSpec((deep, width), lambda i: (0, 0)),
        ],
        out_specs=[
            part, part,
            pl.BlockSpec((width, columns), lambda i: (0, 0)),
            pl.BlockSpec((deep, width), lambda i: (0, 0)),
        ],
        out_shape=[
            jax.ShapeDtypeStruct((steps, half, width), BF16),
            jax.ShapeDtypeStruct((steps, half, width), BF16),
            jax.ShapeDtypeStruct((width, columns), BF16),
            jax.ShapeDtypeStruct((deep, width), F32),
        ],
        scratch_shapes=[
            pltpu.VMEM((width, columns), F32),
            pltpu.VMEM((deep, width), F32),
        ],
        compiler_params=pltpu.CompilerParams(vmem_limit_bytes=VMEM_LIMIT),
        cost_estimate=pl.CostEstimate(
            flops=6 * rows * width * (columns + deep),
            bytes_accessed=8 * rows * width + 8 * width * columns,
            transcendentals=rows * deep,
        ),
        name="experts",
    )(slots, d_outs, wgu, wd)


def unpack_kernel(n, piece, in_ref, gate_ref, up_ref):
    main = piece // 128 * 128
    rest = piece - main
    gates, ups = [], []
    for j in range(n):
        block = in_ref[j].astype(F32)
        gates += [block[:, :main], block[:, 2 * main : 2 * main + rest]]
        ups += [block[:, main : 2 * main], block[:, 2 * main + rest :]]
    gate_ref[...] = jnp.concatenate(gates, axis=1)
    up_ref[...] = jnp.concatenate(ups, axis=1)


def unpack_columns(blocks):
    n, rows, both = blocks.shape
    piece = both // 2
    step = min(rows, 64)
    total = n * piece
    return pl.pallas_call(
        functools.partial(unpack_kernel, n, piece),
        grid=(rows // step,),
        in_specs=[pl.BlockSpec((n, step, both), lambda i: (0, i, 0))],
        out_specs=[pl.BlockSpec((step, total), lambda i: (i, 0))] * 2,
        out_shape=[jax.ShapeDtypeStruct((rows, total), F32)] * 2,
        compiler_params=pltpu.CompilerParams(vmem_limit_bytes=VMEM_LIMIT),
        cost_estimate=pl.CostEstimate(flops=0, bytes_accessed=12 * rows * total, transcendentals=0),
        name="unpack_columns",
    )(blocks)


MESH = pl.DeviceIdType.MESH


def remote(src, dst, send, recv, target):
    return pltpu.make_async_remote_copy(
        src_ref=src, dst_ref=dst, send_sem=send, recv_sem=recv, device_id=target, device_id_type=MESH
    )


def greet(n, ne, dp, ex):
    barrier = pltpu.get_barrier_semaphore()
    for d in range(1, n):
        pl.semaphore_signal(barrier, inc=1, device_id=(lax.rem(dp + d, n), ex), device_id_type=MESH)
    for k in range(1, ne):
        pl.semaphore_signal(barrier, inc=1, device_id=(dp, lax.rem(ex + k, ne)), device_id_type=MESH)
    pl.semaphore_wait(barrier, n + ne - 2)


class Chain:
    def __init__(self, n, dp, ex, own, buffer, send, recv):
        self.n, self.dp, self.ex, self.own = n, dp, ex, own
        self.buffer, self.send_sem, self.recv_sem = buffer, send, recv

    def block(self, hop, side):
        return lax.rem(self.dp + self.n + hop * (2 * side - 1), self.n)

    def copy(self, hop, side, first=False):
        at = self.block(hop, side)
        target = lax.rem(self.dp + self.n + 1 - 2 * side, self.n)
        return remote(
            self.own if first else self.buffer.at[at], self.buffer.at[at],
            self.send_sem.at[hop, side], self.recv_sem.at[hop, side], (target, self.ex),
        )

    def has_next(self, side):
        return (self.dp + 1 < self.n) if side == 0 else (self.dp > 0)

    def start(self):
        for side in range(2):
            @pl.when(self.has_next(side))
            def _():
                self.copy(0, side, True).start()

    def held(self, hop, side):
        return (self.dp > hop) if side == 0 else (self.dp + 1 + hop < self.n)

    def arrive(self, hop, side):
        at = self.block(hop + 1, side)
        remote(
            self.buffer.at[at], self.buffer.at[at], self.send_sem.at[hop, side], self.recv_sem.at[hop, side],
            (self.dp, self.ex),
        ).wait_recv()

        @pl.when(self.has_next(side))
        def _():
            self.copy(hop + 1, side).start()

        return at

    def finish(self):
        for hop in range(self.n - 1):
            for side in range(2):
                mine = self.has_next(side)
                if hop:
                    mine = mine & self.held(hop - 1, side)

                @pl.when(mine)
                def _():
                    self.copy(hop, side, hop == 0).wait_send()


def start_kernel(
    n, ne, cap, cap_pad, piece,
    x, wq, wk, wv, extra, wo, meta_in, wg, wu,
    x_all, lq, lk, lv, lext, lwo, meta_all, packed,
    sq, sk, sv, sext, swo, smeta,
    line_send, line_recv, plane_send, plane_recv, core_send, core_recv, chain_send, chain_recv, own_sem,
):
    dp, ex = lax.axis_index("dp"), lax.axis_index("expert")
    own = sq.shape[2]
    greet(n, ne, dp, ex)
    chain = Chain(n, dp, ex, x, x_all, chain_send, chain_recv)

    def column(ref, t):
        return ref.at[:, pl.ds(pl.multiple_of(t * own, 128), own)]

    def line(kind, d):
        t = lax.rem(dp + d, n)
        src, dst = [
            (column(wq, t), sq.at[dp]), (column(wk, t), sk.at[dp]), (column(wv, t), sv.at[dp]),
            (extra, sext.at[dp]), (wo, swo.at[dp]), (smeta, meta_all.at[dp]),
        ][kind]
        return remote(src, dst, line_send.at[kind, d], line_recv.at[kind, d], (t, ex))

    for d in range(1, n):
        for kind in range(4):
            line(kind, d).start()
    chain.start()
    for d in range(1, n):
        line(4, d).start()
    keep = pltpu.make_async_copy(x, x_all.at[dp], own_sem.at[0])
    keep.start()
    sq[dp] = wq[:, pl.ds(pl.multiple_of(dp * own, 128), own)]
    sk[dp] = wk[:, pl.ds(pl.multiple_of(dp * own, 128), own)]
    sv[dp] = wv[:, pl.ds(pl.multiple_of(dp * own, 128), own)]
    sext[dp] = extra[...]
    swo[dp] = wo[...]

    tok = meta_in.shape[1]
    routes = meta_in[...]
    ids = lax.broadcasted_iota(jnp.int32, (ne, tok), 0)
    first = (ids == routes[0:1, :]).astype(F32)
    second = (ids == routes[1:2, :]).astype(F32)
    before = (
        lax.broadcasted_iota(jnp.int32, (tok, tok), 0) < lax.broadcasted_iota(jnp.int32, (tok, tok), 1)
    ).astype(BF16)
    counts = mm((first + second).astype(BF16), before)
    slot_a = jnp.sum(counts * first, axis=0, keepdims=True)
    slot_b = jnp.sum((counts + first) * second, axis=0, keepdims=True)
    wide = routes.astype(F32)
    dest_a = jnp.where(slot_a < cap, wide[0:1, :] * cap_pad + slot_a, -1.0)
    dest_b = jnp.where(slot_b < cap, wide[1:2, :] * cap_pad + slot_b, -1.0)
    gate = wide[2:3, :] * (1.0 / 65536.0)
    smeta[...] = jnp.concatenate([dest_a, dest_b, gate, jnp.zeros((5, tok), F32)], axis=0)
    for d in range(1, n):
        line(5, d).start()
    keep_meta = pltpu.make_async_copy(smeta, meta_all.at[dp], own_sem.at[1])
    keep_meta.start()

    pairs = [(sq, lq), (sk, lk), (sv, lv), (sext, lext), (swo, lwo)]
    partner = ex + 1 - 2 * lax.rem(ex, 2)

    def plane(kind, k):
        src, dst = pairs[kind]
        return remote(
            src, dst.at[:, ex], plane_send.at[kind, k], plane_recv.at[kind, k],
            (dp, lax.rem(ex + 2 * k, ne)),
        )

    def core(kind, k):
        src, dst = pairs[kind]
        at = lax.rem(ex + ne - 2 * k, ne)
        return remote(
            src if k == 0 else dst.at[:, at], dst.at[:, at],
            core_send.at[kind, k], core_recv.at[kind, k], (dp, partner),
        )

    def spread(kind):
        for d in range(1, n):
            line(kind, d).wait_recv()
        for k in range(1, ne // 2):
            plane(kind, k).start()
        core(kind, 0).start()
        pltpu.make_async_copy(pairs[kind][0], pairs[kind][1].at[:, ex], own_sem.at[2 + kind]).start()

    for kind in range(4):
        spread(kind)

    main = piece // 128 * 128
    step = min(wg.shape[0], 64)

    @pl.loop(0, wg.shape[0] // step)
    def _(i):
        rows = pl.ds(pl.multiple_of(i * step, step), step)
        gate_w, up_w = wg[rows, :], wu[rows, :]
        for j in range(n):
            g = gate_w[:, j * piece : (j + 1) * piece]
            u = up_w[:, j * piece : (j + 1) * piece]
            packed[j, rows, :] = jnp.concatenate([g[:, :main], u[:, :main], g[:, main:], u[:, main:]], axis=1)

    spread(4)

    def pass_on(kind):
        for k in range(1, ne // 2):
            plane(kind, k).wait_recv()
            core(kind, k).start()

    def hop(h):
        for side in range(2):
            @pl.when(chain.held(h, side))
            def _():
                chain.arrive(h, side)

    hop(0)
    for kind in range(4):
        pass_on(kind)
    for h in range(1, n - 1):
        hop(h)
        if h == 1:
            pass_on(4)
    if n < 3:
        pass_on(4)
    for kind in range(5):
        for k in range(ne // 2):
            core(kind, k).wait()
        for k in range(1, ne // 2):
            plane(kind, k).wait_send()
        pltpu.make_async_copy(pairs[kind][0], pairs[kind][1].at[:, ex], own_sem.at[2 + kind]).wait()
    for d in range(1, n):
        for kind in range(6):
            line(kind, d).wait_send()
        line(5, d).wait_recv()
    chain.finish()
    keep.wait()
    keep_meta.wait()


def whole(array):
    return pl.BlockSpec(memory_space=pltpu.VMEM)


ANY = pl.BlockSpec(memory_space=pl.ANY)
VM = pl.BlockSpec(memory_space=pltpu.VMEM)


def start(n, ne, cap, cap_pad, x, wq, wk, wv, extra, wo, meta_in, wg, wu):
    tok, width = x.shape
    wrows = wq.shape[0]
    own = width // n
    piece = wg.shape[1] // n
    return pl.pallas_call(
        functools.partial(start_kernel, n, ne, cap, cap_pad, piece),
        in_specs=[VM] * 9,
        out_specs=[ANY] * 7 + [VM],
        out_shape=[
            jax.ShapeDtypeStruct((n, tok, width), BF16),
            jax.ShapeDtypeStruct((n, ne, wrows, own), BF16),
            jax.ShapeDtypeStruct((n, ne, wrows, own), BF16),
            jax.ShapeDtypeStruct((n, ne, wrows, own), BF16),
            jax.ShapeDtypeStruct((n, ne, 16, own), BF16),
            jax.ShapeDtypeStruct((n, ne, wrows, width), BF16),
            jax.ShapeDtypeStruct((n, 8, tok), F32),
            jax.ShapeDtypeStruct((n, tok, 2 * piece), BF16),
        ],
        scratch_shapes=[
            pltpu.VMEM((n, wrows, own), BF16),
            pltpu.VMEM((n, wrows, own), BF16),
            pltpu.VMEM((n, wrows, own), BF16),
            pltpu.VMEM((n, 16, own), BF16),
            pltpu.VMEM((n, wrows, width), BF16),
            pltpu.VMEM((8, tok), F32),
            pltpu.SemaphoreType.DMA((6, n)),
            pltpu.SemaphoreType.DMA((6, n)),
            pltpu.SemaphoreType.DMA((5, ne // 2)),
            pltpu.SemaphoreType.DMA((5, ne // 2)),
            pltpu.SemaphoreType.DMA((5, ne // 2)),
            pltpu.SemaphoreType.DMA((5, ne // 2)),
            pltpu.SemaphoreType.DMA((n, 2)),
            pltpu.SemaphoreType.DMA((n, 2)),
            pltpu.SemaphoreType.DMA((7,)),
        ],
        compiler_params=pltpu.CompilerParams(
            collective_id=1, has_side_effects=True, vmem_limit_bytes=VMEM_LIMIT
        ),
        name="start",
    )(x, wq, wk, wv, extra, wo, meta_in, wg, wu)


def forward_kernel(
    n, ne, cap_pad,
    x_all, wq, wk, wv, wo, gain_one, gain_two, vectors, cot, meta_all, packed,
    normed, qkv, lse, mixed, resid, slots, d_outs, wgu,
    heads, mixed_in, tiles, cot_all, two_all, two_own, two_rows, cot_rows,
    w_send, w_recv, m_send, m_recv, c_send, c_recv, t_send, t_recv,
    pc_send, pc_recv, pt_send, pt_recv, own_sem,
):
    dp, ex = lax.axis_index("dp"), lax.axis_index("expert")
    block, width = cot.shape
    own = heads.shape[1]
    pairs_n = own // 128
    slots_n = ne * cap_pad
    greet(n, ne, dp, ex)

    def weights(d):
        t = lax.rem(dp + d, n)
        return remote(packed.at[t], wgu.at[dp], w_send.at[d], w_recv.at[d], (t, ex))

    cots = Chain(n, dp, ex, cot, cot_all, c_send, c_recv)
    twos = Chain(n, dp, ex, two_own, two_all, t_send, t_recv)
    cots.start()
    keep_w = pltpu.make_async_copy(packed.at[dp], wgu.at[dp], own_sem.at[0])
    keep_w.start()

    def to_plane(rows, land, send, recv, group, k):
        peer = lax.rem(ex + k, ne)
        return remote(
            rows.at[group, pl.ds(pl.multiple_of(peer * cap_pad, 16), cap_pad)], land.at[group, ex],
            send.at[group, k], recv.at[group, k], (dp, peer),
        )

    def kept(rows, land, group, sem):
        return pltpu.make_async_copy(
            rows.at[group, pl.ds(pl.multiple_of(ex * cap_pad, 16), cap_pad)], land.at[group, ex], sem.at[group, 0]
        )

    def dispatch(group, tokens, rows, land, send, recv, weigh):
        meta = meta_all[group]
        ids = lax.broadcasted_iota(jnp.int32, (slots_n, block), 0).astype(F32)
        hit_a, hit_b = ids == meta[0:1, :], ids == meta[1:2, :]
        chosen = jnp.where(hit_a | hit_b, 1.0, 0.0).astype(BF16)
        found = mm(chosen, tokens)
        if weigh:
            gate = meta[2:3, :]
            factor = jnp.sum(
                jnp.where(hit_a, gate, 0.0) + jnp.where(hit_b, 1.0 - gate, 0.0), axis=1, keepdims=True
            )
            found = found * factor
        rows[group] = found.astype(BF16)
        for k in range(1, ne):
            to_plane(rows, land, send, recv, group, k).start()
        kept(rows, land, group, send).start()

    @pl.loop(0, n)
    def _(j):
        at = pl.ds(pl.multiple_of(j * block, block), block)
        xf = x_all[j].astype(F32)
        inverse = lax.rsqrt(jnp.mean(xf * xf, axis=-1, keepdims=True) + EPSILON)
        low = (xf * inverse * gain_one[...]).astype(BF16)
        normed[at, :] = low
        for w, ref in enumerate((wq, wk, wv)):
            qkv[at, w * own : (w + 1) * own] = mm(low, ref[...]).astype(BF16)

    def attend(pair):
        for side in range(2):
            bias_tile(vectors, 2 * pair + side, tiles.at[side])
        lane = lax.broadcasted_iota(jnp.int32, (block, 128), 1)
        low_half = lane < HEAD_DIM
        k_pair = qkv[:, own + pair * 128 : own + (pair + 1) * 128]
        v_pair = qkv[:, 2 * own + pair * 128 : 2 * own + (pair + 1) * 128]

        @pl.loop(0, n)
        def _(i):
            at = pl.ds(pl.multiple_of(i * block, block), block)
            q_pair = qkv[at, pair * 128 : (pair + 1) * 128]
            outs, logs = [], []
            for side in range(2):
                mask = low_half if side == 0 else jnp.logical_not(low_half)
                logits = logits_of(n, block, i, q_pair, k_pair, mask, tiles.at[side])
                row_max = jnp.max(logits, axis=-1, keepdims=True)
                exponent = jnp.exp(logits - row_max)
                total = jnp.sum(exponent, axis=-1, keepdims=True)
                probs_low = (exponent * (1.0 / total)).astype(BF16)
                outs.append(mm(probs_low, v_pair))
                logs.append(jnp.broadcast_to(row_max + jnp.log(total), (block, 128)))
            heads[at, pair * 128 : (pair + 1) * 128] = jnp.where(low_half, outs[0], outs[1]).astype(BF16)
            lse[at, pair * 128 : (pair + 1) * 128] = jnp.where(low_half, logs[0], logs[1])

    def hop(chain, h, then):
        for side in range(2):
            @pl.when(chain.held(h, side))
            def _():
                then(chain.arrive(h, side))

    attend(0)
    hop(cots, 0, lambda at: None)
    for d in range(1, n):
        weights(d).start()
    for pair in range(1, pairs_n):
        attend(pair)

    def give(d):
        t = lax.rem(dp + d, n)
        return remote(
            heads.at[pl.ds(pl.multiple_of(t * block, block), block)], mixed_in.at[dp], m_send.at[d], m_recv.at[d],
            (t, ex),
        )

    for d in range(1, n):
        give(d).start()
    mixed_in[dp] = heads[pl.ds(pl.multiple_of(dp * block, block), block), :]
    dispatch(dp, cot[...], cot_rows, d_outs, pc_send, pc_recv, True)
    for h in range(1, n - 1):
        hop(cots, h, lambda at: None)
    cots.finish()
    for d in range(1, n):
        give(d).wait()
    mixed[...] = jnp.concatenate([mixed_in[j] for j in range(n)], axis=1)
    total = x_all[dp].astype(F32) + mm(mixed[...], wo[...])
    resid[...] = total
    inverse = lax.rsqrt(jnp.mean(total * total, axis=-1, keepdims=True) + EPSILON)
    two_own[...] = (total * inverse * gain_two[...]).astype(BF16)
    twos.start()

    def send_two(group, tokens):
        dispatch(group, tokens, two_rows, slots, pt_send, pt_recv, False)

    send_two(dp, two_own[...])
    for j in range(1, n):
        at = lax.rem(dp + j, n)
        dispatch(at, cot_all[at], cot_rows, d_outs, pc_send, pc_recv, True)
        hop(twos, j - 1, lambda group: send_two(group, two_all[group]))
    twos.finish()
    keep_w.wait()
    for d in range(1, n):
        weights(d).wait()
    for rows, land, send, recv in (
        (two_rows, slots, pt_send, pt_recv), (cot_rows, d_outs, pc_send, pc_recv),
    ):
        @pl.loop(0, n)
        def _(group):
            kept(rows, land, group, send).wait()
            for k in range(1, ne):
                to_plane(rows, land, send, recv, group, k).wait()


def forward(n, ne, cap_pad, x_all, wq, wk, wv, wo, gain_one, gain_two, vectors, cot, meta_all, packed):
    tok, width = cot.shape
    own = wq.shape[1]
    wide = vectors.shape[1]
    both = packed.shape[2]
    slots_n = ne * cap_pad
    sem = pltpu.SemaphoreType.DMA
    return pl.pallas_call(
        functools.partial(forward_kernel, n, ne, cap_pad),
        in_specs=[VM] * 10 + [ANY],
        out_specs=[VM] * 5 + [ANY] * 3,
        out_shape=[
            jax.ShapeDtypeStruct((n * tok, width), BF16),
            jax.ShapeDtypeStruct((n * tok, 3 * own), BF16),
            jax.ShapeDtypeStruct((n * tok, own), F32),
            jax.ShapeDtypeStruct((tok, width), BF16),
            jax.ShapeDtypeStruct((tok, width), F32),
            jax.ShapeDtypeStruct((n, ne, cap_pad, width), BF16),
            jax.ShapeDtypeStruct((n, ne, cap_pad, width), BF16),
            jax.ShapeDtypeStruct((n, tok, both), BF16),
        ],
        scratch_shapes=[
            pltpu.VMEM((n * tok, own), BF16),
            pltpu.VMEM((n, tok, own), BF16),
            pltpu.VMEM((2, tok, wide), F32),
            pltpu.VMEM((n, tok, width), BF16),
            pltpu.VMEM((n, tok, width), BF16),
            pltpu.VMEM((tok, width), BF16),
            pltpu.VMEM((n, slots_n, width), BF16),
            pltpu.VMEM((n, slots_n, width), BF16),
            sem((n,)), sem((n,)), sem((n,)), sem((n,)),
            sem((n, 2)), sem((n, 2)), sem((n, 2)), sem((n, 2)),
            sem((n, ne)), sem((n, ne)), sem((n, ne)), sem((n, ne)),
            sem((1,)),
        ],
        compiler_params=pltpu.CompilerParams(
            collective_id=2, has_side_effects=True, vmem_limit_bytes=VMEM_LIMIT
        ),
        name="forward",
    )(x_all, wq, wk, wv, wo, gain_one, gain_two, vectors, cot, meta_all, packed)


def shift(value, distance, n):
    return lax.ppermute(value, "dp", [(i, (i + distance) % n) for i in range(n)])


def pick(stacked, index):
    return lax.dynamic_index_in_dim(stacked, index, 0, keepdims=False)


def exchange(value):
    return lax.all_to_all(value, "expert", split_axis=0, concat_axis=0, tiled=True)


def trade(blocks, n, dp):
    got = jnp.stack([pick(blocks, dp)] + [shift(pick(blocks, lax.rem(dp + d, n)), d, n) for d in range(1, n)])
    return jnp.stack([pick(got, lax.rem(dp - j + n, n)) for j in range(n)])


def to_owners(blocks, n, dp):
    total = pick(blocks, dp).astype(F32)
    for d in range(1, n):
        total = total + shift(pick(blocks, lax.rem(dp + d, n)).astype(BF16), d, n).astype(F32)
    return total


def local(
    inputs, cotangent, gain_attn, w_query, w_key, w_value, w_out, position_bias,
    gain_moe, w_gate, w_up, w_down, routes, gate_fixed,
):
    n = lax.axis_size("dp")
    experts_n = lax.axis_size("expert")
    dp = lax.axis_index("dp")
    ex = lax.axis_index("expert")
    tok, width = inputs.shape[1:]
    length = n * tok
    own = HEADS * HEAD_DIM // n
    heads_own = HEADS // n
    wrows = w_query.shape[0]
    capacity = 5 * tok // (2 * experts_n)
    cap_pad = -(-capacity // 16) * 16
    slots_n = experts_n * cap_pad

    n_gain, n_bias = gain_attn.shape[0], position_bias.shape[0]
    extra = jnp.concatenate([gain_attn, gain_moe, position_bias])
    extra = jnp.zeros((16, own), BF16).at[0, : 2 * n_gain + n_bias].set(extra)
    meta_in = jnp.concatenate([routes[0].T, gate_fixed], axis=0)
    x_all, wq, wk, wv, extras, wo, meta_all, packed = start(
        n, experts_n, capacity, cap_pad,
        inputs[0], w_query, w_key, w_value, extra, w_out, meta_in, w_gate[0], w_up[0],
    )
    wq, wk, wv = (w.reshape(width, own) for w in (wq, wk, wv))
    wo = wo.reshape(width, width)
    extras = extras[:, :, 0]
    gain_one = extras[:, :, :n_gain].reshape(1, -1).astype(F32)
    gain_two = extras[:, :, n_gain : 2 * n_gain].reshape(1, -1).astype(F32)
    table = extras[:, :, 2 * n_gain : 2 * n_gain + n_bias].reshape(BUCKETS, HEADS)
    table = lax.dynamic_slice_in_dim(table, dp * heads_own, heads_own, 1)
    wide = 2 * length
    offsets = jnp.arange(wide, dtype=jnp.int32) - length
    in_bucket = (bucket_of(offsets)[:, None] == jnp.arange(BUCKETS, dtype=jnp.int32)).astype(BF16)
    in_bucket = jnp.where(jnp.abs(offsets)[:, None] < length, in_bucket, jnp.zeros_like(in_bucket))
    vectors = mm(table, in_bucket, (((0,), (1,)), ((), ())))

    normed, qkv, lse, mixed, resid, slots, d_outs, wgu = forward(
        n, experts_n, cap_pad, x_all, wq, wk, wv, wo, gain_one, gain_two, vectors, cotangent[0], meta_all, packed
    )
    wgu = wgu.reshape(width, -1)
    deep = w_down.shape[1]
    padded = -(-deep // 128) * 128
    wd = jnp.pad(w_down[0], ((0, padded - deep), (0, 0)))
    steps = 2 * n
    out_rows, dslot_rows, gwgu, gwd = experts(slots, d_outs, wgu, wd, steps)
    grad_w_down = gwd[:deep]

    dest = meta_all[:, :2].astype(jnp.int32)
    select = (dest[..., None] == jnp.arange(slots_n, dtype=jnp.int32)).astype(BF16)
    both = select[:, 0] + select[:, 1]
    first_gate = meta_all[:, 2]
    gates = jnp.stack([first_gate, 1.0 - first_gate], axis=1)

    def from_experts(rows):
        rows = jnp.swapaxes(rows.reshape(n, experts_n, cap_pad, width), 0, 1)
        return jnp.swapaxes(exchange(rows), 0, 1).reshape(n, slots_n, width)

    got = trade(gwgu.reshape(n, width // n, gwgu.shape[1]), n, dp)
    dslot_back = from_experts(dslot_rows)
    dslot_back, got, out_rows = lax.optimization_barrier((dslot_back, got, out_rows))
    partial = jnp.einsum("gts,gsd->gtd", both, dslot_back, preferred_element_type=F32)
    grad_normed_two = to_owners(partial, n, dp)
    gain_one, gain_two = gain_one[0], gain_two[0]
    grad_top = cotangent[0].astype(F32)
    inverse_two = lax.rsqrt(jnp.mean(resid * resid, axis=-1, keepdims=True) + EPSILON)
    grad_gain_two, grad_resid_norm = norm_backward(resid, inverse_two, gain_two, grad_normed_two)
    grad_resid = grad_top + grad_resid_norm
    grad_attn_low = grad_resid.astype(BF16)
    d_mixed = mm(grad_attn_low, wo, NT).astype(BF16)
    d_mixed_heads = trade(jnp.swapaxes(d_mixed.reshape(tok, n, own), 0, 1), n, dp).reshape(length, own)
    grad_w_out_part = mm(mixed, grad_attn_low, TN)

    out_back = from_experts(out_rows)
    out_back, d_mixed_heads = lax.optimization_barrier((out_back, d_mixed_heads))
    picked = jnp.einsum("gcts,gsd->gctd", select, out_back, preferred_element_type=F32)
    moe_sum = to_owners(jnp.sum(picked * gates[..., None], axis=1), n, dp)

    dq, dk, dv, diagonals = attention_backward(n, qkv, lse, d_mixed_heads, vectors)
    d_normed_part = mm(dq, wq, NT) + mm(dk, wk, NT) + mm(dv, wv, NT)
    d_normed_part, moe_sum = lax.optimization_barrier((d_normed_part, moe_sum))
    grad_normed = to_owners(d_normed_part.reshape(n, tok, width), n, dp)
    d_qkv = jnp.concatenate([dq, dk, dv], axis=1)
    grad_wqkv_part = mm(normed, d_qkv, TN)
    tokens = inputs[0].astype(F32)
    inverse_one = lax.rsqrt(jnp.mean(tokens * tokens, axis=-1, keepdims=True) + EPSILON)
    grad_gain_one, grad_tok_norm = norm_backward(tokens, inverse_one, gain_one, grad_normed)
    grad_inputs = (grad_resid + grad_tok_norm).astype(BF16)
    block_out = (resid + moe_sum).astype(BF16)

    grad_w_gate, grad_w_up = unpack_columns(got)

    def plane_sum(parts):
        return jnp.sum(exchange(parts.astype(BF16)).astype(F32), axis=0)

    go = grad_w_out_part.reshape(n, experts_n, wrows, width)
    go = plane_sum(jnp.swapaxes(go, 0, 1))
    grad_w_out = to_owners(go, n, dp)

    gq = grad_wqkv_part.reshape(n, experts_n, wrows, 3 * own)
    gq = plane_sum(jnp.swapaxes(gq, 0, 1)).astype(BF16)
    gq_all = trade(gq, n, dp).astype(F32)
    gq_all = gq_all.reshape(n, wrows, 3, own).transpose(2, 1, 0, 3).reshape(3, wrows, width)

    diag_rows = jnp.roll(diagonals.reshape(heads_own, wide), tok, axis=1)
    grad_table = lax.dot_general(
        in_bucket.astype(F32), diag_rows, (((0,), (1,)), ((), ())), precision=lax.Precision.HIGHEST,
        preferred_element_type=F32,
    )
    grad_table = lax.dynamic_update_slice_in_dim(
        jnp.zeros((BUCKETS, HEADS), F32), grad_table, dp * heads_own, 1
    )
    small = jnp.concatenate([grad_gain_one, grad_gain_two, grad_table.reshape(-1)]).reshape(-1, 128)
    step = 1
    while step < experts_n:
        small = small + lax.ppermute(small, "expert", [(i, i ^ step) for i in range(experts_n)])
        step *= 2
    small = (small + sum(shift(small, d, n) for d in range(1, n))).reshape(-1)
    me = dp * experts_n + ex
    grad_gain_attn = lax.dynamic_slice_in_dim(small, me * n_gain, n_gain)
    grad_gain_moe = lax.dynamic_slice_in_dim(small, width + me * n_gain, n_gain)
    grad_bias = lax.dynamic_slice_in_dim(small, 2 * width + me * n_bias, n_bias)

    return (
        block_out[None],
        grad_inputs[None],
        grad_gain_attn,
        gq_all[0],
        gq_all[1],
        gq_all[2],
        grad_w_out,
        grad_bias,
        grad_gain_moe,
        grad_w_gate[None],
        grad_w_up[None],
        grad_w_down[None],
    )


def solution(mesh):
    vector = P(("dp", "expert"))
    matrix = P(("dp", "expert"), None)
    split = P("expert", "dp", None)
    return jax.shard_map(
        local,
        mesh=mesh,
        in_specs=(
            split, split, vector, matrix, matrix, matrix, matrix, vector, vector,
            split, split, split, split, P("expert", "dp"),
        ),
        out_specs=(
            split, split, vector, matrix, matrix, matrix, matrix, vector, vector,
            split, split, split,
        ),
        check_vma=False,
    )
```

```python
import functools

import jax
import jax.numpy as jnp
from jax import lax
from jax.experimental import pallas as pl
from jax.experimental.pallas import tpu as pltpu
from jax.sharding import PartitionSpec as P

HEADS = 16
HEAD_DIM = 64
BUCKETS = 32
THRESHOLDS = (12, 16, 23, 32, 46, 64, 91)
EPSILON = 1e-06
SCALE = HEAD_DIM ** (-0.5)
BF16 = jnp.bfloat16
F32 = jnp.float32
GELU_C = 0.7978845608028654
GELU_A = 0.044715
VMEM_LIMIT = 56 * 1024 * 1024

NT = (((1,), (1,)), ((), ()))
TN = (((0,), (0,)), ((), ()))
NN = (((1,), (0,)), ((), ()))


def mm(a, b, dims=NN):
    return lax.dot_general(a, b, dims, preferred_element_type=F32)


def bucket_of(offset):
    distance = jnp.abs(offset)
    banded = jnp.full(distance.shape, 8, jnp.int32)
    for cutoff in THRESHOLDS:
        banded = banded + (distance >= cutoff).astype(jnp.int32)
    nearby = jnp.where(distance < 8, distance, banded)
    return nearby + jnp.where(offset > 0, 16, 0).astype(jnp.int32)


def norm_forward(values, gain):
    inverse = lax.rsqrt(jnp.mean(values * values, axis=-1, keepdims=True) + EPSILON)
    return (inverse, (values * inverse * gain).astype(BF16))


def norm_backward(values, inverse, gain, grad_normed):
    scaled = gain * grad_normed
    grad_gain = jnp.sum(grad_normed * values * inverse, axis=0)
    grad_values = inverse * scaled - values * inverse**3 * jnp.mean(
        scaled * values, axis=-1, keepdims=True
    )
    return (grad_gain, grad_values)


def bias_tile(vec_ref, head, tile_ref):
    block, wide = tile_ref.shape
    row = jnp.broadcast_to(vec_ref[pl.ds(head, 1), :], (block, wide))
    tile_ref[...] = pltpu.roll(row, wide - block, 1, stride=1, stride_axis=0)


def tile_offset(n, block, query_block, key_block):
    return pl.multiple_of((key_block - query_block + n - 1) * block, 128)


def logits_of(n, block, query_block, q_pair, k_pair, mask, tile_ref):
    masked = jnp.where(mask, q_pair, jnp.zeros_like(q_pair))
    raw = mm(masked, k_pair, NT) * SCALE
    bias = jnp.concatenate(
        [tile_ref[:, pl.ds(tile_offset(n, block, query_block, j), block)] for j in range(n)], axis=1
    )
    return raw + bias


def diagonal_sum(tile):
    rows, wide = tile.shape
    while rows > 1:
        half = rows // 2
        tile = tile[:half] + pltpu.roll(tile[half:], wide - half, 1)
        rows = half
    return tile


def attention_backward_kernel(
    n, block, q_ref, k_ref, v_ref, lse_ref, dm_ref, vec_ref,
    dq_ref, dk_ref, dv_ref, diag_ref, tiles, sums, dk_acc, dv_acc,
):
    pair, query_block = pl.program_id(0), pl.program_id(1)

    @pl.when(query_block == 0)
    def _():
        for side in range(2):
            bias_tile(vec_ref, 2 * pair + side, tiles.at[side])
        sums[...] = jnp.zeros_like(sums)
        dk_acc[...] = jnp.zeros_like(dk_acc)
        dv_acc[...] = jnp.zeros_like(dv_acc)

    q_pair, k_pair, v_pair, dm_pair = q_ref[...], k_ref[...], v_ref[...], dm_ref[...]
    rows = k_pair.shape[0]
    lane = lax.broadcasted_iota(jnp.int32, (block, 128), 1)
    dqs, dks, dvs = [], [], []
    for side in range(2):
        mask = (lane >= HEAD_DIM) if side else (lane < HEAD_DIM)
        logits = logits_of(n, block, query_block, q_pair, k_pair, mask, tiles.at[side])
        probs = jnp.exp(logits - lse_ref[:, side * HEAD_DIM : side * HEAD_DIM + 1])
        masked = jnp.where(mask, dm_pair, jnp.zeros_like(dm_pair))
        d_probs = mm(masked, v_pair, NT)
        inner = jnp.sum(probs * d_probs, axis=-1, keepdims=True)
        d_logits = (probs * (d_probs - inner)).astype(BF16)
        dvs.append(mm(probs.astype(BF16), dm_pair, TN))
        dqs.append(mm(d_logits, k_pair))
        dks.append(mm(d_logits, q_pair, TN))
        wide = d_logits.astype(F32)
        for j in range(n):
            here = pl.ds(tile_offset(n, block, query_block, j), block)
            sums[side, :, here] += wide[:, j * block : (j + 1) * block]
    dq_ref[...] = (jnp.where(lane < HEAD_DIM, dqs[0], dqs[1]) * SCALE).astype(BF16)
    key_lane = lax.broadcasted_iota(jnp.int32, (rows, 128), 1)
    dk_acc[...] += jnp.where(key_lane < HEAD_DIM, dks[0], dks[1])
    dv_acc[...] += jnp.where(key_lane < HEAD_DIM, dvs[0], dvs[1])

    @pl.when(query_block == n - 1)
    def _():
        dk_ref[...] = (dk_acc[...] * SCALE).astype(BF16)
        dv_ref[...] = dv_acc[...].astype(BF16)
        for side in range(2):
            diag_ref[0, pl.ds(side, 1), :] = diagonal_sum(sums[side])


def attention_backward(n, qkv, lse, d_mixed, vectors):
    rows, triple = qkv.shape
    own = triple // 3
    block = rows // n
    pairs = own // 128
    wide = vectors.shape[1]
    return pl.pallas_call(
        functools.partial(attention_backward_kernel, n, block),
        grid=(pairs, n),
        in_specs=[
            pl.BlockSpec((block, 128), lambda p, i: (i, p)),
            pl.BlockSpec((rows, 128), lambda p, i: (0, pairs + p)),
            pl.BlockSpec((rows, 128), lambda p, i: (0, 2 * pairs + p)),
            pl.BlockSpec((block, 128), lambda p, i: (i, p)),
            pl.BlockSpec((block, 128), lambda p, i: (i, p)),
            pl.BlockSpec((2 * pairs, wide), lambda p, i: (0, 0)),
        ],
        out_specs=[
            pl.BlockSpec((block, 128), lambda p, i: (i, p)),
            pl.BlockSpec((rows, 128), lambda p, i: (0, p)),
            pl.BlockSpec((rows, 128), lambda p, i: (0, p)),
            pl.BlockSpec((1, 2, wide), lambda p, i: (p, 0, 0)),
        ],
        out_shape=[
            jax.ShapeDtypeStruct((rows, own), BF16),
            jax.ShapeDtypeStruct((rows, own), BF16),
            jax.ShapeDtypeStruct((rows, own), BF16),
            jax.ShapeDtypeStruct((pairs, 2, wide), F32),
        ],
        scratch_shapes=[
            pltpu.VMEM((2, block, wide), F32),
            pltpu.VMEM((2, block, wide), F32),
            pltpu.VMEM((rows, 128), F32),
            pltpu.VMEM((rows, 128), F32),
        ],
        compiler_params=pltpu.CompilerParams(vmem_limit_bytes=VMEM_LIMIT),
        cost_estimate=pl.CostEstimate(
            flops=40 * rows * rows * own, bytes_accessed=14 * rows * own, transcendentals=rows * rows * own // 64
        ),
        name="attention_backward",
    )(qkv, qkv, qkv, lse, d_mixed, vectors)


def gelu_pair(v):
    square = v * v
    t = jnp.tanh(GELU_C * (v + GELU_A * v * square))
    half = 0.5 * (1.0 + t)
    slope = half + (0.5 * GELU_C) * v * (1.0 - t * t) * (1.0 + (3.0 * GELU_A) * square)
    return v * half, slope


def unpack_kernel(n, piece, in_ref, gate_ref, up_ref):
    main = piece // 128 * 128
    rest = piece - main
    gates, ups = [], []
    for j in range(n):
        block = in_ref[j].astype(F32)
        gates += [block[:, :main], block[:, 2 * main : 2 * main + rest]]
        ups += [block[:, main : 2 * main], block[:, 2 * main + rest :]]
    gate_ref[...] = jnp.concatenate(gates, axis=1)
    up_ref[...] = jnp.concatenate(ups, axis=1)


def unpack_columns(blocks):
    n, rows, both = blocks.shape
    piece = both // 2
    step = min(rows, 64)
    total = n * piece
    return pl.pallas_call(
        functools.partial(unpack_kernel, n, piece),
        grid=(rows // step,),
        in_specs=[pl.BlockSpec((n, step, both), lambda i: (0, i, 0))],
        out_specs=[pl.BlockSpec((step, total), lambda i: (i, 0))] * 2,
        out_shape=[jax.ShapeDtypeStruct((rows, total), F32)] * 2,
        compiler_params=pltpu.CompilerParams(vmem_limit_bytes=VMEM_LIMIT),
        cost_estimate=pl.CostEstimate(flops=0, bytes_accessed=12 * rows * total, transcendentals=0),
        name="unpack_columns",
    )(blocks)


MESH = pl.DeviceIdType.MESH


def remote(src, dst, send, recv, target):
    return pltpu.make_async_remote_copy(
        src_ref=src, dst_ref=dst, send_sem=send, recv_sem=recv, device_id=target, device_id_type=MESH
    )


def greet(n, ne, dp, ex):
    barrier = pltpu.get_barrier_semaphore()
    for d in range(1, n):
        pl.semaphore_signal(barrier, inc=1, device_id=(lax.rem(dp + d, n), ex), device_id_type=MESH)
    for k in range(1, ne):
        pl.semaphore_signal(barrier, inc=1, device_id=(dp, lax.rem(ex + k, ne)), device_id_type=MESH)
    pl.semaphore_wait(barrier, n + ne - 2)


class Chain:
    def __init__(self, n, dp, ex, own, buffer, send, recv):
        self.n, self.dp, self.ex, self.own = n, dp, ex, own
        self.buffer, self.send_sem, self.recv_sem = buffer, send, recv

    def block(self, hop, side):
        return lax.rem(self.dp + self.n + hop * (2 * side - 1), self.n)

    def copy(self, hop, side, first=False):
        at = self.block(hop, side)
        target = lax.rem(self.dp + self.n + 1 - 2 * side, self.n)
        return remote(
            self.own if first else self.buffer.at[at], self.buffer.at[at],
            self.send_sem.at[hop, side], self.recv_sem.at[hop, side], (target, self.ex),
        )

    def has_next(self, side):
        return (self.dp + 1 < self.n) if side == 0 else (self.dp > 0)

    def start(self):
        for side in range(2):
            @pl.when(self.has_next(side))
            def _():
                self.copy(0, side, True).start()

    def held(self, hop, side):
        return (self.dp > hop) if side == 0 else (self.dp + 1 + hop < self.n)

    def arrive(self, hop, side):
        at = self.block(hop + 1, side)
        remote(
            self.buffer.at[at], self.buffer.at[at], self.send_sem.at[hop, side], self.recv_sem.at[hop, side],
            (self.dp, self.ex),
        ).wait_recv()

        @pl.when(self.has_next(side))
        def _():
            self.copy(hop + 1, side).start()

        return at

    def finish(self):
        for hop in range(self.n - 1):
            for side in range(2):
                mine = self.has_next(side)
                if hop:
                    mine = mine & self.held(hop - 1, side)

                @pl.when(mine)
                def _():
                    self.copy(hop, side, hop == 0).wait_send()


def start_kernel(
    n, ne, cap, cap_pad, piece,
    x, wq, wk, wv, extra, wo, meta_in, wg, wu,
    x_all, lq, lk, lv, lext, lwo, meta_all, packed,
    sq, sk, sv, sext, swo, smeta,
    line_send, line_recv, plane_send, plane_recv, core_send, core_recv, chain_send, chain_recv, own_sem,
):
    dp, ex = lax.axis_index("dp"), lax.axis_index("expert")
    own = sq.shape[2]
    greet(n, ne, dp, ex)
    chain = Chain(n, dp, ex, x, x_all, chain_send, chain_recv)

    def column(ref, t):
        return ref.at[:, pl.ds(pl.multiple_of(t * own, 128), own)]

    def line(kind, d):
        t = lax.rem(dp + d, n)
        src, dst = [
            (column(wq, t), sq.at[dp]), (column(wk, t), sk.at[dp]), (column(wv, t), sv.at[dp]),
            (extra, sext.at[dp]), (wo, swo.at[dp]), (smeta, meta_all.at[dp]),
        ][kind]
        return remote(src, dst, line_send.at[kind, d], line_recv.at[kind, d], (t, ex))

    for d in range(1, n):
        for kind in range(4):
            line(kind, d).start()
    chain.start()
    for d in range(1, n):
        line(4, d).start()
    keep = pltpu.make_async_copy(x, x_all.at[dp], own_sem.at[0])
    keep.start()
    sq[dp] = wq[:, pl.ds(pl.multiple_of(dp * own, 128), own)]
    sk[dp] = wk[:, pl.ds(pl.multiple_of(dp * own, 128), own)]
    sv[dp] = wv[:, pl.ds(pl.multiple_of(dp * own, 128), own)]
    sext[dp] = extra[...]
    swo[dp] = wo[...]

    tok = meta_in.shape[1]
    routes = meta_in[...]
    ids = lax.broadcasted_iota(jnp.int32, (ne, tok), 0)
    first = (ids == routes[0:1, :]).astype(F32)
    second = (ids == routes[1:2, :]).astype(F32)
    before = (
        lax.broadcasted_iota(jnp.int32, (tok, tok), 0) < lax.broadcasted_iota(jnp.int32, (tok, tok), 1)
    ).astype(BF16)
    counts = mm((first + second).astype(BF16), before)
    slot_a = jnp.sum(counts * first, axis=0, keepdims=True)
    slot_b = jnp.sum((counts + first) * second, axis=0, keepdims=True)
    wide = routes.astype(F32)
    dest_a = jnp.where(slot_a < cap, wide[0:1, :] * cap_pad + slot_a, -1.0)
    dest_b = jnp.where(slot_b < cap, wide[1:2, :] * cap_pad + slot_b, -1.0)
    gate = wide[2:3, :] * (1.0 / 65536.0)
    smeta[...] = jnp.concatenate([dest_a, dest_b, gate, jnp.zeros((5, tok), F32)], axis=0)
    for d in range(1, n):
        line(5, d).start()
    keep_meta = pltpu.make_async_copy(smeta, meta_all.at[dp], own_sem.at[1])
    keep_meta.start()

    pairs = [(sq, lq), (sk, lk), (sv, lv), (sext, lext), (swo, lwo)]
    partner = ex + 1 - 2 * lax.rem(ex, 2)

    def plane(kind, k):
        src, dst = pairs[kind]
        return remote(
            src, dst.at[:, ex], plane_send.at[kind, k], plane_recv.at[kind, k],
            (dp, lax.rem(ex + 2 * k, ne)),
        )

    def core(kind, k):
        src, dst = pairs[kind]
        at = lax.rem(ex + ne - 2 * k, ne)
        return remote(
            src if k == 0 else dst.at[:, at], dst.at[:, at],
            core_send.at[kind, k], core_recv.at[kind, k], (dp, partner),
        )

    def spread(kind):
        for d in range(1, n):
            line(kind, d).wait_recv()
        for k in range(1, ne // 2):
            plane(kind, k).start()
        core(kind, 0).start()
        pltpu.make_async_copy(pairs[kind][0], pairs[kind][1].at[:, ex], own_sem.at[2 + kind]).start()

    for kind in range(4):
        spread(kind)

    main = piece // 128 * 128
    step = min(wg.shape[0], 64)

    @pl.loop(0, wg.shape[0] // step)
    def _(i):
        rows = pl.ds(pl.multiple_of(i * step, step), step)
        gate_w, up_w = wg[rows, :], wu[rows, :]
        for j in range(n):
            g = gate_w[:, j * piece : (j + 1) * piece]
            u = up_w[:, j * piece : (j + 1) * piece]
            packed[j, rows, :] = jnp.concatenate([g[:, :main], u[:, :main], g[:, main:], u[:, main:]], axis=1)

    spread(4)

    def pass_on(kind):
        for k in range(1, ne // 2):
            plane(kind, k).wait_recv()
            core(kind, k).start()

    def hop(h):
        for side in range(2):
            @pl.when(chain.held(h, side))
            def _():
                chain.arrive(h, side)

    hop(0)
    for kind in range(4):
        pass_on(kind)
    for h in range(1, n - 1):
        hop(h)
        if h == 1:
            pass_on(4)
    if n < 3:
        pass_on(4)
    for kind in range(5):
        for k in range(ne // 2):
            core(kind, k).wait()
        for k in range(1, ne // 2):
            plane(kind, k).wait_send()
        pltpu.make_async_copy(pairs[kind][0], pairs[kind][1].at[:, ex], own_sem.at[2 + kind]).wait()
    for d in range(1, n):
        for kind in range(6):
            line(kind, d).wait_send()
        line(5, d).wait_recv()
    chain.finish()
    keep.wait()
    keep_meta.wait()


def whole(array):
    return pl.BlockSpec(memory_space=pltpu.VMEM)


ANY = pl.BlockSpec(memory_space=pl.ANY)
VM = pl.BlockSpec(memory_space=pltpu.VMEM)


def start(n, ne, cap, cap_pad, x, wq, wk, wv, extra, wo, meta_in, wg, wu):
    tok, width = x.shape
    wrows = wq.shape[0]
    own = width // n
    piece = wg.shape[1] // n
    return pl.pallas_call(
        functools.partial(start_kernel, n, ne, cap, cap_pad, piece),
        in_specs=[VM] * 9,
        out_specs=[ANY] * 7 + [VM],
        out_shape=[
            jax.ShapeDtypeStruct((n, tok, width), BF16),
            jax.ShapeDtypeStruct((n, ne, wrows, own), BF16),
            jax.ShapeDtypeStruct((n, ne, wrows, own), BF16),
            jax.ShapeDtypeStruct((n, ne, wrows, own), BF16),
            jax.ShapeDtypeStruct((n, ne, 16, own), BF16),
            jax.ShapeDtypeStruct((n, ne, wrows, width), BF16),
            jax.ShapeDtypeStruct((n, 8, tok), F32),
            jax.ShapeDtypeStruct((n, tok, 2 * piece), BF16),
        ],
        scratch_shapes=[
            pltpu.VMEM((n, wrows, own), BF16),
            pltpu.VMEM((n, wrows, own), BF16),
            pltpu.VMEM((n, wrows, own), BF16),
            pltpu.VMEM((n, 16, own), BF16),
            pltpu.VMEM((n, wrows, width), BF16),
            pltpu.VMEM((8, tok), F32),
            pltpu.SemaphoreType.DMA((6, n)),
            pltpu.SemaphoreType.DMA((6, n)),
            pltpu.SemaphoreType.DMA((5, ne // 2)),
            pltpu.SemaphoreType.DMA((5, ne // 2)),
            pltpu.SemaphoreType.DMA((5, ne // 2)),
            pltpu.SemaphoreType.DMA((5, ne // 2)),
            pltpu.SemaphoreType.DMA((n, 2)),
            pltpu.SemaphoreType.DMA((n, 2)),
            pltpu.SemaphoreType.DMA((7,)),
        ],
        compiler_params=pltpu.CompilerParams(
            collective_id=1, has_side_effects=True, vmem_limit_bytes=VMEM_LIMIT
        ),
        name="start",
    )(x, wq, wk, wv, extra, wo, meta_in, wg, wu)


def forward_kernel(
    n, ne, cap_pad,
    x_all, wq, wk, wv, wo, gain_one, gain_two, vectors, cot, meta_all, packed,
    normed, qkv, lse, mixed, resid, slots, d_outs, wgu,
    heads, mixed_in, tiles, cot_all, two_all, two_own, two_rows, cot_rows,
    w_send, w_recv, m_send, m_recv, c_send, c_recv, t_send, t_recv,
    pc_send, pc_recv, pt_send, pt_recv, own_sem,
):
    dp, ex = lax.axis_index("dp"), lax.axis_index("expert")
    block, width = cot.shape
    own = heads.shape[1]
    pairs_n = own // 128
    slots_n = ne * cap_pad
    greet(n, ne, dp, ex)

    def weights(d):
        t = lax.rem(dp + d, n)
        return remote(packed.at[t], wgu.at[dp], w_send.at[d], w_recv.at[d], (t, ex))

    cots = Chain(n, dp, ex, cot, cot_all, c_send, c_recv)
    twos = Chain(n, dp, ex, two_own, two_all, t_send, t_recv)
    cots.start()
    keep_w = pltpu.make_async_copy(packed.at[dp], wgu.at[dp], own_sem.at[0])
    keep_w.start()

    def to_plane(rows, land, send, recv, group, k):
        peer = lax.rem(ex + k, ne)
        return remote(
            rows.at[group, pl.ds(pl.multiple_of(peer * cap_pad, 16), cap_pad)], land.at[group, ex],
            send.at[group, k], recv.at[group, k], (dp, peer),
        )

    def kept(rows, land, group, sem):
        return pltpu.make_async_copy(
            rows.at[group, pl.ds(pl.multiple_of(ex * cap_pad, 16), cap_pad)], land.at[group, ex], sem.at[group, 0]
        )

    def dispatch(group, tokens, rows, land, send, recv, weigh):
        meta = meta_all[group]
        ids = lax.broadcasted_iota(jnp.int32, (slots_n, block), 0).astype(F32)
        hit_a, hit_b = ids == meta[0:1, :], ids == meta[1:2, :]
        chosen = jnp.where(hit_a | hit_b, 1.0, 0.0).astype(BF16)
        found = mm(chosen, tokens)
        if weigh:
            gate = meta[2:3, :]
            factor = jnp.sum(
                jnp.where(hit_a, gate, 0.0) + jnp.where(hit_b, 1.0 - gate, 0.0), axis=1, keepdims=True
            )
            found = found * factor
        rows[group] = found.astype(BF16)
        for k in range(1, ne):
            to_plane(rows, land, send, recv, group, k).start()
        kept(rows, land, group, send).start()

    @pl.loop(0, n)
    def _(j):
        at = pl.ds(pl.multiple_of(j * block, block), block)
        xf = x_all[j].astype(F32)
        inverse = lax.rsqrt(jnp.mean(xf * xf, axis=-1, keepdims=True) + EPSILON)
        low = (xf * inverse * gain_one[...]).astype(BF16)
        normed[at, :] = low
        for w, ref in enumerate((wq, wk, wv)):
            qkv[at, w * own : (w + 1) * own] = mm(low, ref[...]).astype(BF16)

    def attend(pair):
        for side in range(2):
            bias_tile(vectors, 2 * pair + side, tiles.at[side])
        lane = lax.broadcasted_iota(jnp.int32, (block, 128), 1)
        low_half = lane < HEAD_DIM
        k_pair = qkv[:, own + pair * 128 : own + (pair + 1) * 128]
        v_pair = qkv[:, 2 * own + pair * 128 : 2 * own + (pair + 1) * 128]

        @pl.loop(0, n)
        def _(i):
            at = pl.ds(pl.multiple_of(i * block, block), block)
            q_pair = qkv[at, pair * 128 : (pair + 1) * 128]
            outs, logs = [], []
            for side in range(2):
                mask = low_half if side == 0 else jnp.logical_not(low_half)
                logits = logits_of(n, block, i, q_pair, k_pair, mask, tiles.at[side])
                row_max = jnp.max(logits, axis=-1, keepdims=True)
                exponent = jnp.exp(logits - row_max)
                total = jnp.sum(exponent, axis=-1, keepdims=True)
                probs_low = (exponent * (1.0 / total)).astype(BF16)
                outs.append(mm(probs_low, v_pair))
                logs.append(jnp.broadcast_to(row_max + jnp.log(total), (block, 128)))
            heads[at, pair * 128 : (pair + 1) * 128] = jnp.where(low_half, outs[0], outs[1]).astype(BF16)
            lse[at, pair * 128 : (pair + 1) * 128] = jnp.where(low_half, logs[0], logs[1])

    def hop(chain, h, then):
        for side in range(2):
            @pl.when(chain.held(h, side))
            def _():
                then(chain.arrive(h, side))

    attend(0)
    hop(cots, 0, lambda at: None)
    for d in range(1, n):
        weights(d).start()
    for pair in range(1, pairs_n):
        attend(pair)

    def give(d):
        t = lax.rem(dp + d, n)
        return remote(
            heads.at[pl.ds(pl.multiple_of(t * block, block), block)], mixed_in.at[dp], m_send.at[d], m_recv.at[d],
            (t, ex),
        )

    for d in range(1, n):
        give(d).start()
    mixed_in[dp] = heads[pl.ds(pl.multiple_of(dp * block, block), block), :]
    dispatch(dp, cot[...], cot_rows, d_outs, pc_send, pc_recv, True)
    for h in range(1, n - 1):
        hop(cots, h, lambda at: None)
    cots.finish()
    for d in range(1, n):
        give(d).wait()
    mixed[...] = jnp.concatenate([mixed_in[j] for j in range(n)], axis=1)
    total = x_all[dp].astype(F32) + mm(mixed[...], wo[...])
    resid[...] = total
    inverse = lax.rsqrt(jnp.mean(total * total, axis=-1, keepdims=True) + EPSILON)
    two_own[...] = (total * inverse * gain_two[...]).astype(BF16)
    twos.start()

    def send_two(group, tokens):
        dispatch(group, tokens, two_rows, slots, pt_send, pt_recv, False)

    send_two(dp, two_own[...])
    for j in range(1, n):
        at = lax.rem(dp + j, n)
        dispatch(at, cot_all[at], cot_rows, d_outs, pc_send, pc_recv, True)
        hop(twos, j - 1, lambda group: send_two(group, two_all[group]))
    twos.finish()
    keep_w.wait()
    for d in range(1, n):
        weights(d).wait()
    for rows, land, send, recv in (
        (two_rows, slots, pt_send, pt_recv), (cot_rows, d_outs, pc_send, pc_recv),
    ):
        @pl.loop(0, n)
        def _(group):
            kept(rows, land, group, send).wait()
            for k in range(1, ne):
                to_plane(rows, land, send, recv, group, k).wait()


def forward(n, ne, cap_pad, x_all, wq, wk, wv, wo, gain_one, gain_two, vectors, cot, meta_all, packed):
    tok, width = cot.shape
    own = wq.shape[1]
    wide = vectors.shape[1]
    both = packed.shape[2]
    slots_n = ne * cap_pad
    sem = pltpu.SemaphoreType.DMA
    return pl.pallas_call(
        functools.partial(forward_kernel, n, ne, cap_pad),
        in_specs=[VM] * 10 + [ANY],
        out_specs=[VM] * 5 + [ANY] * 3,
        out_shape=[
            jax.ShapeDtypeStruct((n * tok, width), BF16),
            jax.ShapeDtypeStruct((n * tok, 3 * own), BF16),
            jax.ShapeDtypeStruct((n * tok, own), F32),
            jax.ShapeDtypeStruct((tok, width), BF16),
            jax.ShapeDtypeStruct((tok, width), F32),
            jax.ShapeDtypeStruct((n, ne, cap_pad, width), BF16),
            jax.ShapeDtypeStruct((n, ne, cap_pad, width), BF16),
            jax.ShapeDtypeStruct((n, tok, both), BF16),
        ],
        scratch_shapes=[
            pltpu.VMEM((n * tok, own), BF16),
            pltpu.VMEM((n, tok, own), BF16),
            pltpu.VMEM((2, tok, wide), F32),
            pltpu.VMEM((n, tok, width), BF16),
            pltpu.VMEM((n, tok, width), BF16),
            pltpu.VMEM((tok, width), BF16),
            pltpu.VMEM((n, slots_n, width), BF16),
            pltpu.VMEM((n, slots_n, width), BF16),
            sem((n,)), sem((n,)), sem((n,)), sem((n,)),
            sem((n, 2)), sem((n, 2)), sem((n, 2)), sem((n, 2)),
            sem((n, ne)), sem((n, ne)), sem((n, ne)), sem((n, ne)),
            sem((1,)),
        ],
        compiler_params=pltpu.CompilerParams(
            collective_id=2, has_side_effects=True, vmem_limit_bytes=VMEM_LIMIT
        ),
        name="forward",
    )(x_all, wq, wk, wv, wo, gain_one, gain_two, vectors, cot, meta_all, packed)


def experts_kernel(
    n, ne, cap_pad, deep, main,
    slots, d_outs, wgu_ref, wd_ref, meta_all,
    out_rows, d_two, gwgu, gwd,
    s_buf, d_buf, back, part, landed, gwgu_acc,
    load_sem, keep_sem, p_send, p_recv, z_send, z_recv,
):
    dp, ex = lax.axis_index("dp"), lax.axis_index("expert")
    slots_n, width = s_buf.shape[1:]
    tok = d_two.shape[0]
    greet(n, ne, dp, ex)
    toward = 2 * ((2 * dp) // n) - 1

    def group_at(step):
        return lax.rem(dp + n + toward * (1 + step), n)

    def load(step, kind):
        at = group_at(step)
        src, dst = ((slots, s_buf), (d_outs, d_buf))[kind]
        return pltpu.make_async_copy(src.at[at], dst.at[at], load_sem.at[kind, step])

    for step in range(n):
        for kind in range(2):
            load(step, kind).start()
    gwgu_acc[...] = jnp.zeros_like(gwgu_acc)
    gwd[...] = jnp.zeros_like(gwd)

    def rows_of(peer):
        return pl.ds(pl.multiple_of(peer * cap_pad, 16), cap_pad)

    def give(at, k):
        peer = lax.rem(ex + k, ne)
        return remote(
            d_buf.at[at, rows_of(peer)], back.at[at, rows_of(ex)], p_send.at[at, k], p_recv.at[at, k], (dp, peer)
        )

    def take(at, k):
        peer = lax.rem(ex + ne - k, ne)
        return remote(
            d_buf.at[at, rows_of(ex)], back.at[at, rows_of(peer)], p_send.at[at, k], p_recv.at[at, k], (dp, peer)
        )

    def keep(at):
        return pltpu.make_async_copy(s_buf.at[at], out_rows.at[at], keep_sem.at[at])

    def owed(at):
        return remote(part.at[at], landed.at[dp], z_send.at[at], z_recv.at[dp], (at, ex))

    def combine(at):
        for k in range(1, ne):
            take(at, k).wait_recv()
        meta = meta_all[at]
        ids = lax.broadcasted_iota(jnp.int32, (slots_n, tok), 0).astype(F32)
        hit = (ids == meta[0:1, :]) | (ids == meta[1:2, :])
        return mm(jnp.where(hit, 1.0, 0.0).astype(BF16), back[at], TN)

    @pl.loop(0, n)
    def _(step):
        at = group_at(step)
        for kind in range(2):
            load(step, kind).wait()
        wgu, wd = wgu_ref[...], wd_ref[...]
        parts = -(-slots_n // 640)
        size = slots_n // parts
        low_lane = lax.broadcasted_iota(jnp.int32, (size, 128), 1) < 64
        for p in range(parts):
            here = slice(p * size, (p + 1) * size)
            rows, d_out = s_buf[at, here, :], d_buf[at, here, :]
            pre = mm(rows, wgu)
            d_hidden = mm(d_out, wd, NT)
            gate, up, tail = pre[:, :main], pre[:, main : 2 * main], pre[:, 2 * main :]
            tail_up = pltpu.roll(tail, 64, 1)
            act, slope = gelu_pair(gate)
            act_t, slope_t = gelu_pair(tail)
            hidden_t = jnp.where(low_lane, act_t * tail_up, 0.0)
            hidden = jnp.concatenate([(act * up).astype(BF16), hidden_t.astype(BF16)], axis=1)
            dh, dh_t = d_hidden[:, :main], d_hidden[:, main:]
            d_gate = dh * up * slope
            d_up = dh * act
            d_tail = jnp.where(low_lane, dh_t * tail_up * slope_t, pltpu.roll(dh_t * act_t, 64, 1))
            d_pre = jnp.concatenate([d_gate.astype(BF16), d_up.astype(BF16), d_tail.astype(BF16)], axis=1)
            d_rows = mm(d_pre, wgu, NT).astype(BF16)
            gwd[...] += mm(hidden, d_out, TN)[:deep]
            d_buf[at, here, :] = d_rows
            if p == parts - 1:
                for k in range(1, ne):
                    give(at, k).start()
                back[at, rows_of(ex), :] = d_buf[at, rows_of(ex), :]
            gwgu_acc[...] += mm(rows, d_pre, TN)
            s_buf[at, here, :] = mm(hidden, wd).astype(BF16)
        keep(at).start()

        @pl.when(step > 0)
        def _():
            past = group_at(step - 1)
            part[past] = combine(past).astype(BF16)
            owed(past).start()

    gwgu[...] = gwgu_acc[...].astype(BF16)
    total = combine(dp)
    for d in range(1, n):
        src = lax.rem(dp + d, n)
        remote(part.at[src], landed.at[src], z_send.at[src], z_recv.at[src], (src, ex)).wait_recv()
        total = total + landed[src].astype(F32)
    d_two[...] = total
    for d in range(1, n):
        owed(lax.rem(dp + d, n)).wait_send()

    @pl.loop(0, n)
    def _(at):
        keep(at).wait()
        for k in range(1, ne):
            give(at, k).wait_send()


def experts(n, ne, cap_pad, deep, slots, d_outs, wgu, wd, meta_all):
    width, columns = wgu.shape
    tok = meta_all.shape[2]
    main = (columns - 128) // 2
    slots_n = ne * cap_pad
    slots = slots.reshape(n, slots_n, width)
    d_outs = d_outs.reshape(n, slots_n, width)
    sem = pltpu.SemaphoreType.DMA
    return pl.pallas_call(
        functools.partial(experts_kernel, n, ne, cap_pad, deep, main),
        in_specs=[ANY, ANY, VM, VM, VM],
        out_specs=[ANY, VM, VM, VM],
        out_shape=[
            jax.ShapeDtypeStruct((n, slots_n, width), BF16),
            jax.ShapeDtypeStruct((tok, width), F32),
            jax.ShapeDtypeStruct((width, columns), BF16),
            jax.ShapeDtypeStruct((deep, width), F32),
        ],
        scratch_shapes=[
            pltpu.VMEM((n, slots_n, width), BF16),
            pltpu.VMEM((n, slots_n, width), BF16),
            pltpu.VMEM((n, slots_n, width), BF16),
            pltpu.VMEM((n, tok, width), BF16),
            pltpu.VMEM((n, tok, width), BF16),
            pltpu.VMEM((width, columns), F32),
            sem((2, n)), sem((n,)), sem((n, ne)), sem((n, ne)), sem((n,)), sem((n,)),
        ],
        compiler_params=pltpu.CompilerParams(
            collective_id=3, has_side_effects=True, vmem_limit_bytes=60 * 1024 * 1024
        ),
        name="experts",
    )(slots, d_outs, wgu, wd, meta_all)


def shift(value, distance, n):
    return lax.ppermute(value, "dp", [(i, (i + distance) % n) for i in range(n)])


def pick(stacked, index):
    return lax.dynamic_index_in_dim(stacked, index, 0, keepdims=False)


def exchange(value):
    return lax.all_to_all(value, "expert", split_axis=0, concat_axis=0, tiled=True)


def trade(blocks, n, dp):
    got = jnp.stack([pick(blocks, dp)] + [shift(pick(blocks, lax.rem(dp + d, n)), d, n) for d in range(1, n)])
    return jnp.stack([pick(got, lax.rem(dp - j + n, n)) for j in range(n)])


def to_owners(blocks, n, dp):
    total = pick(blocks, dp).astype(F32)
    for d in range(1, n):
        total = total + shift(pick(blocks, lax.rem(dp + d, n)).astype(BF16), d, n).astype(F32)
    return total


def local(
    inputs, cotangent, gain_attn, w_query, w_key, w_value, w_out, position_bias,
    gain_moe, w_gate, w_up, w_down, routes, gate_fixed,
):
    n = lax.axis_size("dp")
    experts_n = lax.axis_size("expert")
    dp = lax.axis_index("dp")
    ex = lax.axis_index("expert")
    tok, width = inputs.shape[1:]
    length = n * tok
    own = HEADS * HEAD_DIM // n
    heads_own = HEADS // n
    wrows = w_query.shape[0]
    capacity = 5 * tok // (2 * experts_n)
    cap_pad = -(-capacity // 16) * 16
    slots_n = experts_n * cap_pad

    n_gain, n_bias = gain_attn.shape[0], position_bias.shape[0]
    extra = jnp.concatenate([gain_attn, gain_moe, position_bias])
    extra = jnp.zeros((16, own), BF16).at[0, : 2 * n_gain + n_bias].set(extra)
    meta_in = jnp.concatenate([routes[0].T, gate_fixed], axis=0)
    x_all, wq, wk, wv, extras, wo, meta_all, packed = start(
        n, experts_n, capacity, cap_pad,
        inputs[0], w_query, w_key, w_value, extra, w_out, meta_in, w_gate[0], w_up[0],
    )
    wq, wk, wv = (w.reshape(width, own) for w in (wq, wk, wv))
    wo = wo.reshape(width, width)
    extras = extras[:, :, 0]
    gain_one = extras[:, :, :n_gain].reshape(1, -1).astype(F32)
    gain_two = extras[:, :, n_gain : 2 * n_gain].reshape(1, -1).astype(F32)
    table = extras[:, :, 2 * n_gain : 2 * n_gain + n_bias].reshape(BUCKETS, HEADS)
    table = lax.dynamic_slice_in_dim(table, dp * heads_own, heads_own, 1)
    wide = 2 * length
    offsets = jnp.arange(wide, dtype=jnp.int32) - length
    in_bucket = (bucket_of(offsets)[:, None] == jnp.arange(BUCKETS, dtype=jnp.int32)).astype(BF16)
    in_bucket = jnp.where(jnp.abs(offsets)[:, None] < length, in_bucket, jnp.zeros_like(in_bucket))
    vectors = mm(table, in_bucket, (((0,), (1,)), ((), ())))

    normed, qkv, lse, mixed, resid, slots, d_outs, wgu = forward(
        n, experts_n, cap_pad, x_all, wq, wk, wv, wo, gain_one, gain_two, vectors, cotangent[0], meta_all, packed
    )
    wgu = wgu.reshape(width, -1)
    deep = w_down.shape[1]
    padded = -(-deep // 128) * 128
    wd = jnp.pad(w_down[0], ((0, padded - deep), (0, 0)))
    out_rows, grad_normed_two, gwgu, grad_w_down = experts(
        n, experts_n, cap_pad, deep, slots, d_outs, wgu, wd, meta_all
    )

    dest = meta_all[:, :2].astype(jnp.int32)
    select = (dest[..., None] == jnp.arange(slots_n, dtype=jnp.int32)).astype(BF16)
    both = select[:, 0] + select[:, 1]
    first_gate = meta_all[:, 2]
    gates = jnp.stack([first_gate, 1.0 - first_gate], axis=1)

    def from_experts(rows):
        rows = jnp.swapaxes(rows.reshape(n, experts_n, cap_pad, width), 0, 1)
        return jnp.swapaxes(exchange(rows), 0, 1).reshape(n, slots_n, width)

    got = trade(gwgu.reshape(n, width // n, gwgu.shape[1]), n, dp)
    gain_one, gain_two = gain_one[0], gain_two[0]
    grad_top = cotangent[0].astype(F32)
    inverse_two = lax.rsqrt(jnp.mean(resid * resid, axis=-1, keepdims=True) + EPSILON)
    grad_gain_two, grad_resid_norm = norm_backward(resid, inverse_two, gain_two, grad_normed_two)
    grad_resid = grad_top + grad_resid_norm
    grad_attn_low = grad_resid.astype(BF16)
    d_mixed = mm(grad_attn_low, wo, NT).astype(BF16)
    d_mixed_heads = trade(jnp.swapaxes(d_mixed.reshape(tok, n, own), 0, 1), n, dp).reshape(length, own)
    grad_w_out_part = mm(mixed, grad_attn_low, TN)

    out_back = from_experts(out_rows)
    out_back, d_mixed_heads = lax.optimization_barrier((out_back, d_mixed_heads))
    picked = jnp.einsum("gcts,gsd->gctd", select, out_back, preferred_element_type=F32)
    moe_sum = to_owners(jnp.sum(picked * gates[..., None], axis=1), n, dp)

    dq, dk, dv, diagonals = attention_backward(n, qkv, lse, d_mixed_heads, vectors)
    d_normed_part = mm(dq, wq, NT) + mm(dk, wk, NT) + mm(dv, wv, NT)
    d_normed_part, moe_sum = lax.optimization_barrier((d_normed_part, moe_sum))
    grad_normed = to_owners(d_normed_part.reshape(n, tok, width), n, dp)
    d_qkv = jnp.concatenate([dq, dk, dv], axis=1)
    grad_wqkv_part = mm(normed, d_qkv, TN)
    tokens = inputs[0].astype(F32)
    inverse_one = lax.rsqrt(jnp.mean(tokens * tokens, axis=-1, keepdims=True) + EPSILON)
    grad_gain_one, grad_tok_norm = norm_backward(tokens, inverse_one, gain_one, grad_normed)
    grad_inputs = (grad_resid + grad_tok_norm).astype(BF16)
    block_out = (resid + moe_sum).astype(BF16)

    grad_w_gate, grad_w_up = unpack_columns(got)

    def plane_sum(parts):
        return jnp.sum(exchange(parts.astype(BF16)).astype(F32), axis=0)

    go = grad_w_out_part.reshape(n, experts_n, wrows, width)
    go = plane_sum(jnp.swapaxes(go, 0, 1))
    grad_w_out = to_owners(go, n, dp)

    gq = grad_wqkv_part.reshape(n, experts_n, wrows, 3 * own)
    gq = plane_sum(jnp.swapaxes(gq, 0, 1)).astype(BF16)
    gq_all = trade(gq, n, dp).astype(F32)
    gq_all = gq_all.reshape(n, wrows, 3, own).transpose(2, 1, 0, 3).reshape(3, wrows, width)

    diag_rows = jnp.roll(diagonals.reshape(heads_own, wide), tok, axis=1)
    grad_table = lax.dot_general(
        in_bucket.astype(F32), diag_rows, (((0,), (1,)), ((), ())), precision=lax.Precision.HIGHEST,
        preferred_element_type=F32,
    )
    grad_table = lax.dynamic_update_slice_in_dim(
        jnp.zeros((BUCKETS, HEADS), F32), grad_table, dp * heads_own, 1
    )
    small = jnp.concatenate([grad_gain_one, grad_gain_two, grad_table.reshape(-1)]).reshape(-1, 128)
    step = 1
    while step < experts_n:
        small = small + lax.ppermute(small, "expert", [(i, i ^ step) for i in range(experts_n)])
        step *= 2
    small = (small + sum(shift(small, d, n) for d in range(1, n))).reshape(-1)
    me = dp * experts_n + ex
    grad_gain_attn = lax.dynamic_slice_in_dim(small, me * n_gain, n_gain)
    grad_gain_moe = lax.dynamic_slice_in_dim(small, width + me * n_gain, n_gain)
    grad_bias = lax.dynamic_slice_in_dim(small, 2 * width + me * n_bias, n_bias)

    return (
        block_out[None],
        grad_inputs[None],
        grad_gain_attn,
        gq_all[0],
        gq_all[1],
        gq_all[2],
        grad_w_out,
        grad_bias,
        grad_gain_moe,
        grad_w_gate[None],
        grad_w_up[None],
        grad_w_down[None],
    )


def solution(mesh):
    vector = P(("dp", "expert"))
    matrix = P(("dp", "expert"), None)
    split = P("expert", "dp", None)
    return jax.shard_map(
        local,
        mesh=mesh,
        in_specs=(
            split, split, vector, matrix, matrix, matrix, matrix, vector, vector,
            split, split, split, split, P("expert", "dp"),
        ),
        out_specs=(
            split, split, vector, matrix, matrix, matrix, matrix, vector, vector,
            split, split, split,
        ),
        check_vma=False,
    )
```

```python
import functools

import jax
import jax.numpy as jnp
from jax import lax
from jax.experimental import pallas as pl
from jax.experimental.pallas import tpu as pltpu
from jax.sharding import PartitionSpec as P

HEADS = 16
HEAD_DIM = 64
BUCKETS = 32
THRESHOLDS = (12, 16, 23, 32, 46, 64, 91)
EPSILON = 1e-06
SCALE = HEAD_DIM ** (-0.5)
BF16 = jnp.bfloat16
F32 = jnp.float32
GELU_C = 0.7978845608028654
GELU_A = 0.044715
VMEM_LIMIT = 56 * 1024 * 1024

NT = (((1,), (1,)), ((), ()))
TN = (((0,), (0,)), ((), ()))
NN = (((1,), (0,)), ((), ()))


def mm(a, b, dims=NN):
    return lax.dot_general(a, b, dims, preferred_element_type=F32)


def bucket_of(offset):
    distance = jnp.abs(offset)
    banded = jnp.full(distance.shape, 8, jnp.int32)
    for cutoff in THRESHOLDS:
        banded = banded + (distance >= cutoff).astype(jnp.int32)
    nearby = jnp.where(distance < 8, distance, banded)
    return nearby + jnp.where(offset > 0, 16, 0).astype(jnp.int32)


def bias_tile(vec_ref, head, tile_ref):
    block, wide = tile_ref.shape
    row = jnp.broadcast_to(vec_ref[pl.ds(head, 1), :], (block, wide))
    tile_ref[...] = pltpu.roll(row, wide - block, 1, stride=1, stride_axis=0)


def tile_offset(n, block, query_block, key_block):
    return pl.multiple_of((key_block - query_block + n - 1) * block, 128)


def logits_of(n, block, query_block, q_pair, k_pair, mask, tile_ref):
    masked = jnp.where(mask, q_pair, jnp.zeros_like(q_pair))
    raw = mm(masked, k_pair, NT) * SCALE
    bias = jnp.concatenate(
        [tile_ref[:, pl.ds(tile_offset(n, block, query_block, j), block)] for j in range(n)], axis=1
    )
    return raw + bias


def diagonal_sum(tile):
    rows, wide = tile.shape
    while rows > 1:
        half = rows // 2
        tile = tile[:half] + pltpu.roll(tile[half:], wide - half, 1)
        rows = half
    return tile


def gelu_pair(v):
    square = v * v
    t = jnp.tanh(GELU_C * (v + GELU_A * v * square))
    half = 0.5 * (1.0 + t)
    slope = half + (0.5 * GELU_C) * v * (1.0 - t * t) * (1.0 + (3.0 * GELU_A) * square)
    return v * half, slope


def unpack_kernel(n, piece, in_ref, gate_ref, up_ref):
    main = piece // 128 * 128
    rest = piece - main
    gates, ups = [], []
    for j in range(n):
        block = in_ref[j].astype(F32)
        gates += [block[:, :main], block[:, 2 * main : 2 * main + rest]]
        ups += [block[:, main : 2 * main], block[:, 2 * main + rest :]]
    gate_ref[...] = jnp.concatenate(gates, axis=1)
    up_ref[...] = jnp.concatenate(ups, axis=1)


def unpack_columns(blocks):
    n, rows, both = blocks.shape
    piece = both // 2
    step = min(rows, 64)
    total = n * piece
    return pl.pallas_call(
        functools.partial(unpack_kernel, n, piece),
        grid=(rows // step,),
        in_specs=[pl.BlockSpec((n, step, both), lambda i: (0, i, 0))],
        out_specs=[pl.BlockSpec((step, total), lambda i: (i, 0))] * 2,
        out_shape=[jax.ShapeDtypeStruct((rows, total), F32)] * 2,
        compiler_params=pltpu.CompilerParams(vmem_limit_bytes=VMEM_LIMIT),
        cost_estimate=pl.CostEstimate(flops=0, bytes_accessed=12 * rows * total, transcendentals=0),
        name="unpack_columns",
    )(blocks)


MESH = pl.DeviceIdType.MESH


def remote(src, dst, send, recv, target):
    return pltpu.make_async_remote_copy(
        src_ref=src, dst_ref=dst, send_sem=send, recv_sem=recv, device_id=target, device_id_type=MESH
    )


def greet(n, ne, dp, ex):
    barrier = pltpu.get_barrier_semaphore()
    for d in range(1, n):
        pl.semaphore_signal(barrier, inc=1, device_id=(lax.rem(dp + d, n), ex), device_id_type=MESH)
    for k in range(1, ne):
        pl.semaphore_signal(barrier, inc=1, device_id=(dp, lax.rem(ex + k, ne)), device_id_type=MESH)
    pl.semaphore_wait(barrier, n + ne - 2)


class Chain:
    def __init__(self, n, dp, ex, own, buffer, send, recv):
        self.n, self.dp, self.ex, self.own = n, dp, ex, own
        self.buffer, self.send_sem, self.recv_sem = buffer, send, recv

    def block(self, hop, side):
        return lax.rem(self.dp + self.n + hop * (2 * side - 1), self.n)

    def copy(self, hop, side, first=False):
        at = self.block(hop, side)
        target = lax.rem(self.dp + self.n + 1 - 2 * side, self.n)
        return remote(
            self.own if first else self.buffer.at[at], self.buffer.at[at],
            self.send_sem.at[hop, side], self.recv_sem.at[hop, side], (target, self.ex),
        )

    def has_next(self, side):
        return (self.dp + 1 < self.n) if side == 0 else (self.dp > 0)

    def start(self):
        for side in range(2):
            @pl.when(self.has_next(side))
            def _():
                self.copy(0, side, True).start()

    def held(self, hop, side):
        return (self.dp > hop) if side == 0 else (self.dp + 1 + hop < self.n)

    def arrive(self, hop, side):
        at = self.block(hop + 1, side)
        remote(
            self.buffer.at[at], self.buffer.at[at], self.send_sem.at[hop, side], self.recv_sem.at[hop, side],
            (self.dp, self.ex),
        ).wait_recv()

        @pl.when(self.has_next(side))
        def _():
            self.copy(hop + 1, side).start()

        return at

    def finish(self):
        for hop in range(self.n - 1):
            for side in range(2):
                mine = self.has_next(side)
                if hop:
                    mine = mine & self.held(hop - 1, side)

                @pl.when(mine)
                def _():
                    self.copy(hop, side, hop == 0).wait_send()


def start_kernel(
    n, ne, cap, cap_pad, piece,
    x, wq, wk, wv, extra, wo, meta_in, wg, wu,
    x_all, lq, lk, lv, lext, lwo, meta_all, packed,
    sq, sk, sv, sext, swo, smeta,
    line_send, line_recv, plane_send, plane_recv, core_send, core_recv, chain_send, chain_recv, own_sem,
):
    dp, ex = lax.axis_index("dp"), lax.axis_index("expert")
    own = sq.shape[2]
    greet(n, ne, dp, ex)
    chain = Chain(n, dp, ex, x, x_all, chain_send, chain_recv)

    def column(ref, t):
        return ref.at[:, pl.ds(pl.multiple_of(t * own, 128), own)]

    def line(kind, d):
        t = lax.rem(dp + d, n)
        src, dst = [
            (column(wq, t), sq.at[dp]), (column(wk, t), sk.at[dp]), (column(wv, t), sv.at[dp]),
            (extra, sext.at[dp]), (wo, swo.at[dp]), (smeta, meta_all.at[dp]),
        ][kind]
        return remote(src, dst, line_send.at[kind, d], line_recv.at[kind, d], (t, ex))

    for d in range(1, n):
        for kind in range(4):
            line(kind, d).start()
    chain.start()
    for d in range(1, n):
        line(4, d).start()
    keep = pltpu.make_async_copy(x, x_all.at[dp], own_sem.at[0])
    keep.start()
    sq[dp] = wq[:, pl.ds(pl.multiple_of(dp * own, 128), own)]
    sk[dp] = wk[:, pl.ds(pl.multiple_of(dp * own, 128), own)]
    sv[dp] = wv[:, pl.ds(pl.multiple_of(dp * own, 128), own)]
    sext[dp] = extra[...]
    swo[dp] = wo[...]

    tok = meta_in.shape[1]
    routes = meta_in[...]
    ids = lax.broadcasted_iota(jnp.int32, (ne, tok), 0)
    first = (ids == routes[0:1, :]).astype(F32)
    second = (ids == routes[1:2, :]).astype(F32)
    before = (
        lax.broadcasted_iota(jnp.int32, (tok, tok), 0) < lax.broadcasted_iota(jnp.int32, (tok, tok), 1)
    ).astype(BF16)
    counts = mm((first + second).astype(BF16), before)
    slot_a = jnp.sum(counts * first, axis=0, keepdims=True)
    slot_b = jnp.sum((counts + first) * second, axis=0, keepdims=True)
    wide = routes.astype(F32)
    dest_a = jnp.where(slot_a < cap, wide[0:1, :] * cap_pad + slot_a, -1.0)
    dest_b = jnp.where(slot_b < cap, wide[1:2, :] * cap_pad + slot_b, -1.0)
    gate = wide[2:3, :] * (1.0 / 65536.0)
    smeta[...] = jnp.concatenate([dest_a, dest_b, gate, jnp.zeros((5, tok), F32)], axis=0)
    for d in range(1, n):
        line(5, d).start()
    keep_meta = pltpu.make_async_copy(smeta, meta_all.at[dp], own_sem.at[1])
    keep_meta.start()

    pairs = [(sq, lq), (sk, lk), (sv, lv), (sext, lext), (swo, lwo)]
    partner = ex + 1 - 2 * lax.rem(ex, 2)

    def plane(kind, k):
        src, dst = pairs[kind]
        return remote(
            src, dst.at[:, ex], plane_send.at[kind, k], plane_recv.at[kind, k],
            (dp, lax.rem(ex + 2 * k, ne)),
        )

    def core(kind, k):
        src, dst = pairs[kind]
        at = lax.rem(ex + ne - 2 * k, ne)
        return remote(
            src if k == 0 else dst.at[:, at], dst.at[:, at],
            core_send.at[kind, k], core_recv.at[kind, k], (dp, partner),
        )

    def spread(kind):
        for d in range(1, n):
            line(kind, d).wait_recv()
        for k in range(1, ne // 2):
            plane(kind, k).start()
        core(kind, 0).start()
        pltpu.make_async_copy(pairs[kind][0], pairs[kind][1].at[:, ex], own_sem.at[2 + kind]).start()

    for kind in range(4):
        spread(kind)

    main = piece // 128 * 128
    step = min(wg.shape[0], 64)

    @pl.loop(0, wg.shape[0] // step)
    def _(i):
        rows = pl.ds(pl.multiple_of(i * step, step), step)
        gate_w, up_w = wg[rows, :], wu[rows, :]
        for j in range(n):
            g = gate_w[:, j * piece : (j + 1) * piece]
            u = up_w[:, j * piece : (j + 1) * piece]
            packed[j, rows, :] = jnp.concatenate([g[:, :main], u[:, :main], g[:, main:], u[:, main:]], axis=1)

    spread(4)

    def pass_on(kind):
        for k in range(1, ne // 2):
            plane(kind, k).wait_recv()
            core(kind, k).start()

    def hop(h):
        for side in range(2):
            @pl.when(chain.held(h, side))
            def _():
                chain.arrive(h, side)

    hop(0)
    for kind in range(4):
        pass_on(kind)
    for h in range(1, n - 1):
        hop(h)
        if h == 1:
            pass_on(4)
    if n < 3:
        pass_on(4)
    for kind in range(5):
        for k in range(ne // 2):
            core(kind, k).wait()
        for k in range(1, ne // 2):
            plane(kind, k).wait_send()
        pltpu.make_async_copy(pairs[kind][0], pairs[kind][1].at[:, ex], own_sem.at[2 + kind]).wait()
    for d in range(1, n):
        for kind in range(6):
            line(kind, d).wait_send()
        line(5, d).wait_recv()
    chain.finish()
    keep.wait()
    keep_meta.wait()


def whole(array):
    return pl.BlockSpec(memory_space=pltpu.VMEM)


ANY = pl.BlockSpec(memory_space=pl.ANY)
VM = pl.BlockSpec(memory_space=pltpu.VMEM)


def start(n, ne, cap, cap_pad, x, wq, wk, wv, extra, wo, meta_in, wg, wu):
    tok, width = x.shape
    wrows = wq.shape[0]
    own = width // n
    piece = wg.shape[1] // n
    return pl.pallas_call(
        functools.partial(start_kernel, n, ne, cap, cap_pad, piece),
        in_specs=[VM] * 9,
        out_specs=[ANY] * 7 + [VM],
        out_shape=[
            jax.ShapeDtypeStruct((n, tok, width), BF16),
            jax.ShapeDtypeStruct((n, ne, wrows, own), BF16),
            jax.ShapeDtypeStruct((n, ne, wrows, own), BF16),
            jax.ShapeDtypeStruct((n, ne, wrows, own), BF16),
            jax.ShapeDtypeStruct((n, ne, 16, own), BF16),
            jax.ShapeDtypeStruct((n, ne, wrows, width), BF16),
            jax.ShapeDtypeStruct((n, 8, tok), F32),
            jax.ShapeDtypeStruct((n, tok, 2 * piece), BF16),
        ],
        scratch_shapes=[
            pltpu.VMEM((n, wrows, own), BF16),
            pltpu.VMEM((n, wrows, own), BF16),
            pltpu.VMEM((n, wrows, own), BF16),
            pltpu.VMEM((n, 16, own), BF16),
            pltpu.VMEM((n, wrows, width), BF16),
            pltpu.VMEM((8, tok), F32),
            pltpu.SemaphoreType.DMA((6, n)),
            pltpu.SemaphoreType.DMA((6, n)),
            pltpu.SemaphoreType.DMA((5, ne // 2)),
            pltpu.SemaphoreType.DMA((5, ne // 2)),
            pltpu.SemaphoreType.DMA((5, ne // 2)),
            pltpu.SemaphoreType.DMA((5, ne // 2)),
            pltpu.SemaphoreType.DMA((n, 2)),
            pltpu.SemaphoreType.DMA((n, 2)),
            pltpu.SemaphoreType.DMA((7,)),
        ],
        compiler_params=pltpu.CompilerParams(
            collective_id=1, has_side_effects=True, vmem_limit_bytes=VMEM_LIMIT
        ),
        name="start",
    )(x, wq, wk, wv, extra, wo, meta_in, wg, wu)


def forward_kernel(
    n, ne, cap_pad,
    x_all, wq, wk, wv, wo, gain_one, gain_two, vectors, cot, meta_all, packed,
    normed, qkv, lse, mixed, resid, slots, d_outs, wgu,
    heads, mixed_in, tiles, cot_all, two_all, two_own, two_rows, cot_rows,
    w_send, w_recv, m_send, m_recv, c_send, c_recv, t_send, t_recv,
    pc_send, pc_recv, pt_send, pt_recv, own_sem,
):
    dp, ex = lax.axis_index("dp"), lax.axis_index("expert")
    block, width = cot.shape
    own = heads.shape[1]
    pairs_n = own // 128
    slots_n = ne * cap_pad
    greet(n, ne, dp, ex)

    def weights(d):
        t = lax.rem(dp + d, n)
        return remote(packed.at[t], wgu.at[dp], w_send.at[d], w_recv.at[d], (t, ex))

    cots = Chain(n, dp, ex, cot, cot_all, c_send, c_recv)
    twos = Chain(n, dp, ex, two_own, two_all, t_send, t_recv)
    cots.start()
    keep_w = pltpu.make_async_copy(packed.at[dp], wgu.at[dp], own_sem.at[0])
    keep_w.start()

    def to_plane(rows, land, send, recv, group, k):
        peer = lax.rem(ex + k, ne)
        return remote(
            rows.at[group, pl.ds(pl.multiple_of(peer * cap_pad, 16), cap_pad)], land.at[group, ex],
            send.at[group, k], recv.at[group, k], (dp, peer),
        )

    def kept(rows, land, group, sem):
        return pltpu.make_async_copy(
            rows.at[group, pl.ds(pl.multiple_of(ex * cap_pad, 16), cap_pad)], land.at[group, ex], sem.at[group, 0]
        )

    def dispatch(group, tokens, rows, land, send, recv, weigh):
        meta = meta_all[group]
        ids = lax.broadcasted_iota(jnp.int32, (slots_n, block), 0).astype(F32)
        hit_a, hit_b = ids == meta[0:1, :], ids == meta[1:2, :]
        chosen = jnp.where(hit_a | hit_b, 1.0, 0.0).astype(BF16)
        found = mm(chosen, tokens)
        if weigh:
            gate = meta[2:3, :]
            factor = jnp.sum(
                jnp.where(hit_a, gate, 0.0) + jnp.where(hit_b, 1.0 - gate, 0.0), axis=1, keepdims=True
            )
            found = found * factor
        rows[group] = found.astype(BF16)
        for k in range(1, ne):
            to_plane(rows, land, send, recv, group, k).start()
        kept(rows, land, group, send).start()

    @pl.loop(0, n)
    def _(j):
        at = pl.ds(pl.multiple_of(j * block, block), block)
        xf = x_all[j].astype(F32)
        inverse = lax.rsqrt(jnp.mean(xf * xf, axis=-1, keepdims=True) + EPSILON)
        low = (xf * inverse * gain_one[...]).astype(BF16)
        normed[at, :] = low
        for w, ref in enumerate((wq, wk, wv)):
            qkv[at, w * own : (w + 1) * own] = mm(low, ref[...]).astype(BF16)

    def attend(pair):
        for side in range(2):
            bias_tile(vectors, 2 * pair + side, tiles.at[side])
        lane = lax.broadcasted_iota(jnp.int32, (block, 128), 1)
        low_half = lane < HEAD_DIM
        k_pair = qkv[:, own + pair * 128 : own + (pair + 1) * 128]
        v_pair = qkv[:, 2 * own + pair * 128 : 2 * own + (pair + 1) * 128]

        @pl.loop(0, n)
        def _(i):
            at = pl.ds(pl.multiple_of(i * block, block), block)
            q_pair = qkv[at, pair * 128 : (pair + 1) * 128]
            outs, logs = [], []
            for side in range(2):
                mask = low_half if side == 0 else jnp.logical_not(low_half)
                logits = logits_of(n, block, i, q_pair, k_pair, mask, tiles.at[side])
                row_max = jnp.max(logits, axis=-1, keepdims=True)
                exponent = jnp.exp(logits - row_max)
                total = jnp.sum(exponent, axis=-1, keepdims=True)
                probs_low = (exponent * (1.0 / total)).astype(BF16)
                outs.append(mm(probs_low, v_pair))
                logs.append(jnp.broadcast_to(row_max + jnp.log(total), (block, 128)))
            heads[at, pair * 128 : (pair + 1) * 128] = jnp.where(low_half, outs[0], outs[1]).astype(BF16)
            lse[at, pair * 128 : (pair + 1) * 128] = jnp.where(low_half, logs[0], logs[1])

    def hop(chain, h, then):
        for side in range(2):
            @pl.when(chain.held(h, side))
            def _():
                then(chain.arrive(h, side))

    attend(0)
    hop(cots, 0, lambda at: None)
    for d in range(1, n):
        weights(d).start()
    for pair in range(1, pairs_n):
        attend(pair)

    def give(d):
        t = lax.rem(dp + d, n)
        return remote(
            heads.at[pl.ds(pl.multiple_of(t * block, block), block)], mixed_in.at[dp], m_send.at[d], m_recv.at[d],
            (t, ex),
        )

    for d in range(1, n):
        give(d).start()
    mixed_in[dp] = heads[pl.ds(pl.multiple_of(dp * block, block), block), :]
    dispatch(dp, cot[...], cot_rows, d_outs, pc_send, pc_recv, True)
    for h in range(1, n - 1):
        hop(cots, h, lambda at: None)
    cots.finish()
    for d in range(1, n):
        give(d).wait()
    mixed[...] = jnp.concatenate([mixed_in[j] for j in range(n)], axis=1)
    total = x_all[dp].astype(F32) + mm(mixed[...], wo[...])
    resid[...] = total
    inverse = lax.rsqrt(jnp.mean(total * total, axis=-1, keepdims=True) + EPSILON)
    two_own[...] = (total * inverse * gain_two[...]).astype(BF16)
    twos.start()

    def send_two(group, tokens):
        dispatch(group, tokens, two_rows, slots, pt_send, pt_recv, False)

    send_two(dp, two_own[...])
    for j in range(1, n):
        at = lax.rem(dp + j, n)
        dispatch(at, cot_all[at], cot_rows, d_outs, pc_send, pc_recv, True)
        hop(twos, j - 1, lambda group: send_two(group, two_all[group]))
    twos.finish()
    keep_w.wait()
    for d in range(1, n):
        weights(d).wait()
    for rows, land, send, recv in (
        (two_rows, slots, pt_send, pt_recv), (cot_rows, d_outs, pc_send, pc_recv),
    ):
        @pl.loop(0, n)
        def _(group):
            kept(rows, land, group, send).wait()
            for k in range(1, ne):
                to_plane(rows, land, send, recv, group, k).wait()


def forward(n, ne, cap_pad, x_all, wq, wk, wv, wo, gain_one, gain_two, vectors, cot, meta_all, packed):
    tok, width = cot.shape
    own = wq.shape[1]
    wide = vectors.shape[1]
    both = packed.shape[2]
    slots_n = ne * cap_pad
    sem = pltpu.SemaphoreType.DMA
    return pl.pallas_call(
        functools.partial(forward_kernel, n, ne, cap_pad),
        in_specs=[VM] * 10 + [ANY],
        out_specs=[VM] * 5 + [ANY] * 3,
        out_shape=[
            jax.ShapeDtypeStruct((n * tok, width), BF16),
            jax.ShapeDtypeStruct((n * tok, 3 * own), BF16),
            jax.ShapeDtypeStruct((n * tok, own), F32),
            jax.ShapeDtypeStruct((tok, width), BF16),
            jax.ShapeDtypeStruct((tok, width), F32),
            jax.ShapeDtypeStruct((n, ne, cap_pad, width), BF16),
            jax.ShapeDtypeStruct((n, ne, cap_pad, width), BF16),
            jax.ShapeDtypeStruct((n, tok, both), BF16),
        ],
        scratch_shapes=[
            pltpu.VMEM((n * tok, own), BF16),
            pltpu.VMEM((n, tok, own), BF16),
            pltpu.VMEM((2, tok, wide), F32),
            pltpu.VMEM((n, tok, width), BF16),
            pltpu.VMEM((n, tok, width), BF16),
            pltpu.VMEM((tok, width), BF16),
            pltpu.VMEM((n, slots_n, width), BF16),
            pltpu.VMEM((n, slots_n, width), BF16),
            sem((n,)), sem((n,)), sem((n,)), sem((n,)),
            sem((n, 2)), sem((n, 2)), sem((n, 2)), sem((n, 2)),
            sem((n, ne)), sem((n, ne)), sem((n, ne)), sem((n, ne)),
            sem((1,)),
        ],
        compiler_params=pltpu.CompilerParams(
            collective_id=2, has_side_effects=True, vmem_limit_bytes=VMEM_LIMIT
        ),
        name="forward",
    )(x_all, wq, wk, wv, wo, gain_one, gain_two, vectors, cot, meta_all, packed)


def experts_kernel(
    n, ne, cap_pad, deep, main,
    slots, d_outs, wgu_ref, wd_ref, meta_all,
    out_rows, d_two, gwgu, gwd,
    s_buf, d_buf, back, part, landed, gwgu_acc,
    load_sem, keep_sem, p_send, p_recv, z_send, z_recv,
):
    dp, ex = lax.axis_index("dp"), lax.axis_index("expert")
    slots_n, width = s_buf.shape[1:]
    tok = d_two.shape[0]
    greet(n, ne, dp, ex)
    toward = 2 * ((2 * dp) // n) - 1

    def group_at(step):
        return lax.rem(dp + n + toward * (1 + step), n)

    def load(step, kind):
        at = group_at(step)
        src, dst = ((slots, s_buf), (d_outs, d_buf))[kind]
        return pltpu.make_async_copy(src.at[at], dst.at[at], load_sem.at[kind, step])

    for step in range(n):
        for kind in range(2):
            load(step, kind).start()
    gwgu_acc[...] = jnp.zeros_like(gwgu_acc)
    gwd[...] = jnp.zeros_like(gwd)

    def rows_of(peer):
        return pl.ds(pl.multiple_of(peer * cap_pad, 16), cap_pad)

    def give(at, k):
        peer = lax.rem(ex + k, ne)
        return remote(
            d_buf.at[at, rows_of(peer)], back.at[at, rows_of(ex)], p_send.at[at, k], p_recv.at[at, k], (dp, peer)
        )

    def take(at, k):
        peer = lax.rem(ex + ne - k, ne)
        return remote(
            d_buf.at[at, rows_of(ex)], back.at[at, rows_of(peer)], p_send.at[at, k], p_recv.at[at, k], (dp, peer)
        )

    def keep(at):
        return pltpu.make_async_copy(s_buf.at[at], out_rows.at[at], keep_sem.at[at])

    def owed(at):
        return remote(part.at[at], landed.at[dp], z_send.at[at], z_recv.at[dp], (at, ex))

    def combine(at):
        for k in range(1, ne):
            take(at, k).wait_recv()
        meta = meta_all[at]
        ids = lax.broadcasted_iota(jnp.int32, (slots_n, tok), 0).astype(F32)
        hit = (ids == meta[0:1, :]) | (ids == meta[1:2, :])
        return mm(jnp.where(hit, 1.0, 0.0).astype(BF16), back[at], TN)

    @pl.loop(0, n)
    def _(step):
        at = group_at(step)
        for kind in range(2):
            load(step, kind).wait()
        wgu, wd = wgu_ref[...], wd_ref[...]
        parts = -(-slots_n // 640)
        size = slots_n // parts
        low_lane = lax.broadcasted_iota(jnp.int32, (size, 128), 1) < 64
        for p in range(parts):
            here = slice(p * size, (p + 1) * size)
            rows, d_out = s_buf[at, here, :], d_buf[at, here, :]
            pre = mm(rows, wgu)
            d_hidden = mm(d_out, wd, NT)
            gate, up, tail = pre[:, :main], pre[:, main : 2 * main], pre[:, 2 * main :]
            tail_up = pltpu.roll(tail, 64, 1)
            act, slope = gelu_pair(gate)
            act_t, slope_t = gelu_pair(tail)
            hidden_t = jnp.where(low_lane, act_t * tail_up, 0.0)
            hidden = jnp.concatenate([(act * up).astype(BF16), hidden_t.astype(BF16)], axis=1)
            dh, dh_t = d_hidden[:, :main], d_hidden[:, main:]
            d_gate = dh * up * slope
            d_up = dh * act
            d_tail = jnp.where(low_lane, dh_t * tail_up * slope_t, pltpu.roll(dh_t * act_t, 64, 1))
            d_pre = jnp.concatenate([d_gate.astype(BF16), d_up.astype(BF16), d_tail.astype(BF16)], axis=1)
            d_rows = mm(d_pre, wgu, NT).astype(BF16)
            gwd[...] += mm(hidden, d_out, TN)[:deep]
            d_buf[at, here, :] = d_rows
            if p == parts - 1:
                for k in range(1, ne):
                    give(at, k).start()
                back[at, rows_of(ex), :] = d_buf[at, rows_of(ex), :]
            gwgu_acc[...] += mm(rows, d_pre, TN)
            s_buf[at, here, :] = mm(hidden, wd).astype(BF16)
        keep(at).start()

        @pl.when(step > 0)
        def _():
            past = group_at(step - 1)
            part[past] = combine(past).astype(BF16)
            owed(past).start()

    gwgu[...] = gwgu_acc[...].astype(BF16)
    total = combine(dp)
    for d in range(1, n):
        src = lax.rem(dp + d, n)
        remote(part.at[src], landed.at[src], z_send.at[src], z_recv.at[src], (src, ex)).wait_recv()
        total = total + landed[src].astype(F32)
    d_two[...] = total
    for d in range(1, n):
        owed(lax.rem(dp + d, n)).wait_send()

    @pl.loop(0, n)
    def _(at):
        keep(at).wait()
        for k in range(1, ne):
            give(at, k).wait_send()


def experts(n, ne, cap_pad, deep, slots, d_outs, wgu, wd, meta_all):
    width, columns = wgu.shape
    tok = meta_all.shape[2]
    main = (columns - 128) // 2
    slots_n = ne * cap_pad
    slots = slots.reshape(n, slots_n, width)
    d_outs = d_outs.reshape(n, slots_n, width)
    sem = pltpu.SemaphoreType.DMA
    return pl.pallas_call(
        functools.partial(experts_kernel, n, ne, cap_pad, deep, main),
        in_specs=[ANY, ANY, VM, VM, VM],
        out_specs=[ANY, VM, VM, VM],
        out_shape=[
            jax.ShapeDtypeStruct((n, slots_n, width), BF16),
            jax.ShapeDtypeStruct((tok, width), F32),
            jax.ShapeDtypeStruct((width, columns), BF16),
            jax.ShapeDtypeStruct((deep, width), F32),
        ],
        scratch_shapes=[
            pltpu.VMEM((n, slots_n, width), BF16),
            pltpu.VMEM((n, slots_n, width), BF16),
            pltpu.VMEM((n, slots_n, width), BF16),
            pltpu.VMEM((n, tok, width), BF16),
            pltpu.VMEM((n, tok, width), BF16),
            pltpu.VMEM((width, columns), F32),
            sem((2, n)), sem((n,)), sem((n, ne)), sem((n, ne)), sem((n,)), sem((n,)),
        ],
        compiler_params=pltpu.CompilerParams(
            collective_id=3, has_side_effects=True, vmem_limit_bytes=60 * 1024 * 1024
        ),
        name="experts",
    )(slots, d_outs, wgu, wd, meta_all)


def backward_kernel(
    n, ne, cap_pad,
    d_two, resid, cot, x, gain_one, gain_two, mixed, wo, qkv, lse, normed, vectors, wq, wk, wv, meta_all, in_bucket,
    gwgu, out_rows,
    block_out, grad_in, gq, gk, gv, go, small_all, gw_in, out_in,
    dm, dm_in, tiles, sums, dq_s, dk_s, dv_s, dk_acc, dv_acc, diag, d_res,
    dn_part, dn_land, moe_part, moe_land, out_one,
    g_send, g_land, g2_send, g2_land, o_send, o_land, o2_send, o2_land,
    small_own, small_land, small_sum,
    out_s, out_r, w_s, w_r, dm_s, dm_r, dn_s, dn_r, moe_s, moe_r, g_s, g_r, o_s, o_r, g2_s, g2_r, o2_s, o2_r,
    sp_s, sp_r, sz_s, sz_r, keep_sem,
):
    dp, ex = lax.axis_index("dp"), lax.axis_index("expert")
    tok, width = cot.shape
    own = dq_s.shape[1]
    pairs_n = own // 128
    slots_n = ne * cap_pad
    wrows = go.shape[0]
    greet(n, ne, dp, ex)
    toward = 2 * ((2 * dp) // n) - 1

    def group_at(step):
        return lax.rem(dp + n + toward * (1 + step), n)

    def rows_of(peer):
        return pl.ds(pl.multiple_of(peer * cap_pad, 16), cap_pad)

    def to_line(src, dst, send, recv, t):
        return remote(src.at[t], dst.at[dp], send.at[t], recv.at[dp], (t, ex))

    def from_line(src, dst, send, recv, t):
        return remote(src.at[t], dst.at[t], send.at[t], recv.at[t], (t, ex))

    def to_plane(src, dst, send, recv, k):
        return remote(src, dst.at[ex], send.at[k], recv.at[k], (dp, lax.rem(ex + k, ne)))

    def from_plane(src, dst, send, recv, k):
        peer = lax.rem(ex + ne - k, ne)
        return remote(src, dst.at[peer], send.at[k], recv.at[k], (dp, peer))

    def out_give(at, k):
        peer = lax.rem(ex + k, ne)
        return remote(
            out_rows.at[at, rows_of(peer)], out_in.at[at, rows_of(ex)], out_s.at[at, k], out_r.at[at, k], (dp, peer)
        )

    def out_take(at, k):
        peer = lax.rem(ex + ne - k, ne)
        return remote(
            out_rows.at[at, rows_of(ex)], out_in.at[at, rows_of(peer)], out_s.at[at, k], out_r.at[at, k], (dp, peer)
        )

    def out_keep(at):
        return pltpu.make_async_copy(out_rows.at[at, rows_of(ex)], out_in.at[at, rows_of(ex)], out_s.at[at, 0])

    values = resid[...]
    d_normed = d_two[...]
    inverse = lax.rsqrt(jnp.mean(values * values, axis=-1, keepdims=True) + EPSILON)
    scaled = gain_two[...] * d_normed
    gain_rows_two = jnp.sum(d_normed * values * inverse, axis=0, keepdims=True)
    mean = jnp.mean(scaled * values, axis=-1, keepdims=True)
    d_resid = cot[...].astype(F32) + inverse * scaled - values * (inverse * inverse * inverse * mean)
    d_res[...] = d_resid
    d_attn = d_resid.astype(BF16)
    d_mixed = mm(d_attn, wo[...], NT).astype(BF16)
    for j in range(n):
        dm[j] = d_mixed[:, j * own : (j + 1) * own]
    for d in range(1, n):
        to_line(dm, dm_in, dm_s, dm_r, lax.rem(dp + d, n)).start()
    dm_in[dp] = dm[dp]
    for d in range(1, n):
        to_line(gwgu, gw_in, w_s, w_r, lax.rem(dp + d, n)).start()
    keep_w = pltpu.make_async_copy(gwgu.at[dp], gw_in.at[dp], keep_sem.at[0])
    keep_w.start()

    @pl.loop(0, n)
    def _(step):
        at = group_at(step)
        for k in range(1, ne):
            out_give(at, k).start()
        out_keep(at).start()

    o_send[...] = mm(mixed[...], d_attn, TN).reshape(n, ne, wrows, width).astype(BF16)
    for k in range(1, ne):
        to_plane(o_send.at[:, lax.rem(ex + k, ne)], o_land, o_s, o_r, k).start()
    o_land[ex] = o_send[:, ex]
    for i in range(width // 128):
        small_own[8 + i : 9 + i, :] = gain_rows_two[:, i * 128 : (i + 1) * 128]
    for d in range(1, n):
        from_line(dm, dm_in, dm_s, dm_r, lax.rem(dp + d, n)).wait_recv()

    lane = lax.broadcasted_iota(jnp.int32, (tok, 128), 1)
    low_half = lane < HEAD_DIM
    key_low = lax.broadcasted_iota(jnp.int32, (n * tok, 128), 1) < HEAD_DIM
    diag[...] = jnp.zeros_like(diag)
    for pair in range(pairs_n):
        cols = slice(pair * 128, (pair + 1) * 128)
        for side in range(2):
            bias_tile(vectors, 2 * pair + side, tiles.at[side])
        sums[...] = jnp.zeros_like(sums)
        dk_acc[...] = jnp.zeros_like(dk_acc)
        dv_acc[...] = jnp.zeros_like(dv_acc)
        k_pair = qkv[:, own + pair * 128 : own + (pair + 1) * 128]
        v_pair = qkv[:, 2 * own + pair * 128 : 2 * own + (pair + 1) * 128]

        @pl.loop(0, n)
        def _(i):
            at = pl.ds(pl.multiple_of(i * tok, tok), tok)
            q_pair = qkv[at, cols]
            dm_pair = dm_in[i, :, cols]
            dqs, dks, dvs = [], [], []
            for side in range(2):
                mask = low_half if side == 0 else jnp.logical_not(low_half)
                logits = logits_of(n, tok, i, q_pair, k_pair, mask, tiles.at[side])
                first = pair * 128 + side * HEAD_DIM
                probs = jnp.exp(logits - lse[at, first : first + 1])
                d_probs = mm(jnp.where(mask, dm_pair, jnp.zeros_like(dm_pair)), v_pair, NT)
                inner = jnp.sum(probs * d_probs, axis=-1, keepdims=True)
                d_logits = (probs * (d_probs - inner)).astype(BF16)
                dvs.append(mm(probs.astype(BF16), dm_pair, TN))
                dqs.append(mm(d_logits, k_pair))
                dks.append(mm(d_logits, q_pair, TN))
                wide = d_logits.astype(F32)
                for j in range(n):
                    here = pl.ds(tile_offset(n, tok, i, j), tok)
                    sums[side, :, here] += wide[:, j * tok : (j + 1) * tok]
            dq_s[at, cols] = (jnp.where(low_half, dqs[0], dqs[1]) * SCALE).astype(BF16)
            dk_acc[...] += jnp.where(key_low, dks[0], dks[1])
            dv_acc[...] += jnp.where(key_low, dvs[0], dvs[1])

        dk_s[:, cols] = (dk_acc[...] * SCALE).astype(BF16)
        dv_s[:, cols] = dv_acc[...].astype(BF16)
        for side in range(2):
            diag[2 * pair + side : 2 * pair + side + 1, :] = diagonal_sum(sums[side])

    def d_norm(t):
        at = pl.ds(pl.multiple_of(t * tok, tok), tok)
        return mm(dq_s[at, :], wq[...], NT) + mm(dk_s[at, :], wk[...], NT) + mm(dv_s[at, :], wv[...], NT)

    @pl.loop(0, n - 1)
    def _(step):
        t = group_at(step)
        dn_part[t] = d_norm(t).astype(BF16)
        to_line(dn_part, dn_land, dn_s, dn_r, t).start()

    for w, ref in enumerate((dq_s, dk_s, dv_s)):
        g_send[:, :, w] = mm(normed[...], ref[...], TN).reshape(n, ne, wrows, own).astype(BF16)
    for k in range(1, ne):
        to_plane(g_send.at[:, lax.rem(ex + k, ne)], g_land, g_s, g_r, k).start()
    g_land[ex] = g_send[:, ex]

    rest = diag[...]
    table = jnp.zeros((8, 128), F32)
    for _ in range(3):
        piece = rest.astype(BF16)
        table = table + mm(piece, in_bucket[...])
        rest = rest - piece.astype(F32)
    small_own[16:24, :] = table

    for k in range(1, ne):
        from_plane(o_send.at[:, ex], o_land, o_s, o_r, k).wait_recv()
    total = o_land[0].astype(F32)
    for e in range(1, ne):
        total = total + o_land[e].astype(F32)
    o2_send[...] = total.astype(BF16)
    for d in range(1, n):
        to_line(o2_send, o2_land, o2_s, o2_r, lax.rem(dp + d, n)).start()
    o2_land[dp] = o2_send[dp]

    def moe(at):
        for k in range(1, ne):
            out_take(at, k).wait_recv()
        out_keep(at).wait()
        load = pltpu.make_async_copy(out_in.at[at], out_one, keep_sem.at[1])
        load.start()
        meta = meta_all[at]
        ids = lax.broadcasted_iota(jnp.int32, (slots_n, tok), 0).astype(F32)
        gate = meta[2:3, :]
        weight = jnp.where(ids == meta[0:1, :], gate, 0.0) + jnp.where(ids == meta[1:2, :], 1.0 - gate, 0.0)
        load.wait()
        return mm(weight.astype(BF16), out_one[...], TN)

    @pl.loop(0, n - 1)
    def _(step):
        t = group_at(step)
        moe_part[t] = moe(t).astype(BF16)
        to_line(moe_part, moe_land, moe_s, moe_r, t).start()

    for k in range(1, ne):
        from_plane(g_send.at[:, ex], g_land, g_s, g_r, k).wait_recv()
    total = g_land[0].astype(F32)
    for e in range(1, ne):
        total = total + g_land[e].astype(F32)
    g2_send[...] = total.astype(BF16)
    for d in range(1, n):
        to_line(g2_send, g2_land, g2_s, g2_r, lax.rem(dp + d, n)).start()
    g2_land[dp] = g2_send[dp]

    total = d_norm(dp)
    for d in range(1, n):
        t = lax.rem(dp + d, n)
        from_line(dn_part, dn_land, dn_s, dn_r, t).wait_recv()
        total = total + dn_land[t].astype(F32)
    values = x[...].astype(F32)
    inverse = lax.rsqrt(jnp.mean(values * values, axis=-1, keepdims=True) + EPSILON)
    scaled = gain_one[...] * total
    gain_rows_one = jnp.sum(total * values * inverse, axis=0, keepdims=True)
    mean = jnp.mean(scaled * values, axis=-1, keepdims=True)
    grad_in[...] = (d_res[...] + inverse * scaled - values * (inverse * inverse * inverse * mean)).astype(BF16)
    for i in range(width // 128):
        small_own[i : i + 1, :] = gain_rows_one[:, i * 128 : (i + 1) * 128]
    for k in range(1, ne):
        to_plane(small_own, small_land, sp_s, sp_r, k).start()
    small_land[ex] = small_own[...]
    for k in range(1, ne):
        from_plane(small_own, small_land, sp_s, sp_r, k).wait_recv()
    total = small_land[0]
    for e in range(1, ne):
        total = total + small_land[e]
    small_sum[...] = total
    for d in range(1, n):
        t = lax.rem(dp + d, n)
        remote(small_sum, small_all.at[dp], sz_s.at[t], sz_r.at[dp], (t, ex)).start()
    small_all[dp] = total

    total = resid[...] + moe(dp)
    for d in range(1, n):
        t = lax.rem(dp + d, n)
        from_line(moe_part, moe_land, moe_s, moe_r, t).wait_recv()
        total = total + moe_land[t].astype(F32)
    block_out[...] = total.astype(BF16)

    for d in range(1, n):
        t = lax.rem(dp + d, n)
        from_line(o2_send, o2_land, o2_s, o2_r, t).wait_recv()
        from_line(g2_send, g2_land, g2_s, g2_r, t).wait_recv()
        remote(small_sum, small_all.at[t], sz_s.at[t], sz_r.at[t], (t, ex)).wait_recv()
    total = o2_land[0].astype(F32)
    for j in range(1, n):
        total = total + o2_land[j].astype(F32)
    go[...] = total
    for w, ref in enumerate((gq, gk, gv)):
        ref[...] = jnp.concatenate([g2_land[j, w] for j in range(n)], axis=1).astype(F32)
    for d in range(1, n):
        t = lax.rem(dp + d, n)
        from_line(gwgu, gw_in, w_s, w_r, t).wait_recv()
        for src, dst, send, recv in (
            (gwgu, gw_in, w_s, w_r), (dm, dm_in, dm_s, dm_r), (dn_part, dn_land, dn_s, dn_r),
            (moe_part, moe_land, moe_s, moe_r), (o2_send, o2_land, o2_s, o2_r), (g2_send, g2_land, g2_s, g2_r),
        ):
            to_line(src, dst, send, recv, t).wait_send()
        remote(small_sum, small_all.at[dp], sz_s.at[t], sz_r.at[dp], (t, ex)).wait_send()
    keep_w.wait()
    for k in range(1, ne):
        to_plane(o_send.at[:, ex], o_land, o_s, o_r, k).wait_send()
        to_plane(g_send.at[:, ex], g_land, g_s, g_r, k).wait_send()
        to_plane(small_own, small_land, sp_s, sp_r, k).wait_send()

    @pl.loop(0, n)
    def _(at):
        for k in range(1, ne):
            out_give(at, k).wait_send()


def backward(
    n, ne, cap_pad, wrows, d_two, resid, cot, x, gain_one, gain_two, mixed, wo, qkv, lse, normed, vectors,
    wq, wk, wv, meta_all, in_bucket, gwgu, out_rows,
):
    tok, width = cot.shape
    own = wq.shape[1]
    wide = vectors.shape[1]
    both = gwgu.shape[2]
    slots_n = ne * cap_pad
    length = n * tok
    sem = pltpu.SemaphoreType.DMA
    shape = jax.ShapeDtypeStruct
    return pl.pallas_call(
        functools.partial(backward_kernel, n, ne, cap_pad),
        in_specs=[VM] * 17 + [ANY] * 2,
        out_specs=[VM] * 7 + [ANY] * 2,
        out_shape=[
            shape((tok, width), BF16),
            shape((tok, width), BF16),
            shape((wrows, width), F32),
            shape((wrows, width), F32),
            shape((wrows, width), F32),
            shape((wrows, width), F32),
            shape((n, 24, 128), F32),
            shape((n, tok, both), BF16),
            shape((n, slots_n, width), BF16),
        ],
        scratch_shapes=[
            pltpu.VMEM((n, tok, own), BF16),
            pltpu.VMEM((n, tok, own), BF16),
            pltpu.VMEM((2, tok, wide), F32),
            pltpu.VMEM((2, tok, wide), F32),
            pltpu.VMEM((length, own), BF16),
            pltpu.VMEM((length, own), BF16),
            pltpu.VMEM((length, own), BF16),
            pltpu.VMEM((length, 128), F32),
            pltpu.VMEM((length, 128), F32),
            pltpu.VMEM((8, wide), F32),
            pltpu.VMEM((tok, width), F32),
            pltpu.VMEM((n, tok, width), BF16),
            pltpu.VMEM((n, tok, width), BF16),
            pltpu.VMEM((n, tok, width), BF16),
            pltpu.VMEM((n, tok, width), BF16),
            pltpu.VMEM((slots_n, width), BF16),
            pltpu.VMEM((n, ne, 3, wrows, own), BF16),
            pltpu.VMEM((ne, n, 3, wrows, own), BF16),
            pltpu.VMEM((n, 3, wrows, own), BF16),
            pltpu.VMEM((n, 3, wrows, own), BF16),
            pltpu.VMEM((n, ne, wrows, width), BF16),
            pltpu.VMEM((ne, n, wrows, width), BF16),
            pltpu.VMEM((n, wrows, width), BF16),
            pltpu.VMEM((n, wrows, width), BF16),
            pltpu.VMEM((24, 128), F32),
            pltpu.VMEM((ne, 24, 128), F32),
            pltpu.VMEM((24, 128), F32),
            sem((n, ne)), sem((n, ne)), sem((n,)), sem((n,)), sem((n,)), sem((n,)), sem((n,)), sem((n,)),
            sem((n,)), sem((n,)), sem((ne,)), sem((ne,)), sem((ne,)), sem((ne,)), sem((n,)), sem((n,)),
            sem((n,)), sem((n,)), sem((ne,)), sem((ne,)), sem((n,)), sem((n,)), sem((2,)),
        ],
        compiler_params=pltpu.CompilerParams(
            collective_id=4, has_side_effects=True, vmem_limit_bytes=60 * 1024 * 1024
        ),
        name="backward",
    )(
        d_two, resid, cot, x, gain_one, gain_two, mixed, wo, qkv, lse, normed, vectors, wq, wk, wv, meta_all,
        in_bucket, gwgu, out_rows,
    )


def local(
    inputs, cotangent, gain_attn, w_query, w_key, w_value, w_out, position_bias,
    gain_moe, w_gate, w_up, w_down, routes, gate_fixed,
):
    n = lax.axis_size("dp")
    experts_n = lax.axis_size("expert")
    dp = lax.axis_index("dp")
    ex = lax.axis_index("expert")
    tok, width = inputs.shape[1:]
    length = n * tok
    own = HEADS * HEAD_DIM // n
    heads_own = HEADS // n
    wrows = w_query.shape[0]
    capacity = 5 * tok // (2 * experts_n)
    cap_pad = -(-capacity // 16) * 16
    slots_n = experts_n * cap_pad

    n_gain, n_bias = gain_attn.shape[0], position_bias.shape[0]
    extra = jnp.concatenate([gain_attn, gain_moe, position_bias])
    extra = jnp.zeros((16, own), BF16).at[0, : 2 * n_gain + n_bias].set(extra)
    meta_in = jnp.concatenate([routes[0].T, gate_fixed], axis=0)
    x_all, wq, wk, wv, extras, wo, meta_all, packed = start(
        n, experts_n, capacity, cap_pad,
        inputs[0], w_query, w_key, w_value, extra, w_out, meta_in, w_gate[0], w_up[0],
    )
    wq, wk, wv = (w.reshape(width, own) for w in (wq, wk, wv))
    wo = wo.reshape(width, width)
    extras = extras[:, :, 0]
    gain_one = extras[:, :, :n_gain].reshape(1, -1).astype(F32)
    gain_two = extras[:, :, n_gain : 2 * n_gain].reshape(1, -1).astype(F32)
    table = extras[:, :, 2 * n_gain : 2 * n_gain + n_bias].reshape(BUCKETS, HEADS)
    table = lax.dynamic_slice_in_dim(table, dp * heads_own, heads_own, 1)
    wide = 2 * length
    offsets = jnp.arange(wide, dtype=jnp.int32) - length
    in_bucket = (bucket_of(offsets)[:, None] == jnp.arange(BUCKETS, dtype=jnp.int32)).astype(BF16)
    in_bucket = jnp.where(jnp.abs(offsets)[:, None] < length, in_bucket, jnp.zeros_like(in_bucket))
    vectors = mm(table, in_bucket, (((0,), (1,)), ((), ())))

    normed, qkv, lse, mixed, resid, slots, d_outs, wgu = forward(
        n, experts_n, cap_pad, x_all, wq, wk, wv, wo, gain_one, gain_two, vectors, cotangent[0], meta_all, packed
    )
    wgu = wgu.reshape(width, -1)
    deep = w_down.shape[1]
    padded = -(-deep // 128) * 128
    wd = jnp.pad(w_down[0], ((0, padded - deep), (0, 0)))
    out_rows, grad_normed_two, gwgu, grad_w_down = experts(
        n, experts_n, cap_pad, deep, slots, d_outs, wgu, wd, meta_all
    )

    by_diagonal = jnp.pad(jnp.roll(in_bucket, -tok, axis=0), ((0, 0), (0, 128 - BUCKETS)))
    block_out, grad_inputs, gq, gk, gv, go, small, got, _ = backward(
        n, experts_n, cap_pad, wrows, grad_normed_two, resid, cotangent[0], inputs[0], gain_one, gain_two, mixed, wo,
        qkv, lse, normed, vectors, wq, wk, wv, meta_all, by_diagonal, gwgu.reshape(n, width // n, -1), out_rows,
    )
    grad_w_gate, grad_w_up = unpack_columns(got)

    me = dp * experts_n + ex
    gains = jnp.sum(small[:, :16], axis=0).reshape(2, width)
    mine = lax.dynamic_slice_in_dim(gains, me * n_gain, n_gain, 1)
    grad_table = small[:, 16 : 16 + heads_own, :BUCKETS].reshape(HEADS, BUCKETS).T.reshape(-1)
    grad_bias = lax.dynamic_slice_in_dim(grad_table, me * n_bias, n_bias)

    return (
        block_out[None],
        grad_inputs[None],
        mine[0],
        gq,
        gk,
        gv,
        go,
        grad_bias,
        mine[1],
        grad_w_gate[None],
        grad_w_up[None],
        grad_w_down[None],
    )


def solution(mesh):
    vector = P(("dp", "expert"))
    matrix = P(("dp", "expert"), None)
    split = P("expert", "dp", None)
    return jax.shard_map(
        local,
        mesh=mesh,
        in_specs=(
            split, split, vector, matrix, matrix, matrix, matrix, vector, vector,
            split, split, split, split, P("expert", "dp"),
        ),
        out_specs=(
            split, split, vector, matrix, matrix, matrix, matrix, vector, vector,
            split, split, split,
        ),
        check_vma=False,
    )
```

```python
import functools

import jax
import jax.numpy as jnp
from jax import lax
from jax.experimental import pallas as pl
from jax.experimental.pallas import tpu as pltpu
from jax.sharding import PartitionSpec as P

HEADS = 16
HEAD_DIM = 64
BUCKETS = 32
THRESHOLDS = (12, 16, 23, 32, 46, 64, 91)
EPSILON = 1e-06
SCALE = HEAD_DIM ** (-0.5)
BF16 = jnp.bfloat16
F32 = jnp.float32
GELU_C = 0.7978845608028654
GELU_A = 0.044715
VMEM_LIMIT = 56 * 1024 * 1024

NT = (((1,), (1,)), ((), ()))
TN = (((0,), (0,)), ((), ()))
NN = (((1,), (0,)), ((), ()))


def mm(a, b, dims=NN):
    return lax.dot_general(a, b, dims, preferred_element_type=F32)


def bucket_of(offset):
    distance = jnp.abs(offset)
    banded = jnp.full(distance.shape, 8, jnp.int32)
    for cutoff in THRESHOLDS:
        banded = banded + (distance >= cutoff).astype(jnp.int32)
    nearby = jnp.where(distance < 8, distance, banded)
    return nearby + jnp.where(offset > 0, 16, 0).astype(jnp.int32)


def bias_tile(vec_ref, head, tile_ref):
    block, wide = tile_ref.shape
    row = jnp.broadcast_to(vec_ref[pl.ds(head, 1), :], (block, wide))
    tile_ref[...] = pltpu.roll(row, wide - block, 1, stride=1, stride_axis=0)


def tile_offset(n, block, query_block, key_block):
    return pl.multiple_of((key_block - query_block + n - 1) * block, 128)


def logits_of(n, block, query_block, q_pair, k_pair, mask, tile_ref):
    masked = jnp.where(mask, q_pair, jnp.zeros_like(q_pair))
    raw = mm(masked, k_pair, NT) * SCALE
    bias = jnp.concatenate(
        [tile_ref[:, pl.ds(tile_offset(n, block, query_block, j), block)] for j in range(n)], axis=1
    )
    return raw + bias


def diagonal_sum(tile):
    rows, wide = tile.shape
    while rows > 1:
        half = rows // 2
        tile = tile[:half] + pltpu.roll(tile[half:], wide - half, 1)
        rows = half
    return tile


def gelu_pair(v):
    square = v * v
    t = jnp.tanh(GELU_C * (v + GELU_A * v * square))
    half = 0.5 * (1.0 + t)
    slope = half + (0.5 * GELU_C) * v * (1.0 - t * t) * (1.0 + (3.0 * GELU_A) * square)
    return v * half, slope


MESH = pl.DeviceIdType.MESH


def remote(src, dst, send, recv, target):
    return pltpu.make_async_remote_copy(
        src_ref=src, dst_ref=dst, send_sem=send, recv_sem=recv, device_id=target, device_id_type=MESH
    )


def greet(n, ne, dp, ex):
    barrier = pltpu.get_barrier_semaphore()
    for d in range(1, n):
        pl.semaphore_signal(barrier, inc=1, device_id=(lax.rem(dp + d, n), ex), device_id_type=MESH)
    for k in range(1, ne):
        pl.semaphore_signal(barrier, inc=1, device_id=(dp, lax.rem(ex + k, ne)), device_id_type=MESH)
    pl.semaphore_wait(barrier, n + ne - 2)


class Chain:
    def __init__(self, n, dp, ex, own, buffer, send, recv):
        self.n, self.dp, self.ex, self.own = n, dp, ex, own
        self.buffer, self.send_sem, self.recv_sem = buffer, send, recv

    def block(self, hop, side):
        return lax.rem(self.dp + self.n + hop * (2 * side - 1), self.n)

    def copy(self, hop, side, first=False):
        at = self.block(hop, side)
        target = lax.rem(self.dp + self.n + 1 - 2 * side, self.n)
        return remote(
            self.own if first else self.buffer.at[at], self.buffer.at[at],
            self.send_sem.at[hop, side], self.recv_sem.at[hop, side], (target, self.ex),
        )

    def has_next(self, side):
        return (self.dp + 1 < self.n) if side == 0 else (self.dp > 0)

    def start(self):
        for side in range(2):
            @pl.when(self.has_next(side))
            def _():
                self.copy(0, side, True).start()

    def held(self, hop, side):
        return (self.dp > hop) if side == 0 else (self.dp + 1 + hop < self.n)

    def arrive(self, hop, side):
        at = self.block(hop + 1, side)
        remote(
            self.buffer.at[at], self.buffer.at[at], self.send_sem.at[hop, side], self.recv_sem.at[hop, side],
            (self.dp, self.ex),
        ).wait_recv()

        @pl.when(self.has_next(side))
        def _():
            self.copy(hop + 1, side).start()

        return at

    def finish(self):
        for hop in range(self.n - 1):
            for side in range(2):
                mine = self.has_next(side)
                if hop:
                    mine = mine & self.held(hop - 1, side)

                @pl.when(mine)
                def _():
                    self.copy(hop, side, hop == 0).wait_send()


def start_kernel(
    n, ne, cap, cap_pad, piece,
    x, wq, wk, wv, extra, wo, meta_in, wg, wu,
    x_all, lq, lk, lv, lext, lwo, meta_all, packed,
    sq, sk, sv, sext, swo, smeta,
    line_send, line_recv, plane_send, plane_recv, core_send, core_recv, chain_send, chain_recv, own_sem,
):
    dp, ex = lax.axis_index("dp"), lax.axis_index("expert")
    own = sq.shape[2]
    greet(n, ne, dp, ex)
    chain = Chain(n, dp, ex, x, x_all, chain_send, chain_recv)

    def column(ref, t):
        return ref.at[:, pl.ds(pl.multiple_of(t * own, 128), own)]

    def line(kind, d):
        t = lax.rem(dp + d, n)
        src, dst = [
            (column(wq, t), sq.at[dp]), (column(wk, t), sk.at[dp]), (column(wv, t), sv.at[dp]),
            (extra, sext.at[dp]), (wo, swo.at[dp]), (smeta, meta_all.at[dp]),
        ][kind]
        return remote(src, dst, line_send.at[kind, d], line_recv.at[kind, d], (t, ex))

    for d in range(1, n):
        for kind in range(4):
            line(kind, d).start()
    chain.start()
    for d in range(1, n):
        line(4, d).start()
    keep = pltpu.make_async_copy(x, x_all.at[dp], own_sem.at[0])
    keep.start()
    sq[dp] = wq[:, pl.ds(pl.multiple_of(dp * own, 128), own)]
    sk[dp] = wk[:, pl.ds(pl.multiple_of(dp * own, 128), own)]
    sv[dp] = wv[:, pl.ds(pl.multiple_of(dp * own, 128), own)]
    sext[dp] = extra[...]
    swo[dp] = wo[...]

    tok = meta_in.shape[1]
    routes = meta_in[...]
    ids = lax.broadcasted_iota(jnp.int32, (ne, tok), 0)
    first = (ids == routes[0:1, :]).astype(F32)
    second = (ids == routes[1:2, :]).astype(F32)
    before = (
        lax.broadcasted_iota(jnp.int32, (tok, tok), 0) < lax.broadcasted_iota(jnp.int32, (tok, tok), 1)
    ).astype(BF16)
    counts = mm((first + second).astype(BF16), before)
    slot_a = jnp.sum(counts * first, axis=0, keepdims=True)
    slot_b = jnp.sum((counts + first) * second, axis=0, keepdims=True)
    wide = routes.astype(F32)
    dest_a = jnp.where(slot_a < cap, wide[0:1, :] * cap_pad + slot_a, -1.0)
    dest_b = jnp.where(slot_b < cap, wide[1:2, :] * cap_pad + slot_b, -1.0)
    gate = wide[2:3, :] * (1.0 / 65536.0)
    smeta[...] = jnp.concatenate([dest_a, dest_b, gate, jnp.zeros((5, tok), F32)], axis=0)
    for d in range(1, n):
        line(5, d).start()
    keep_meta = pltpu.make_async_copy(smeta, meta_all.at[dp], own_sem.at[1])
    keep_meta.start()

    pairs = [(sq, lq), (sk, lk), (sv, lv), (sext, lext), (swo, lwo)]
    partner = ex + 1 - 2 * lax.rem(ex, 2)

    def plane(kind, k):
        src, dst = pairs[kind]
        return remote(
            src, dst.at[:, ex], plane_send.at[kind, k], plane_recv.at[kind, k],
            (dp, lax.rem(ex + 2 * k, ne)),
        )

    def core(kind, k):
        src, dst = pairs[kind]
        at = lax.rem(ex + ne - 2 * k, ne)
        return remote(
            src if k == 0 else dst.at[:, at], dst.at[:, at],
            core_send.at[kind, k], core_recv.at[kind, k], (dp, partner),
        )

    def spread(kind):
        for d in range(1, n):
            line(kind, d).wait_recv()
        for k in range(1, ne // 2):
            plane(kind, k).start()
        core(kind, 0).start()
        pltpu.make_async_copy(pairs[kind][0], pairs[kind][1].at[:, ex], own_sem.at[2 + kind]).start()

    for kind in range(4):
        spread(kind)

    main = piece // 128 * 128
    step = min(wg.shape[0], 64)

    @pl.loop(0, wg.shape[0] // step)
    def _(i):
        rows = pl.ds(pl.multiple_of(i * step, step), step)
        gate_w, up_w = wg[rows, :], wu[rows, :]
        for j in range(n):
            g = gate_w[:, j * piece : (j + 1) * piece]
            u = up_w[:, j * piece : (j + 1) * piece]
            packed[j, rows, :] = jnp.concatenate([g[:, :main], u[:, :main], g[:, main:], u[:, main:]], axis=1)

    spread(4)

    def pass_on(kind):
        for k in range(1, ne // 2):
            plane(kind, k).wait_recv()
            core(kind, k).start()

    def hop(h):
        for side in range(2):
            @pl.when(chain.held(h, side))
            def _():
                chain.arrive(h, side)

    hop(0)
    for kind in range(4):
        pass_on(kind)
    for h in range(1, n - 1):
        hop(h)
        if h == 1:
            pass_on(4)
    if n < 3:
        pass_on(4)
    for kind in range(5):
        for k in range(ne // 2):
            core(kind, k).wait()
        for k in range(1, ne // 2):
            plane(kind, k).wait_send()
        pltpu.make_async_copy(pairs[kind][0], pairs[kind][1].at[:, ex], own_sem.at[2 + kind]).wait()
    for d in range(1, n):
        for kind in range(6):
            line(kind, d).wait_send()
        line(5, d).wait_recv()
    chain.finish()
    keep.wait()
    keep_meta.wait()


def whole(array):
    return pl.BlockSpec(memory_space=pltpu.VMEM)


ANY = pl.BlockSpec(memory_space=pl.ANY)
VM = pl.BlockSpec(memory_space=pltpu.VMEM)


def start(n, ne, cap, cap_pad, x, wq, wk, wv, extra, wo, meta_in, wg, wu):
    tok, width = x.shape
    wrows = wq.shape[0]
    own = width // n
    piece = wg.shape[1] // n
    return pl.pallas_call(
        functools.partial(start_kernel, n, ne, cap, cap_pad, piece),
        in_specs=[VM] * 9,
        out_specs=[ANY] * 7 + [VM],
        out_shape=[
            jax.ShapeDtypeStruct((n, tok, width), BF16),
            jax.ShapeDtypeStruct((n, ne, wrows, own), BF16),
            jax.ShapeDtypeStruct((n, ne, wrows, own), BF16),
            jax.ShapeDtypeStruct((n, ne, wrows, own), BF16),
            jax.ShapeDtypeStruct((n, ne, 16, own), BF16),
            jax.ShapeDtypeStruct((n, ne, wrows, width), BF16),
            jax.ShapeDtypeStruct((n, 8, tok), F32),
            jax.ShapeDtypeStruct((n, tok, 2 * piece), BF16),
        ],
        scratch_shapes=[
            pltpu.VMEM((n, wrows, own), BF16),
            pltpu.VMEM((n, wrows, own), BF16),
            pltpu.VMEM((n, wrows, own), BF16),
            pltpu.VMEM((n, 16, own), BF16),
            pltpu.VMEM((n, wrows, width), BF16),
            pltpu.VMEM((8, tok), F32),
            pltpu.SemaphoreType.DMA((6, n)),
            pltpu.SemaphoreType.DMA((6, n)),
            pltpu.SemaphoreType.DMA((5, ne // 2)),
            pltpu.SemaphoreType.DMA((5, ne // 2)),
            pltpu.SemaphoreType.DMA((5, ne // 2)),
            pltpu.SemaphoreType.DMA((5, ne // 2)),
            pltpu.SemaphoreType.DMA((n, 2)),
            pltpu.SemaphoreType.DMA((n, 2)),
            pltpu.SemaphoreType.DMA((7,)),
        ],
        compiler_params=pltpu.CompilerParams(
            collective_id=1, has_side_effects=True, vmem_limit_bytes=VMEM_LIMIT
        ),
        name="start",
    )(x, wq, wk, wv, extra, wo, meta_in, wg, wu)


def forward_kernel(
    n, ne, cap_pad,
    x_all, wq, wk, wv, wo, gain_one, gain_two, vectors, cot, meta_all, packed,
    normed, qkv, lse, mixed, resid, slots, d_outs, wgu,
    heads, mixed_in, tiles, cot_all, two_all, two_own, two_rows, cot_rows,
    w_send, w_recv, m_send, m_recv, c_send, c_recv, t_send, t_recv,
    pc_send, pc_recv, pt_send, pt_recv, own_sem,
):
    dp, ex = lax.axis_index("dp"), lax.axis_index("expert")
    block, width = cot.shape
    own = heads.shape[1]
    pairs_n = own // 128
    slots_n = ne * cap_pad
    greet(n, ne, dp, ex)

    def weights(d):
        t = lax.rem(dp + d, n)
        return remote(packed.at[t], wgu.at[dp], w_send.at[d], w_recv.at[d], (t, ex))

    cots = Chain(n, dp, ex, cot, cot_all, c_send, c_recv)
    twos = Chain(n, dp, ex, two_own, two_all, t_send, t_recv)
    cots.start()
    keep_w = pltpu.make_async_copy(packed.at[dp], wgu.at[dp], own_sem.at[0])
    keep_w.start()

    def to_plane(rows, land, send, recv, group, k):
        peer = lax.rem(ex + k, ne)
        return remote(
            rows.at[group, pl.ds(pl.multiple_of(peer * cap_pad, 16), cap_pad)], land.at[group, ex],
            send.at[group, k], recv.at[group, k], (dp, peer),
        )

    def kept(rows, land, group, sem):
        return pltpu.make_async_copy(
            rows.at[group, pl.ds(pl.multiple_of(ex * cap_pad, 16), cap_pad)], land.at[group, ex], sem.at[group, 0]
        )

    def dispatch(group, tokens, rows, land, send, recv, weigh):
        meta = meta_all[group]
        ids = lax.broadcasted_iota(jnp.int32, (slots_n, block), 0).astype(F32)
        hit_a, hit_b = ids == meta[0:1, :], ids == meta[1:2, :]
        chosen = jnp.where(hit_a | hit_b, 1.0, 0.0).astype(BF16)
        found = mm(chosen, tokens)
        if weigh:
            gate = meta[2:3, :]
            factor = jnp.sum(
                jnp.where(hit_a, gate, 0.0) + jnp.where(hit_b, 1.0 - gate, 0.0), axis=1, keepdims=True
            )
            found = found * factor
        rows[group] = found.astype(BF16)
        for k in range(1, ne):
            to_plane(rows, land, send, recv, group, k).start()
        kept(rows, land, group, send).start()

    def send_cot(group, tokens):
        dispatch(group, tokens, cot_rows, d_outs, pc_send, pc_recv, True)

    send_cot(dp, cot[...])

    @pl.loop(0, n)
    def _(j):
        at = pl.ds(pl.multiple_of(j * block, block), block)
        xf = x_all[j].astype(F32)
        inverse = lax.rsqrt(jnp.mean(xf * xf, axis=-1, keepdims=True) + EPSILON)
        low = (xf * inverse * gain_one[...]).astype(BF16)
        normed[at, :] = low
        for w, ref in enumerate((wq, wk, wv)):
            qkv[at, w * own : (w + 1) * own] = mm(low, ref[...]).astype(BF16)

    def attend(pair):
        for side in range(2):
            bias_tile(vectors, 2 * pair + side, tiles.at[side])
        lane = lax.broadcasted_iota(jnp.int32, (block, 128), 1)
        low_half = lane < HEAD_DIM
        k_pair = qkv[:, own + pair * 128 : own + (pair + 1) * 128]
        v_pair = qkv[:, 2 * own + pair * 128 : 2 * own + (pair + 1) * 128]

        @pl.loop(0, n)
        def _(i):
            at = pl.ds(pl.multiple_of(i * block, block), block)
            q_pair = qkv[at, pair * 128 : (pair + 1) * 128]
            outs, logs = [], []
            for side in range(2):
                mask = low_half if side == 0 else jnp.logical_not(low_half)
                logits = logits_of(n, block, i, q_pair, k_pair, mask, tiles.at[side])
                row_max = jnp.max(logits, axis=-1, keepdims=True)
                exponent = jnp.exp(logits - row_max)
                total = jnp.sum(exponent, axis=-1, keepdims=True)
                probs_low = (exponent * (1.0 / total)).astype(BF16)
                outs.append(mm(probs_low, v_pair))
                logs.append(jnp.broadcast_to(row_max + jnp.log(total), (block, 128)))
            heads[at, pair * 128 : (pair + 1) * 128] = jnp.where(low_half, outs[0], outs[1]).astype(BF16)
            lse[at, pair * 128 : (pair + 1) * 128] = jnp.where(low_half, logs[0], logs[1])

    def hop(chain, h, then):
        for side in range(2):
            @pl.when(chain.held(h, side))
            def _():
                then(chain.arrive(h, side))

    def cot_hop(h):
        hop(cots, h, lambda group: send_cot(group, cot_all[group]))

    cot_hop(0)
    for d in range(1, n):
        weights(d).start()
    attend(0)
    if n > 2:
        cot_hop(1)
    for pair in range(1, pairs_n):
        attend(pair)

    def give(d):
        t = lax.rem(dp + d, n)
        return remote(
            heads.at[pl.ds(pl.multiple_of(t * block, block), block)], mixed_in.at[dp], m_send.at[d], m_recv.at[d],
            (t, ex),
        )

    for d in range(1, n):
        give(d).start()
    mixed_in[dp] = heads[pl.ds(pl.multiple_of(dp * block, block), block), :]
    for h in range(2, n - 1):
        cot_hop(h)
    for d in range(1, n):
        give(d).wait()
    mixed[...] = jnp.concatenate([mixed_in[j] for j in range(n)], axis=1)
    total = x_all[dp].astype(F32) + mm(mixed[...], wo[...])
    resid[...] = total
    inverse = lax.rsqrt(jnp.mean(total * total, axis=-1, keepdims=True) + EPSILON)
    two_own[...] = (total * inverse * gain_two[...]).astype(BF16)
    twos.start()

    def send_two(group, tokens):
        dispatch(group, tokens, two_rows, slots, pt_send, pt_recv, False)

    send_two(dp, two_own[...])
    for h in range(n - 1):
        hop(twos, h, lambda group: send_two(group, two_all[group]))
    cots.finish()
    twos.finish()
    keep_w.wait()
    for d in range(1, n):
        weights(d).wait()
    for rows, land, send, recv in (
        (two_rows, slots, pt_send, pt_recv), (cot_rows, d_outs, pc_send, pc_recv),
    ):
        @pl.loop(0, n)
        def _(group):
            kept(rows, land, group, send).wait()
            for k in range(1, ne):
                to_plane(rows, land, send, recv, group, k).wait()


def forward(n, ne, cap_pad, x_all, wq, wk, wv, wo, gain_one, gain_two, vectors, cot, meta_all, packed):
    tok, width = cot.shape
    own = wq.shape[1]
    wide = vectors.shape[1]
    both = packed.shape[2]
    slots_n = ne * cap_pad
    sem = pltpu.SemaphoreType.DMA
    return pl.pallas_call(
        functools.partial(forward_kernel, n, ne, cap_pad),
        in_specs=[VM] * 10 + [ANY],
        out_specs=[VM] * 5 + [ANY] * 3,
        out_shape=[
            jax.ShapeDtypeStruct((n * tok, width), BF16),
            jax.ShapeDtypeStruct((n * tok, 3 * own), BF16),
            jax.ShapeDtypeStruct((n * tok, own), F32),
            jax.ShapeDtypeStruct((tok, width), BF16),
            jax.ShapeDtypeStruct((tok, width), F32),
            jax.ShapeDtypeStruct((n, ne, cap_pad, width), BF16),
            jax.ShapeDtypeStruct((n, ne, cap_pad, width), BF16),
            jax.ShapeDtypeStruct((n, tok, both), BF16),
        ],
        scratch_shapes=[
            pltpu.VMEM((n * tok, own), BF16),
            pltpu.VMEM((n, tok, own), BF16),
            pltpu.VMEM((2, tok, wide), F32),
            pltpu.VMEM((n, tok, width), BF16),
            pltpu.VMEM((n, tok, width), BF16),
            pltpu.VMEM((tok, width), BF16),
            pltpu.VMEM((n, slots_n, width), BF16),
            pltpu.VMEM((n, slots_n, width), BF16),
            sem((n,)), sem((n,)), sem((n,)), sem((n,)),
            sem((n, 2)), sem((n, 2)), sem((n, 2)), sem((n, 2)),
            sem((n, ne)), sem((n, ne)), sem((n, ne)), sem((n, ne)),
            sem((1,)),
        ],
        compiler_params=pltpu.CompilerParams(
            collective_id=2, has_side_effects=True, vmem_limit_bytes=VMEM_LIMIT
        ),
        name="forward",
    )(x_all, wq, wk, wv, wo, gain_one, gain_two, vectors, cot, meta_all, packed)


def experts_kernel(
    n, ne, cap_pad, deep, main,
    slots, d_outs, wgu_ref, wd_ref, meta_all,
    out_rows, d_two, gwgu, gwd,
    s_buf, d_buf, back, part, landed, gwgu_acc,
    load_sem, keep_sem, p_send, p_recv, z_send, z_recv,
):
    dp, ex = lax.axis_index("dp"), lax.axis_index("expert")
    slots_n, width = s_buf.shape[1:]
    tok = d_two.shape[0]
    greet(n, ne, dp, ex)
    toward = 2 * ((2 * dp) // n) - 1

    def group_at(step):
        return lax.rem(dp + n + toward * (1 + step), n)

    def load(step, kind):
        at = group_at(step)
        src, dst = ((slots, s_buf), (d_outs, d_buf))[kind]
        return pltpu.make_async_copy(src.at[at], dst.at[at], load_sem.at[kind, step])

    for step in range(n):
        for kind in range(2):
            load(step, kind).start()
    gwgu_acc[...] = jnp.zeros_like(gwgu_acc)
    gwd[...] = jnp.zeros_like(gwd)

    def rows_of(peer):
        return pl.ds(pl.multiple_of(peer * cap_pad, 16), cap_pad)

    def give(at, k):
        peer = lax.rem(ex + k, ne)
        return remote(
            d_buf.at[at, rows_of(peer)], back.at[at, rows_of(ex)], p_send.at[at, k], p_recv.at[at, k], (dp, peer)
        )

    def take(at, k):
        peer = lax.rem(ex + ne - k, ne)
        return remote(
            d_buf.at[at, rows_of(ex)], back.at[at, rows_of(peer)], p_send.at[at, k], p_recv.at[at, k], (dp, peer)
        )

    def keep(at):
        return pltpu.make_async_copy(s_buf.at[at], out_rows.at[at], keep_sem.at[at])

    def owed(at):
        return remote(part.at[at], landed.at[dp], z_send.at[at], z_recv.at[dp], (at, ex))

    def combine(at):
        for k in range(1, ne):
            take(at, k).wait_recv()
        meta = meta_all[at]
        ids = lax.broadcasted_iota(jnp.int32, (slots_n, tok), 0).astype(F32)
        hit = (ids == meta[0:1, :]) | (ids == meta[1:2, :])
        return mm(jnp.where(hit, 1.0, 0.0).astype(BF16), back[at], TN)

    @pl.loop(0, n)
    def _(step):
        at = group_at(step)
        for kind in range(2):
            load(step, kind).wait()
        wgu, wd = wgu_ref[...], wd_ref[...]
        parts = -(-slots_n // 640)
        size = slots_n // parts
        low_lane = lax.broadcasted_iota(jnp.int32, (size, 128), 1) < 64
        for p in range(parts):
            here = slice(p * size, (p + 1) * size)
            rows, d_out = s_buf[at, here, :], d_buf[at, here, :]
            pre = mm(rows, wgu)
            d_hidden = mm(d_out, wd, NT)
            gate, up, tail = pre[:, :main], pre[:, main : 2 * main], pre[:, 2 * main :]
            tail_up = pltpu.roll(tail, 64, 1)
            act, slope = gelu_pair(gate)
            act_t, slope_t = gelu_pair(tail)
            hidden_t = jnp.where(low_lane, act_t * tail_up, 0.0)
            hidden = jnp.concatenate([(act * up).astype(BF16), hidden_t.astype(BF16)], axis=1)
            dh, dh_t = d_hidden[:, :main], d_hidden[:, main:]
            d_gate = dh * up * slope
            d_up = dh * act
            d_tail = jnp.where(low_lane, dh_t * tail_up * slope_t, pltpu.roll(dh_t * act_t, 64, 1))
            d_pre = jnp.concatenate([d_gate.astype(BF16), d_up.astype(BF16), d_tail.astype(BF16)], axis=1)
            d_rows = mm(d_pre, wgu, NT).astype(BF16)
            gwd[...] += mm(hidden, d_out, TN)[:deep]
            d_buf[at, here, :] = d_rows
            if p == parts - 1:
                for k in range(1, ne):
                    give(at, k).start()
                back[at, rows_of(ex), :] = d_buf[at, rows_of(ex), :]
            gwgu_acc[...] += mm(rows, d_pre, TN)
            s_buf[at, here, :] = mm(hidden, wd).astype(BF16)
        keep(at).start()

        @pl.when(step > 0)
        def _():
            past = group_at(step - 1)
            part[past] = combine(past).astype(BF16)
            owed(past).start()

    gwgu[...] = gwgu_acc[...].astype(BF16)
    total = combine(dp)
    for d in range(1, n):
        src = lax.rem(dp + d, n)
        remote(part.at[src], landed.at[src], z_send.at[src], z_recv.at[src], (src, ex)).wait_recv()
        total = total + landed[src].astype(F32)
    d_two[...] = total
    for d in range(1, n):
        owed(lax.rem(dp + d, n)).wait_send()

    @pl.loop(0, n)
    def _(at):
        keep(at).wait()
        for k in range(1, ne):
            give(at, k).wait_send()


def experts(n, ne, cap_pad, deep, slots, d_outs, wgu, wd, meta_all):
    width, columns = wgu.shape
    tok = meta_all.shape[2]
    main = (columns - 128) // 2
    slots_n = ne * cap_pad
    slots = slots.reshape(n, slots_n, width)
    d_outs = d_outs.reshape(n, slots_n, width)
    sem = pltpu.SemaphoreType.DMA
    return pl.pallas_call(
        functools.partial(experts_kernel, n, ne, cap_pad, deep, main),
        in_specs=[ANY, ANY, VM, VM, VM],
        out_specs=[ANY, VM, VM, VM],
        out_shape=[
            jax.ShapeDtypeStruct((n, slots_n, width), BF16),
            jax.ShapeDtypeStruct((tok, width), F32),
            jax.ShapeDtypeStruct((width, columns), BF16),
            jax.ShapeDtypeStruct((deep, width), F32),
        ],
        scratch_shapes=[
            pltpu.VMEM((n, slots_n, width), BF16),
            pltpu.VMEM((n, slots_n, width), BF16),
            pltpu.VMEM((n, slots_n, width), BF16),
            pltpu.VMEM((n, tok, width), BF16),
            pltpu.VMEM((n, tok, width), BF16),
            pltpu.VMEM((width, columns), F32),
            sem((2, n)), sem((n,)), sem((n, ne)), sem((n, ne)), sem((n,)), sem((n,)),
        ],
        compiler_params=pltpu.CompilerParams(
            collective_id=3, has_side_effects=True, vmem_limit_bytes=60 * 1024 * 1024
        ),
        name="experts",
    )(slots, d_outs, wgu, wd, meta_all)


def backward_kernel(
    n, ne, cap_pad,
    d_two, resid, cot, x, gain_one, gain_two, mixed, wo, qkv, lse, normed, vectors, wq, wk, wv, meta_all, in_bucket,
    gwgu, out_rows,
    block_out, grad_in, g_all, small_all, gw_in, out_in,
    dm, dm_in, tiles, sums, dq_s, dk_s, dv_s, dk_acc, dv_acc, diag, d_res,
    dn_part, dn_land, moe_part, moe_land, out_one,
    g_send, g_land, g2_send, g2_land, o_send, o_land, o2_send, o2_land,
    small_own, small_land, small_sum,
    out_s, out_r, w_s, w_r, dm_s, dm_r, dn_s, dn_r, moe_s, moe_r, g_s, g_r, o_s, o_r, g2_s, g2_r, o2_s, o2_r,
    sp_s, sp_r, sz_s, sz_r, keep_sem,
):
    dp, ex = lax.axis_index("dp"), lax.axis_index("expert")
    tok, width = cot.shape
    own = dq_s.shape[1]
    pairs_n = own // 128
    slots_n = ne * cap_pad
    wrows = g_all.shape[1]
    greet(n, ne, dp, ex)
    toward = 2 * ((2 * dp) // n) - 1

    def group_at(step):
        return lax.rem(dp + n + toward * (1 + step), n)

    def rows_of(peer):
        return pl.ds(pl.multiple_of(peer * cap_pad, 16), cap_pad)

    def to_line(src, dst, send, recv, t):
        return remote(src.at[t], dst.at[dp], send.at[t], recv.at[dp], (t, ex))

    def from_line(src, dst, send, recv, t):
        return remote(src.at[t], dst.at[t], send.at[t], recv.at[t], (t, ex))

    def to_plane(src, dst, send, recv, k):
        return remote(src, dst.at[ex], send.at[k], recv.at[k], (dp, lax.rem(ex + k, ne)))

    def from_plane(src, dst, send, recv, k):
        peer = lax.rem(ex + ne - k, ne)
        return remote(src, dst.at[peer], send.at[k], recv.at[k], (dp, peer))

    def out_give(at, k):
        peer = lax.rem(ex + k, ne)
        return remote(
            out_rows.at[at, rows_of(peer)], out_in.at[at, rows_of(ex)], out_s.at[at, k], out_r.at[at, k], (dp, peer)
        )

    def out_take(at, k):
        peer = lax.rem(ex + ne - k, ne)
        return remote(
            out_rows.at[at, rows_of(ex)], out_in.at[at, rows_of(peer)], out_s.at[at, k], out_r.at[at, k], (dp, peer)
        )

    def out_keep(at):
        return pltpu.make_async_copy(out_rows.at[at, rows_of(ex)], out_in.at[at, rows_of(ex)], out_s.at[at, 0])

    values = resid[...]
    d_normed = d_two[...]
    inverse = lax.rsqrt(jnp.mean(values * values, axis=-1, keepdims=True) + EPSILON)
    scaled = gain_two[...] * d_normed
    gain_rows_two = jnp.sum(d_normed * values * inverse, axis=0, keepdims=True)
    mean = jnp.mean(scaled * values, axis=-1, keepdims=True)
    d_resid = cot[...].astype(F32) + inverse * scaled - values * (inverse * inverse * inverse * mean)
    d_res[...] = d_resid
    d_attn = d_resid.astype(BF16)
    d_mixed = mm(d_attn, wo[...], NT).astype(BF16)
    for j in range(n):
        dm[j] = d_mixed[:, j * own : (j + 1) * own]
    for d in range(1, n):
        to_line(dm, dm_in, dm_s, dm_r, lax.rem(dp + d, n)).start()
    dm_in[dp] = dm[dp]
    for d in range(1, n):
        to_line(gwgu, gw_in, w_s, w_r, lax.rem(dp + d, n)).start()
    keep_w = pltpu.make_async_copy(gwgu.at[dp], gw_in.at[dp], keep_sem.at[0])
    keep_w.start()

    @pl.loop(0, n)
    def _(step):
        at = group_at(step)
        for k in range(1, ne):
            out_give(at, k).start()
        out_keep(at).start()

    o_send[...] = mm(mixed[...], d_attn, TN).reshape(n, ne, wrows, width).astype(BF16)
    for k in range(1, ne):
        to_plane(o_send.at[:, lax.rem(ex + k, ne)], o_land, o_s, o_r, k).start()
    o_land[ex] = o_send[:, ex]
    for i in range(width // 128):
        small_own[8 + i : 9 + i, :] = gain_rows_two[:, i * 128 : (i + 1) * 128]
    for d in range(1, n):
        from_line(dm, dm_in, dm_s, dm_r, lax.rem(dp + d, n)).wait_recv()

    lane = lax.broadcasted_iota(jnp.int32, (tok, 128), 1)
    low_half = lane < HEAD_DIM
    key_low = lax.broadcasted_iota(jnp.int32, (n * tok, 128), 1) < HEAD_DIM
    diag[...] = jnp.zeros_like(diag)
    for pair in range(pairs_n):
        cols = slice(pair * 128, (pair + 1) * 128)
        for side in range(2):
            bias_tile(vectors, 2 * pair + side, tiles.at[side])
        sums[...] = jnp.zeros_like(sums)
        dk_acc[...] = jnp.zeros_like(dk_acc)
        dv_acc[...] = jnp.zeros_like(dv_acc)
        k_pair = qkv[:, own + pair * 128 : own + (pair + 1) * 128]
        v_pair = qkv[:, 2 * own + pair * 128 : 2 * own + (pair + 1) * 128]

        @pl.loop(0, n)
        def _(i):
            at = pl.ds(pl.multiple_of(i * tok, tok), tok)
            q_pair = qkv[at, cols]
            dm_pair = dm_in[i, :, cols]
            dqs, dks, dvs = [], [], []
            for side in range(2):
                mask = low_half if side == 0 else jnp.logical_not(low_half)
                logits = logits_of(n, tok, i, q_pair, k_pair, mask, tiles.at[side])
                first = pair * 128 + side * HEAD_DIM
                probs = jnp.exp(logits - lse[at, first : first + 1])
                d_probs = mm(jnp.where(mask, dm_pair, jnp.zeros_like(dm_pair)), v_pair, NT)
                inner = jnp.sum(probs * d_probs, axis=-1, keepdims=True)
                d_logits = (probs * (d_probs - inner)).astype(BF16)
                dvs.append(mm(probs.astype(BF16), dm_pair, TN))
                dqs.append(mm(d_logits, k_pair))
                dks.append(mm(d_logits, q_pair, TN))
                wide = d_logits.astype(F32)
                for j in range(n):
                    here = pl.ds(tile_offset(n, tok, i, j), tok)
                    sums[side, :, here] += wide[:, j * tok : (j + 1) * tok]
            dq_s[at, cols] = (jnp.where(low_half, dqs[0], dqs[1]) * SCALE).astype(BF16)
            dk_acc[...] += jnp.where(key_low, dks[0], dks[1])
            dv_acc[...] += jnp.where(key_low, dvs[0], dvs[1])

        dk_s[:, cols] = (dk_acc[...] * SCALE).astype(BF16)
        dv_s[:, cols] = dv_acc[...].astype(BF16)
        for side in range(2):
            diag[2 * pair + side : 2 * pair + side + 1, :] = diagonal_sum(sums[side])

    def d_norm(t):
        at = pl.ds(pl.multiple_of(t * tok, tok), tok)
        return mm(dq_s[at, :], wq[...], NT) + mm(dk_s[at, :], wk[...], NT) + mm(dv_s[at, :], wv[...], NT)

    def sum_copy(part, land, send, recv, r, side):
        t = lax.rem(dp + n + (n - r) * (1 - 2 * side), n)
        target = lax.rem(dp + n + 1 - 2 * side, n)
        return t, remote(part.at[t], land.at[r - 1, side], send.at[r - 1, side], recv.at[r - 1, side], (target, ex))

    def takes_part(r, side):
        return ((side == 0) & (dp < r) & (dp + 1 < n)) | ((side == 1) & (dp + r >= n) & (dp > 0))

    def is_fed(r, side):
        return ((side == 0) & (dp > 0) & (r > 1)) | ((side == 1) & (dp + 1 < n) & (r > 1))

    def fed(part, land, send, recv, r, side):
        remote(
            part.at[dp], land.at[r - 1, side], send.at[r - 1, side], recv.at[r - 1, side], (dp, ex)
        ).wait_recv()

    def sum_round(part, land, send, recv, term, r):
        @pl.loop(0, 2)
        def _(side):
            @pl.when(takes_part(r, side))
            def _():
                t, copy = sum_copy(part, land, send, recv, r, side)
                mine = term(t)

                @pl.when(is_fed(r, side))
                def _():
                    fed(part, land, send, recv, r - 1, side)
                    part[t] = (mine + land[max(r - 2, 0), side].astype(F32)).astype(BF16)

                @pl.when(jnp.logical_not(is_fed(r, side)))
                def _():
                    part[t] = mine.astype(BF16)

                copy.start()

    def sum_end(part, land, send, recv, mine):
        @pl.when(dp > 0)
        def _():
            fed(part, land, send, recv, n - 1, 0)

        @pl.when(dp + 1 < n)
        def _():
            fed(part, land, send, recv, n - 1, 1)

        left = jnp.where(dp > 0, land[n - 2, 0].astype(F32), 0.0)
        right = jnp.where(dp + 1 < n, land[n - 2, 1].astype(F32), 0.0)
        return mine + left + right

    def sum_sent(part, land, send, recv):
        for r in range(1, n):
            for side in range(2):
                @pl.when(takes_part(r, side))
                def _():
                    sum_copy(part, land, send, recv, r, side)[1].wait_send()

    dn = (dn_part, dn_land, dn_s, dn_r)
    moes = (moe_part, moe_land, moe_s, moe_r)
    sum_round(*dn, d_norm, 1)

    for w, ref in enumerate((dq_s, dk_s, dv_s)):
        g_send[:, :, w] = mm(normed[...], ref[...], TN).reshape(n, ne, wrows, own).astype(BF16)
    for k in range(1, ne):
        to_plane(g_send.at[:, lax.rem(ex + k, ne)], g_land, g_s, g_r, k).start()
    g_land[ex] = g_send[:, ex]

    for r in range(2, n):
        sum_round(*dn, d_norm, r)

    rest = diag[...]
    table = jnp.zeros((8, 128), F32)
    for _ in range(3):
        piece = rest.astype(BF16)
        table = table + mm(piece, in_bucket[...])
        rest = rest - piece.astype(F32)
    small_own[16:24, :] = table

    for k in range(1, ne):
        from_plane(o_send.at[:, ex], o_land, o_s, o_r, k).wait_recv()
    total = o_land[0].astype(F32)
    for e in range(1, ne):
        total = total + o_land[e].astype(F32)
    o2_send[...] = total.astype(BF16)
    for d in range(1, n):
        to_line(o2_send, o2_land, o2_s, o2_r, lax.rem(dp + d, n)).start()
    o2_land[dp] = o2_send[dp]

    def moe(at):
        for k in range(1, ne):
            out_take(at, k).wait_recv()
        out_keep(at).wait()
        load = pltpu.make_async_copy(out_in.at[at], out_one, keep_sem.at[1])
        load.start()
        meta = meta_all[at]
        ids = lax.broadcasted_iota(jnp.int32, (slots_n, tok), 0).astype(F32)
        gate = meta[2:3, :]
        weight = jnp.where(ids == meta[0:1, :], gate, 0.0) + jnp.where(ids == meta[1:2, :], 1.0 - gate, 0.0)
        load.wait()
        return mm(weight.astype(BF16), out_one[...], TN)

    for r in range(1, n):
        sum_round(*moes, moe, r)

    for k in range(1, ne):
        from_plane(g_send.at[:, ex], g_land, g_s, g_r, k).wait_recv()
    total = g_land[0].astype(F32)
    for e in range(1, ne):
        total = total + g_land[e].astype(F32)
    g2_send[...] = total.astype(BF16)
    for d in range(1, n):
        to_line(g2_send, g2_land, g2_s, g2_r, lax.rem(dp + d, n)).start()
    g2_land[dp] = g2_send[dp]

    total = sum_end(*dn, d_norm(dp))
    values = x[...].astype(F32)
    inverse = lax.rsqrt(jnp.mean(values * values, axis=-1, keepdims=True) + EPSILON)
    scaled = gain_one[...] * total
    gain_rows_one = jnp.sum(total * values * inverse, axis=0, keepdims=True)
    mean = jnp.mean(scaled * values, axis=-1, keepdims=True)
    grad_in[...] = (d_res[...] + inverse * scaled - values * (inverse * inverse * inverse * mean)).astype(BF16)
    for i in range(width // 128):
        small_own[i : i + 1, :] = gain_rows_one[:, i * 128 : (i + 1) * 128]
    for k in range(1, ne):
        to_plane(small_own, small_land, sp_s, sp_r, k).start()
    small_land[ex] = small_own[...]
    for k in range(1, ne):
        from_plane(small_own, small_land, sp_s, sp_r, k).wait_recv()
    total = small_land[0]
    for e in range(1, ne):
        total = total + small_land[e]
    small_sum[...] = total
    for d in range(1, n):
        t = lax.rem(dp + d, n)
        remote(small_sum, small_all.at[dp], sz_s.at[t], sz_r.at[dp], (t, ex)).start()
    small_all[dp] = total

    block_out[...] = sum_end(*moes, resid[...] + moe(dp)).astype(BF16)

    for d in range(1, n):
        t = lax.rem(dp + d, n)
        from_line(o2_send, o2_land, o2_s, o2_r, t).wait_recv()
        from_line(g2_send, g2_land, g2_s, g2_r, t).wait_recv()
        remote(small_sum, small_all.at[t], sz_s.at[t], sz_r.at[t], (t, ex)).wait_recv()
    total = o2_land[0].astype(F32)
    for j in range(1, n):
        total = total + o2_land[j].astype(F32)
    g_all[3] = total
    for w in range(3):
        g_all[w] = jnp.concatenate([g2_land[j, w] for j in range(n)], axis=1).astype(F32)
    for d in range(1, n):
        t = lax.rem(dp + d, n)
        from_line(gwgu, gw_in, w_s, w_r, t).wait_recv()
        for src, dst, send, recv in (
            (gwgu, gw_in, w_s, w_r), (dm, dm_in, dm_s, dm_r),
            (o2_send, o2_land, o2_s, o2_r), (g2_send, g2_land, g2_s, g2_r),
        ):
            to_line(src, dst, send, recv, t).wait_send()
        remote(small_sum, small_all.at[dp], sz_s.at[t], sz_r.at[dp], (t, ex)).wait_send()
    keep_w.wait()
    sum_sent(*dn)
    sum_sent(*moes)
    for k in range(1, ne):
        to_plane(o_send.at[:, ex], o_land, o_s, o_r, k).wait_send()
        to_plane(g_send.at[:, ex], g_land, g_s, g_r, k).wait_send()
        to_plane(small_own, small_land, sp_s, sp_r, k).wait_send()

    @pl.loop(0, n)
    def _(at):
        for k in range(1, ne):
            out_give(at, k).wait_send()


def backward(
    n, ne, cap_pad, wrows, d_two, resid, cot, x, gain_one, gain_two, mixed, wo, qkv, lse, normed, vectors,
    wq, wk, wv, meta_all, in_bucket, gwgu, out_rows,
):
    tok, width = cot.shape
    own = wq.shape[1]
    wide = vectors.shape[1]
    both = gwgu.shape[2]
    slots_n = ne * cap_pad
    length = n * tok
    sem = pltpu.SemaphoreType.DMA
    shape = jax.ShapeDtypeStruct
    return pl.pallas_call(
        functools.partial(backward_kernel, n, ne, cap_pad),
        in_specs=[VM] * 17 + [ANY] * 2,
        out_specs=[VM] * 4 + [ANY] * 2,
        out_shape=[
            shape((tok, width), BF16),
            shape((tok, width), BF16),
            shape((4, wrows, width), F32),
            shape((n, 24, 128), F32),
            shape((n, tok, both), BF16),
            shape((n, slots_n, width), BF16),
        ],
        scratch_shapes=[
            pltpu.VMEM((n, tok, own), BF16),
            pltpu.VMEM((n, tok, own), BF16),
            pltpu.VMEM((2, tok, wide), F32),
            pltpu.VMEM((2, tok, wide), F32),
            pltpu.VMEM((length, own), BF16),
            pltpu.VMEM((length, own), BF16),
            pltpu.VMEM((length, own), BF16),
            pltpu.VMEM((length, 128), F32),
            pltpu.VMEM((length, 128), F32),
            pltpu.VMEM((8, wide), F32),
            pltpu.VMEM((tok, width), F32),
            pltpu.VMEM((n, tok, width), BF16),
            pltpu.VMEM((n - 1, 2, tok, width), BF16),
            pltpu.VMEM((n, tok, width), BF16),
            pltpu.VMEM((n - 1, 2, tok, width), BF16),
            pltpu.VMEM((slots_n, width), BF16),
            pltpu.VMEM((n, ne, 3, wrows, own), BF16),
            pltpu.VMEM((ne, n, 3, wrows, own), BF16),
            pltpu.VMEM((n, 3, wrows, own), BF16),
            pltpu.VMEM((n, 3, wrows, own), BF16),
            pltpu.VMEM((n, ne, wrows, width), BF16),
            pltpu.VMEM((ne, n, wrows, width), BF16),
            pltpu.VMEM((n, wrows, width), BF16),
            pltpu.VMEM((n, wrows, width), BF16),
            pltpu.VMEM((24, 128), F32),
            pltpu.VMEM((ne, 24, 128), F32),
            pltpu.VMEM((24, 128), F32),
            sem((n, ne)), sem((n, ne)), sem((n,)), sem((n,)), sem((n,)), sem((n,)), sem((n, 2)), sem((n, 2)),
            sem((n, 2)), sem((n, 2)), sem((ne,)), sem((ne,)), sem((ne,)), sem((ne,)), sem((n,)), sem((n,)),
            sem((n,)), sem((n,)), sem((ne,)), sem((ne,)), sem((n,)), sem((n,)), sem((2,)),
        ],
        compiler_params=pltpu.CompilerParams(
            collective_id=4, has_side_effects=True, vmem_limit_bytes=60 * 1024 * 1024
        ),
        name="backward",
    )(
        d_two, resid, cot, x, gain_one, gain_two, mixed, wo, qkv, lse, normed, vectors, wq, wk, wv, meta_all,
        in_bucket, gwgu, out_rows,
    )


def split_pieces(value):
    pieces = []
    for _ in range(3):
        piece = value.astype(BF16)
        pieces.append(piece)
        value = value - piece.astype(F32)
    return pieces


def finish_kernel(
    n, ne, heads_own, piece, blocks, g_all, small, out_in, grad_in, gwd_in,
    gate_ref, up_ref, gq, gk, gv, go, gain_one, gain_two, bias, block_out, grad_out, gwd,
):
    main = piece // 128 * 128
    rest = piece - main
    gates, ups = [], []
    for j in range(n):
        block = blocks[j].astype(F32)
        gates += [block[:, :main], block[:, 2 * main : 2 * main + rest]]
        ups += [block[:, main : 2 * main], block[:, 2 * main + rest :]]
    gate_ref[...] = jnp.concatenate(gates, axis=1)
    up_ref[...] = jnp.concatenate(ups, axis=1)
    block_out[...] = out_in[...]
    grad_out[...] = grad_in[...]
    gwd[...] = gwd_in[...]

    @pl.when(pl.program_id(0) == 0)
    def _():
        for i, ref in enumerate((gq, gk, gv, go)):
            ref[...] = g_all[i]
        me = lax.axis_index("dp") * ne + lax.axis_index("expert")
        total = small[0, :16]
        for j in range(1, n):
            total = total + small[j, :16]
        rows = lax.broadcasted_iota(jnp.int32, (8, 128), 0)
        lanes = lax.broadcasted_iota(jnp.int32, (8, 128), 1)
        for i, ref in enumerate((gain_one, gain_two)):
            count = ref.shape[1]
            at = me * count
            row = jnp.sum(jnp.where(rows == at // 128, total[8 * i : 8 * i + 8], 0.0), axis=0, keepdims=True)
            row = jnp.broadcast_to(row, (8, 128))
            ref[...] = pltpu.roll(row, lax.rem(128 - lax.rem(at, 128), 128), 1)[:1, :count]
        table = jnp.concatenate([small[j, 16 : 16 + heads_own] for j in range(n)], axis=0)
        heads = n * heads_own
        count = bias.shape[1]
        at = me * count
        table = jnp.concatenate([table, jnp.zeros((128 - heads, 128), F32)], axis=0)
        hot = jnp.where(lanes == at // heads, 1.0, 0.0).astype(BF16)
        row = sum(mm(hot, part, NT) for part in split_pieces(table))
        bias[...] = pltpu.roll(row, lax.rem(128 - lax.rem(at, heads), 128), 1)[:1, :count]


def finish(n, ne, heads_own, n_gain, n_bias, blocks, g_all, small, block_out, grad_in, gwd):
    tok, both = blocks.shape[1:]
    wrows, width = g_all.shape[1:]
    deep = gwd.shape[0]
    piece = both // 2
    steps = 4
    step, part = tok // steps, deep // steps
    total = n * piece
    shape = jax.ShapeDtypeStruct
    fixed2 = lambda i: (0, 0)
    fixed3 = lambda i: (0, 0, 0)
    move = lambda i: (i, 0)
    return pl.pallas_call(
        functools.partial(finish_kernel, n, ne, heads_own, piece),
        grid=(steps,),
        in_specs=[
            pl.BlockSpec((n, step, both), lambda i: (0, i, 0)),
            pl.BlockSpec((4, wrows, width), fixed3),
            pl.BlockSpec(small.shape, fixed3),
            pl.BlockSpec((step, width), move),
            pl.BlockSpec((step, width), move),
            pl.BlockSpec((part, width), move),
        ],
        out_specs=[pl.BlockSpec((step, total), move)] * 2
        + [pl.BlockSpec((wrows, width), fixed2)] * 4
        + [pl.BlockSpec((1, n_gain), fixed2)] * 2
        + [pl.BlockSpec((1, n_bias), fixed2)]
        + [pl.BlockSpec((step, width), move)] * 2
        + [pl.BlockSpec((part, width), move)],
        out_shape=[shape((tok, total), F32)] * 2
        + [shape((wrows, width), F32)] * 4
        + [shape((1, n_gain), F32)] * 2
        + [shape((1, n_bias), F32)]
        + [shape((tok, width), BF16)] * 2
        + [shape((deep, width), F32)],
        compiler_params=pltpu.CompilerParams(vmem_limit_bytes=VMEM_LIMIT),
        name="finish",
    )(blocks, g_all, small, block_out, grad_in, gwd)


def local(
    inputs, cotangent, gain_attn, w_query, w_key, w_value, w_out, position_bias,
    gain_moe, w_gate, w_up, w_down, routes, gate_fixed,
):
    n = lax.axis_size("dp")
    experts_n = lax.axis_size("expert")
    dp = lax.axis_index("dp")
    ex = lax.axis_index("expert")
    tok, width = inputs.shape[1:]
    length = n * tok
    own = HEADS * HEAD_DIM // n
    heads_own = HEADS // n
    wrows = w_query.shape[0]
    capacity = 5 * tok // (2 * experts_n)
    cap_pad = -(-capacity // 16) * 16
    slots_n = experts_n * cap_pad

    n_gain, n_bias = gain_attn.shape[0], position_bias.shape[0]
    extra = jnp.concatenate([gain_attn, gain_moe, position_bias])
    extra = jnp.zeros((16, own), BF16).at[0, : 2 * n_gain + n_bias].set(extra)
    meta_in = jnp.concatenate([routes[0].T, gate_fixed], axis=0)
    x_all, wq, wk, wv, extras, wo, meta_all, packed = start(
        n, experts_n, capacity, cap_pad,
        inputs[0], w_query, w_key, w_value, extra, w_out, meta_in, w_gate[0], w_up[0],
    )
    wq, wk, wv = (w.reshape(width, own) for w in (wq, wk, wv))
    wo = wo.reshape(width, width)
    extras = extras[:, :, 0]
    gain_one = extras[:, :, :n_gain].reshape(1, -1).astype(F32)
    gain_two = extras[:, :, n_gain : 2 * n_gain].reshape(1, -1).astype(F32)
    table = extras[:, :, 2 * n_gain : 2 * n_gain + n_bias].reshape(BUCKETS, HEADS)
    table = lax.dynamic_slice_in_dim(table, dp * heads_own, heads_own, 1)
    wide = 2 * length
    offsets = jnp.arange(wide, dtype=jnp.int32) - length
    in_bucket = (bucket_of(offsets)[:, None] == jnp.arange(BUCKETS, dtype=jnp.int32)).astype(BF16)
    in_bucket = jnp.where(jnp.abs(offsets)[:, None] < length, in_bucket, jnp.zeros_like(in_bucket))
    vectors = mm(table, in_bucket, (((0,), (1,)), ((), ())))

    normed, qkv, lse, mixed, resid, slots, d_outs, wgu = forward(
        n, experts_n, cap_pad, x_all, wq, wk, wv, wo, gain_one, gain_two, vectors, cotangent[0], meta_all, packed
    )
    wgu = wgu.reshape(width, -1)
    deep = w_down.shape[1]
    padded = -(-deep // 128) * 128
    wd = jnp.pad(w_down[0], ((0, padded - deep), (0, 0)))
    out_rows, grad_normed_two, gwgu, grad_w_down = experts(
        n, experts_n, cap_pad, deep, slots, d_outs, wgu, wd, meta_all
    )

    by_diagonal = jnp.pad(jnp.roll(in_bucket, -tok, axis=0), ((0, 0), (0, 128 - BUCKETS)))
    block_out, grad_inputs, g_all, small, got, _ = backward(
        n, experts_n, cap_pad, wrows, grad_normed_two, resid, cotangent[0], inputs[0], gain_one, gain_two, mixed, wo,
        qkv, lse, normed, vectors, wq, wk, wv, meta_all, by_diagonal, gwgu.reshape(n, width // n, -1), out_rows,
    )
    (
        grad_w_gate, grad_w_up, gq, gk, gv, go, grad_gain_one, grad_gain_two, grad_bias, block_out, grad_inputs,
        grad_w_down,
    ) = finish(n, experts_n, heads_own, n_gain, n_bias, got, g_all, small, block_out, grad_inputs, grad_w_down)

    return (
        block_out[None],
        grad_inputs[None],
        grad_gain_one[0],
        gq,
        gk,
        gv,
        go,
        grad_bias[0],
        grad_gain_two[0],
        grad_w_gate[None],
        grad_w_up[None],
        grad_w_down[None],
    )


def solution(mesh):
    vector = P(("dp", "expert"))
    matrix = P(("dp", "expert"), None)
    split = P("expert", "dp", None)
    return jax.shard_map(
        local,
        mesh=mesh,
        in_specs=(
            split, split, vector, matrix, matrix, matrix, matrix, vector, vector,
            split, split, split, split, P("expert", "dp"),
        ),
        out_specs=(
            split, split, vector, matrix, matrix, matrix, matrix, vector, vector,
            split, split, split,
        ),
        check_vma=False,
    )
```

```python
import functools

import jax
import jax.numpy as jnp
from jax import lax
from jax.experimental import pallas as pl
from jax.experimental.pallas import tpu as pltpu
from jax.sharding import PartitionSpec as P

HEADS = 16
HEAD_DIM = 64
BUCKETS = 32
THRESHOLDS = (12, 16, 23, 32, 46, 64, 91)
EPSILON = 1e-06
SCALE = HEAD_DIM ** (-0.5)
BF16 = jnp.bfloat16
F32 = jnp.float32
GELU_C = 0.7978845608028654
GELU_A = 0.044715
VMEM_LIMIT = 56 * 1024 * 1024

NT = (((1,), (1,)), ((), ()))
TN = (((0,), (0,)), ((), ()))
NN = (((1,), (0,)), ((), ()))


def mm(a, b, dims=NN):
    return lax.dot_general(a, b, dims, preferred_element_type=F32)


def bucket_of(offset):
    distance = jnp.abs(offset)
    banded = jnp.full(distance.shape, 8, jnp.int32)
    for cutoff in THRESHOLDS:
        banded = banded + (distance >= cutoff).astype(jnp.int32)
    nearby = jnp.where(distance < 8, distance, banded)
    return nearby + jnp.where(offset > 0, 16, 0).astype(jnp.int32)


def bias_tile(vec_ref, head, tile_ref):
    block, wide = tile_ref.shape
    row = jnp.broadcast_to(vec_ref[pl.ds(head, 1), :], (block, wide))
    tile_ref[...] = pltpu.roll(row, wide - block, 1, stride=1, stride_axis=0)


def tile_offset(n, block, query_block, key_block):
    return pl.multiple_of((key_block - query_block + n - 1) * block, 128)


def logits_of(n, block, query_block, q_pair, k_pair, mask, tile_ref):
    masked = jnp.where(mask, q_pair, jnp.zeros_like(q_pair))
    raw = mm(masked, k_pair, NT) * SCALE
    bias = jnp.concatenate(
        [tile_ref[:, pl.ds(tile_offset(n, block, query_block, j), block)] for j in range(n)], axis=1
    )
    return raw + bias


def diagonal_sum(tile):
    rows, wide = tile.shape
    while rows > 1:
        half = rows // 2
        tile = tile[:half] + pltpu.roll(tile[half:], wide - half, 1)
        rows = half
    return tile


def gelu_pair(v):
    square = v * v
    t = jnp.tanh(GELU_C * (v + GELU_A * v * square))
    half = 0.5 * (1.0 + t)
    slope = half + (0.5 * GELU_C) * v * (1.0 - t * t) * (1.0 + (3.0 * GELU_A) * square)
    return v * half, slope


MESH = pl.DeviceIdType.MESH


def remote(src, dst, send, recv, target):
    return pltpu.make_async_remote_copy(
        src_ref=src, dst_ref=dst, send_sem=send, recv_sem=recv, device_id=target, device_id_type=MESH
    )


def greet(n, ne, dp, ex):
    barrier = pltpu.get_barrier_semaphore()
    for d in range(1, n):
        pl.semaphore_signal(barrier, inc=1, device_id=(lax.rem(dp + d, n), ex), device_id_type=MESH)
    for k in range(1, ne):
        pl.semaphore_signal(barrier, inc=1, device_id=(dp, lax.rem(ex + k, ne)), device_id_type=MESH)


def meet(n, ne):
    pl.semaphore_wait(pltpu.get_barrier_semaphore(), n + ne - 2)


class Copies:
    def __init__(self, sem, pairs):
        self.copies = [pltpu.make_async_copy(src, dst, sem.at[i]) for i, (src, dst) in enumerate(pairs)]

    def start(self, *which):
        for i in which:
            self.copies[i].start()

    def wait(self, *which):
        for i in which:
            self.copies[i].wait()


class Chain:
    def __init__(self, n, dp, ex, own, buffer, send, recv):
        self.n, self.dp, self.ex, self.own = n, dp, ex, own
        self.buffer, self.send_sem, self.recv_sem = buffer, send, recv

    def block(self, hop, side):
        return lax.rem(self.dp + self.n + hop * (2 * side - 1), self.n)

    def copy(self, hop, side, first=False):
        at = self.block(hop, side)
        target = lax.rem(self.dp + self.n + 1 - 2 * side, self.n)
        return remote(
            self.own if first else self.buffer.at[at], self.buffer.at[at],
            self.send_sem.at[hop, side], self.recv_sem.at[hop, side], (target, self.ex),
        )

    def has_next(self, side):
        return (self.dp + 1 < self.n) if side == 0 else (self.dp > 0)

    def start(self):
        for side in range(2):
            @pl.when(self.has_next(side))
            def _():
                self.copy(0, side, True).start()

    def held(self, hop, side):
        return (self.dp > hop) if side == 0 else (self.dp + 1 + hop < self.n)

    def arrive(self, hop, side):
        at = self.block(hop + 1, side)
        remote(
            self.buffer.at[at], self.buffer.at[at], self.send_sem.at[hop, side], self.recv_sem.at[hop, side],
            (self.dp, self.ex),
        ).wait_recv()

        @pl.when(self.has_next(side))
        def _():
            self.copy(hop + 1, side).start()

        return at

    def finish(self):
        for hop in range(self.n - 1):
            for side in range(2):
                mine = self.has_next(side)
                if hop:
                    mine = mine & self.held(hop - 1, side)

                @pl.when(mine)
                def _():
                    self.copy(hop, side, hop == 0).wait_send()


ANY = pl.BlockSpec(memory_space=pl.ANY)
VM = pl.BlockSpec(memory_space=pltpu.VMEM)


def bucket_hot(wide, turn, length):
    at = lax.broadcasted_iota(jnp.int32, (wide, 128), 0) + turn
    offset = jnp.where(at >= wide, at - wide, at) - length
    hit = bucket_of(offset) == lax.broadcasted_iota(jnp.int32, (wide, 128), 1)
    return jnp.where(hit & (jnp.abs(offset) < length), 1.0, 0.0).astype(BF16)


def rows_flat(ref):
    n, ne, rows, columns = ref.shape
    if rows % 16 == 0:
        return ref[...].reshape(n * ne * rows, columns)
    return ref[...].astype(F32).reshape(n * ne * rows, columns).astype(BF16)


def front_kernel(
    n, ne, cap, cap_pad, piece,
    x_in, wq, wk, wv, wo, gain_attn, gain_moe, position_bias, meta_in, wg_in, wu_in, cot_in,
    normed_out, qkv_out, lse_out, mixed_out, resid_out, lq_out, lk_out, lv_out, lwo_out, meta_all, vectors, gains,
    slots, d_outs, wgu,
    x, wg, wu, cot, normed, qkv, lse, mixed, resid, lq, lk, lv, lwo,
    extra, sq, sk, sv, sext, swo, smeta, lext, packed,
    x_all, heads, mixed_in, tiles, cot_all, two_all, two_own, two_rows, cot_rows,
    line_send, line_recv, plane_send, plane_recv, core_send, core_recv, chain_send, chain_recv, own_sem,
    w_send, w_recv, m_send, m_recv, c_send, c_recv, t_send, t_recv,
    pc_send, pc_recv, pt_send, pt_recv, in_sem, out_sem,
):
    dp, ex = lax.axis_index("dp"), lax.axis_index("expert")
    greet(n, ne, dp, ex)
    loads = Copies(in_sem, [(x_in, x), (cot_in, cot), (wg_in, wg), (wu_in, wu)])
    loads.start(0, 1, 2, 3)
    stores = Copies(
        out_sem,
        [
            (normed, normed_out), (qkv, qkv_out), (lse, lse_out), (mixed, mixed_out), (resid, resid_out),
            (lq, lq_out), (lk, lk_out), (lv, lv_out), (lwo, lwo_out),
        ],
    )
    own = sq.shape[2]
    block, width = cot.shape
    pairs_n = own // 128
    slots_n = ne * cap_pad
    n_gain, n_bias = gain_attn.shape[1], position_bias.shape[1]
    line_of = jnp.concatenate(
        [
            gain_attn[...].astype(F32), gain_moe[...].astype(F32), position_bias[...].astype(F32),
            jnp.zeros((1, own - 2 * n_gain - n_bias), F32),
        ],
        axis=1,
    )
    extra[...] = jnp.broadcast_to(line_of, (16, own)).astype(BF16)
    loads.wait(0)
    meet(n, ne)
    chain = Chain(n, dp, ex, x, x_all, chain_send, chain_recv)
    cots = Chain(n, dp, ex, cot, cot_all, c_send, c_recv)
    twos = Chain(n, dp, ex, two_own, two_all, t_send, t_recv)

    def column(ref, t):
        return ref.at[:, pl.ds(pl.multiple_of(t * own, 128), own)]

    def line(kind, d):
        t = lax.rem(dp + d, n)
        src, dst = [
            (column(wq, t), sq.at[dp]), (column(wk, t), sk.at[dp]), (column(wv, t), sv.at[dp]),
            (extra, sext.at[dp]), (wo, swo.at[dp]), (smeta, meta_all.at[dp]),
        ][kind]
        return remote(src, dst, line_send.at[kind, d], line_recv.at[kind, d], (t, ex))

    for d in range(1, n):
        for kind in range(4):
            line(kind, d).start()
    chain.start()
    for d in range(1, n):
        line(4, d).start()
    here = pl.ds(pl.multiple_of(dp * own, 128), own)
    sq[dp] = wq[:, here]
    sk[dp] = wk[:, here]
    sv[dp] = wv[:, here]
    sext[dp] = extra[...]
    swo[dp] = wo[...]
    x_all[dp] = x[...]

    tok = meta_in.shape[1]
    routes = meta_in[...]
    ids = lax.broadcasted_iota(jnp.int32, (ne, tok), 0)
    first = (ids == routes[0:1, :]).astype(F32)
    second = (ids == routes[1:2, :]).astype(F32)
    before = (
        lax.broadcasted_iota(jnp.int32, (tok, tok), 0) < lax.broadcasted_iota(jnp.int32, (tok, tok), 1)
    ).astype(BF16)
    counts = mm((first + second).astype(BF16), before)
    slot_a = jnp.sum(counts * first, axis=0, keepdims=True)
    slot_b = jnp.sum((counts + first) * second, axis=0, keepdims=True)
    asked = routes.astype(F32)
    dest_a = jnp.where(slot_a < cap, asked[0:1, :] * cap_pad + slot_a, -1.0)
    dest_b = jnp.where(slot_b < cap, asked[1:2, :] * cap_pad + slot_b, -1.0)
    gate = asked[2:3, :] * (1.0 / 65536.0)
    smeta[...] = jnp.concatenate([dest_a, dest_b, gate, jnp.zeros((5, tok), F32)], axis=0)
    meta_all[dp] = smeta[...]
    for d in range(1, n):
        line(5, d).start()

    pairs = [(sq, lq), (sk, lk), (sv, lv), (sext, lext), (swo, lwo)]
    partner = ex + 1 - 2 * lax.rem(ex, 2)

    def plane(kind, k):
        src, dst = pairs[kind]
        return remote(
            src, dst.at[:, ex], plane_send.at[kind, k], plane_recv.at[kind, k],
            (dp, lax.rem(ex + 2 * k, ne)),
        )

    def core(kind, k):
        src, dst = pairs[kind]
        at = lax.rem(ex + ne - 2 * k, ne)
        return remote(
            src if k == 0 else dst.at[:, at], dst.at[:, at],
            core_send.at[kind, k], core_recv.at[kind, k], (dp, partner),
        )

    def keep_own(kind):
        return pltpu.make_async_copy(pairs[kind][0], pairs[kind][1].at[:, ex], own_sem.at[kind])

    def spread(kind):
        for d in range(1, n):
            line(kind, d).wait_recv()
        for k in range(1, ne // 2):
            plane(kind, k).start()
        core(kind, 0).start()
        keep_own(kind).start()

    def pass_on(kind):
        for k in range(1, ne // 2):
            plane(kind, k).wait_recv()
            core(kind, k).start()

    def settle(kind):
        keep_own(kind).wait()
        for k in range(ne // 2):
            core(kind, k).wait()
        for k in range(1, ne // 2):
            plane(kind, k).wait_send()

    for kind in range(4):
        spread(kind)

    def to_plane(rows, land, send, recv, group, k):
        peer = lax.rem(ex + k, ne)
        return remote(
            rows.at[group, pl.ds(pl.multiple_of(peer * cap_pad, 16), cap_pad)], land.at[group, ex],
            send.at[group, k], recv.at[group, k], (dp, peer),
        )

    def kept(rows, land, group, sem):
        return pltpu.make_async_copy(
            rows.at[group, pl.ds(pl.multiple_of(ex * cap_pad, 16), cap_pad)], land.at[group, ex], sem.at[group, 0]
        )

    def dispatch(group, tokens, rows, land, send, recv, weigh):
        meta = meta_all[group]
        slot_ids = lax.broadcasted_iota(jnp.int32, (slots_n, block), 0).astype(F32)
        hit_a, hit_b = slot_ids == meta[0:1, :], slot_ids == meta[1:2, :]
        chosen = jnp.where(hit_a | hit_b, 1.0, 0.0).astype(BF16)
        found = mm(chosen, tokens)
        if weigh:
            share = meta[2:3, :]
            factor = jnp.sum(
                jnp.where(hit_a, share, 0.0) + jnp.where(hit_b, 1.0 - share, 0.0), axis=1, keepdims=True
            )
            found = found * factor
        rows[group] = found.astype(BF16)
        for k in range(1, ne):
            to_plane(rows, land, send, recv, group, k).start()
        kept(rows, land, group, send).start()

    def send_cot(group, tokens):
        dispatch(group, tokens, cot_rows, d_outs, pc_send, pc_recv, True)

    def send_two(group, tokens):
        dispatch(group, tokens, two_rows, slots, pt_send, pt_recv, False)

    loads.wait(1)
    send_cot(dp, cot[...])

    def weights(d):
        t = lax.rem(dp + d, n)
        return remote(packed.at[t], wgu.at[dp], w_send.at[d], w_recv.at[d], (t, ex))

    keep_w = pltpu.make_async_copy(packed.at[dp], wgu.at[dp], own_sem.at[5])

    def hop(line_chain, h, then):
        for side in range(2):
            @pl.when(line_chain.held(h, side))
            def _():
                then(line_chain.arrive(h, side))

    def x_hop(h):
        hop(chain, h, lambda at: None)

    main = piece // 128 * 128
    step = min(wg.shape[0], 64)

    def pack(i):
        rows = pl.ds(pl.multiple_of(i * step, step), step)
        gate_w, up_w = wg[rows, :], wu[rows, :]
        for j in range(n):
            g = gate_w[:, j * piece : (j + 1) * piece]
            u = up_w[:, j * piece : (j + 1) * piece]
            packed[j, rows, :] = jnp.concatenate([g[:, :main], u[:, :main], g[:, main:], u[:, main:]], axis=1)

    loads.wait(2, 3)
    pl.loop(0, wg.shape[0] // step)(pack)
    x_hop(0)
    spread(4)
    for kind in range(4):
        pass_on(kind)
    if n > 2:
        x_hop(1)
    for kind in range(4):
        settle(kind)
    stores.start(5, 6, 7)

    devices = n * ne
    shared = jnp.max(lext[...].astype(F32), axis=2).reshape(devices, own).astype(BF16)

    def laid_out(first_lane, count, total):
        lanes = lax.broadcasted_iota(jnp.int32, (own, total), 1)
        rows = lax.broadcasted_iota(jnp.int32, (own, total), 0)
        spreading = jnp.where(lax.rem(lanes, count) + first_lane == rows, 1.0, 0.0).astype(BF16)
        everywhere = mm(shared, spreading)
        owner = lax.broadcasted_iota(jnp.int32, (devices, total), 0)
        lane_owner = lax.broadcasted_iota(jnp.int32, (devices, total), 1) // count
        return jnp.sum(jnp.where(owner == lane_owner, everywhere, 0.0), axis=0, keepdims=True)

    gain_one = laid_out(0, n_gain, width)
    gain_two = laid_out(n_gain, n_gain, width)
    gains[...] = jnp.concatenate([gain_one, gain_two, jnp.zeros((6, width), F32)], axis=0)
    entries = HEADS * BUCKETS
    flat = laid_out(2 * n_gain, n_bias, entries)
    lanes = lax.broadcasted_iota(jnp.int32, (8, entries), 1)
    head_of = lax.broadcasted_iota(jnp.int32, (8, entries), 0) + dp * (HEADS // n)
    by_head = jnp.where(lax.rem(lanes, HEADS) == head_of, jnp.broadcast_to(flat, (8, entries)), 0.0).astype(BF16)
    bucket_rows = lax.broadcasted_iota(jnp.int32, (entries, 128), 0) // HEADS
    to_bucket = jnp.where(
        bucket_rows == lax.broadcasted_iota(jnp.int32, (entries, 128), 1), 1.0, 0.0
    ).astype(BF16)
    table = mm(by_head, to_bucket).astype(BF16)
    wide = vectors.shape[1]
    vectors[...] = mm(table, bucket_hot(wide, 0, wide // 2), NT)

    def project(j):
        at = pl.ds(pl.multiple_of(j * block, block), block)
        xf = x_all[j].astype(F32)
        inverse = lax.rsqrt(jnp.mean(xf * xf, axis=-1, keepdims=True) + EPSILON)
        low = (xf * inverse * gains[0:1, :]).astype(BF16)
        normed[at, :] = low
        for w, ref in enumerate((lq, lk, lv)):
            qkv[at, w * own : (w + 1) * own] = mm(low, rows_flat(ref)).astype(BF16)

    project(dp)

    def project_hop(h):
        @pl.loop(0, 2)
        def _(side):
            @pl.when(((side == 0) & (dp > h)) | ((side == 1) & (dp + 1 + h < n)))
            def _():
                project(chain.block(h + 1, side))

    for h in range(n - 2):
        project_hop(h)
    pass_on(4)
    x_hop(n - 2)
    cots.start()
    keep_w.start()

    def send_weights(to_ends):
        for d in range(1, n):
            t = lax.rem(dp + d, n)
            at_end = (t == 0) | (t == n - 1)

            @pl.when(at_end if to_ends else jnp.logical_not(at_end))
            def _():
                weights(d).start()

    send_weights(False)
    project_hop(n - 2)
    stores.start(0, 1)

    def attend(pair):
        for side in range(2):
            bias_tile(vectors, 2 * pair + side, tiles.at[side])
        lane = lax.broadcasted_iota(jnp.int32, (block, 128), 1)
        low_half = lane < HEAD_DIM
        k_pair = qkv[:, own + pair * 128 : own + (pair + 1) * 128]
        v_pair = qkv[:, 2 * own + pair * 128 : 2 * own + (pair + 1) * 128]

        @pl.loop(0, n)
        def _(i):
            at = pl.ds(pl.multiple_of(i * block, block), block)
            q_pair = qkv[at, pair * 128 : (pair + 1) * 128]
            outs, logs = [], []
            for side in range(2):
                mask = low_half if side == 0 else jnp.logical_not(low_half)
                logits = logits_of(n, block, i, q_pair, k_pair, mask, tiles.at[side])
                row_max = jnp.max(logits, axis=-1, keepdims=True)
                exponent = jnp.exp(logits - row_max)
                total = jnp.sum(exponent, axis=-1, keepdims=True)
                probs_low = (exponent * (1.0 / total)).astype(BF16)
                outs.append(mm(probs_low, v_pair))
                logs.append(jnp.broadcast_to(row_max + jnp.log(total), (block, 128)))
            heads[at, pair * 128 : (pair + 1) * 128] = jnp.where(low_half, outs[0], outs[1]).astype(BF16)
            lse[at, pair * 128 : (pair + 1) * 128] = jnp.where(low_half, logs[0], logs[1])

    def cot_hop(h):
        hop(cots, h, lambda group: send_cot(group, cot_all[group]))

    for d in range(1, n):
        line(5, d).wait_recv()
    def give(d):
        t = lax.rem(dp + d, n)
        return remote(
            heads.at[pl.ds(pl.multiple_of(t * block, block), block)], mixed_in.at[dp], m_send.at[d], m_recv.at[d],
            (t, ex),
        )

    for pair in range(pairs_n):
        attend(pair)
        if pair == pairs_n - 1:
            for d in range(1, n):
                give(d).start()
        if pair < n - 1:
            cot_hop(pair)
    mixed_in[dp] = heads[pl.ds(pl.multiple_of(dp * block, block), block), :]
    settle(4)
    stores.start(8, 2)
    for d in range(1, n):
        give(d).wait()
    mixed[...] = jnp.concatenate([mixed_in[j] for j in range(n)], axis=1)
    total = x[...].astype(F32) + mm(mixed[...], rows_flat(lwo))
    resid[...] = total
    inverse = lax.rsqrt(jnp.mean(total * total, axis=-1, keepdims=True) + EPSILON)
    two_own[...] = (total * inverse * gains[1:2, :]).astype(BF16)
    twos.start()
    stores.start(3, 4)

    send_two(dp, two_own[...])
    for h in range(pairs_n, n - 1):
        cot_hop(h)
    for h in range(n - 1):
        hop(twos, h, lambda group: send_two(group, two_all[group]))
    send_weights(True)
    stores.wait(*range(9))
    chain.finish()
    cots.finish()
    twos.finish()
    for d in range(1, n):
        for kind in range(6):
            line(kind, d).wait_send()
    keep_w.wait()
    for d in range(1, n):
        weights(d).wait()
    for rows, land, send, recv in (
        (two_rows, slots, pt_send, pt_recv), (cot_rows, d_outs, pc_send, pc_recv),
    ):
        @pl.loop(0, n)
        def _(group):
            kept(rows, land, group, send).wait()
            for k in range(1, ne):
                to_plane(rows, land, send, recv, group, k).wait()


def front(n, ne, cap, cap_pad, x, wq, wk, wv, wo, gain_attn, gain_moe, position_bias, meta_in, wg, wu, cot):
    tok, width = x.shape
    wrows = wq.shape[0]
    own = width // n
    piece = wg.shape[1] // n
    wide = 2 * n * tok
    slots_n = ne * cap_pad
    sem = pltpu.SemaphoreType.DMA
    shape = jax.ShapeDtypeStruct
    return pl.pallas_call(
        functools.partial(front_kernel, n, ne, cap, cap_pad, piece),
        in_specs=[ANY] + [VM] * 8 + [ANY] * 3,
        out_specs=[ANY] * 9 + [VM] * 3 + [ANY] * 3,
        out_shape=[
            shape((n * tok, width), BF16),
            shape((n * tok, 3 * own), BF16),
            shape((n * tok, own), F32),
            shape((tok, width), BF16),
            shape((tok, width), F32),
            shape((n, ne, wrows, own), BF16),
            shape((n, ne, wrows, own), BF16),
            shape((n, ne, wrows, own), BF16),
            shape((n, ne, wrows, width), BF16),
            shape((n, 8, tok), F32),
            shape((8, wide), F32),
            shape((8, width), F32),
            shape((n, ne, cap_pad, width), BF16),
            shape((n, ne, cap_pad, width), BF16),
            shape((n, tok, 2 * piece), BF16),
        ],
        scratch_shapes=[
            pltpu.VMEM((tok, width), BF16),
            pltpu.VMEM(wg.shape, BF16),
            pltpu.VMEM(wu.shape, BF16),
            pltpu.VMEM((tok, width), BF16),
            pltpu.VMEM((n * tok, width), BF16),
            pltpu.VMEM((n * tok, 3 * own), BF16),
            pltpu.VMEM((n * tok, own), F32),
            pltpu.VMEM((tok, width), BF16),
            pltpu.VMEM((tok, width), F32),
            pltpu.VMEM((n, ne, wrows, own), BF16),
            pltpu.VMEM((n, ne, wrows, own), BF16),
            pltpu.VMEM((n, ne, wrows, own), BF16),
            pltpu.VMEM((n, ne, wrows, width), BF16),
            pltpu.VMEM((16, own), BF16),
            pltpu.VMEM((n, wrows, own), BF16),
            pltpu.VMEM((n, wrows, own), BF16),
            pltpu.VMEM((n, wrows, own), BF16),
            pltpu.VMEM((n, 16, own), BF16),
            pltpu.VMEM((n, wrows, width), BF16),
            pltpu.VMEM((8, tok), F32),
            pltpu.VMEM((n, ne, 16, own), BF16),
            pltpu.VMEM((n, tok, 2 * piece), BF16),
            pltpu.VMEM((n, tok, width), BF16),
            pltpu.VMEM((n * tok, own), BF16),
            pltpu.VMEM((n, tok, own), BF16),
            pltpu.VMEM((2, tok, wide), F32),
            pltpu.VMEM((n, tok, width), BF16),
            pltpu.VMEM((n, tok, width), BF16),
            pltpu.VMEM((tok, width), BF16),
            pltpu.VMEM((n, slots_n, width), BF16),
            pltpu.VMEM((n, slots_n, width), BF16),
            sem((6, n)), sem((6, n)),
            sem((5, ne // 2)), sem((5, ne // 2)), sem((5, ne // 2)), sem((5, ne // 2)),
            sem((n, 2)), sem((n, 2)), sem((6,)),
            sem((n,)), sem((n,)), sem((n,)), sem((n,)),
            sem((n, 2)), sem((n, 2)), sem((n, 2)), sem((n, 2)),
            sem((n, ne)), sem((n, ne)), sem((n, ne)), sem((n, ne)), sem((4,)), sem((9,)),
        ],
        compiler_params=pltpu.CompilerParams(
            collective_id=1, has_side_effects=True, vmem_limit_bytes=60 * 1024 * 1024
        ),
        name="front",
    )(x, wq, wk, wv, wo, gain_attn, gain_moe, position_bias, meta_in, wg, wu, cot)


def experts_kernel(
    n, ne, cap_pad, deep, main,
    slots, d_outs, wgu_in, wd_in, meta_all,
    out_rows, d_two, gwgu_out, gwd_out,
    wgu_ref, gwgu, gwd, wd_ref, s_buf, d_buf, back, part, landed, gwgu_acc,
    load_sem, keep_sem, p_send, p_recv, z_send, z_recv, wd_sem,
):
    dp, ex = lax.axis_index("dp"), lax.axis_index("expert")
    slots_n, width = s_buf.shape[1:]
    tok = d_two.shape[0]
    greet(n, ne, dp, ex)
    toward = 2 * ((2 * dp) // n) - 1

    def group_at(step):
        return lax.rem(dp + n + toward * (1 + step), n)

    def load(step, kind):
        at = group_at(step)
        src, dst = ((slots, s_buf), (d_outs, d_buf))[kind]
        return pltpu.make_async_copy(src.at[at], dst.at[at], load_sem.at[kind, step])

    whole = Copies(
        wd_sem,
        [(wgu_in, wgu_ref), (wd_in, wd_ref.at[pl.ds(0, deep)]), (gwgu, gwgu_out), (gwd, gwd_out)],
    )
    whole.start(0, 1)
    for step in range(n):
        for kind in range(2):
            load(step, kind).start()
    wd_ref[deep:, :] = jnp.zeros((wd_ref.shape[0] - deep, width), BF16)
    gwgu_acc[...] = jnp.zeros_like(gwgu_acc)
    gwd[...] = jnp.zeros_like(gwd)
    whole.wait(0, 1)
    meet(n, ne)

    def rows_of(peer):
        return pl.ds(pl.multiple_of(peer * cap_pad, 16), cap_pad)

    def give(at, k):
        peer = lax.rem(ex + k, ne)
        return remote(
            d_buf.at[at, rows_of(peer)], back.at[at, rows_of(ex)], p_send.at[at, k], p_recv.at[at, k], (dp, peer)
        )

    def take(at, k):
        peer = lax.rem(ex + ne - k, ne)
        return remote(
            d_buf.at[at, rows_of(ex)], back.at[at, rows_of(peer)], p_send.at[at, k], p_recv.at[at, k], (dp, peer)
        )

    def keep(at):
        return pltpu.make_async_copy(s_buf.at[at], out_rows.at[at], keep_sem.at[at])

    def owed(at):
        return remote(part.at[at], landed.at[dp], z_send.at[at], z_recv.at[dp], (at, ex))

    def combine(at):
        for k in range(1, ne):
            take(at, k).wait_recv()
        meta = meta_all[at]
        ids = lax.broadcasted_iota(jnp.int32, (slots_n, tok), 0).astype(F32)
        hit = (ids == meta[0:1, :]) | (ids == meta[1:2, :])
        return mm(jnp.where(hit, 1.0, 0.0).astype(BF16), back[at], TN)

    @pl.loop(0, n)
    def _(step):
        at = group_at(step)
        for kind in range(2):
            load(step, kind).wait()
        wgu, wd = wgu_ref[...], wd_ref[...]
        parts = -(-slots_n // 640)
        size = slots_n // parts
        low_lane = lax.broadcasted_iota(jnp.int32, (size, 128), 1) < 64
        for p in range(parts):
            here = slice(p * size, (p + 1) * size)
            rows, d_out = s_buf[at, here, :], d_buf[at, here, :]
            pre = mm(rows, wgu)
            d_hidden = mm(d_out, wd, NT)
            gate, up, tail = pre[:, :main], pre[:, main : 2 * main], pre[:, 2 * main :]
            tail_up = pltpu.roll(tail, 64, 1)
            act, slope = gelu_pair(gate)
            act_t, slope_t = gelu_pair(tail)
            hidden_t = jnp.where(low_lane, act_t * tail_up, 0.0)
            hidden = jnp.concatenate([(act * up).astype(BF16), hidden_t.astype(BF16)], axis=1)
            dh, dh_t = d_hidden[:, :main], d_hidden[:, main:]
            d_gate = dh * up * slope
            d_up = dh * act
            d_tail = jnp.where(low_lane, dh_t * tail_up * slope_t, pltpu.roll(dh_t * act_t, 64, 1))
            d_pre = jnp.concatenate([d_gate.astype(BF16), d_up.astype(BF16), d_tail.astype(BF16)], axis=1)
            d_rows = mm(d_pre, wgu, NT).astype(BF16)
            gwd[...] += mm(hidden, d_out, TN)[:deep]
            d_buf[at, here, :] = d_rows
            if p == parts - 1:
                for k in range(1, ne):
                    give(at, k).start()
                back[at, rows_of(ex), :] = d_buf[at, rows_of(ex), :]
            gwgu_acc[...] += mm(rows, d_pre, TN)
            s_buf[at, here, :] = mm(hidden, wd).astype(BF16)
        keep(at).start()

        @pl.when(step > 0)
        def _():
            past = group_at(step - 1)
            part[past] = combine(past).astype(BF16)
            owed(past).start()

    gwgu[...] = gwgu_acc[...].astype(BF16)
    whole.start(2, 3)
    total = combine(dp)
    for d in range(1, n):
        src = lax.rem(dp + d, n)
        remote(part.at[src], landed.at[src], z_send.at[src], z_recv.at[src], (src, ex)).wait_recv()
        total = total + landed[src].astype(F32)
    d_two[...] = total
    whole.wait(2, 3)
    for d in range(1, n):
        owed(lax.rem(dp + d, n)).wait_send()

    @pl.loop(0, n)
    def _(at):
        keep(at).wait()
        for k in range(1, ne):
            give(at, k).wait_send()


def experts(n, ne, cap_pad, deep, slots, d_outs, wgu, wd, meta_all):
    width, columns = wgu.shape
    tok = meta_all.shape[2]
    main = (columns - 128) // 2
    slots_n = ne * cap_pad
    slots = slots.reshape(n, slots_n, width)
    d_outs = d_outs.reshape(n, slots_n, width)
    sem = pltpu.SemaphoreType.DMA
    return pl.pallas_call(
        functools.partial(experts_kernel, n, ne, cap_pad, deep, main),
        in_specs=[ANY, ANY, ANY, ANY, VM],
        out_specs=[ANY, VM, ANY, ANY],
        out_shape=[
            jax.ShapeDtypeStruct((n, slots_n, width), BF16),
            jax.ShapeDtypeStruct((tok, width), F32),
            jax.ShapeDtypeStruct((width, columns), BF16),
            jax.ShapeDtypeStruct((deep, width), F32),
        ],
        scratch_shapes=[
            pltpu.VMEM((width, columns), BF16),
            pltpu.VMEM((width, columns), BF16),
            pltpu.VMEM((deep, width), F32),
            pltpu.VMEM((-(-deep // 128) * 128, width), BF16),
            pltpu.VMEM((n, slots_n, width), BF16),
            pltpu.VMEM((n, slots_n, width), BF16),
            pltpu.VMEM((n, slots_n, width), BF16),
            pltpu.VMEM((n, tok, width), BF16),
            pltpu.VMEM((n, tok, width), BF16),
            pltpu.VMEM((width, columns), F32),
            sem((2, n)), sem((n,)), sem((n, ne)), sem((n, ne)), sem((n,)), sem((n,)), sem((4,)),
        ],
        compiler_params=pltpu.CompilerParams(
            collective_id=3, has_side_effects=True, vmem_limit_bytes=60 * 1024 * 1024
        ),
        name="experts",
    )(slots, d_outs, wgu, wd, meta_all)


def backward_kernel(
    n, ne, cap_pad,
    gains, vectors, meta_all,
    d_two_in, resid_in, cot_in, wo_in, x_in, mixed_in, qkv_in, lse_in, normed_in, wq_in, wk_in, wv_in,
    gwgu, out_rows,
    block_out, grad_in, g_all, small_all, gw_in, out_in,
    d_two, resid, cot, wo, x, mixed, qkv, lse, normed, wq, wk, wv,
    dm, dm_in, tiles, sums, dq_s, dk_s, dv_s, dk_acc, dv_acc, diag, d_res,
    dn_part, dn_land, moe_part, moe_land, out_one,
    g_send, g_land, g2_send, g2_land, o_send, o_land, o2_send, o2_land,
    small_own, small_land, small_sum,
    out_s, out_r, w_s, w_r, dm_s, dm_r, dn_s, dn_r, moe_s, moe_r, g_s, g_r, o_s, o_r, g2_s, g2_r, o2_s, o2_r,
    sp_s, sp_r, sz_s, sz_r, keep_sem, in_sem,
):
    dp, ex = lax.axis_index("dp"), lax.axis_index("expert")
    tok, width = cot.shape
    own = dq_s.shape[1]
    pairs_n = own // 128
    slots_n = ne * cap_pad
    wrows = g_all.shape[1]
    greet(n, ne, dp, ex)
    loads = Copies(
        in_sem,
        [
            (d_two_in, d_two), (resid_in, resid), (cot_in, cot), (wo_in, wo), (x_in, x), (mixed_in, mixed),
            (qkv_in, qkv), (lse_in, lse), (normed_in, normed), (wq_in, wq), (wk_in, wk), (wv_in, wv),
        ],
    )
    loads.start(0, 1, 2, 3, 5, 6, 7, 9, 10, 11, 8, 4)
    toward = 2 * ((2 * dp) // n) - 1

    def group_at(step):
        return lax.rem(dp + n + toward * (1 + step), n)

    def rows_of(peer):
        return pl.ds(pl.multiple_of(peer * cap_pad, 16), cap_pad)

    def to_line(src, dst, send, recv, t):
        return remote(src.at[t], dst.at[dp], send.at[t], recv.at[dp], (t, ex))

    def from_line(src, dst, send, recv, t):
        return remote(src.at[t], dst.at[t], send.at[t], recv.at[t], (t, ex))

    def to_plane(src, dst, send, recv, k):
        return remote(src, dst.at[ex], send.at[k], recv.at[k], (dp, lax.rem(ex + k, ne)))

    def from_plane(src, dst, send, recv, k):
        peer = lax.rem(ex + ne - k, ne)
        return remote(src, dst.at[peer], send.at[k], recv.at[k], (dp, peer))

    def out_give(at, k):
        peer = lax.rem(ex + k, ne)
        return remote(
            out_rows.at[at, rows_of(peer)], out_in.at[at, rows_of(ex)], out_s.at[at, k], out_r.at[at, k], (dp, peer)
        )

    def out_take(at, k):
        peer = lax.rem(ex + ne - k, ne)
        return remote(
            out_rows.at[at, rows_of(ex)], out_in.at[at, rows_of(peer)], out_s.at[at, k], out_r.at[at, k], (dp, peer)
        )

    def out_keep(at):
        return pltpu.make_async_copy(out_rows.at[at, rows_of(ex)], out_in.at[at, rows_of(ex)], out_s.at[at, 0])

    loads.wait(0, 1, 2)
    values = resid[...]
    d_normed = d_two[...]
    inverse = lax.rsqrt(jnp.mean(values * values, axis=-1, keepdims=True) + EPSILON)
    scaled = gains[1:2, :] * d_normed
    gain_rows_two = jnp.sum(d_normed * values * inverse, axis=0, keepdims=True)
    mean = jnp.mean(scaled * values, axis=-1, keepdims=True)
    d_resid = cot[...].astype(F32) + inverse * scaled - values * (inverse * inverse * inverse * mean)
    d_res[...] = d_resid
    d_attn = d_resid.astype(BF16)
    loads.wait(3)
    d_mixed = mm(d_attn, wo[...], NT).astype(BF16)
    meet(n, ne)
    for j in range(n):
        dm[j] = d_mixed[:, j * own : (j + 1) * own]
    for d in range(1, n):
        to_line(dm, dm_in, dm_s, dm_r, lax.rem(dp + d, n)).start()
    dm_in[dp] = dm[dp]
    for d in range(1, n):
        to_line(gwgu, gw_in, w_s, w_r, lax.rem(dp + d, n)).start()
    keep_w = pltpu.make_async_copy(gwgu.at[dp], gw_in.at[dp], keep_sem.at[0])
    keep_w.start()

    @pl.loop(0, n)
    def _(step):
        at = group_at(step)
        for k in range(1, ne):
            out_give(at, k).start()
        out_keep(at).start()

    loads.wait(5)
    o_send[...] = mm(mixed[...], d_attn, TN).reshape(n, ne, wrows, width).astype(BF16)
    for k in range(1, ne):
        to_plane(o_send.at[:, lax.rem(ex + k, ne)], o_land, o_s, o_r, k).start()
    o_land[ex] = o_send[:, ex]
    for i in range(width // 128):
        small_own[8 + i : 9 + i, :] = gain_rows_two[:, i * 128 : (i + 1) * 128]
    for d in range(1, n):
        from_line(dm, dm_in, dm_s, dm_r, lax.rem(dp + d, n)).wait_recv()

    loads.wait(6, 7, 9, 10, 11)
    lane = lax.broadcasted_iota(jnp.int32, (tok, 128), 1)
    low_half = lane < HEAD_DIM
    key_low = lax.broadcasted_iota(jnp.int32, (n * tok, 128), 1) < HEAD_DIM
    diag[...] = jnp.zeros_like(diag)
    for pair in range(pairs_n):
        cols = slice(pair * 128, (pair + 1) * 128)
        for side in range(2):
            bias_tile(vectors, 2 * pair + side, tiles.at[side])
        sums[...] = jnp.zeros_like(sums)
        dk_acc[...] = jnp.zeros_like(dk_acc)
        dv_acc[...] = jnp.zeros_like(dv_acc)
        k_pair = qkv[:, own + pair * 128 : own + (pair + 1) * 128]
        v_pair = qkv[:, 2 * own + pair * 128 : 2 * own + (pair + 1) * 128]

        @pl.loop(0, n)
        def _(i):
            at = pl.ds(pl.multiple_of(i * tok, tok), tok)
            q_pair = qkv[at, cols]
            dm_pair = dm_in[i, :, cols]
            dqs, dks, dvs = [], [], []
            for side in range(2):
                mask = low_half if side == 0 else jnp.logical_not(low_half)
                logits = logits_of(n, tok, i, q_pair, k_pair, mask, tiles.at[side])
                first = pair * 128 + side * HEAD_DIM
                probs = jnp.exp(logits - lse[at, first : first + 1])
                d_probs = mm(jnp.where(mask, dm_pair, jnp.zeros_like(dm_pair)), v_pair, NT)
                inner = jnp.sum(probs * d_probs, axis=-1, keepdims=True)
                d_logits = (probs * (d_probs - inner)).astype(BF16)
                dvs.append(mm(probs.astype(BF16), dm_pair, TN))
                dqs.append(mm(d_logits, k_pair))
                dks.append(mm(d_logits, q_pair, TN))
                wide = d_logits.astype(F32)
                for j in range(n):
                    here = pl.ds(tile_offset(n, tok, i, j), tok)
                    sums[side, :, here] += wide[:, j * tok : (j + 1) * tok]
            dq_s[at, cols] = (jnp.where(low_half, dqs[0], dqs[1]) * SCALE).astype(BF16)
            dk_acc[...] += jnp.where(key_low, dks[0], dks[1])
            dv_acc[...] += jnp.where(key_low, dvs[0], dvs[1])

        dk_s[:, cols] = (dk_acc[...] * SCALE).astype(BF16)
        dv_s[:, cols] = dv_acc[...].astype(BF16)
        for side in range(2):
            diag[2 * pair + side : 2 * pair + side + 1, :] = diagonal_sum(sums[side])

    def d_norm(t):
        at = pl.ds(pl.multiple_of(t * tok, tok), tok)
        return mm(dq_s[at, :], wq[...], NT) + mm(dk_s[at, :], wk[...], NT) + mm(dv_s[at, :], wv[...], NT)

    def sum_copy(part, land, send, recv, r, side):
        t = lax.rem(dp + n + (n - r) * (1 - 2 * side), n)
        target = lax.rem(dp + n + 1 - 2 * side, n)
        return t, remote(part.at[t], land.at[r - 1, side], send.at[r - 1, side], recv.at[r - 1, side], (target, ex))

    def takes_part(r, side):
        return ((side == 0) & (dp < r) & (dp + 1 < n)) | ((side == 1) & (dp + r >= n) & (dp > 0))

    def is_fed(r, side):
        return ((side == 0) & (dp > 0) & (r > 1)) | ((side == 1) & (dp + 1 < n) & (r > 1))

    def fed(part, land, send, recv, r, side):
        remote(
            part.at[dp], land.at[r - 1, side], send.at[r - 1, side], recv.at[r - 1, side], (dp, ex)
        ).wait_recv()

    def sum_round(part, land, send, recv, term, r):
        @pl.loop(0, 2)
        def _(side):
            @pl.when(takes_part(r, side))
            def _():
                t, copy = sum_copy(part, land, send, recv, r, side)
                mine = term(t)

                @pl.when(is_fed(r, side))
                def _():
                    fed(part, land, send, recv, r - 1, side)
                    part[t] = (mine + land[max(r - 2, 0), side].astype(F32)).astype(BF16)

                @pl.when(jnp.logical_not(is_fed(r, side)))
                def _():
                    part[t] = mine.astype(BF16)

                copy.start()

    def sum_end(part, land, send, recv, mine):
        @pl.when(dp > 0)
        def _():
            fed(part, land, send, recv, n - 1, 0)

        @pl.when(dp + 1 < n)
        def _():
            fed(part, land, send, recv, n - 1, 1)

        left = jnp.where(dp > 0, land[n - 2, 0].astype(F32), 0.0)
        right = jnp.where(dp + 1 < n, land[n - 2, 1].astype(F32), 0.0)
        return mine + left + right

    def sum_sent(part, land, send, recv):
        for r in range(1, n):
            for side in range(2):
                @pl.when(takes_part(r, side))
                def _():
                    sum_copy(part, land, send, recv, r, side)[1].wait_send()

    dn = (dn_part, dn_land, dn_s, dn_r)
    moes = (moe_part, moe_land, moe_s, moe_r)
    sum_round(*dn, d_norm, 1)

    loads.wait(8, 4)
    for w, ref in enumerate((dq_s, dk_s, dv_s)):
        g_send[:, :, w] = mm(normed[...], ref[...], TN).reshape(n, ne, wrows, own).astype(BF16)
    for k in range(1, ne):
        to_plane(g_send.at[:, lax.rem(ex + k, ne)], g_land, g_s, g_r, k).start()
    g_land[ex] = g_send[:, ex]

    for r in range(2, n):
        sum_round(*dn, d_norm, r)

    rest = diag[...]
    table = jnp.zeros((8, 128), F32)
    wide = vectors.shape[1]
    hot = bucket_hot(wide, tok, wide // 2)
    for _ in range(3):
        piece = rest.astype(BF16)
        table = table + mm(piece, hot)
        rest = rest - piece.astype(F32)
    small_own[16:24, :] = table

    for k in range(1, ne):
        from_plane(o_send.at[:, ex], o_land, o_s, o_r, k).wait_recv()
    total = o_land[0].astype(F32)
    for e in range(1, ne):
        total = total + o_land[e].astype(F32)
    o2_send[...] = total.astype(BF16)
    for d in range(1, n):
        to_line(o2_send, o2_land, o2_s, o2_r, lax.rem(dp + d, n)).start()
    o2_land[dp] = o2_send[dp]

    def moe(at):
        for k in range(1, ne):
            out_take(at, k).wait_recv()
        out_keep(at).wait()
        load = pltpu.make_async_copy(out_in.at[at], out_one, keep_sem.at[1])
        load.start()
        meta = meta_all[at]
        ids = lax.broadcasted_iota(jnp.int32, (slots_n, tok), 0).astype(F32)
        gate = meta[2:3, :]
        weight = jnp.where(ids == meta[0:1, :], gate, 0.0) + jnp.where(ids == meta[1:2, :], 1.0 - gate, 0.0)
        load.wait()
        return mm(weight.astype(BF16), out_one[...], TN)

    for r in range(1, n):
        sum_round(*moes, moe, r)

    for k in range(1, ne):
        from_plane(g_send.at[:, ex], g_land, g_s, g_r, k).wait_recv()
    total = g_land[0].astype(F32)
    for e in range(1, ne):
        total = total + g_land[e].astype(F32)
    g2_send[...] = total.astype(BF16)
    for d in range(1, n):
        to_line(g2_send, g2_land, g2_s, g2_r, lax.rem(dp + d, n)).start()
    g2_land[dp] = g2_send[dp]

    total = sum_end(*dn, d_norm(dp))
    values = x[...].astype(F32)
    inverse = lax.rsqrt(jnp.mean(values * values, axis=-1, keepdims=True) + EPSILON)
    scaled = gains[0:1, :] * total
    gain_rows_one = jnp.sum(total * values * inverse, axis=0, keepdims=True)
    mean = jnp.mean(scaled * values, axis=-1, keepdims=True)
    grad_in[...] = (d_res[...] + inverse * scaled - values * (inverse * inverse * inverse * mean)).astype(BF16)
    for i in range(width // 128):
        small_own[i : i + 1, :] = gain_rows_one[:, i * 128 : (i + 1) * 128]
    for k in range(1, ne):
        to_plane(small_own, small_land, sp_s, sp_r, k).start()
    small_land[ex] = small_own[...]
    for k in range(1, ne):
        from_plane(small_own, small_land, sp_s, sp_r, k).wait_recv()
    total = small_land[0]
    for e in range(1, ne):
        total = total + small_land[e]
    small_sum[...] = total
    for d in range(1, n):
        t = lax.rem(dp + d, n)
        remote(small_sum, small_all.at[dp], sz_s.at[t], sz_r.at[dp], (t, ex)).start()
    small_all[dp] = total

    block_out[...] = sum_end(*moes, resid[...] + moe(dp)).astype(BF16)

    for d in range(1, n):
        t = lax.rem(dp + d, n)
        from_line(o2_send, o2_land, o2_s, o2_r, t).wait_recv()
        from_line(g2_send, g2_land, g2_s, g2_r, t).wait_recv()
        remote(small_sum, small_all.at[t], sz_s.at[t], sz_r.at[t], (t, ex)).wait_recv()
    total = o2_land[0].astype(F32)
    for j in range(1, n):
        total = total + o2_land[j].astype(F32)
    g_all[3] = total
    for w in range(3):
        g_all[w] = jnp.concatenate([g2_land[j, w] for j in range(n)], axis=1).astype(F32)
    for d in range(1, n):
        t = lax.rem(dp + d, n)
        from_line(gwgu, gw_in, w_s, w_r, t).wait_recv()
        for src, dst, send, recv in (
            (gwgu, gw_in, w_s, w_r), (dm, dm_in, dm_s, dm_r),
            (o2_send, o2_land, o2_s, o2_r), (g2_send, g2_land, g2_s, g2_r),
        ):
            to_line(src, dst, send, recv, t).wait_send()
        remote(small_sum, small_all.at[dp], sz_s.at[t], sz_r.at[dp], (t, ex)).wait_send()
    keep_w.wait()
    sum_sent(*dn)
    sum_sent(*moes)
    for k in range(1, ne):
        to_plane(o_send.at[:, ex], o_land, o_s, o_r, k).wait_send()
        to_plane(g_send.at[:, ex], g_land, g_s, g_r, k).wait_send()
        to_plane(small_own, small_land, sp_s, sp_r, k).wait_send()

    @pl.loop(0, n)
    def _(at):
        for k in range(1, ne):
            out_give(at, k).wait_send()


def backward(
    n, ne, cap_pad, wrows, d_two, resid, cot, x, gains, mixed, wo, qkv, lse, normed, vectors,
    wq, wk, wv, meta_all, gwgu, out_rows,
):
    tok, width = cot.shape
    own = wq.shape[1]
    wide = vectors.shape[1]
    both = gwgu.shape[2]
    slots_n = ne * cap_pad
    length = n * tok
    sem = pltpu.SemaphoreType.DMA
    shape = jax.ShapeDtypeStruct
    return pl.pallas_call(
        functools.partial(backward_kernel, n, ne, cap_pad),
        in_specs=[VM] * 3 + [ANY] * 14,
        out_specs=[VM] * 4 + [ANY] * 2,
        out_shape=[
            shape((tok, width), BF16),
            shape((tok, width), BF16),
            shape((4, wrows, width), F32),
            shape((n, 24, 128), F32),
            shape((n, tok, both), BF16),
            shape((n, slots_n, width), BF16),
        ],
        scratch_shapes=[
            pltpu.VMEM((tok, width), F32),
            pltpu.VMEM((tok, width), F32),
            pltpu.VMEM((tok, width), BF16),
            pltpu.VMEM((width, width), BF16),
            pltpu.VMEM((tok, width), BF16),
            pltpu.VMEM((tok, width), BF16),
            pltpu.VMEM((length, 3 * own), BF16),
            pltpu.VMEM((length, own), F32),
            pltpu.VMEM((length, width), BF16),
            pltpu.VMEM((width, own), BF16),
            pltpu.VMEM((width, own), BF16),
            pltpu.VMEM((width, own), BF16),
            pltpu.VMEM((n, tok, own), BF16),
            pltpu.VMEM((n, tok, own), BF16),
            pltpu.VMEM((2, tok, wide), F32),
            pltpu.VMEM((2, tok, wide), F32),
            pltpu.VMEM((length, own), BF16),
            pltpu.VMEM((length, own), BF16),
            pltpu.VMEM((length, own), BF16),
            pltpu.VMEM((length, 128), F32),
            pltpu.VMEM((length, 128), F32),
            pltpu.VMEM((8, wide), F32),
            pltpu.VMEM((tok, width), F32),
            pltpu.VMEM((n, tok, width), BF16),
            pltpu.VMEM((n - 1, 2, tok, width), BF16),
            pltpu.VMEM((n, tok, width), BF16),
            pltpu.VMEM((n - 1, 2, tok, width), BF16),
            pltpu.VMEM((slots_n, width), BF16),
            pltpu.VMEM((n, ne, 3, wrows, own), BF16),
            pltpu.VMEM((ne, n, 3, wrows, own), BF16),
            pltpu.VMEM((n, 3, wrows, own), BF16),
            pltpu.VMEM((n, 3, wrows, own), BF16),
            pltpu.VMEM((n, ne, wrows, width), BF16),
            pltpu.VMEM((ne, n, wrows, width), BF16),
            pltpu.VMEM((n, wrows, width), BF16),
            pltpu.VMEM((n, wrows, width), BF16),
            pltpu.VMEM((24, 128), F32),
            pltpu.VMEM((ne, 24, 128), F32),
            pltpu.VMEM((24, 128), F32),
            sem((n, ne)), sem((n, ne)), sem((n,)), sem((n,)), sem((n,)), sem((n,)), sem((n, 2)), sem((n, 2)),
            sem((n, 2)), sem((n, 2)), sem((ne,)), sem((ne,)), sem((ne,)), sem((ne,)), sem((n,)), sem((n,)),
            sem((n,)), sem((n,)), sem((ne,)), sem((ne,)), sem((n,)), sem((n,)), sem((2,)), sem((12,)),
        ],
        compiler_params=pltpu.CompilerParams(
            collective_id=4, has_side_effects=True, vmem_limit_bytes=60 * 1024 * 1024
        ),
        name="backward",
    )(
        gains, vectors, meta_all, d_two, resid, cot, wo, x, mixed, qkv, lse, normed, wq, wk, wv, gwgu, out_rows
    )


def split_pieces(value):
    pieces = []
    for _ in range(3):
        piece = value.astype(BF16)
        pieces.append(piece)
        value = value - piece.astype(F32)
    return pieces


def finish_kernel(
    n, ne, heads_own, piece, blocks, g_all, small, out_in, grad_in, gwd_in,
    gate_ref, up_ref, gq, gk, gv, go, gain_one, gain_two, bias, block_out, grad_out, gwd,
):
    main = piece // 128 * 128
    rest = piece - main
    gates, ups = [], []
    for j in range(n):
        block = blocks[j].astype(F32)
        gates += [block[:, :main], block[:, 2 * main : 2 * main + rest]]
        ups += [block[:, main : 2 * main], block[:, 2 * main + rest :]]
    gate_ref[...] = jnp.concatenate(gates, axis=1)
    up_ref[...] = jnp.concatenate(ups, axis=1)
    block_out[...] = out_in[...]
    grad_out[...] = grad_in[...]
    gwd[...] = gwd_in[...]

    @pl.when(pl.program_id(0) == 0)
    def _():
        for i, ref in enumerate((gq, gk, gv, go)):
            ref[...] = g_all[i]
        me = lax.axis_index("dp") * ne + lax.axis_index("expert")
        total = small[0, :16]
        for j in range(1, n):
            total = total + small[j, :16]
        rows = lax.broadcasted_iota(jnp.int32, (8, 128), 0)
        lanes = lax.broadcasted_iota(jnp.int32, (8, 128), 1)
        for i, ref in enumerate((gain_one, gain_two)):
            count = ref.shape[1]
            at = me * count
            row = jnp.sum(jnp.where(rows == at // 128, total[8 * i : 8 * i + 8], 0.0), axis=0, keepdims=True)
            row = jnp.broadcast_to(row, (8, 128))
            ref[...] = pltpu.roll(row, lax.rem(128 - lax.rem(at, 128), 128), 1)[:1, :count]
        table = jnp.concatenate([small[j, 16 : 16 + heads_own] for j in range(n)], axis=0)
        heads = n * heads_own
        count = bias.shape[1]
        at = me * count
        table = jnp.concatenate([table, jnp.zeros((128 - heads, 128), F32)], axis=0)
        hot = jnp.where(lanes == at // heads, 1.0, 0.0).astype(BF16)
        row = sum(mm(hot, part, NT) for part in split_pieces(table))
        bias[...] = pltpu.roll(row, lax.rem(128 - lax.rem(at, heads), 128), 1)[:1, :count]


def finish(n, ne, heads_own, n_gain, n_bias, blocks, g_all, small, block_out, grad_in, gwd):
    tok, both = blocks.shape[1:]
    wrows, width = g_all.shape[1:]
    deep = gwd.shape[0]
    piece = both // 2
    steps = 4
    step, part = tok // steps, deep // steps
    total = n * piece
    shape = jax.ShapeDtypeStruct
    fixed2 = lambda i: (0, 0)
    fixed3 = lambda i: (0, 0, 0)
    move = lambda i: (i, 0)
    return pl.pallas_call(
        functools.partial(finish_kernel, n, ne, heads_own, piece),
        grid=(steps,),
        in_specs=[
            pl.BlockSpec((n, step, both), lambda i: (0, i, 0)),
            pl.BlockSpec((4, wrows, width), fixed3),
            pl.BlockSpec(small.shape, fixed3),
            pl.BlockSpec((step, width), move),
            pl.BlockSpec((step, width), move),
            pl.BlockSpec((part, width), move),
        ],
        out_specs=[pl.BlockSpec((step, total), move)] * 2
        + [pl.BlockSpec((wrows, width), fixed2)] * 4
        + [pl.BlockSpec((1, n_gain), fixed2)] * 2
        + [pl.BlockSpec((1, n_bias), fixed2)]
        + [pl.BlockSpec((step, width), move)] * 2
        + [pl.BlockSpec((part, width), move)],
        out_shape=[shape((tok, total), F32)] * 2
        + [shape((wrows, width), F32)] * 4
        + [shape((1, n_gain), F32)] * 2
        + [shape((1, n_bias), F32)]
        + [shape((tok, width), BF16)] * 2
        + [shape((deep, width), F32)],
        compiler_params=pltpu.CompilerParams(vmem_limit_bytes=VMEM_LIMIT),
        name="finish",
    )(blocks, g_all, small, block_out, grad_in, gwd)


def local(
    inputs, cotangent, gain_attn, w_query, w_key, w_value, w_out, position_bias,
    gain_moe, w_gate, w_up, w_down, routes, gate_fixed,
):
    n = lax.axis_size("dp")
    experts_n = lax.axis_size("expert")
    dp = lax.axis_index("dp")
    ex = lax.axis_index("expert")
    tok, width = inputs.shape[1:]
    length = n * tok
    own = HEADS * HEAD_DIM // n
    heads_own = HEADS // n
    wrows = w_query.shape[0]
    capacity = 5 * tok // (2 * experts_n)
    cap_pad = -(-capacity // 16) * 16
    slots_n = experts_n * cap_pad

    n_gain, n_bias = gain_attn.shape[0], position_bias.shape[0]
    meta_in = jnp.concatenate([routes[0].T, gate_fixed], axis=0)
    normed, qkv, lse, mixed, resid, wq, wk, wv, wo, meta_all, vectors, gains, slots, d_outs, wgu = front(
        n, experts_n, capacity, cap_pad, inputs[0], w_query, w_key, w_value, w_out,
        gain_attn.reshape(1, -1), gain_moe.reshape(1, -1), position_bias.reshape(1, -1),
        meta_in, w_gate[0], w_up[0], cotangent[0],
    )
    wq, wk, wv = (w.reshape(width, own) for w in (wq, wk, wv))
    wo = wo.reshape(width, width)
    wgu = wgu.reshape(width, -1)
    deep = w_down.shape[1]
    out_rows, grad_normed_two, gwgu, grad_w_down = experts(
        n, experts_n, cap_pad, deep, slots, d_outs, wgu, w_down[0], meta_all
    )

    block_out, grad_inputs, g_all, small, got, _ = backward(
        n, experts_n, cap_pad, wrows, grad_normed_two, resid, cotangent[0], inputs[0], gains, mixed, wo,
        qkv, lse, normed, vectors, wq, wk, wv, meta_all, gwgu.reshape(n, width // n, -1), out_rows,
    )
    (
        grad_w_gate, grad_w_up, gq, gk, gv, go, grad_gain_one, grad_gain_two, grad_bias, block_out, grad_inputs,
        grad_w_down,
    ) = finish(n, experts_n, heads_own, n_gain, n_bias, got, g_all, small, block_out, grad_inputs, grad_w_down)

    return (
        block_out[None],
        grad_inputs[None],
        grad_gain_one[0],
        gq,
        gk,
        gv,
        go,
        grad_bias[0],
        grad_gain_two[0],
        grad_w_gate[None],
        grad_w_up[None],
        grad_w_down[None],
    )


def solution(mesh):
    vector = P(("dp", "expert"))
    matrix = P(("dp", "expert"), None)
    split = P("expert", "dp", None)
    return jax.shard_map(
        local,
        mesh=mesh,
        in_specs=(
            split, split, vector, matrix, matrix, matrix, matrix, vector, vector,
            split, split, split, split, P("expert", "dp"),
        ),
        out_specs=(
            split, split, vector, matrix, matrix, matrix, matrix, vector, vector,
            split, split, split,
        ),
        check_vma=False,
    )
```

```python
import functools

import jax
import jax.numpy as jnp
from jax import lax
from jax.experimental import pallas as pl
from jax.experimental.pallas import tpu as pltpu
from jax.sharding import PartitionSpec as P

HEADS = 16
HEAD_DIM = 64
BUCKETS = 32
THRESHOLDS = (12, 16, 23, 32, 46, 64, 91)
EPSILON = 1e-06
SCALE = HEAD_DIM ** (-0.5)
BF16 = jnp.bfloat16
F32 = jnp.float32
GELU_C = 0.7978845608028654
GELU_A = 0.044715
VMEM_LIMIT = 56 * 1024 * 1024

NT = (((1,), (1,)), ((), ()))
TN = (((0,), (0,)), ((), ()))
NN = (((1,), (0,)), ((), ()))


def mm(a, b, dims=NN):
    return lax.dot_general(a, b, dims, preferred_element_type=F32)


def bucket_of(offset):
    distance = jnp.abs(offset)
    banded = jnp.full(distance.shape, 8, jnp.int32)
    for cutoff in THRESHOLDS:
        banded = banded + (distance >= cutoff).astype(jnp.int32)
    nearby = jnp.where(distance < 8, distance, banded)
    return nearby + jnp.where(offset > 0, 16, 0).astype(jnp.int32)


def bias_tile(vec_ref, head, tile_ref):
    block, wide = tile_ref.shape
    row = jnp.broadcast_to(vec_ref[pl.ds(head, 1), :], (block, wide))
    tile_ref[...] = pltpu.roll(row, wide - block, 1, stride=1, stride_axis=0)


def tile_offset(n, block, query_block, key_block):
    return pl.multiple_of((key_block - query_block + n - 1) * block, 128)


def logits_of(n, block, query_block, q_pair, k_pair, mask, tile_ref):
    masked = jnp.where(mask, q_pair, jnp.zeros_like(q_pair))
    raw = mm(masked, k_pair, NT) * SCALE
    bias = jnp.concatenate(
        [tile_ref[:, pl.ds(tile_offset(n, block, query_block, j), block)] for j in range(n)], axis=1
    )
    return raw + bias


def diagonal_sum(tile):
    rows, wide = tile.shape
    while rows > 1:
        half = rows // 2
        tile = tile[:half] + pltpu.roll(tile[half:], wide - half, 1)
        rows = half
    return tile


def gelu_pair(v):
    square = v * v
    t = jnp.tanh(GELU_C * (v + GELU_A * v * square))
    half = 0.5 * (1.0 + t)
    slope = half + (0.5 * GELU_C) * v * (1.0 - t * t) * (1.0 + (3.0 * GELU_A) * square)
    return v * half, slope


MESH = pl.DeviceIdType.MESH


def remote(src, dst, send, recv, target):
    return pltpu.make_async_remote_copy(
        src_ref=src, dst_ref=dst, send_sem=send, recv_sem=recv, device_id=target, device_id_type=MESH
    )


def greet(n, ne, dp, ex):
    barrier = pltpu.get_barrier_semaphore()
    for d in range(1, n):
        pl.semaphore_signal(barrier, inc=1, device_id=(lax.rem(dp + d, n), ex), device_id_type=MESH)
    for k in range(1, ne):
        pl.semaphore_signal(barrier, inc=1, device_id=(dp, lax.rem(ex + k, ne)), device_id_type=MESH)


def meet(n, ne):
    pl.semaphore_wait(pltpu.get_barrier_semaphore(), n + ne - 2)


class Copies:
    def __init__(self, sem, pairs):
        self.copies = [pltpu.make_async_copy(src, dst, sem.at[i]) for i, (src, dst) in enumerate(pairs)]

    def start(self, *which):
        for i in which:
            self.copies[i].start()

    def wait(self, *which):
        for i in which:
            self.copies[i].wait()


class Chain:
    def __init__(self, n, dp, ex, own, buffer, send, recv):
        self.n, self.dp, self.ex, self.own = n, dp, ex, own
        self.buffer, self.send_sem, self.recv_sem = buffer, send, recv

    def block(self, hop, side):
        return lax.rem(self.dp + self.n + hop * (2 * side - 1), self.n)

    def copy(self, hop, side, first=False):
        at = self.block(hop, side)
        target = lax.rem(self.dp + self.n + 1 - 2 * side, self.n)
        return remote(
            self.own if first else self.buffer.at[at], self.buffer.at[at],
            self.send_sem.at[hop, side], self.recv_sem.at[hop, side], (target, self.ex),
        )

    def has_next(self, side):
        return (self.dp + 1 < self.n) if side == 0 else (self.dp > 0)

    def start(self):
        for side in range(2):
            @pl.when(self.has_next(side))
            def _():
                self.copy(0, side, True).start()

    def held(self, hop, side):
        return (self.dp > hop) if side == 0 else (self.dp + 1 + hop < self.n)

    def arrive(self, hop, side):
        at = self.block(hop + 1, side)
        remote(
            self.buffer.at[at], self.buffer.at[at], self.send_sem.at[hop, side], self.recv_sem.at[hop, side],
            (self.dp, self.ex),
        ).wait_recv()

        @pl.when(self.has_next(side))
        def _():
            self.copy(hop + 1, side).start()

        return at

    def finish(self):
        for hop in range(self.n - 1):
            for side in range(2):
                mine = self.has_next(side)
                if hop:
                    mine = mine & self.held(hop - 1, side)

                @pl.when(mine)
                def _():
                    self.copy(hop, side, hop == 0).wait_send()


ANY = pl.BlockSpec(memory_space=pl.ANY)
VM = pl.BlockSpec(memory_space=pltpu.VMEM)


def bucket_hot(wide, turn, length):
    at = lax.broadcasted_iota(jnp.int32, (wide, 128), 0) + turn
    offset = jnp.where(at >= wide, at - wide, at) - length
    hit = bucket_of(offset) == lax.broadcasted_iota(jnp.int32, (wide, 128), 1)
    return jnp.where(hit & (jnp.abs(offset) < length), 1.0, 0.0).astype(BF16)


def rows_flat(ref):
    n, ne, rows, columns = ref.shape
    if rows % 16 == 0:
        return ref[...].reshape(n * ne * rows, columns)
    return ref[...].astype(F32).reshape(n * ne * rows, columns).astype(BF16)


def front_kernel(
    n, ne, cap, cap_pad, piece,
    x_in, wq, wk, wv, wo, gain_attn, gain_moe, position_bias, meta_in, wg_in, wu_in, cot_in,
    normed_out, qkv_out, lse_out, mixed_out, resid_out, lq_out, lk_out, lv_out, lwo_out, meta_all, vectors, gains,
    slots, d_outs, wgu,
    x, wg, wu, cot, normed, qkv, lse, mixed, resid, lq, lk, lv, lwo,
    extra, sq, sk, sv, sext, swo, smeta, lext, packed,
    x_all, heads, mixed_in, tiles, cot_all, two_all, two_own, two_rows, cot_rows,
    line_send, line_recv, plane_send, plane_recv, core_send, core_recv, chain_send, chain_recv, own_sem,
    w_send, w_recv, m_send, m_recv, c_send, c_recv, t_send, t_recv,
    pc_send, pc_recv, pt_send, pt_recv, in_sem, out_sem,
):
    dp, ex = lax.axis_index("dp"), lax.axis_index("expert")
    greet(n, ne, dp, ex)
    loads = Copies(in_sem, [(x_in, x), (cot_in, cot), (wg_in, wg), (wu_in, wu)])
    loads.start(0, 1, 2, 3)
    stores = Copies(
        out_sem,
        [
            (normed, normed_out), (qkv, qkv_out), (lse, lse_out), (mixed, mixed_out), (resid, resid_out),
            (lq, lq_out), (lk, lk_out), (lv, lv_out), (lwo, lwo_out),
        ],
    )
    own = sq.shape[2]
    block, width = cot.shape
    pairs_n = own // 128
    slots_n = ne * cap_pad
    n_gain, n_bias = gain_attn.shape[1], position_bias.shape[1]
    line_of = jnp.concatenate(
        [
            gain_attn[...].astype(F32), gain_moe[...].astype(F32), position_bias[...].astype(F32),
            jnp.zeros((1, own - 2 * n_gain - n_bias), F32),
        ],
        axis=1,
    )
    extra[...] = jnp.broadcast_to(line_of, (16, own)).astype(BF16)
    loads.wait(0)
    meet(n, ne)
    chain = Chain(n, dp, ex, x, x_all, chain_send, chain_recv)
    cots = Chain(n, dp, ex, cot, cot_all, c_send, c_recv)
    twos = Chain(n, dp, ex, two_own, two_all, t_send, t_recv)

    def column(ref, t):
        return ref.at[:, pl.ds(pl.multiple_of(t * own, 128), own)]

    def line(kind, d):
        t = lax.rem(dp + d, n)
        src, dst = [
            (column(wq, t), sq.at[dp]), (column(wk, t), sk.at[dp]), (column(wv, t), sv.at[dp]),
            (extra, sext.at[dp]), (wo, swo.at[dp]), (smeta, meta_all.at[dp]),
        ][kind]
        return remote(src, dst, line_send.at[kind, d], line_recv.at[kind, d], (t, ex))

    for d in range(1, n):
        for kind in range(4):
            line(kind, d).start()
    chain.start()
    for d in range(1, n):
        line(4, d).start()
    here = pl.ds(pl.multiple_of(dp * own, 128), own)
    sq[dp] = wq[:, here]
    sk[dp] = wk[:, here]
    sv[dp] = wv[:, here]
    sext[dp] = extra[...]
    swo[dp] = wo[...]
    x_all[dp] = x[...]

    tok = meta_in.shape[1]
    routes = meta_in[...]
    ids = lax.broadcasted_iota(jnp.int32, (ne, tok), 0)
    first = (ids == routes[0:1, :]).astype(F32)
    second = (ids == routes[1:2, :]).astype(F32)
    before = (
        lax.broadcasted_iota(jnp.int32, (tok, tok), 0) < lax.broadcasted_iota(jnp.int32, (tok, tok), 1)
    ).astype(BF16)
    counts = mm((first + second).astype(BF16), before)
    slot_a = jnp.sum(counts * first, axis=0, keepdims=True)
    slot_b = jnp.sum((counts + first) * second, axis=0, keepdims=True)
    asked = routes.astype(F32)
    dest_a = jnp.where(slot_a < cap, asked[0:1, :] * cap_pad + slot_a, -1.0)
    dest_b = jnp.where(slot_b < cap, asked[1:2, :] * cap_pad + slot_b, -1.0)
    gate = asked[2:3, :] * (1.0 / 65536.0)
    smeta[...] = jnp.concatenate([dest_a, dest_b, gate, jnp.zeros((5, tok), F32)], axis=0)
    meta_all[dp] = smeta[...]
    for d in range(1, n):
        line(5, d).start()

    pairs = [(sq, lq), (sk, lk), (sv, lv), (sext, lext), (swo, lwo)]
    partner = ex + 1 - 2 * lax.rem(ex, 2)

    def plane(kind, k):
        src, dst = pairs[kind]
        return remote(
            src, dst.at[:, ex], plane_send.at[kind, k], plane_recv.at[kind, k],
            (dp, lax.rem(ex + 2 * k, ne)),
        )

    def core(kind, k):
        src, dst = pairs[kind]
        at = lax.rem(ex + ne - 2 * k, ne)
        return remote(
            src if k == 0 else dst.at[:, at], dst.at[:, at],
            core_send.at[kind, k], core_recv.at[kind, k], (dp, partner),
        )

    def keep_own(kind):
        return pltpu.make_async_copy(pairs[kind][0], pairs[kind][1].at[:, ex], own_sem.at[kind])

    def spread(kind):
        for d in range(1, n):
            line(kind, d).wait_recv()
        for k in range(1, ne // 2):
            plane(kind, k).start()
        core(kind, 0).start()
        keep_own(kind).start()

    def pass_on(kind):
        for k in range(1, ne // 2):
            plane(kind, k).wait_recv()
            core(kind, k).start()

    def settle(kind):
        keep_own(kind).wait()
        for k in range(ne // 2):
            core(kind, k).wait()
        for k in range(1, ne // 2):
            plane(kind, k).wait_send()

    for kind in range(4):
        spread(kind)

    def to_plane(rows, land, send, recv, group, k):
        peer = lax.rem(ex + k, ne)
        return remote(
            rows.at[group, pl.ds(pl.multiple_of(peer * cap_pad, 16), cap_pad)], land.at[group, ex],
            send.at[group, k], recv.at[group, k], (dp, peer),
        )

    def kept(rows, land, group, sem):
        return pltpu.make_async_copy(
            rows.at[group, pl.ds(pl.multiple_of(ex * cap_pad, 16), cap_pad)], land.at[group, ex], sem.at[group, 0]
        )

    def dispatch(group, tokens, rows, land, send, recv, weigh):
        meta = meta_all[group]
        slot_ids = lax.broadcasted_iota(jnp.int32, (slots_n, block), 0).astype(F32)
        hit_a, hit_b = slot_ids == meta[0:1, :], slot_ids == meta[1:2, :]
        chosen = jnp.where(hit_a | hit_b, 1.0, 0.0).astype(BF16)
        found = mm(chosen, tokens)
        if weigh:
            share = meta[2:3, :]
            factor = jnp.sum(
                jnp.where(hit_a, share, 0.0) + jnp.where(hit_b, 1.0 - share, 0.0), axis=1, keepdims=True
            )
            found = found * factor
        rows[group] = found.astype(BF16)
        for k in range(1, ne):
            to_plane(rows, land, send, recv, group, k).start()
        kept(rows, land, group, send).start()

    def send_cot(group, tokens):
        dispatch(group, tokens, cot_rows, d_outs, pc_send, pc_recv, True)

    def send_two(group, tokens):
        dispatch(group, tokens, two_rows, slots, pt_send, pt_recv, False)

    loads.wait(1)
    send_cot(dp, cot[...])

    def weights(d):
        t = lax.rem(dp + d, n)
        return remote(packed.at[t], wgu.at[dp], w_send.at[d], w_recv.at[d], (t, ex))

    keep_w = pltpu.make_async_copy(packed.at[dp], wgu.at[dp], own_sem.at[5])

    def hop(line_chain, h, then):
        for side in range(2):
            @pl.when(line_chain.held(h, side))
            def _():
                then(line_chain.arrive(h, side))

    def x_hop(h):
        hop(chain, h, lambda at: None)

    def send_weights(early):
        for d in range(1, n):
            t = lax.rem(dp + d, n)
            inside = (t > 0) & (t < n - 1) & ((t == dp + 1) | (t + 1 == dp))

            @pl.when(inside if early else jnp.logical_not(inside))
            def _():
                weights(d).start()

    main = piece // 128 * 128
    step = min(wg.shape[0], 64)

    def pack(i):
        rows = pl.ds(pl.multiple_of(i * step, step), step)
        gate_w, up_w = wg[rows, :], wu[rows, :]
        for j in range(n):
            g = gate_w[:, j * piece : (j + 1) * piece]
            u = up_w[:, j * piece : (j + 1) * piece]
            packed[j, rows, :] = jnp.concatenate([g[:, :main], u[:, :main], g[:, main:], u[:, main:]], axis=1)

    loads.wait(2, 3)
    pl.loop(0, wg.shape[0] // step)(pack)
    x_hop(0)
    spread(4)
    for kind in range(4):
        pass_on(kind)
    if n > 2:
        x_hop(1)
    send_weights(True)
    for kind in range(4):
        settle(kind)
    stores.start(5, 6, 7)

    devices = n * ne
    shared = jnp.max(lext[...].astype(F32), axis=2).reshape(devices, own).astype(BF16)

    def laid_out(first_lane, count, total):
        lanes = lax.broadcasted_iota(jnp.int32, (own, total), 1)
        rows = lax.broadcasted_iota(jnp.int32, (own, total), 0)
        spreading = jnp.where(lax.rem(lanes, count) + first_lane == rows, 1.0, 0.0).astype(BF16)
        everywhere = mm(shared, spreading)
        owner = lax.broadcasted_iota(jnp.int32, (devices, total), 0)
        lane_owner = lax.broadcasted_iota(jnp.int32, (devices, total), 1) // count
        return jnp.sum(jnp.where(owner == lane_owner, everywhere, 0.0), axis=0, keepdims=True)

    gain_one = laid_out(0, n_gain, width)
    gain_two = laid_out(n_gain, n_gain, width)
    gains[...] = jnp.concatenate([gain_one, gain_two, jnp.zeros((6, width), F32)], axis=0)
    entries = HEADS * BUCKETS
    flat = laid_out(2 * n_gain, n_bias, entries)
    lanes = lax.broadcasted_iota(jnp.int32, (8, entries), 1)
    head_of = lax.broadcasted_iota(jnp.int32, (8, entries), 0) + dp * (HEADS // n)
    by_head = jnp.where(lax.rem(lanes, HEADS) == head_of, jnp.broadcast_to(flat, (8, entries)), 0.0).astype(BF16)
    bucket_rows = lax.broadcasted_iota(jnp.int32, (entries, 128), 0) // HEADS
    to_bucket = jnp.where(
        bucket_rows == lax.broadcasted_iota(jnp.int32, (entries, 128), 1), 1.0, 0.0
    ).astype(BF16)
    table = mm(by_head, to_bucket).astype(BF16)
    wide = vectors.shape[1]
    vectors[...] = mm(table, bucket_hot(wide, 0, wide // 2), NT)

    def project(j):
        at = pl.ds(pl.multiple_of(j * block, block), block)
        xf = x_all[j].astype(F32)
        inverse = lax.rsqrt(jnp.mean(xf * xf, axis=-1, keepdims=True) + EPSILON)
        low = (xf * inverse * gains[0:1, :]).astype(BF16)
        normed[at, :] = low
        for w, ref in enumerate((lq, lk, lv)):
            qkv[at, w * own : (w + 1) * own] = mm(low, rows_flat(ref)).astype(BF16)

    project(dp)

    def project_hop(h):
        @pl.loop(0, 2)
        def _(side):
            @pl.when(((side == 0) & (dp > h)) | ((side == 1) & (dp + 1 + h < n)))
            def _():
                project(chain.block(h + 1, side))

    for h in range(n - 2):
        project_hop(h)
    pass_on(4)
    x_hop(n - 2)
    cots.start()
    keep_w.start()
    project_hop(n - 2)
    stores.start(0, 1)

    def attend(pair):
        for side in range(2):
            bias_tile(vectors, 2 * pair + side, tiles.at[side])
        lane = lax.broadcasted_iota(jnp.int32, (block, 128), 1)
        low_half = lane < HEAD_DIM
        k_pair = qkv[:, own + pair * 128 : own + (pair + 1) * 128]
        v_pair = qkv[:, 2 * own + pair * 128 : 2 * own + (pair + 1) * 128]

        @pl.loop(0, n)
        def _(i):
            at = pl.ds(pl.multiple_of(i * block, block), block)
            q_pair = qkv[at, pair * 128 : (pair + 1) * 128]
            outs, logs = [], []
            for side in range(2):
                mask = low_half if side == 0 else jnp.logical_not(low_half)
                logits = logits_of(n, block, i, q_pair, k_pair, mask, tiles.at[side])
                row_max = jnp.max(logits, axis=-1, keepdims=True)
                exponent = jnp.exp(logits - row_max)
                total = jnp.sum(exponent, axis=-1, keepdims=True)
                probs_low = (exponent * (1.0 / total)).astype(BF16)
                outs.append(mm(probs_low, v_pair))
                logs.append(jnp.broadcast_to(row_max + jnp.log(total), (block, 128)))
            heads[at, pair * 128 : (pair + 1) * 128] = jnp.where(low_half, outs[0], outs[1]).astype(BF16)
            lse[at, pair * 128 : (pair + 1) * 128] = jnp.where(low_half, logs[0], logs[1])

    def cot_hop(h):
        hop(cots, h, lambda group: send_cot(group, cot_all[group]))

    for d in range(1, n):
        line(5, d).wait_recv()
    def give(d):
        t = lax.rem(dp + d, n)
        return remote(
            heads.at[pl.ds(pl.multiple_of(t * block, block), block)], mixed_in.at[dp], m_send.at[d], m_recv.at[d],
            (t, ex),
        )

    for pair in range(pairs_n):
        attend(pair)
        if pair == pairs_n - 1:
            for d in range(1, n):
                give(d).start()
        if pair < n - 1:
            cot_hop(pair)
    mixed_in[dp] = heads[pl.ds(pl.multiple_of(dp * block, block), block), :]
    settle(4)
    stores.start(8, 2)
    for d in range(1, n):
        give(d).wait()
    mixed[...] = jnp.concatenate([mixed_in[j] for j in range(n)], axis=1)
    total = x[...].astype(F32) + mm(mixed[...], rows_flat(lwo))
    resid[...] = total
    inverse = lax.rsqrt(jnp.mean(total * total, axis=-1, keepdims=True) + EPSILON)
    two_own[...] = (total * inverse * gains[1:2, :]).astype(BF16)
    twos.start()
    stores.start(3, 4)

    send_two(dp, two_own[...])
    for h in range(pairs_n, n - 1):
        cot_hop(h)
    for h in range(n - 1):
        hop(twos, h, lambda group: send_two(group, two_all[group]))
    send_weights(False)
    stores.wait(*range(9))
    chain.finish()
    cots.finish()
    twos.finish()
    for d in range(1, n):
        for kind in range(6):
            line(kind, d).wait_send()
    keep_w.wait()
    for d in range(1, n):
        weights(d).wait()
    for rows, land, send, recv in (
        (two_rows, slots, pt_send, pt_recv), (cot_rows, d_outs, pc_send, pc_recv),
    ):
        @pl.loop(0, n)
        def _(group):
            kept(rows, land, group, send).wait()
            for k in range(1, ne):
                to_plane(rows, land, send, recv, group, k).wait()


def front(n, ne, cap, cap_pad, x, wq, wk, wv, wo, gain_attn, gain_moe, position_bias, meta_in, wg, wu, cot):
    tok, width = x.shape
    wrows = wq.shape[0]
    own = width // n
    piece = wg.shape[1] // n
    wide = 2 * n * tok
    slots_n = ne * cap_pad
    sem = pltpu.SemaphoreType.DMA
    shape = jax.ShapeDtypeStruct
    return pl.pallas_call(
        functools.partial(front_kernel, n, ne, cap, cap_pad, piece),
        in_specs=[ANY] + [VM] * 8 + [ANY] * 3,
        out_specs=[ANY] * 9 + [VM] * 3 + [ANY] * 3,
        out_shape=[
            shape((n * tok, width), BF16),
            shape((n * tok, 3 * own), BF16),
            shape((n * tok, own), F32),
            shape((tok, width), BF16),
            shape((tok, width), F32),
            shape((n, ne, wrows, own), BF16),
            shape((n, ne, wrows, own), BF16),
            shape((n, ne, wrows, own), BF16),
            shape((n, ne, wrows, width), BF16),
            shape((n, 8, tok), F32),
            shape((8, wide), F32),
            shape((8, width), F32),
            shape((n, ne, cap_pad, width), BF16),
            shape((n, ne, cap_pad, width), BF16),
            shape((n, tok, 2 * piece), BF16),
        ],
        scratch_shapes=[
            pltpu.VMEM((tok, width), BF16),
            pltpu.VMEM(wg.shape, BF16),
            pltpu.VMEM(wu.shape, BF16),
            pltpu.VMEM((tok, width), BF16),
            pltpu.VMEM((n * tok, width), BF16),
            pltpu.VMEM((n * tok, 3 * own), BF16),
            pltpu.VMEM((n * tok, own), F32),
            pltpu.VMEM((tok, width), BF16),
            pltpu.VMEM((tok, width), F32),
            pltpu.VMEM((n, ne, wrows, own), BF16),
            pltpu.VMEM((n, ne, wrows, own), BF16),
            pltpu.VMEM((n, ne, wrows, own), BF16),
            pltpu.VMEM((n, ne, wrows, width), BF16),
            pltpu.VMEM((16, own), BF16),
            pltpu.VMEM((n, wrows, own), BF16),
            pltpu.VMEM((n, wrows, own), BF16),
            pltpu.VMEM((n, wrows, own), BF16),
            pltpu.VMEM((n, 16, own), BF16),
            pltpu.VMEM((n, wrows, width), BF16),
            pltpu.VMEM((8, tok), F32),
            pltpu.VMEM((n, ne, 16, own), BF16),
            pltpu.VMEM((n, tok, 2 * piece), BF16),
            pltpu.VMEM((n, tok, width), BF16),
            pltpu.VMEM((n * tok, own), BF16),
            pltpu.VMEM((n, tok, own), BF16),
            pltpu.VMEM((2, tok, wide), F32),
            pltpu.VMEM((n, tok, width), BF16),
            pltpu.VMEM((n, tok, width), BF16),
            pltpu.VMEM((tok, width), BF16),
            pltpu.VMEM((n, slots_n, width), BF16),
            pltpu.VMEM((n, slots_n, width), BF16),
            sem((6, n)), sem((6, n)),
            sem((5, ne // 2)), sem((5, ne // 2)), sem((5, ne // 2)), sem((5, ne // 2)),
            sem((n, 2)), sem((n, 2)), sem((6,)),
            sem((n,)), sem((n,)), sem((n,)), sem((n,)),
            sem((n, 2)), sem((n, 2)), sem((n, 2)), sem((n, 2)),
            sem((n, ne)), sem((n, ne)), sem((n, ne)), sem((n, ne)), sem((4,)), sem((9,)),
        ],
        compiler_params=pltpu.CompilerParams(
            collective_id=1, has_side_effects=True, vmem_limit_bytes=60 * 1024 * 1024
        ),
        name="front",
    )(x, wq, wk, wv, wo, gain_attn, gain_moe, position_bias, meta_in, wg, wu, cot)


def experts_kernel(
    n, ne, cap_pad, deep, main,
    slots, d_outs, wgu_in, wd_in, meta_all,
    out_rows, d_two, gwgu_out, gwd_out,
    wgu_ref, gwgu, gwd, wd_ref, s_buf, d_buf, back, part, landed, gwgu_acc,
    load_sem, keep_sem, p_send, p_recv, z_send, z_recv, wd_sem,
):
    dp, ex = lax.axis_index("dp"), lax.axis_index("expert")
    slots_n, width = s_buf.shape[1:]
    tok = d_two.shape[0]
    greet(n, ne, dp, ex)
    toward = 2 * ((2 * dp) // n) - 1

    def group_at(step):
        return lax.rem(dp + n + toward * (1 + step), n)

    def load(step, kind):
        at = group_at(step)
        src, dst = ((slots, s_buf), (d_outs, d_buf))[kind]
        return pltpu.make_async_copy(src.at[at], dst.at[at], load_sem.at[kind, step])

    whole = Copies(
        wd_sem,
        [(wgu_in, wgu_ref), (wd_in, wd_ref.at[pl.ds(0, deep)]), (gwgu, gwgu_out), (gwd, gwd_out)],
    )
    whole.start(0, 1)
    for step in range(n):
        for kind in range(2):
            load(step, kind).start()
    wd_ref[deep:, :] = jnp.zeros((wd_ref.shape[0] - deep, width), BF16)
    gwgu_acc[...] = jnp.zeros_like(gwgu_acc)
    gwd[...] = jnp.zeros_like(gwd)
    whole.wait(0, 1)
    meet(n, ne)

    def rows_of(peer):
        return pl.ds(pl.multiple_of(peer * cap_pad, 16), cap_pad)

    def give(at, k):
        peer = lax.rem(ex + k, ne)
        return remote(
            d_buf.at[at, rows_of(peer)], back.at[at, rows_of(ex)], p_send.at[at, k], p_recv.at[at, k], (dp, peer)
        )

    def take(at, k):
        peer = lax.rem(ex + ne - k, ne)
        return remote(
            d_buf.at[at, rows_of(ex)], back.at[at, rows_of(peer)], p_send.at[at, k], p_recv.at[at, k], (dp, peer)
        )

    def keep(at):
        return pltpu.make_async_copy(s_buf.at[at], out_rows.at[at], keep_sem.at[at])

    def owed(at):
        return remote(part.at[at], landed.at[dp], z_send.at[at], z_recv.at[dp], (at, ex))

    def combine(at):
        for k in range(1, ne):
            take(at, k).wait_recv()
        meta = meta_all[at]
        ids = lax.broadcasted_iota(jnp.int32, (slots_n, tok), 0).astype(F32)
        hit = (ids == meta[0:1, :]) | (ids == meta[1:2, :])
        return mm(jnp.where(hit, 1.0, 0.0).astype(BF16), back[at], TN)

    @pl.loop(0, n)
    def _(step):
        at = group_at(step)
        for kind in range(2):
            load(step, kind).wait()
        wgu, wd = wgu_ref[...], wd_ref[...]
        parts = -(-slots_n // 640)
        size = slots_n // parts
        low_lane = lax.broadcasted_iota(jnp.int32, (size, 128), 1) < 64
        for p in range(parts):
            here = slice(p * size, (p + 1) * size)
            rows, d_out = s_buf[at, here, :], d_buf[at, here, :]
            pre = mm(rows, wgu)
            d_hidden = mm(d_out, wd, NT)
            gate, up, tail = pre[:, :main], pre[:, main : 2 * main], pre[:, 2 * main :]
            tail_up = pltpu.roll(tail, 64, 1)
            act, slope = gelu_pair(gate)
            act_t, slope_t = gelu_pair(tail)
            hidden_t = jnp.where(low_lane, act_t * tail_up, 0.0)
            hidden = jnp.concatenate([(act * up).astype(BF16), hidden_t.astype(BF16)], axis=1)
            dh, dh_t = d_hidden[:, :main], d_hidden[:, main:]
            d_gate = dh * up * slope
            d_up = dh * act
            d_tail = jnp.where(low_lane, dh_t * tail_up * slope_t, pltpu.roll(dh_t * act_t, 64, 1))
            d_pre = jnp.concatenate([d_gate.astype(BF16), d_up.astype(BF16), d_tail.astype(BF16)], axis=1)
            d_rows = mm(d_pre, wgu, NT).astype(BF16)
            gwd[...] += mm(hidden, d_out, TN)[:deep]
            d_buf[at, here, :] = d_rows
            if p == parts - 1:
                for k in range(1, ne):
                    give(at, k).start()
                back[at, rows_of(ex), :] = d_buf[at, rows_of(ex), :]
            gwgu_acc[...] += mm(rows, d_pre, TN)
            s_buf[at, here, :] = mm(hidden, wd).astype(BF16)
        keep(at).start()

        @pl.when(step > 0)
        def _():
            past = group_at(step - 1)
            part[past] = combine(past).astype(BF16)
            owed(past).start()

    gwgu[...] = gwgu_acc[...].astype(BF16)
    whole.start(2, 3)
    total = combine(dp)
    for d in range(1, n):
        src = lax.rem(dp + d, n)
        remote(part.at[src], landed.at[src], z_send.at[src], z_recv.at[src], (src, ex)).wait_recv()
        total = total + landed[src].astype(F32)
    d_two[...] = total
    whole.wait(2, 3)
    for d in range(1, n):
        owed(lax.rem(dp + d, n)).wait_send()

    @pl.loop(0, n)
    def _(at):
        keep(at).wait()
        for k in range(1, ne):
            give(at, k).wait_send()


def experts(n, ne, cap_pad, deep, slots, d_outs, wgu, wd, meta_all):
    width, columns = wgu.shape
    tok = meta_all.shape[2]
    main = (columns - 128) // 2
    slots_n = ne * cap_pad
    slots = slots.reshape(n, slots_n, width)
    d_outs = d_outs.reshape(n, slots_n, width)
    sem = pltpu.SemaphoreType.DMA
    return pl.pallas_call(
        functools.partial(experts_kernel, n, ne, cap_pad, deep, main),
        in_specs=[ANY, ANY, ANY, ANY, VM],
        out_specs=[ANY, VM, ANY, ANY],
        out_shape=[
            jax.ShapeDtypeStruct((n, slots_n, width), BF16),
            jax.ShapeDtypeStruct((tok, width), F32),
            jax.ShapeDtypeStruct((width, columns), BF16),
            jax.ShapeDtypeStruct((deep, width), F32),
        ],
        scratch_shapes=[
            pltpu.VMEM((width, columns), BF16),
            pltpu.VMEM((width, columns), BF16),
            pltpu.VMEM((deep, width), F32),
            pltpu.VMEM((-(-deep // 128) * 128, width), BF16),
            pltpu.VMEM((n, slots_n, width), BF16),
            pltpu.VMEM((n, slots_n, width), BF16),
            pltpu.VMEM((n, slots_n, width), BF16),
            pltpu.VMEM((n, tok, width), BF16),
            pltpu.VMEM((n, tok, width), BF16),
            pltpu.VMEM((width, columns), F32),
            sem((2, n)), sem((n,)), sem((n, ne)), sem((n, ne)), sem((n,)), sem((n,)), sem((4,)),
        ],
        compiler_params=pltpu.CompilerParams(
            collective_id=3, has_side_effects=True, vmem_limit_bytes=60 * 1024 * 1024
        ),
        name="experts",
    )(slots, d_outs, wgu, wd, meta_all)


def backward_kernel(
    n, ne, cap_pad,
    gains, vectors, meta_all,
    d_two_in, resid_in, cot_in, wo_in, x_in, mixed_in, qkv_in, lse_in, normed_in, wq_in, wk_in, wv_in,
    gwgu, out_rows,
    block_out, grad_in, g_all, small_all, gw_in, out_in,
    d_two, resid, cot, wo, x, mixed, qkv, lse, normed, wq, wk, wv,
    dm, dm_in, tiles, sums, dq_s, dk_s, dv_s, dk_acc, dv_acc, diag, d_res,
    dn_part, dn_land, moe_part, moe_land, out_one,
    g_send, g_land, g2_send, g2_land, o_send, o_land, o2_send, o2_land,
    small_own, small_land, small_sum,
    out_s, out_r, w_s, w_r, dm_s, dm_r, dn_s, dn_r, moe_s, moe_r, g_s, g_r, o_s, o_r, g2_s, g2_r, o2_s, o2_r,
    sp_s, sp_r, sz_s, sz_r, keep_sem, in_sem,
):
    dp, ex = lax.axis_index("dp"), lax.axis_index("expert")
    tok, width = cot.shape
    own = dq_s.shape[1]
    pairs_n = own // 128
    slots_n = ne * cap_pad
    wrows = g_all.shape[1]
    greet(n, ne, dp, ex)
    loads = Copies(
        in_sem,
        [
            (d_two_in, d_two), (resid_in, resid), (cot_in, cot), (wo_in, wo), (x_in, x), (mixed_in, mixed),
            (qkv_in, qkv), (lse_in, lse), (normed_in, normed), (wq_in, wq), (wk_in, wk), (wv_in, wv),
        ],
    )
    loads.start(0, 1, 2, 3, 5, 6, 7, 9, 10, 11, 8, 4)
    toward = 2 * ((2 * dp) // n) - 1

    def group_at(step):
        return lax.rem(dp + n + toward * (1 + step), n)

    def rows_of(peer):
        return pl.ds(pl.multiple_of(peer * cap_pad, 16), cap_pad)

    def to_line(src, dst, send, recv, t):
        return remote(src.at[t], dst.at[dp], send.at[t], recv.at[dp], (t, ex))

    def from_line(src, dst, send, recv, t):
        return remote(src.at[t], dst.at[t], send.at[t], recv.at[t], (t, ex))

    def to_plane(src, dst, send, recv, k):
        return remote(src, dst.at[ex], send.at[k], recv.at[k], (dp, lax.rem(ex + k, ne)))

    def from_plane(src, dst, send, recv, k):
        peer = lax.rem(ex + ne - k, ne)
        return remote(src, dst.at[peer], send.at[k], recv.at[k], (dp, peer))

    def out_give(at, k):
        peer = lax.rem(ex + k, ne)
        return remote(
            out_rows.at[at, rows_of(peer)], out_in.at[at, rows_of(ex)], out_s.at[at, k], out_r.at[at, k], (dp, peer)
        )

    def out_take(at, k):
        peer = lax.rem(ex + ne - k, ne)
        return remote(
            out_rows.at[at, rows_of(ex)], out_in.at[at, rows_of(peer)], out_s.at[at, k], out_r.at[at, k], (dp, peer)
        )

    def out_keep(at):
        return pltpu.make_async_copy(out_rows.at[at, rows_of(ex)], out_in.at[at, rows_of(ex)], out_s.at[at, 0])

    loads.wait(0, 1, 2)
    values = resid[...]
    d_normed = d_two[...]
    inverse = lax.rsqrt(jnp.mean(values * values, axis=-1, keepdims=True) + EPSILON)
    scaled = gains[1:2, :] * d_normed
    gain_rows_two = jnp.sum(d_normed * values * inverse, axis=0, keepdims=True)
    mean = jnp.mean(scaled * values, axis=-1, keepdims=True)
    d_resid = cot[...].astype(F32) + inverse * scaled - values * (inverse * inverse * inverse * mean)
    d_res[...] = d_resid
    d_attn = d_resid.astype(BF16)
    loads.wait(3)
    d_mixed = mm(d_attn, wo[...], NT).astype(BF16)
    meet(n, ne)
    for j in range(n):
        dm[j] = d_mixed[:, j * own : (j + 1) * own]
    for d in range(1, n):
        to_line(dm, dm_in, dm_s, dm_r, lax.rem(dp + d, n)).start()
    dm_in[dp] = dm[dp]
    for d in range(1, n):
        to_line(gwgu, gw_in, w_s, w_r, lax.rem(dp + d, n)).start()
    keep_w = pltpu.make_async_copy(gwgu.at[dp], gw_in.at[dp], keep_sem.at[0])
    keep_w.start()

    @pl.loop(0, n)
    def _(step):
        at = group_at(step)
        for k in range(1, ne):
            out_give(at, k).start()
        out_keep(at).start()

    loads.wait(5)
    o_send[...] = mm(mixed[...], d_attn, TN).reshape(n, ne, wrows, width).astype(BF16)
    for k in range(1, ne):
        to_plane(o_send.at[:, lax.rem(ex + k, ne)], o_land, o_s, o_r, k).start()
    o_land[ex] = o_send[:, ex]
    for i in range(width // 128):
        small_own[8 + i : 9 + i, :] = gain_rows_two[:, i * 128 : (i + 1) * 128]
    for d in range(1, n):
        from_line(dm, dm_in, dm_s, dm_r, lax.rem(dp + d, n)).wait_recv()

    loads.wait(6, 7, 9, 10, 11)
    lane = lax.broadcasted_iota(jnp.int32, (tok, 128), 1)
    low_half = lane < HEAD_DIM
    key_low = lax.broadcasted_iota(jnp.int32, (n * tok, 128), 1) < HEAD_DIM
    diag[...] = jnp.zeros_like(diag)
    for pair in range(pairs_n):
        cols = slice(pair * 128, (pair + 1) * 128)
        for side in range(2):
            bias_tile(vectors, 2 * pair + side, tiles.at[side])
        sums[...] = jnp.zeros_like(sums)
        dk_acc[...] = jnp.zeros_like(dk_acc)
        dv_acc[...] = jnp.zeros_like(dv_acc)
        k_pair = qkv[:, own + pair * 128 : own + (pair + 1) * 128]
        v_pair = qkv[:, 2 * own + pair * 128 : 2 * own + (pair + 1) * 128]

        @pl.loop(0, n)
        def _(i):
            at = pl.ds(pl.multiple_of(i * tok, tok), tok)
            q_pair = qkv[at, cols]
            dm_pair = dm_in[i, :, cols]
            dqs, dks, dvs = [], [], []
            for side in range(2):
                mask = low_half if side == 0 else jnp.logical_not(low_half)
                logits = logits_of(n, tok, i, q_pair, k_pair, mask, tiles.at[side])
                first = pair * 128 + side * HEAD_DIM
                probs = jnp.exp(logits - lse[at, first : first + 1])
                d_probs = mm(jnp.where(mask, dm_pair, jnp.zeros_like(dm_pair)), v_pair, NT)
                inner = jnp.sum(probs * d_probs, axis=-1, keepdims=True)
                d_logits = (probs * (d_probs - inner)).astype(BF16)
                dvs.append(mm(probs.astype(BF16), dm_pair, TN))
                dqs.append(mm(d_logits, k_pair))
                dks.append(mm(d_logits, q_pair, TN))
                wide = d_logits.astype(F32)
                for j in range(n):
                    here = pl.ds(tile_offset(n, tok, i, j), tok)
                    sums[side, :, here] += wide[:, j * tok : (j + 1) * tok]
            dq_s[at, cols] = (jnp.where(low_half, dqs[0], dqs[1]) * SCALE).astype(BF16)
            dk_acc[...] += jnp.where(key_low, dks[0], dks[1])
            dv_acc[...] += jnp.where(key_low, dvs[0], dvs[1])

        dk_s[:, cols] = (dk_acc[...] * SCALE).astype(BF16)
        dv_s[:, cols] = dv_acc[...].astype(BF16)
        for side in range(2):
            diag[2 * pair + side : 2 * pair + side + 1, :] = diagonal_sum(sums[side])

    def d_norm(t):
        at = pl.ds(pl.multiple_of(t * tok, tok), tok)
        return mm(dq_s[at, :], wq[...], NT) + mm(dk_s[at, :], wk[...], NT) + mm(dv_s[at, :], wv[...], NT)

    def sum_copy(part, land, send, recv, r, side):
        t = lax.rem(dp + n + (n - r) * (1 - 2 * side), n)
        target = lax.rem(dp + n + 1 - 2 * side, n)
        return t, remote(part.at[t], land.at[r - 1, side], send.at[r - 1, side], recv.at[r - 1, side], (target, ex))

    def takes_part(r, side):
        return ((side == 0) & (dp < r) & (dp + 1 < n)) | ((side == 1) & (dp + r >= n) & (dp > 0))

    def is_fed(r, side):
        return ((side == 0) & (dp > 0) & (r > 1)) | ((side == 1) & (dp + 1 < n) & (r > 1))

    def fed(part, land, send, recv, r, side):
        remote(
            part.at[dp], land.at[r - 1, side], send.at[r - 1, side], recv.at[r - 1, side], (dp, ex)
        ).wait_recv()

    def sum_round(part, land, send, recv, term, r):
        @pl.loop(0, 2)
        def _(side):
            @pl.when(takes_part(r, side))
            def _():
                t, copy = sum_copy(part, land, send, recv, r, side)
                mine = term(t)

                @pl.when(is_fed(r, side))
                def _():
                    fed(part, land, send, recv, r - 1, side)
                    part[t] = (mine + land[max(r - 2, 0), side].astype(F32)).astype(BF16)

                @pl.when(jnp.logical_not(is_fed(r, side)))
                def _():
                    part[t] = mine.astype(BF16)

                copy.start()

    def sum_end(part, land, send, recv, mine):
        @pl.when(dp > 0)
        def _():
            fed(part, land, send, recv, n - 1, 0)

        @pl.when(dp + 1 < n)
        def _():
            fed(part, land, send, recv, n - 1, 1)

        left = jnp.where(dp > 0, land[n - 2, 0].astype(F32), 0.0)
        right = jnp.where(dp + 1 < n, land[n - 2, 1].astype(F32), 0.0)
        return mine + left + right

    def sum_sent(part, land, send, recv):
        for r in range(1, n):
            for side in range(2):
                @pl.when(takes_part(r, side))
                def _():
                    sum_copy(part, land, send, recv, r, side)[1].wait_send()

    dn = (dn_part, dn_land, dn_s, dn_r)
    moes = (moe_part, moe_land, moe_s, moe_r)
    sum_round(*dn, d_norm, 1)

    loads.wait(8, 4)
    for w, ref in enumerate((dq_s, dk_s, dv_s)):
        g_send[:, :, w] = mm(normed[...], ref[...], TN).reshape(n, ne, wrows, own).astype(BF16)
    for k in range(1, ne):
        to_plane(g_send.at[:, lax.rem(ex + k, ne)], g_land, g_s, g_r, k).start()
    g_land[ex] = g_send[:, ex]

    for r in range(2, n):
        sum_round(*dn, d_norm, r)

    rest = diag[...]
    table = jnp.zeros((8, 128), F32)
    wide = vectors.shape[1]
    hot = bucket_hot(wide, tok, wide // 2)
    for _ in range(3):
        piece = rest.astype(BF16)
        table = table + mm(piece, hot)
        rest = rest - piece.astype(F32)
    small_own[16:24, :] = table

    for k in range(1, ne):
        from_plane(o_send.at[:, ex], o_land, o_s, o_r, k).wait_recv()
    total = o_land[0].astype(F32)
    for e in range(1, ne):
        total = total + o_land[e].astype(F32)
    o2_send[...] = total.astype(BF16)
    for d in range(1, n):
        to_line(o2_send, o2_land, o2_s, o2_r, lax.rem(dp + d, n)).start()
    o2_land[dp] = o2_send[dp]

    def moe(at):
        for k in range(1, ne):
            out_take(at, k).wait_recv()
        out_keep(at).wait()
        load = pltpu.make_async_copy(out_in.at[at], out_one, keep_sem.at[1])
        load.start()
        meta = meta_all[at]
        ids = lax.broadcasted_iota(jnp.int32, (slots_n, tok), 0).astype(F32)
        gate = meta[2:3, :]
        weight = jnp.where(ids == meta[0:1, :], gate, 0.0) + jnp.where(ids == meta[1:2, :], 1.0 - gate, 0.0)
        load.wait()
        return mm(weight.astype(BF16), out_one[...], TN)

    for r in range(1, n):
        sum_round(*moes, moe, r)

    for k in range(1, ne):
        from_plane(g_send.at[:, ex], g_land, g_s, g_r, k).wait_recv()
    total = g_land[0].astype(F32)
    for e in range(1, ne):
        total = total + g_land[e].astype(F32)
    g2_send[...] = total.astype(BF16)
    for d in range(1, n):
        to_line(g2_send, g2_land, g2_s, g2_r, lax.rem(dp + d, n)).start()
    g2_land[dp] = g2_send[dp]

    total = sum_end(*dn, d_norm(dp))
    values = x[...].astype(F32)
    inverse = lax.rsqrt(jnp.mean(values * values, axis=-1, keepdims=True) + EPSILON)
    scaled = gains[0:1, :] * total
    gain_rows_one = jnp.sum(total * values * inverse, axis=0, keepdims=True)
    mean = jnp.mean(scaled * values, axis=-1, keepdims=True)
    grad_in[...] = (d_res[...] + inverse * scaled - values * (inverse * inverse * inverse * mean)).astype(BF16)
    for i in range(width // 128):
        small_own[i : i + 1, :] = gain_rows_one[:, i * 128 : (i + 1) * 128]
    for k in range(1, ne):
        to_plane(small_own, small_land, sp_s, sp_r, k).start()
    small_land[ex] = small_own[...]
    for k in range(1, ne):
        from_plane(small_own, small_land, sp_s, sp_r, k).wait_recv()
    total = small_land[0]
    for e in range(1, ne):
        total = total + small_land[e]
    small_sum[...] = total
    for d in range(1, n):
        t = lax.rem(dp + d, n)
        remote(small_sum, small_all.at[dp], sz_s.at[t], sz_r.at[dp], (t, ex)).start()
    small_all[dp] = total

    block_out[...] = sum_end(*moes, resid[...] + moe(dp)).astype(BF16)

    for d in range(1, n):
        t = lax.rem(dp + d, n)
        from_line(o2_send, o2_land, o2_s, o2_r, t).wait_recv()
        from_line(g2_send, g2_land, g2_s, g2_r, t).wait_recv()
        remote(small_sum, small_all.at[t], sz_s.at[t], sz_r.at[t], (t, ex)).wait_recv()
    total = o2_land[0].astype(F32)
    for j in range(1, n):
        total = total + o2_land[j].astype(F32)
    g_all[3] = total
    for w in range(3):
        g_all[w] = jnp.concatenate([g2_land[j, w] for j in range(n)], axis=1).astype(F32)
    for d in range(1, n):
        t = lax.rem(dp + d, n)
        from_line(gwgu, gw_in, w_s, w_r, t).wait_recv()
        for src, dst, send, recv in (
            (gwgu, gw_in, w_s, w_r), (dm, dm_in, dm_s, dm_r),
            (o2_send, o2_land, o2_s, o2_r), (g2_send, g2_land, g2_s, g2_r),
        ):
            to_line(src, dst, send, recv, t).wait_send()
        remote(small_sum, small_all.at[dp], sz_s.at[t], sz_r.at[dp], (t, ex)).wait_send()
    keep_w.wait()
    sum_sent(*dn)
    sum_sent(*moes)
    for k in range(1, ne):
        to_plane(o_send.at[:, ex], o_land, o_s, o_r, k).wait_send()
        to_plane(g_send.at[:, ex], g_land, g_s, g_r, k).wait_send()
        to_plane(small_own, small_land, sp_s, sp_r, k).wait_send()

    @pl.loop(0, n)
    def _(at):
        for k in range(1, ne):
            out_give(at, k).wait_send()


def backward(
    n, ne, cap_pad, wrows, d_two, resid, cot, x, gains, mixed, wo, qkv, lse, normed, vectors,
    wq, wk, wv, meta_all, gwgu, out_rows,
):
    tok, width = cot.shape
    own = wq.shape[1]
    wide = vectors.shape[1]
    both = gwgu.shape[2]
    slots_n = ne * cap_pad
    length = n * tok
    sem = pltpu.SemaphoreType.DMA
    shape = jax.ShapeDtypeStruct
    return pl.pallas_call(
        functools.partial(backward_kernel, n, ne, cap_pad),
        in_specs=[VM] * 3 + [ANY] * 14,
        out_specs=[VM] * 4 + [ANY] * 2,
        out_shape=[
            shape((tok, width), BF16),
            shape((tok, width), BF16),
            shape((4, wrows, width), F32),
            shape((n, 24, 128), F32),
            shape((n, tok, both), BF16),
            shape((n, slots_n, width), BF16),
        ],
        scratch_shapes=[
            pltpu.VMEM((tok, width), F32),
            pltpu.VMEM((tok, width), F32),
            pltpu.VMEM((tok, width), BF16),
            pltpu.VMEM((width, width), BF16),
            pltpu.VMEM((tok, width), BF16),
            pltpu.VMEM((tok, width), BF16),
            pltpu.VMEM((length, 3 * own), BF16),
            pltpu.VMEM((length, own), F32),
            pltpu.VMEM((length, width), BF16),
            pltpu.VMEM((width, own), BF16),
            pltpu.VMEM((width, own), BF16),
            pltpu.VMEM((width, own), BF16),
            pltpu.VMEM((n, tok, own), BF16),
            pltpu.VMEM((n, tok, own), BF16),
            pltpu.VMEM((2, tok, wide), F32),
            pltpu.VMEM((2, tok, wide), F32),
            pltpu.VMEM((length, own), BF16),
            pltpu.VMEM((length, own), BF16),
            pltpu.VMEM((length, own), BF16),
            pltpu.VMEM((length, 128), F32),
            pltpu.VMEM((length, 128), F32),
            pltpu.VMEM((8, wide), F32),
            pltpu.VMEM((tok, width), F32),
            pltpu.VMEM((n, tok, width), BF16),
            pltpu.VMEM((n - 1, 2, tok, width), BF16),
            pltpu.VMEM((n, tok, width), BF16),
            pltpu.VMEM((n - 1, 2, tok, width), BF16),
            pltpu.VMEM((slots_n, width), BF16),
            pltpu.VMEM((n, ne, 3, wrows, own), BF16),
            pltpu.VMEM((ne, n, 3, wrows, own), BF16),
            pltpu.VMEM((n, 3, wrows, own), BF16),
            pltpu.VMEM((n, 3, wrows, own), BF16),
            pltpu.VMEM((n, ne, wrows, width), BF16),
            pltpu.VMEM((ne, n, wrows, width), BF16),
            pltpu.VMEM((n, wrows, width), BF16),
            pltpu.VMEM((n, wrows, width), BF16),
            pltpu.VMEM((24, 128), F32),
            pltpu.VMEM((ne, 24, 128), F32),
            pltpu.VMEM((24, 128), F32),
            sem((n, ne)), sem((n, ne)), sem((n,)), sem((n,)), sem((n,)), sem((n,)), sem((n, 2)), sem((n, 2)),
            sem((n, 2)), sem((n, 2)), sem((ne,)), sem((ne,)), sem((ne,)), sem((ne,)), sem((n,)), sem((n,)),
            sem((n,)), sem((n,)), sem((ne,)), sem((ne,)), sem((n,)), sem((n,)), sem((2,)), sem((12,)),
        ],
        compiler_params=pltpu.CompilerParams(
            collective_id=4, has_side_effects=True, vmem_limit_bytes=60 * 1024 * 1024
        ),
        name="backward",
    )(
        gains, vectors, meta_all, d_two, resid, cot, wo, x, mixed, qkv, lse, normed, wq, wk, wv, gwgu, out_rows
    )


def split_pieces(value):
    pieces = []
    for _ in range(3):
        piece = value.astype(BF16)
        pieces.append(piece)
        value = value - piece.astype(F32)
    return pieces


def finish_kernel(
    n, ne, heads_own, piece, blocks, g_all, small, out_in, grad_in, gwd_in,
    gate_ref, up_ref, gq, gk, gv, go, gain_one, gain_two, bias, block_out, grad_out, gwd,
):
    main = piece // 128 * 128
    rest = piece - main
    gates, ups = [], []
    for j in range(n):
        block = blocks[j].astype(F32)
        gates += [block[:, :main], block[:, 2 * main : 2 * main + rest]]
        ups += [block[:, main : 2 * main], block[:, 2 * main + rest :]]
    gate_ref[...] = jnp.concatenate(gates, axis=1)
    up_ref[...] = jnp.concatenate(ups, axis=1)
    block_out[...] = out_in[...]
    grad_out[...] = grad_in[...]
    gwd[...] = gwd_in[...]

    @pl.when(pl.program_id(0) == 0)
    def _():
        for i, ref in enumerate((gq, gk, gv, go)):
            ref[...] = g_all[i]
        me = lax.axis_index("dp") * ne + lax.axis_index("expert")
        total = small[0, :16]
        for j in range(1, n):
            total = total + small[j, :16]
        rows = lax.broadcasted_iota(jnp.int32, (8, 128), 0)
        lanes = lax.broadcasted_iota(jnp.int32, (8, 128), 1)
        for i, ref in enumerate((gain_one, gain_two)):
            count = ref.shape[1]
            at = me * count
            row = jnp.sum(jnp.where(rows == at // 128, total[8 * i : 8 * i + 8], 0.0), axis=0, keepdims=True)
            row = jnp.broadcast_to(row, (8, 128))
            ref[...] = pltpu.roll(row, lax.rem(128 - lax.rem(at, 128), 128), 1)[:1, :count]
        table = jnp.concatenate([small[j, 16 : 16 + heads_own] for j in range(n)], axis=0)
        heads = n * heads_own
        count = bias.shape[1]
        at = me * count
        table = jnp.concatenate([table, jnp.zeros((128 - heads, 128), F32)], axis=0)
        hot = jnp.where(lanes == at // heads, 1.0, 0.0).astype(BF16)
        row = sum(mm(hot, part, NT) for part in split_pieces(table))
        bias[...] = pltpu.roll(row, lax.rem(128 - lax.rem(at, heads), 128), 1)[:1, :count]


def finish(n, ne, heads_own, n_gain, n_bias, blocks, g_all, small, block_out, grad_in, gwd):
    tok, both = blocks.shape[1:]
    wrows, width = g_all.shape[1:]
    deep = gwd.shape[0]
    piece = both // 2
    steps = 4
    step, part = tok // steps, deep // steps
    total = n * piece
    shape = jax.ShapeDtypeStruct
    fixed2 = lambda i: (0, 0)
    fixed3 = lambda i: (0, 0, 0)
    move = lambda i: (i, 0)
    return pl.pallas_call(
        functools.partial(finish_kernel, n, ne, heads_own, piece),
        grid=(steps,),
        in_specs=[
            pl.BlockSpec((n, step, both), lambda i: (0, i, 0)),
            pl.BlockSpec((4, wrows, width), fixed3),
            pl.BlockSpec(small.shape, fixed3),
            pl.BlockSpec((step, width), move),
            pl.BlockSpec((step, width), move),
            pl.BlockSpec((part, width), move),
        ],
        out_specs=[pl.BlockSpec((step, total), move)] * 2
        + [pl.BlockSpec((wrows, width), fixed2)] * 4
        + [pl.BlockSpec((1, n_gain), fixed2)] * 2
        + [pl.BlockSpec((1, n_bias), fixed2)]
        + [pl.BlockSpec((step, width), move)] * 2
        + [pl.BlockSpec((part, width), move)],
        out_shape=[shape((tok, total), F32)] * 2
        + [shape((wrows, width), F32)] * 4
        + [shape((1, n_gain), F32)] * 2
        + [shape((1, n_bias), F32)]
        + [shape((tok, width), BF16)] * 2
        + [shape((deep, width), F32)],
        compiler_params=pltpu.CompilerParams(vmem_limit_bytes=VMEM_LIMIT),
        name="finish",
    )(blocks, g_all, small, block_out, grad_in, gwd)


def local(
    inputs, cotangent, gain_attn, w_query, w_key, w_value, w_out, position_bias,
    gain_moe, w_gate, w_up, w_down, routes, gate_fixed,
):
    n = lax.axis_size("dp")
    experts_n = lax.axis_size("expert")
    dp = lax.axis_index("dp")
    ex = lax.axis_index("expert")
    tok, width = inputs.shape[1:]
    length = n * tok
    own = HEADS * HEAD_DIM // n
    heads_own = HEADS // n
    wrows = w_query.shape[0]
    capacity = 5 * tok // (2 * experts_n)
    cap_pad = -(-capacity // 16) * 16
    slots_n = experts_n * cap_pad

    n_gain, n_bias = gain_attn.shape[0], position_bias.shape[0]
    meta_in = jnp.concatenate([routes[0].T, gate_fixed], axis=0)
    normed, qkv, lse, mixed, resid, wq, wk, wv, wo, meta_all, vectors, gains, slots, d_outs, wgu = front(
        n, experts_n, capacity, cap_pad, inputs[0], w_query, w_key, w_value, w_out,
        gain_attn.reshape(1, -1), gain_moe.reshape(1, -1), position_bias.reshape(1, -1),
        meta_in, w_gate[0], w_up[0], cotangent[0],
    )
    wq, wk, wv = (w.reshape(width, own) for w in (wq, wk, wv))
    wo = wo.reshape(width, width)
    wgu = wgu.reshape(width, -1)
    deep = w_down.shape[1]
    out_rows, grad_normed_two, gwgu, grad_w_down = experts(
        n, experts_n, cap_pad, deep, slots, d_outs, wgu, w_down[0], meta_all
    )

    block_out, grad_inputs, g_all, small, got, _ = backward(
        n, experts_n, cap_pad, wrows, grad_normed_two, resid, cotangent[0], inputs[0], gains, mixed, wo,
        qkv, lse, normed, vectors, wq, wk, wv, meta_all, gwgu.reshape(n, width // n, -1), out_rows,
    )
    (
        grad_w_gate, grad_w_up, gq, gk, gv, go, grad_gain_one, grad_gain_two, grad_bias, block_out, grad_inputs,
        grad_w_down,
    ) = finish(n, experts_n, heads_own, n_gain, n_bias, got, g_all, small, block_out, grad_inputs, grad_w_down)

    return (
        block_out[None],
        grad_inputs[None],
        grad_gain_one[0],
        gq,
        gk,
        gv,
        go,
        grad_bias[0],
        grad_gain_two[0],
        grad_w_gate[None],
        grad_w_up[None],
        grad_w_down[None],
    )


def solution(mesh):
    vector = P(("dp", "expert"))
    matrix = P(("dp", "expert"), None)
    split = P("expert", "dp", None)
    return jax.shard_map(
        local,
        mesh=mesh,
        in_specs=(
            split, split, vector, matrix, matrix, matrix, matrix, vector, vector,
            split, split, split, split, P("expert", "dp"),
        ),
        out_specs=(
            split, split, vector, matrix, matrix, matrix, matrix, vector, vector,
            split, split, split,
        ),
        check_vma=False,
    )
```

```python
import functools

import jax
import jax.numpy as jnp
from jax import lax
from jax.experimental import pallas as pl
from jax.experimental.pallas import tpu as pltpu
from jax.sharding import PartitionSpec as P

HEADS = 16
HEAD_DIM = 64
BUCKETS = 32
THRESHOLDS = (12, 16, 23, 32, 46, 64, 91)
EPSILON = 1e-06
SCALE = HEAD_DIM ** (-0.5)
BF16 = jnp.bfloat16
F32 = jnp.float32
GELU_C = 0.7978845608028654
GELU_A = 0.044715
VMEM_LIMIT = 56 * 1024 * 1024

NT = (((1,), (1,)), ((), ()))
TN = (((0,), (0,)), ((), ()))
NN = (((1,), (0,)), ((), ()))


def mm(a, b, dims=NN):
    return lax.dot_general(a, b, dims, preferred_element_type=F32)


def bucket_of(offset):
    distance = jnp.abs(offset)
    banded = jnp.full(distance.shape, 8, jnp.int32)
    for cutoff in THRESHOLDS:
        banded = banded + (distance >= cutoff).astype(jnp.int32)
    nearby = jnp.where(distance < 8, distance, banded)
    return nearby + jnp.where(offset > 0, 16, 0).astype(jnp.int32)


def bias_tile(vec_ref, head, tile_ref):
    block, wide = tile_ref.shape
    row = jnp.broadcast_to(vec_ref[pl.ds(head, 1), :], (block, wide))
    tile_ref[...] = pltpu.roll(row, wide - block, 1, stride=1, stride_axis=0)


def tile_offset(n, block, query_block, key_block):
    return pl.multiple_of((key_block - query_block + n - 1) * block, 128)


def logits_of(n, block, query_block, q_pair, k_pair, mask, tile_ref):
    masked = jnp.where(mask, q_pair, jnp.zeros_like(q_pair))
    raw = mm(masked, k_pair, NT) * SCALE
    bias = jnp.concatenate(
        [tile_ref[:, pl.ds(tile_offset(n, block, query_block, j), block)] for j in range(n)], axis=1
    )
    return raw + bias


def diagonal_sum(tile):
    rows, wide = tile.shape
    while rows > 1:
        half = rows // 2
        tile = tile[:half] + pltpu.roll(tile[half:], wide - half, 1)
        rows = half
    return tile


def gelu_pair(v):
    square = v * v
    t = jnp.tanh(GELU_C * (v + GELU_A * v * square))
    half = 0.5 * (1.0 + t)
    slope = half + (0.5 * GELU_C) * v * (1.0 - t * t) * (1.0 + (3.0 * GELU_A) * square)
    return v * half, slope


MESH = pl.DeviceIdType.MESH


def remote(src, dst, send, recv, target):
    return pltpu.make_async_remote_copy(
        src_ref=src, dst_ref=dst, send_sem=send, recv_sem=recv, device_id=target, device_id_type=MESH
    )


def greet(n, ne, dp, ex):
    barrier = pltpu.get_barrier_semaphore()
    for d in range(1, n):
        pl.semaphore_signal(barrier, inc=1, device_id=(lax.rem(dp + d, n), ex), device_id_type=MESH)
    for k in range(1, ne):
        pl.semaphore_signal(barrier, inc=1, device_id=(dp, lax.rem(ex + k, ne)), device_id_type=MESH)


def meet(n, ne):
    pl.semaphore_wait(pltpu.get_barrier_semaphore(), n + ne - 2)


class Copies:
    def __init__(self, sem, pairs):
        self.copies = [pltpu.make_async_copy(src, dst, sem.at[i]) for i, (src, dst) in enumerate(pairs)]

    def start(self, *which):
        for i in which:
            self.copies[i].start()

    def wait(self, *which):
        for i in which:
            self.copies[i].wait()


class Chain:
    def __init__(self, n, dp, ex, own, buffer, send, recv):
        self.n, self.dp, self.ex, self.own = n, dp, ex, own
        self.buffer, self.send_sem, self.recv_sem = buffer, send, recv

    def block(self, hop, side):
        return lax.rem(self.dp + self.n + hop * (2 * side - 1), self.n)

    def copy(self, hop, side, first=False):
        at = self.block(hop, side)
        target = lax.rem(self.dp + self.n + 1 - 2 * side, self.n)
        return remote(
            self.own if first else self.buffer.at[at], self.buffer.at[at],
            self.send_sem.at[hop, side], self.recv_sem.at[hop, side], (target, self.ex),
        )

    def has_next(self, side):
        return (self.dp + 1 < self.n) if side == 0 else (self.dp > 0)

    def start(self):
        for side in range(2):
            @pl.when(self.has_next(side))
            def _():
                self.copy(0, side, True).start()

    def held(self, hop, side):
        return (self.dp > hop) if side == 0 else (self.dp + 1 + hop < self.n)

    def arrive(self, hop, side):
        at = self.block(hop + 1, side)
        remote(
            self.buffer.at[at], self.buffer.at[at], self.send_sem.at[hop, side], self.recv_sem.at[hop, side],
            (self.dp, self.ex),
        ).wait_recv()

        @pl.when(self.has_next(side))
        def _():
            self.copy(hop + 1, side).start()

        return at

    def finish(self):
        for hop in range(self.n - 1):
            for side in range(2):
                mine = self.has_next(side)
                if hop:
                    mine = mine & self.held(hop - 1, side)

                @pl.when(mine)
                def _():
                    self.copy(hop, side, hop == 0).wait_send()


ANY = pl.BlockSpec(memory_space=pl.ANY)
VM = pl.BlockSpec(memory_space=pltpu.VMEM)


def bucket_hot(wide, turn, length):
    at = lax.broadcasted_iota(jnp.int32, (wide, 128), 0) + turn
    offset = jnp.where(at >= wide, at - wide, at) - length
    hit = bucket_of(offset) == lax.broadcasted_iota(jnp.int32, (wide, 128), 1)
    return jnp.where(hit & (jnp.abs(offset) < length), 1.0, 0.0).astype(BF16)


def rows_flat(ref):
    n, ne, rows, columns = ref.shape
    if rows % 16 == 0:
        return ref[...].reshape(n * ne * rows, columns)
    return ref[...].astype(F32).reshape(n * ne * rows, columns).astype(BF16)


def front_kernel(
    n, ne, cap, cap_pad, piece,
    x_in, wq, wk, wv, wo, gain_attn, gain_moe, position_bias, meta_in, wg_in, wu_in, cot_in,
    normed_out, qkv_out, lse_out, mixed_out, resid_out, lq_out, lk_out, lv_out, lwo_out, meta_all, vectors, gains,
    slots, d_outs, wgu,
    x, wg, wu, cot, normed, qkv, lse, mixed, resid, lq, lk, lv, lwo,
    extra, sq, sk, sv, sext, swo, smeta, lext, packed,
    x_all, heads, mixed_in, tiles, cot_all, two_all, two_own, two_rows, cot_rows,
    line_send, line_recv, plane_send, plane_recv, core_send, core_recv, chain_send, chain_recv, own_sem,
    w_send, w_recv, m_send, m_recv, c_send, c_recv, t_send, t_recv,
    pc_send, pc_recv, pt_send, pt_recv, in_sem, out_sem,
):
    dp, ex = lax.axis_index("dp"), lax.axis_index("expert")
    greet(n, ne, dp, ex)
    loads = Copies(in_sem, [(x_in, x), (cot_in, cot), (wg_in, wg), (wu_in, wu)])
    loads.start(0, 1, 2, 3)
    stores = Copies(
        out_sem,
        [
            (normed, normed_out), (qkv, qkv_out), (lse, lse_out), (mixed, mixed_out), (resid, resid_out),
            (lq, lq_out), (lk, lk_out), (lv, lv_out), (lwo, lwo_out),
        ],
    )
    own = sq.shape[2]
    block, width = cot.shape
    pairs_n = own // 128
    slots_n = ne * cap_pad
    n_gain, n_bias = gain_attn.shape[1], position_bias.shape[1]
    line_of = jnp.concatenate(
        [
            gain_attn[...].astype(F32), gain_moe[...].astype(F32), position_bias[...].astype(F32),
            jnp.zeros((1, own - 2 * n_gain - n_bias), F32),
        ],
        axis=1,
    )
    extra[...] = jnp.broadcast_to(line_of, (16, own)).astype(BF16)
    loads.wait(0)
    meet(n, ne)
    chain = Chain(n, dp, ex, x, x_all, chain_send, chain_recv)
    cots = Chain(n, dp, ex, cot, cot_all, c_send, c_recv)
    twos = Chain(n, dp, ex, two_own, two_all, t_send, t_recv)

    def column(ref, t):
        return ref.at[:, pl.ds(pl.multiple_of(t * own, 128), own)]

    def line(kind, d):
        t = lax.rem(dp + d, n)
        src, dst = [
            (column(wq, t), sq.at[dp]), (column(wk, t), sk.at[dp]), (column(wv, t), sv.at[dp]),
            (extra, sext.at[dp]), (wo, swo.at[dp]), (smeta, meta_all.at[dp]),
        ][kind]
        return remote(src, dst, line_send.at[kind, d], line_recv.at[kind, d], (t, ex))

    for d in range(1, n):
        for kind in range(4):
            line(kind, d).start()
    chain.start()
    for d in range(1, n):
        line(4, d).start()
    here = pl.ds(pl.multiple_of(dp * own, 128), own)
    sq[dp] = wq[:, here]
    sk[dp] = wk[:, here]
    sv[dp] = wv[:, here]
    sext[dp] = extra[...]
    swo[dp] = wo[...]
    x_all[dp] = x[...]

    tok = meta_in.shape[1]
    routes = meta_in[...]
    ids = lax.broadcasted_iota(jnp.int32, (ne, tok), 0)
    first = (ids == routes[0:1, :]).astype(F32)
    second = (ids == routes[1:2, :]).astype(F32)
    before = (
        lax.broadcasted_iota(jnp.int32, (tok, tok), 0) < lax.broadcasted_iota(jnp.int32, (tok, tok), 1)
    ).astype(BF16)
    counts = mm((first + second).astype(BF16), before)
    slot_a = jnp.sum(counts * first, axis=0, keepdims=True)
    slot_b = jnp.sum((counts + first) * second, axis=0, keepdims=True)
    asked = routes.astype(F32)
    dest_a = jnp.where(slot_a < cap, asked[0:1, :] * cap_pad + slot_a, -1.0)
    dest_b = jnp.where(slot_b < cap, asked[1:2, :] * cap_pad + slot_b, -1.0)
    gate = asked[2:3, :] * (1.0 / 65536.0)
    smeta[...] = jnp.concatenate([dest_a, dest_b, gate, jnp.zeros((5, tok), F32)], axis=0)
    meta_all[dp] = smeta[...]
    for d in range(1, n):
        line(5, d).start()

    pairs = [(sq, lq), (sk, lk), (sv, lv), (sext, lext), (swo, lwo)]
    partner = ex + 1 - 2 * lax.rem(ex, 2)

    def plane(kind, k):
        src, dst = pairs[kind]
        return remote(
            src, dst.at[:, ex], plane_send.at[kind, k], plane_recv.at[kind, k],
            (dp, lax.rem(ex + 2 * k, ne)),
        )

    def core(kind, k):
        src, dst = pairs[kind]
        at = lax.rem(ex + ne - 2 * k, ne)
        return remote(
            src if k == 0 else dst.at[:, at], dst.at[:, at],
            core_send.at[kind, k], core_recv.at[kind, k], (dp, partner),
        )

    def keep_own(kind):
        return pltpu.make_async_copy(pairs[kind][0], pairs[kind][1].at[:, ex], own_sem.at[kind])

    def spread(kind):
        for d in range(1, n):
            line(kind, d).wait_recv()
        for k in range(1, ne // 2):
            plane(kind, k).start()
        core(kind, 0).start()
        keep_own(kind).start()

    def pass_on(kind):
        for k in range(1, ne // 2):
            plane(kind, k).wait_recv()
            core(kind, k).start()

    def settle(kind):
        keep_own(kind).wait()
        for k in range(ne // 2):
            core(kind, k).wait()
        for k in range(1, ne // 2):
            plane(kind, k).wait_send()

    for kind in range(4):
        spread(kind)

    def to_plane(rows, land, send, recv, group, k):
        peer = lax.rem(ex + k, ne)
        return remote(
            rows.at[group, pl.ds(pl.multiple_of(peer * cap_pad, 16), cap_pad)], land.at[group, ex],
            send.at[group, k], recv.at[group, k], (dp, peer),
        )

    def kept(rows, land, group, sem):
        return pltpu.make_async_copy(
            rows.at[group, pl.ds(pl.multiple_of(ex * cap_pad, 16), cap_pad)], land.at[group, ex], sem.at[group, 0]
        )

    def dispatch(group, tokens, rows, land, send, recv, weigh):
        meta = meta_all[group]
        slot_ids = lax.broadcasted_iota(jnp.int32, (slots_n, block), 0).astype(F32)
        hit_a, hit_b = slot_ids == meta[0:1, :], slot_ids == meta[1:2, :]
        chosen = jnp.where(hit_a | hit_b, 1.0, 0.0).astype(BF16)
        found = mm(chosen, tokens)
        if weigh:
            share = meta[2:3, :]
            factor = jnp.sum(
                jnp.where(hit_a, share, 0.0) + jnp.where(hit_b, 1.0 - share, 0.0), axis=1, keepdims=True
            )
            found = found * factor
        rows[group] = found.astype(BF16)
        for k in range(1, ne):
            to_plane(rows, land, send, recv, group, k).start()
        kept(rows, land, group, send).start()

    def send_cot(group, tokens):
        dispatch(group, tokens, cot_rows, d_outs, pc_send, pc_recv, True)

    def send_two(group, tokens):
        dispatch(group, tokens, two_rows, slots, pt_send, pt_recv, False)

    loads.wait(1)
    send_cot(dp, cot[...])

    def weights(d):
        t = lax.rem(dp + d, n)
        return remote(packed.at[t], wgu.at[dp], w_send.at[d], w_recv.at[d], (t, ex))

    keep_w = pltpu.make_async_copy(packed.at[dp], wgu.at[dp], own_sem.at[5])

    def hop(line_chain, h, then):
        for side in range(2):
            @pl.when(line_chain.held(h, side))
            def _():
                then(line_chain.arrive(h, side))

    def x_hop(h):
        hop(chain, h, lambda at: None)

    def send_weights(early):
        for d in range(1, n):
            t = lax.rem(dp + d, n)
            inside = (t > 0) & (t < n - 1) & ((t == dp + 1) | (t + 1 == dp))

            @pl.when(inside if early else jnp.logical_not(inside))
            def _():
                weights(d).start()

    main = piece // 128 * 128
    step = min(wg.shape[0], 64)

    def pack(i):
        rows = pl.ds(pl.multiple_of(i * step, step), step)
        gate_w, up_w = wg[rows, :], wu[rows, :]
        for j in range(n):
            g = gate_w[:, j * piece : (j + 1) * piece]
            u = up_w[:, j * piece : (j + 1) * piece]
            packed[j, rows, :] = jnp.concatenate([g[:, :main], u[:, :main], g[:, main:], u[:, main:]], axis=1)

    loads.wait(2, 3)
    pl.loop(0, wg.shape[0] // step)(pack)
    x_hop(0)
    spread(4)
    for kind in range(4):
        pass_on(kind)
    if n > 2:
        x_hop(1)
    send_weights(True)
    for kind in range(4):
        settle(kind)
    stores.start(5, 6, 7)

    devices = n * ne
    shared = jnp.max(lext[...].astype(F32), axis=2).reshape(devices, own).astype(BF16)

    def laid_out(first_lane, count, total):
        lanes = lax.broadcasted_iota(jnp.int32, (own, total), 1)
        rows = lax.broadcasted_iota(jnp.int32, (own, total), 0)
        spreading = jnp.where(lax.rem(lanes, count) + first_lane == rows, 1.0, 0.0).astype(BF16)
        everywhere = mm(shared, spreading)
        owner = lax.broadcasted_iota(jnp.int32, (devices, total), 0)
        lane_owner = lax.broadcasted_iota(jnp.int32, (devices, total), 1) // count
        return jnp.sum(jnp.where(owner == lane_owner, everywhere, 0.0), axis=0, keepdims=True)

    gain_one = laid_out(0, n_gain, width)
    gain_two = laid_out(n_gain, n_gain, width)
    gains[...] = jnp.concatenate([gain_one, gain_two, jnp.zeros((6, width), F32)], axis=0)
    entries = HEADS * BUCKETS
    flat = laid_out(2 * n_gain, n_bias, entries)
    lanes = lax.broadcasted_iota(jnp.int32, (8, entries), 1)
    head_of = lax.broadcasted_iota(jnp.int32, (8, entries), 0) + dp * (HEADS // n)
    by_head = jnp.where(lax.rem(lanes, HEADS) == head_of, jnp.broadcast_to(flat, (8, entries)), 0.0).astype(BF16)
    bucket_rows = lax.broadcasted_iota(jnp.int32, (entries, 128), 0) // HEADS
    to_bucket = jnp.where(
        bucket_rows == lax.broadcasted_iota(jnp.int32, (entries, 128), 1), 1.0, 0.0
    ).astype(BF16)
    table = mm(by_head, to_bucket).astype(BF16)
    wide = vectors.shape[1]
    vectors[...] = mm(table, bucket_hot(wide, 0, wide // 2), NT)

    def project(j):
        at = pl.ds(pl.multiple_of(j * block, block), block)
        xf = x_all[j].astype(F32)
        inverse = lax.rsqrt(jnp.mean(xf * xf, axis=-1, keepdims=True) + EPSILON)
        low = (xf * inverse * gains[0:1, :]).astype(BF16)
        normed[at, :] = low
        for w, ref in enumerate((lq, lk, lv)):
            qkv[at, w * own : (w + 1) * own] = mm(low, rows_flat(ref)).astype(BF16)

    project(dp)

    def project_hop(h):
        @pl.loop(0, 2)
        def _(side):
            @pl.when(((side == 0) & (dp > h)) | ((side == 1) & (dp + 1 + h < n)))
            def _():
                project(chain.block(h + 1, side))

    for h in range(n - 2):
        project_hop(h)
    pass_on(4)
    x_hop(n - 2)
    cots.start()
    keep_w.start()
    project_hop(n - 2)
    stores.start(0, 1)

    def attend(pair):
        for side in range(2):
            bias_tile(vectors, 2 * pair + side, tiles.at[side])
        lane = lax.broadcasted_iota(jnp.int32, (block, 128), 1)
        low_half = lane < HEAD_DIM
        k_pair = qkv[:, own + pair * 128 : own + (pair + 1) * 128]
        v_pair = qkv[:, 2 * own + pair * 128 : 2 * own + (pair + 1) * 128]

        @pl.loop(0, n)
        def _(i):
            at = pl.ds(pl.multiple_of(i * block, block), block)
            q_pair = qkv[at, pair * 128 : (pair + 1) * 128]
            outs, logs = [], []
            for side in range(2):
                mask = low_half if side == 0 else jnp.logical_not(low_half)
                logits = logits_of(n, block, i, q_pair, k_pair, mask, tiles.at[side])
                row_max = jnp.max(logits, axis=-1, keepdims=True)
                exponent = jnp.exp(logits - row_max)
                total = jnp.sum(exponent, axis=-1, keepdims=True)
                probs_low = (exponent * (1.0 / total)).astype(BF16)
                outs.append(mm(probs_low, v_pair))
                logs.append(jnp.broadcast_to(row_max + jnp.log(total), (block, 128)))
            heads[at, pair * 128 : (pair + 1) * 128] = jnp.where(low_half, outs[0], outs[1]).astype(BF16)
            lse[at, pair * 128 : (pair + 1) * 128] = jnp.where(low_half, logs[0], logs[1])

    def cot_hop(h):
        hop(cots, h, lambda group: send_cot(group, cot_all[group]))

    for d in range(1, n):
        line(5, d).wait_recv()
    def give(d):
        t = lax.rem(dp + d, n)
        return remote(
            heads.at[pl.ds(pl.multiple_of(t * block, block), block)], mixed_in.at[dp], m_send.at[d], m_recv.at[d],
            (t, ex),
        )

    for pair in range(pairs_n):
        attend(pair)
        if pair == pairs_n - 1:
            for d in range(1, n):
                give(d).start()
    mixed_in[dp] = heads[pl.ds(pl.multiple_of(dp * block, block), block), :]
    settle(4)
    stores.start(8, 2)
    cot_hop(0)
    for d in range(1, n):
        give(d).wait()
    mixed[...] = jnp.concatenate([mixed_in[j] for j in range(n)], axis=1)
    total = x[...].astype(F32) + mm(mixed[...], rows_flat(lwo))
    resid[...] = total
    inverse = lax.rsqrt(jnp.mean(total * total, axis=-1, keepdims=True) + EPSILON)
    two_own[...] = (total * inverse * gains[1:2, :]).astype(BF16)
    twos.start()
    stores.start(3, 4)

    send_two(dp, two_own[...])
    for h in range(1, n - 1):
        cot_hop(h)
    for h in range(n - 1):
        hop(twos, h, lambda group: send_two(group, two_all[group]))
    for to_end in (True, False):
        for d in range(1, n):
            t = lax.rem(dp + d, n)
            inside = (t > 0) & (t < n - 1) & ((t == dp + 1) | (t + 1 == dp))
            end = (t == 0) | (t == n - 1)

            @pl.when(jnp.logical_not(inside) & (end if to_end else jnp.logical_not(end)))
            def _():
                weights(d).start()

    stores.wait(*range(9))
    chain.finish()
    cots.finish()
    twos.finish()
    for d in range(1, n):
        for kind in range(6):
            line(kind, d).wait_send()
    keep_w.wait()
    for d in range(1, n):
        weights(d).wait()
    for rows, land, send, recv in (
        (two_rows, slots, pt_send, pt_recv), (cot_rows, d_outs, pc_send, pc_recv),
    ):
        @pl.loop(0, n)
        def _(group):
            kept(rows, land, group, send).wait()
            for k in range(1, ne):
                to_plane(rows, land, send, recv, group, k).wait()


def front(n, ne, cap, cap_pad, x, wq, wk, wv, wo, gain_attn, gain_moe, position_bias, meta_in, wg, wu, cot):
    tok, width = x.shape
    wrows = wq.shape[0]
    own = width // n
    piece = wg.shape[1] // n
    wide = 2 * n * tok
    slots_n = ne * cap_pad
    sem = pltpu.SemaphoreType.DMA
    shape = jax.ShapeDtypeStruct
    return pl.pallas_call(
        functools.partial(front_kernel, n, ne, cap, cap_pad, piece),
        in_specs=[ANY] + [VM] * 8 + [ANY] * 3,
        out_specs=[ANY] * 9 + [VM] * 3 + [ANY] * 3,
        out_shape=[
            shape((n * tok, width), BF16),
            shape((n * tok, 3 * own), BF16),
            shape((n * tok, own), F32),
            shape((tok, width), BF16),
            shape((tok, width), F32),
            shape((n, ne, wrows, own), BF16),
            shape((n, ne, wrows, own), BF16),
            shape((n, ne, wrows, own), BF16),
            shape((n, ne, wrows, width), BF16),
            shape((n, 8, tok), F32),
            shape((8, wide), F32),
            shape((8, width), F32),
            shape((n, ne, cap_pad, width), BF16),
            shape((n, ne, cap_pad, width), BF16),
            shape((n, tok, 2 * piece), BF16),
        ],
        scratch_shapes=[
            pltpu.VMEM((tok, width), BF16),
            pltpu.VMEM(wg.shape, BF16),
            pltpu.VMEM(wu.shape, BF16),
            pltpu.VMEM((tok, width), BF16),
            pltpu.VMEM((n * tok, width), BF16),
            pltpu.VMEM((n * tok, 3 * own), BF16),
            pltpu.VMEM((n * tok, own), F32),
            pltpu.VMEM((tok, width), BF16),
            pltpu.VMEM((tok, width), F32),
            pltpu.VMEM((n, ne, wrows, own), BF16),
            pltpu.VMEM((n, ne, wrows, own), BF16),
            pltpu.VMEM((n, ne, wrows, own), BF16),
            pltpu.VMEM((n, ne, wrows, width), BF16),
            pltpu.VMEM((16, own), BF16),
            pltpu.VMEM((n, wrows, own), BF16),
            pltpu.VMEM((n, wrows, own), BF16),
            pltpu.VMEM((n, wrows, own), BF16),
            pltpu.VMEM((n, 16, own), BF16),
            pltpu.VMEM((n, wrows, width), BF16),
            pltpu.VMEM((8, tok), F32),
            pltpu.VMEM((n, ne, 16, own), BF16),
            pltpu.VMEM((n, tok, 2 * piece), BF16),
            pltpu.VMEM((n, tok, width), BF16),
            pltpu.VMEM((n * tok, own), BF16),
            pltpu.VMEM((n, tok, own), BF16),
            pltpu.VMEM((2, tok, wide), F32),
            pltpu.VMEM((n, tok, width), BF16),
            pltpu.VMEM((n, tok, width), BF16),
            pltpu.VMEM((tok, width), BF16),
            pltpu.VMEM((n, slots_n, width), BF16),
            pltpu.VMEM((n, slots_n, width), BF16),
            sem((6, n)), sem((6, n)),
            sem((5, ne // 2)), sem((5, ne // 2)), sem((5, ne // 2)), sem((5, ne // 2)),
            sem((n, 2)), sem((n, 2)), sem((6,)),
            sem((n,)), sem((n,)), sem((n,)), sem((n,)),
            sem((n, 2)), sem((n, 2)), sem((n, 2)), sem((n, 2)),
            sem((n, ne)), sem((n, ne)), sem((n, ne)), sem((n, ne)), sem((4,)), sem((9,)),
        ],
        compiler_params=pltpu.CompilerParams(
            collective_id=1, has_side_effects=True, vmem_limit_bytes=60 * 1024 * 1024
        ),
        name="front",
    )(x, wq, wk, wv, wo, gain_attn, gain_moe, position_bias, meta_in, wg, wu, cot)


def experts_kernel(
    n, ne, cap_pad, deep, main,
    slots, d_outs, wgu_in, wd_in, meta_all,
    out_rows, d_two, gwgu_out, gwd_out,
    wgu_ref, gwgu, gwd, wd_ref, s_buf, d_buf, back, part, landed, gwgu_acc,
    load_sem, keep_sem, p_send, p_recv, z_send, z_recv, wd_sem,
):
    dp, ex = lax.axis_index("dp"), lax.axis_index("expert")
    slots_n, width = s_buf.shape[1:]
    tok = d_two.shape[0]
    greet(n, ne, dp, ex)
    toward = 2 * ((2 * dp) // n) - 1

    def group_at(step):
        return lax.rem(dp + n + toward * (1 + step), n)

    def load(step, kind):
        at = group_at(step)
        src, dst = ((slots, s_buf), (d_outs, d_buf))[kind]
        return pltpu.make_async_copy(src.at[at], dst.at[at], load_sem.at[kind, step])

    whole = Copies(
        wd_sem,
        [(wgu_in, wgu_ref), (wd_in, wd_ref.at[pl.ds(0, deep)]), (gwgu, gwgu_out), (gwd, gwd_out)],
    )
    whole.start(0, 1)
    for step in range(n):
        for kind in range(2):
            load(step, kind).start()
    wd_ref[deep:, :] = jnp.zeros((wd_ref.shape[0] - deep, width), BF16)
    gwgu_acc[...] = jnp.zeros_like(gwgu_acc)
    gwd[...] = jnp.zeros_like(gwd)
    whole.wait(0, 1)
    meet(n, ne)

    def rows_of(peer):
        return pl.ds(pl.multiple_of(peer * cap_pad, 16), cap_pad)

    def give(at, k):
        peer = lax.rem(ex + k, ne)
        return remote(
            d_buf.at[at, rows_of(peer)], back.at[at, rows_of(ex)], p_send.at[at, k], p_recv.at[at, k], (dp, peer)
        )

    def take(at, k):
        peer = lax.rem(ex + ne - k, ne)
        return remote(
            d_buf.at[at, rows_of(ex)], back.at[at, rows_of(peer)], p_send.at[at, k], p_recv.at[at, k], (dp, peer)
        )

    def keep(at):
        return pltpu.make_async_copy(s_buf.at[at], out_rows.at[at], keep_sem.at[at])

    def owed(at):
        return remote(part.at[at], landed.at[dp], z_send.at[at], z_recv.at[dp], (at, ex))

    def combine(at):
        for k in range(1, ne):
            take(at, k).wait_recv()
        meta = meta_all[at]
        ids = lax.broadcasted_iota(jnp.int32, (slots_n, tok), 0).astype(F32)
        hit = (ids == meta[0:1, :]) | (ids == meta[1:2, :])
        return mm(jnp.where(hit, 1.0, 0.0).astype(BF16), back[at], TN)

    @pl.loop(0, n)
    def _(step):
        at = group_at(step)
        for kind in range(2):
            load(step, kind).wait()
        wgu, wd = wgu_ref[...], wd_ref[...]
        parts = -(-slots_n // 640)
        size = slots_n // parts
        low_lane = lax.broadcasted_iota(jnp.int32, (size, 128), 1) < 64
        for p in range(parts):
            here = slice(p * size, (p + 1) * size)
            rows, d_out = s_buf[at, here, :], d_buf[at, here, :]
            pre = mm(rows, wgu)
            d_hidden = mm(d_out, wd, NT)
            gate, up, tail = pre[:, :main], pre[:, main : 2 * main], pre[:, 2 * main :]
            tail_up = pltpu.roll(tail, 64, 1)
            act, slope = gelu_pair(gate)
            act_t, slope_t = gelu_pair(tail)
            hidden_t = jnp.where(low_lane, act_t * tail_up, 0.0)
            hidden = jnp.concatenate([(act * up).astype(BF16), hidden_t.astype(BF16)], axis=1)
            dh, dh_t = d_hidden[:, :main], d_hidden[:, main:]
            d_gate = dh * up * slope
            d_up = dh * act
            d_tail = jnp.where(low_lane, dh_t * tail_up * slope_t, pltpu.roll(dh_t * act_t, 64, 1))
            d_pre = jnp.concatenate([d_gate.astype(BF16), d_up.astype(BF16), d_tail.astype(BF16)], axis=1)
            d_rows = mm(d_pre, wgu, NT).astype(BF16)
            gwd[...] += mm(hidden, d_out, TN)[:deep]
            d_buf[at, here, :] = d_rows
            if p == parts - 1:
                for k in range(1, ne):
                    give(at, k).start()
                back[at, rows_of(ex), :] = d_buf[at, rows_of(ex), :]
            gwgu_acc[...] += mm(rows, d_pre, TN)
            s_buf[at, here, :] = mm(hidden, wd).astype(BF16)
        keep(at).start()

        @pl.when(step > 0)
        def _():
            past = group_at(step - 1)
            part[past] = combine(past).astype(BF16)
            owed(past).start()

    gwgu[...] = gwgu_acc[...].astype(BF16)
    whole.start(2, 3)
    total = combine(dp)
    for d in range(1, n):
        src = lax.rem(dp + d, n)
        remote(part.at[src], landed.at[src], z_send.at[src], z_recv.at[src], (src, ex)).wait_recv()
        total = total + landed[src].astype(F32)
    d_two[...] = total
    whole.wait(2, 3)
    for d in range(1, n):
        owed(lax.rem(dp + d, n)).wait_send()

    @pl.loop(0, n)
    def _(at):
        keep(at).wait()
        for k in range(1, ne):
            give(at, k).wait_send()


def experts(n, ne, cap_pad, deep, slots, d_outs, wgu, wd, meta_all):
    width, columns = wgu.shape
    tok = meta_all.shape[2]
    main = (columns - 128) // 2
    slots_n = ne * cap_pad
    slots = slots.reshape(n, slots_n, width)
    d_outs = d_outs.reshape(n, slots_n, width)
    sem = pltpu.SemaphoreType.DMA
    return pl.pallas_call(
        functools.partial(experts_kernel, n, ne, cap_pad, deep, main),
        in_specs=[ANY, ANY, ANY, ANY, VM],
        out_specs=[ANY, VM, ANY, ANY],
        out_shape=[
            jax.ShapeDtypeStruct((n, slots_n, width), BF16),
            jax.ShapeDtypeStruct((tok, width), F32),
            jax.ShapeDtypeStruct((width, columns), BF16),
            jax.ShapeDtypeStruct((deep, width), F32),
        ],
        scratch_shapes=[
            pltpu.VMEM((width, columns), BF16),
            pltpu.VMEM((width, columns), BF16),
            pltpu.VMEM((deep, width), F32),
            pltpu.VMEM((-(-deep // 128) * 128, width), BF16),
            pltpu.VMEM((n, slots_n, width), BF16),
            pltpu.VMEM((n, slots_n, width), BF16),
            pltpu.VMEM((n, slots_n, width), BF16),
            pltpu.VMEM((n, tok, width), BF16),
            pltpu.VMEM((n, tok, width), BF16),
            pltpu.VMEM((width, columns), F32),
            sem((2, n)), sem((n,)), sem((n, ne)), sem((n, ne)), sem((n,)), sem((n,)), sem((4,)),
        ],
        compiler_params=pltpu.CompilerParams(
            collective_id=3, has_side_effects=True, vmem_limit_bytes=60 * 1024 * 1024
        ),
        name="experts",
    )(slots, d_outs, wgu, wd, meta_all)


def backward_kernel(
    n, ne, cap_pad,
    gains, vectors, meta_all,
    d_two_in, resid_in, cot_in, wo_in, x_in, mixed_in, qkv_in, lse_in, normed_in, wq_in, wk_in, wv_in,
    gwgu, out_rows,
    block_out, grad_in, g_all, small_all, gw_in, out_in,
    d_two, resid, cot, wo, x, mixed, qkv, lse, normed, wq, wk, wv,
    dm, dm_in, tiles, sums, dq_s, dk_s, dv_s, dk_acc, dv_acc, diag, d_res,
    dn_part, dn_land, moe_part, moe_land, out_one,
    g_send, g_land, g2_send, g2_land, o_send, o_land, o2_send, o2_land,
    small_own, small_land, small_sum,
    out_s, out_r, w_s, w_r, dm_s, dm_r, dn_s, dn_r, moe_s, moe_r, g_s, g_r, o_s, o_r, g2_s, g2_r, o2_s, o2_r,
    sp_s, sp_r, sz_s, sz_r, keep_sem, in_sem,
):
    dp, ex = lax.axis_index("dp"), lax.axis_index("expert")
    tok, width = cot.shape
    own = dq_s.shape[1]
    pairs_n = own // 128
    slots_n = ne * cap_pad
    wrows = g_all.shape[1]
    greet(n, ne, dp, ex)
    loads = Copies(
        in_sem,
        [
            (d_two_in, d_two), (resid_in, resid), (cot_in, cot), (wo_in, wo), (x_in, x), (mixed_in, mixed),
            (qkv_in, qkv), (lse_in, lse), (normed_in, normed), (wq_in, wq), (wk_in, wk), (wv_in, wv),
        ],
    )
    loads.start(0, 1, 2, 3, 5, 6, 7, 9, 10, 11, 8, 4)
    toward = 2 * ((2 * dp) // n) - 1

    def group_at(step):
        return lax.rem(dp + n + toward * (1 + step), n)

    def rows_of(peer):
        return pl.ds(pl.multiple_of(peer * cap_pad, 16), cap_pad)

    def to_line(src, dst, send, recv, t):
        return remote(src.at[t], dst.at[dp], send.at[t], recv.at[dp], (t, ex))

    def from_line(src, dst, send, recv, t):
        return remote(src.at[t], dst.at[t], send.at[t], recv.at[t], (t, ex))

    def to_plane(src, dst, send, recv, k):
        return remote(src, dst.at[ex], send.at[k], recv.at[k], (dp, lax.rem(ex + k, ne)))

    def from_plane(src, dst, send, recv, k):
        peer = lax.rem(ex + ne - k, ne)
        return remote(src, dst.at[peer], send.at[k], recv.at[k], (dp, peer))

    def out_give(at, k):
        peer = lax.rem(ex + k, ne)
        return remote(
            out_rows.at[at, rows_of(peer)], out_in.at[at, rows_of(ex)], out_s.at[at, k], out_r.at[at, k], (dp, peer)
        )

    def out_take(at, k):
        peer = lax.rem(ex + ne - k, ne)
        return remote(
            out_rows.at[at, rows_of(ex)], out_in.at[at, rows_of(peer)], out_s.at[at, k], out_r.at[at, k], (dp, peer)
        )

    def out_keep(at):
        return pltpu.make_async_copy(out_rows.at[at, rows_of(ex)], out_in.at[at, rows_of(ex)], out_s.at[at, 0])

    loads.wait(0, 1, 2)
    values = resid[...]
    d_normed = d_two[...]
    inverse = lax.rsqrt(jnp.mean(values * values, axis=-1, keepdims=True) + EPSILON)
    scaled = gains[1:2, :] * d_normed
    gain_rows_two = jnp.sum(d_normed * values * inverse, axis=0, keepdims=True)
    mean = jnp.mean(scaled * values, axis=-1, keepdims=True)
    d_resid = cot[...].astype(F32) + inverse * scaled - values * (inverse * inverse * inverse * mean)
    d_res[...] = d_resid
    d_attn = d_resid.astype(BF16)
    loads.wait(3)
    d_mixed = mm(d_attn, wo[...], NT).astype(BF16)
    meet(n, ne)
    for j in range(n):
        dm[j] = d_mixed[:, j * own : (j + 1) * own]
    for d in range(1, n):
        to_line(dm, dm_in, dm_s, dm_r, lax.rem(dp + d, n)).start()
    dm_in[dp] = dm[dp]
    for d in range(1, n):
        to_line(gwgu, gw_in, w_s, w_r, lax.rem(dp + d, n)).start()
    keep_w = pltpu.make_async_copy(gwgu.at[dp], gw_in.at[dp], keep_sem.at[0])
    keep_w.start()

    @pl.loop(0, n)
    def _(step):
        at = group_at(step)
        for k in range(1, ne):
            out_give(at, k).start()
        out_keep(at).start()

    loads.wait(5)
    o_send[...] = mm(mixed[...], d_attn, TN).reshape(n, ne, wrows, width).astype(BF16)
    for k in range(1, ne):
        to_plane(o_send.at[:, lax.rem(ex + k, ne)], o_land, o_s, o_r, k).start()
    o_land[ex] = o_send[:, ex]
    for i in range(width // 128):
        small_own[8 + i : 9 + i, :] = gain_rows_two[:, i * 128 : (i + 1) * 128]
    for d in range(1, n):
        from_line(dm, dm_in, dm_s, dm_r, lax.rem(dp + d, n)).wait_recv()

    loads.wait(6, 7, 9, 10, 11)
    lane = lax.broadcasted_iota(jnp.int32, (tok, 128), 1)
    low_half = lane < HEAD_DIM
    key_low = lax.broadcasted_iota(jnp.int32, (n * tok, 128), 1) < HEAD_DIM
    diag[...] = jnp.zeros_like(diag)
    for pair in range(pairs_n):
        cols = slice(pair * 128, (pair + 1) * 128)
        for side in range(2):
            bias_tile(vectors, 2 * pair + side, tiles.at[side])
        sums[...] = jnp.zeros_like(sums)
        dk_acc[...] = jnp.zeros_like(dk_acc)
        dv_acc[...] = jnp.zeros_like(dv_acc)
        k_pair = qkv[:, own + pair * 128 : own + (pair + 1) * 128]
        v_pair = qkv[:, 2 * own + pair * 128 : 2 * own + (pair + 1) * 128]

        @pl.loop(0, n)
        def _(i):
            at = pl.ds(pl.multiple_of(i * tok, tok), tok)
            q_pair = qkv[at, cols]
            dm_pair = dm_in[i, :, cols]
            dqs, dks, dvs = [], [], []
            for side in range(2):
                mask = low_half if side == 0 else jnp.logical_not(low_half)
                logits = logits_of(n, tok, i, q_pair, k_pair, mask, tiles.at[side])
                first = pair * 128 + side * HEAD_DIM
                probs = jnp.exp(logits - lse[at, first : first + 1])
                d_probs = mm(jnp.where(mask, dm_pair, jnp.zeros_like(dm_pair)), v_pair, NT)
                inner = jnp.sum(probs * d_probs, axis=-1, keepdims=True)
                d_logits = (probs * (d_probs - inner)).astype(BF16)
                dvs.append(mm(probs.astype(BF16), dm_pair, TN))
                dqs.append(mm(d_logits, k_pair))
                dks.append(mm(d_logits, q_pair, TN))
                wide = d_logits.astype(F32)
                for j in range(n):
                    here = pl.ds(tile_offset(n, tok, i, j), tok)
                    sums[side, :, here] += wide[:, j * tok : (j + 1) * tok]
            dq_s[at, cols] = (jnp.where(low_half, dqs[0], dqs[1]) * SCALE).astype(BF16)
            dk_acc[...] += jnp.where(key_low, dks[0], dks[1])
            dv_acc[...] += jnp.where(key_low, dvs[0], dvs[1])

        dk_s[:, cols] = (dk_acc[...] * SCALE).astype(BF16)
        dv_s[:, cols] = dv_acc[...].astype(BF16)
        for side in range(2):
            diag[2 * pair + side : 2 * pair + side + 1, :] = diagonal_sum(sums[side])

    def d_norm(t):
        at = pl.ds(pl.multiple_of(t * tok, tok), tok)
        return mm(dq_s[at, :], wq[...], NT) + mm(dk_s[at, :], wk[...], NT) + mm(dv_s[at, :], wv[...], NT)

    def sum_copy(part, land, send, recv, r, side):
        t = lax.rem(dp + n + (n - r) * (1 - 2 * side), n)
        target = lax.rem(dp + n + 1 - 2 * side, n)
        return t, remote(part.at[t], land.at[r - 1, side], send.at[r - 1, side], recv.at[r - 1, side], (target, ex))

    def takes_part(r, side):
        return ((side == 0) & (dp < r) & (dp + 1 < n)) | ((side == 1) & (dp + r >= n) & (dp > 0))

    def is_fed(r, side):
        return ((side == 0) & (dp > 0) & (r > 1)) | ((side == 1) & (dp + 1 < n) & (r > 1))

    def fed(part, land, send, recv, r, side):
        remote(
            part.at[dp], land.at[r - 1, side], send.at[r - 1, side], recv.at[r - 1, side], (dp, ex)
        ).wait_recv()

    def sum_round(part, land, send, recv, term, r):
        @pl.loop(0, 2)
        def _(side):
            @pl.when(takes_part(r, side))
            def _():
                t, copy = sum_copy(part, land, send, recv, r, side)
                mine = term(t)

                @pl.when(is_fed(r, side))
                def _():
                    fed(part, land, send, recv, r - 1, side)
                    part[t] = (mine + land[max(r - 2, 0), side].astype(F32)).astype(BF16)

                @pl.when(jnp.logical_not(is_fed(r, side)))
                def _():
                    part[t] = mine.astype(BF16)

                copy.start()

    def sum_end(part, land, send, recv, mine):
        @pl.when(dp > 0)
        def _():
            fed(part, land, send, recv, n - 1, 0)

        @pl.when(dp + 1 < n)
        def _():
            fed(part, land, send, recv, n - 1, 1)

        left = jnp.where(dp > 0, land[n - 2, 0].astype(F32), 0.0)
        right = jnp.where(dp + 1 < n, land[n - 2, 1].astype(F32), 0.0)
        return mine + left + right

    def sum_sent(part, land, send, recv):
        for r in range(1, n):
            for side in range(2):
                @pl.when(takes_part(r, side))
                def _():
                    sum_copy(part, land, send, recv, r, side)[1].wait_send()

    dn = (dn_part, dn_land, dn_s, dn_r)
    moes = (moe_part, moe_land, moe_s, moe_r)
    sum_round(*dn, d_norm, 1)

    loads.wait(8, 4)
    for w, ref in enumerate((dq_s, dk_s, dv_s)):
        g_send[:, :, w] = mm(normed[...], ref[...], TN).reshape(n, ne, wrows, own).astype(BF16)
    for k in range(1, ne):
        to_plane(g_send.at[:, lax.rem(ex + k, ne)], g_land, g_s, g_r, k).start()
    g_land[ex] = g_send[:, ex]

    def moe(at):
        for k in range(1, ne):
            out_take(at, k).wait_recv()
        out_keep(at).wait()
        load = pltpu.make_async_copy(out_in.at[at], out_one, keep_sem.at[1])
        load.start()
        meta = meta_all[at]
        ids = lax.broadcasted_iota(jnp.int32, (slots_n, tok), 0).astype(F32)
        gate = meta[2:3, :]
        weight = jnp.where(ids == meta[0:1, :], gate, 0.0) + jnp.where(ids == meta[1:2, :], 1.0 - gate, 0.0)
        load.wait()
        return mm(weight.astype(BF16), out_one[...], TN)

    sum_round(*moes, moe, 1)
    for r in range(2, n):
        sum_round(*dn, d_norm, r)
        sum_round(*moes, moe, r)

    rest = diag[...]
    table = jnp.zeros((8, 128), F32)
    wide = vectors.shape[1]
    hot = bucket_hot(wide, tok, wide // 2)
    for _ in range(3):
        piece = rest.astype(BF16)
        table = table + mm(piece, hot)
        rest = rest - piece.astype(F32)
    small_own[16:24, :] = table

    for k in range(1, ne):
        from_plane(o_send.at[:, ex], o_land, o_s, o_r, k).wait_recv()
    total = o_land[0].astype(F32)
    for e in range(1, ne):
        total = total + o_land[e].astype(F32)
    o2_send[...] = total.astype(BF16)
    for d in range(1, n):
        to_line(o2_send, o2_land, o2_s, o2_r, lax.rem(dp + d, n)).start()
    o2_land[dp] = o2_send[dp]

    for k in range(1, ne):
        from_plane(g_send.at[:, ex], g_land, g_s, g_r, k).wait_recv()
    total = g_land[0].astype(F32)
    for e in range(1, ne):
        total = total + g_land[e].astype(F32)
    g2_send[...] = total.astype(BF16)
    for d in range(1, n):
        to_line(g2_send, g2_land, g2_s, g2_r, lax.rem(dp + d, n)).start()
    g2_land[dp] = g2_send[dp]

    total = sum_end(*dn, d_norm(dp))
    values = x[...].astype(F32)
    inverse = lax.rsqrt(jnp.mean(values * values, axis=-1, keepdims=True) + EPSILON)
    scaled = gains[0:1, :] * total
    gain_rows_one = jnp.sum(total * values * inverse, axis=0, keepdims=True)
    mean = jnp.mean(scaled * values, axis=-1, keepdims=True)
    grad_in[...] = (d_res[...] + inverse * scaled - values * (inverse * inverse * inverse * mean)).astype(BF16)
    for i in range(width // 128):
        small_own[i : i + 1, :] = gain_rows_one[:, i * 128 : (i + 1) * 128]
    for k in range(1, ne):
        to_plane(small_own, small_land, sp_s, sp_r, k).start()
    small_land[ex] = small_own[...]
    for k in range(1, ne):
        from_plane(small_own, small_land, sp_s, sp_r, k).wait_recv()
    total = small_land[0]
    for e in range(1, ne):
        total = total + small_land[e]
    small_sum[...] = total
    for d in range(1, n):
        t = lax.rem(dp + d, n)
        remote(small_sum, small_all.at[dp], sz_s.at[t], sz_r.at[dp], (t, ex)).start()
    small_all[dp] = total

    block_out[...] = sum_end(*moes, resid[...] + moe(dp)).astype(BF16)

    for d in range(1, n):
        t = lax.rem(dp + d, n)
        from_line(o2_send, o2_land, o2_s, o2_r, t).wait_recv()
        from_line(g2_send, g2_land, g2_s, g2_r, t).wait_recv()
        remote(small_sum, small_all.at[t], sz_s.at[t], sz_r.at[t], (t, ex)).wait_recv()
    total = o2_land[0].astype(F32)
    for j in range(1, n):
        total = total + o2_land[j].astype(F32)
    g_all[3] = total
    for w in range(3):
        g_all[w] = jnp.concatenate([g2_land[j, w] for j in range(n)], axis=1).astype(F32)
    for d in range(1, n):
        t = lax.rem(dp + d, n)
        from_line(gwgu, gw_in, w_s, w_r, t).wait_recv()
        for src, dst, send, recv in (
            (gwgu, gw_in, w_s, w_r), (dm, dm_in, dm_s, dm_r),
            (o2_send, o2_land, o2_s, o2_r), (g2_send, g2_land, g2_s, g2_r),
        ):
            to_line(src, dst, send, recv, t).wait_send()
        remote(small_sum, small_all.at[dp], sz_s.at[t], sz_r.at[dp], (t, ex)).wait_send()
    keep_w.wait()
    sum_sent(*dn)
    sum_sent(*moes)
    for k in range(1, ne):
        to_plane(o_send.at[:, ex], o_land, o_s, o_r, k).wait_send()
        to_plane(g_send.at[:, ex], g_land, g_s, g_r, k).wait_send()
        to_plane(small_own, small_land, sp_s, sp_r, k).wait_send()

    @pl.loop(0, n)
    def _(at):
        for k in range(1, ne):
            out_give(at, k).wait_send()


def backward(
    n, ne, cap_pad, wrows, d_two, resid, cot, x, gains, mixed, wo, qkv, lse, normed, vectors,
    wq, wk, wv, meta_all, gwgu, out_rows,
):
    tok, width = cot.shape
    own = wq.shape[1]
    wide = vectors.shape[1]
    both = gwgu.shape[2]
    slots_n = ne * cap_pad
    length = n * tok
    sem = pltpu.SemaphoreType.DMA
    shape = jax.ShapeDtypeStruct
    return pl.pallas_call(
        functools.partial(backward_kernel, n, ne, cap_pad),
        in_specs=[VM] * 3 + [ANY] * 14,
        out_specs=[VM] * 4 + [ANY] * 2,
        out_shape=[
            shape((tok, width), BF16),
            shape((tok, width), BF16),
            shape((4, wrows, width), F32),
            shape((n, 24, 128), F32),
            shape((n, tok, both), BF16),
            shape((n, slots_n, width), BF16),
        ],
        scratch_shapes=[
            pltpu.VMEM((tok, width), F32),
            pltpu.VMEM((tok, width), F32),
            pltpu.VMEM((tok, width), BF16),
            pltpu.VMEM((width, width), BF16),
            pltpu.VMEM((tok, width), BF16),
            pltpu.VMEM((tok, width), BF16),
            pltpu.VMEM((length, 3 * own), BF16),
            pltpu.VMEM((length, own), F32),
            pltpu.VMEM((length, width), BF16),
            pltpu.VMEM((width, own), BF16),
            pltpu.VMEM((width, own), BF16),
            pltpu.VMEM((width, own), BF16),
            pltpu.VMEM((n, tok, own), BF16),
            pltpu.VMEM((n, tok, own), BF16),
            pltpu.VMEM((2, tok, wide), F32),
            pltpu.VMEM((2, tok, wide), F32),
            pltpu.VMEM((length, own), BF16),
            pltpu.VMEM((length, own), BF16),
            pltpu.VMEM((length, own), BF16),
            pltpu.VMEM((length, 128), F32),
            pltpu.VMEM((length, 128), F32),
            pltpu.VMEM((8, wide), F32),
            pltpu.VMEM((tok, width), F32),
            pltpu.VMEM((n, tok, width), BF16),
            pltpu.VMEM((n - 1, 2, tok, width), BF16),
            pltpu.VMEM((n, tok, width), BF16),
            pltpu.VMEM((n - 1, 2, tok, width), BF16),
            pltpu.VMEM((slots_n, width), BF16),
            pltpu.VMEM((n, ne, 3, wrows, own), BF16),
            pltpu.VMEM((ne, n, 3, wrows, own), BF16),
            pltpu.VMEM((n, 3, wrows, own), BF16),
            pltpu.VMEM((n, 3, wrows, own), BF16),
            pltpu.VMEM((n, ne, wrows, width), BF16),
            pltpu.VMEM((ne, n, wrows, width), BF16),
            pltpu.VMEM((n, wrows, width), BF16),
            pltpu.VMEM((n, wrows, width), BF16),
            pltpu.VMEM((24, 128), F32),
            pltpu.VMEM((ne, 24, 128), F32),
            pltpu.VMEM((24, 128), F32),
            sem((n, ne)), sem((n, ne)), sem((n,)), sem((n,)), sem((n,)), sem((n,)), sem((n, 2)), sem((n, 2)),
            sem((n, 2)), sem((n, 2)), sem((ne,)), sem((ne,)), sem((ne,)), sem((ne,)), sem((n,)), sem((n,)),
            sem((n,)), sem((n,)), sem((ne,)), sem((ne,)), sem((n,)), sem((n,)), sem((2,)), sem((12,)),
        ],
        compiler_params=pltpu.CompilerParams(
            collective_id=4, has_side_effects=True, vmem_limit_bytes=60 * 1024 * 1024
        ),
        name="backward",
    )(
        gains, vectors, meta_all, d_two, resid, cot, wo, x, mixed, qkv, lse, normed, wq, wk, wv, gwgu, out_rows
    )


def split_pieces(value):
    pieces = []
    for _ in range(3):
        piece = value.astype(BF16)
        pieces.append(piece)
        value = value - piece.astype(F32)
    return pieces


def finish_kernel(
    n, ne, heads_own, piece, blocks, g_all, small, out_in, grad_in, gwd_in,
    gate_ref, up_ref, gq, gk, gv, go, gain_one, gain_two, bias, block_out, grad_out, gwd,
):
    main = piece // 128 * 128
    rest = piece - main
    gates, ups = [], []
    for j in range(n):
        block = blocks[j].astype(F32)
        gates += [block[:, :main], block[:, 2 * main : 2 * main + rest]]
        ups += [block[:, main : 2 * main], block[:, 2 * main + rest :]]
    gate_ref[...] = jnp.concatenate(gates, axis=1)
    up_ref[...] = jnp.concatenate(ups, axis=1)
    block_out[...] = out_in[...]
    grad_out[...] = grad_in[...]
    gwd[...] = gwd_in[...]

    @pl.when(pl.program_id(0) == 0)
    def _():
        for i, ref in enumerate((gq, gk, gv, go)):
            ref[...] = g_all[i]
        me = lax.axis_index("dp") * ne + lax.axis_index("expert")
        total = small[0, :16]
        for j in range(1, n):
            total = total + small[j, :16]
        rows = lax.broadcasted_iota(jnp.int32, (8, 128), 0)
        lanes = lax.broadcasted_iota(jnp.int32, (8, 128), 1)
        for i, ref in enumerate((gain_one, gain_two)):
            count = ref.shape[1]
            at = me * count
            row = jnp.sum(jnp.where(rows == at // 128, total[8 * i : 8 * i + 8], 0.0), axis=0, keepdims=True)
            row = jnp.broadcast_to(row, (8, 128))
            ref[...] = pltpu.roll(row, lax.rem(128 - lax.rem(at, 128), 128), 1)[:1, :count]
        table = jnp.concatenate([small[j, 16 : 16 + heads_own] for j in range(n)], axis=0)
        heads = n * heads_own
        count = bias.shape[1]
        at = me * count
        table = jnp.concatenate([table, jnp.zeros((128 - heads, 128), F32)], axis=0)
        hot = jnp.where(lanes == at // heads, 1.0, 0.0).astype(BF16)
        row = sum(mm(hot, part, NT) for part in split_pieces(table))
        bias[...] = pltpu.roll(row, lax.rem(128 - lax.rem(at, heads), 128), 1)[:1, :count]


def finish(n, ne, heads_own, n_gain, n_bias, blocks, g_all, small, block_out, grad_in, gwd):
    tok, both = blocks.shape[1:]
    wrows, width = g_all.shape[1:]
    deep = gwd.shape[0]
    piece = both // 2
    steps = 4
    step, part = tok // steps, deep // steps
    total = n * piece
    shape = jax.ShapeDtypeStruct
    fixed2 = lambda i: (0, 0)
    fixed3 = lambda i: (0, 0, 0)
    move = lambda i: (i, 0)
    return pl.pallas_call(
        functools.partial(finish_kernel, n, ne, heads_own, piece),
        grid=(steps,),
        in_specs=[
            pl.BlockSpec((n, step, both), lambda i: (0, i, 0)),
            pl.BlockSpec((4, wrows, width), fixed3),
            pl.BlockSpec(small.shape, fixed3),
            pl.BlockSpec((step, width), move),
            pl.BlockSpec((step, width), move),
            pl.BlockSpec((part, width), move),
        ],
        out_specs=[pl.BlockSpec((step, total), move)] * 2
        + [pl.BlockSpec((wrows, width), fixed2)] * 4
        + [pl.BlockSpec((1, n_gain), fixed2)] * 2
        + [pl.BlockSpec((1, n_bias), fixed2)]
        + [pl.BlockSpec((step, width), move)] * 2
        + [pl.BlockSpec((part, width), move)],
        out_shape=[shape((tok, total), F32)] * 2
        + [shape((wrows, width), F32)] * 4
        + [shape((1, n_gain), F32)] * 2
        + [shape((1, n_bias), F32)]
        + [shape((tok, width), BF16)] * 2
        + [shape((deep, width), F32)],
        compiler_params=pltpu.CompilerParams(vmem_limit_bytes=VMEM_LIMIT),
        name="finish",
    )(blocks, g_all, small, block_out, grad_in, gwd)


def local(
    inputs, cotangent, gain_attn, w_query, w_key, w_value, w_out, position_bias,
    gain_moe, w_gate, w_up, w_down, routes, gate_fixed,
):
    n = lax.axis_size("dp")
    experts_n = lax.axis_size("expert")
    dp = lax.axis_index("dp")
    ex = lax.axis_index("expert")
    tok, width = inputs.shape[1:]
    length = n * tok
    own = HEADS * HEAD_DIM // n
    heads_own = HEADS // n
    wrows = w_query.shape[0]
    capacity = 5 * tok // (2 * experts_n)
    cap_pad = -(-capacity // 16) * 16
    slots_n = experts_n * cap_pad

    n_gain, n_bias = gain_attn.shape[0], position_bias.shape[0]
    meta_in = jnp.concatenate([routes[0].T, gate_fixed], axis=0)
    normed, qkv, lse, mixed, resid, wq, wk, wv, wo, meta_all, vectors, gains, slots, d_outs, wgu = front(
        n, experts_n, capacity, cap_pad, inputs[0], w_query, w_key, w_value, w_out,
        gain_attn.reshape(1, -1), gain_moe.reshape(1, -1), position_bias.reshape(1, -1),
        meta_in, w_gate[0], w_up[0], cotangent[0],
    )
    wq, wk, wv = (w.reshape(width, own) for w in (wq, wk, wv))
    wo = wo.reshape(width, width)
    wgu = wgu.reshape(width, -1)
    deep = w_down.shape[1]
    out_rows, grad_normed_two, gwgu, grad_w_down = experts(
        n, experts_n, cap_pad, deep, slots, d_outs, wgu, w_down[0], meta_all
    )

    block_out, grad_inputs, g_all, small, got, _ = backward(
        n, experts_n, cap_pad, wrows, grad_normed_two, resid, cotangent[0], inputs[0], gains, mixed, wo,
        qkv, lse, normed, vectors, wq, wk, wv, meta_all, gwgu.reshape(n, width // n, -1), out_rows,
    )
    (
        grad_w_gate, grad_w_up, gq, gk, gv, go, grad_gain_one, grad_gain_two, grad_bias, block_out, grad_inputs,
        grad_w_down,
    ) = finish(n, experts_n, heads_own, n_gain, n_bias, got, g_all, small, block_out, grad_inputs, grad_w_down)

    return (
        block_out[None],
        grad_inputs[None],
        grad_gain_one[0],
        gq,
        gk,
        gv,
        go,
        grad_bias[0],
        grad_gain_two[0],
        grad_w_gate[None],
        grad_w_up[None],
        grad_w_down[None],
    )


def solution(mesh):
    vector = P(("dp", "expert"))
    matrix = P(("dp", "expert"), None)
    split = P("expert", "dp", None)
    return jax.shard_map(
        local,
        mesh=mesh,
        in_specs=(
            split, split, vector, matrix, matrix, matrix, matrix, vector, vector,
            split, split, split, split, P("expert", "dp"),
        ),
        out_specs=(
            split, split, vector, matrix, matrix, matrix, matrix, vector, vector,
            split, split, split,
        ),
        check_vma=False,
    )
```

```python
import functools

import jax
import jax.numpy as jnp
from jax import lax
from jax.experimental import pallas as pl
from jax.experimental.pallas import tpu as pltpu
from jax.sharding import PartitionSpec as P

HEADS = 16
HEAD_DIM = 64
BUCKETS = 32
THRESHOLDS = (12, 16, 23, 32, 46, 64, 91)
EPSILON = 1e-06
SCALE = HEAD_DIM ** (-0.5)
BF16 = jnp.bfloat16
F32 = jnp.float32
GELU_C = 0.7978845608028654
GELU_A = 0.044715
VMEM_LIMIT = 56 * 1024 * 1024

NT = (((1,), (1,)), ((), ()))
TN = (((0,), (0,)), ((), ()))
NN = (((1,), (0,)), ((), ()))


def mm(a, b, dims=NN):
    return lax.dot_general(a, b, dims, preferred_element_type=F32)


def bucket_of(offset):
    distance = jnp.abs(offset)
    banded = jnp.full(distance.shape, 8, jnp.int32)
    for cutoff in THRESHOLDS:
        banded = banded + (distance >= cutoff).astype(jnp.int32)
    nearby = jnp.where(distance < 8, distance, banded)
    return nearby + jnp.where(offset > 0, 16, 0).astype(jnp.int32)


def bias_tile(vec_ref, head, tile_ref):
    block, wide = tile_ref.shape
    row = jnp.broadcast_to(vec_ref[pl.ds(head, 1), :], (block, wide))
    tile_ref[...] = pltpu.roll(row, wide - block, 1, stride=1, stride_axis=0)


def tile_offset(n, block, query_block, key_block):
    return pl.multiple_of((key_block - query_block + n - 1) * block, 128)


def logits_of(n, block, query_block, q_pair, k_pair, mask, tile_ref):
    masked = jnp.where(mask, q_pair, jnp.zeros_like(q_pair))
    raw = mm(masked, k_pair, NT) * SCALE
    bias = jnp.concatenate(
        [tile_ref[:, pl.ds(tile_offset(n, block, query_block, j), block)] for j in range(n)], axis=1
    )
    return raw + bias


def diagonal_sum(tile):
    rows, wide = tile.shape
    while rows > 1:
        half = rows // 2
        tile = tile[:half] + pltpu.roll(tile[half:], wide - half, 1)
        rows = half
    return tile


def gelu_pair(v):
    square = v * v
    t = jnp.tanh(GELU_C * (v + GELU_A * v * square))
    half = 0.5 * (1.0 + t)
    slope = half + (0.5 * GELU_C) * v * (1.0 - t * t) * (1.0 + (3.0 * GELU_A) * square)
    return v * half, slope


MESH = pl.DeviceIdType.MESH


def remote(src, dst, send, recv, target):
    return pltpu.make_async_remote_copy(
        src_ref=src, dst_ref=dst, send_sem=send, recv_sem=recv, device_id=target, device_id_type=MESH
    )


def greet(n, ne, dp, ex):
    barrier = pltpu.get_barrier_semaphore()
    for d in range(1, n):
        pl.semaphore_signal(barrier, inc=1, device_id=(lax.rem(dp + d, n), ex), device_id_type=MESH)
    for k in range(1, ne):
        pl.semaphore_signal(barrier, inc=1, device_id=(dp, lax.rem(ex + k, ne)), device_id_type=MESH)


def meet(n, ne):
    pl.semaphore_wait(pltpu.get_barrier_semaphore(), n + ne - 2)


class Copies:
    def __init__(self, sem, pairs):
        self.copies = [pltpu.make_async_copy(src, dst, sem.at[i]) for i, (src, dst) in enumerate(pairs)]

    def start(self, *which):
        for i in which:
            self.copies[i].start()

    def wait(self, *which):
        for i in which:
            self.copies[i].wait()


class Chain:
    def __init__(self, n, dp, ex, own, buffer, send, recv):
        self.n, self.dp, self.ex, self.own = n, dp, ex, own
        self.buffer, self.send_sem, self.recv_sem = buffer, send, recv

    def block(self, hop, side):
        return lax.rem(self.dp + self.n + hop * (2 * side - 1), self.n)

    def copy(self, hop, side, first=False):
        at = self.block(hop, side)
        target = lax.rem(self.dp + self.n + 1 - 2 * side, self.n)
        return remote(
            self.own if first else self.buffer.at[at], self.buffer.at[at],
            self.send_sem.at[hop, side], self.recv_sem.at[hop, side], (target, self.ex),
        )

    def has_next(self, side):
        return (self.dp + 1 < self.n) if side == 0 else (self.dp > 0)

    def start(self):
        for side in range(2):
            @pl.when(self.has_next(side))
            def _():
                self.copy(0, side, True).start()

    def held(self, hop, side):
        return (self.dp > hop) if side == 0 else (self.dp + 1 + hop < self.n)

    def arrive(self, hop, side):
        at = self.block(hop + 1, side)
        remote(
            self.buffer.at[at], self.buffer.at[at], self.send_sem.at[hop, side], self.recv_sem.at[hop, side],
            (self.dp, self.ex),
        ).wait_recv()

        @pl.when(self.has_next(side))
        def _():
            self.copy(hop + 1, side).start()

        return at

    def finish(self):
        for hop in range(self.n - 1):
            for side in range(2):
                mine = self.has_next(side)
                if hop:
                    mine = mine & self.held(hop - 1, side)

                @pl.when(mine)
                def _():
                    self.copy(hop, side, hop == 0).wait_send()


ANY = pl.BlockSpec(memory_space=pl.ANY)
VM = pl.BlockSpec(memory_space=pltpu.VMEM)


def bucket_hot(wide, turn, length):
    at = lax.broadcasted_iota(jnp.int32, (wide, 128), 0) + turn
    offset = jnp.where(at >= wide, at - wide, at) - length
    hit = bucket_of(offset) == lax.broadcasted_iota(jnp.int32, (wide, 128), 1)
    return jnp.where(hit & (jnp.abs(offset) < length), 1.0, 0.0).astype(BF16)


def rows_flat(ref):
    n, ne, rows, columns = ref.shape
    if rows % 16 == 0:
        return ref[...].reshape(n * ne * rows, columns)
    return ref[...].astype(F32).reshape(n * ne * rows, columns).astype(BF16)


def front_kernel(
    n, ne, cap, cap_pad, piece,
    x_in, wq, wk, wv, wo, gain_attn, gain_moe, position_bias, meta_in, wg_in, wu_in, cot_in,
    normed_out, qkv_out, lse_out, mixed_out, resid_out, lq_out, lk_out, lv_out, lwo_out, meta_all, vectors, gains,
    slots, d_outs, wgu,
    x, wg, wu, cot, normed, qkv, lse, mixed, resid, lq, lk, lv, lwo,
    extra, sq, sk, sv, sext, swo, smeta, lext, packed,
    x_all, heads, mixed_in, tiles, cot_all, two_all, two_own, two_rows, cot_rows,
    line_send, line_recv, plane_send, plane_recv, core_send, core_recv, chain_send, chain_recv, own_sem,
    w_send, w_recv, m_send, m_recv, c_send, c_recv, t_send, t_recv,
    pc_send, pc_recv, pt_send, pt_recv, in_sem, out_sem,
):
    dp, ex = lax.axis_index("dp"), lax.axis_index("expert")
    greet(n, ne, dp, ex)
    loads = Copies(in_sem, [(x_in, x), (cot_in, cot), (wg_in, wg), (wu_in, wu)])
    loads.start(0, 1, 2, 3)
    stores = Copies(
        out_sem,
        [
            (normed, normed_out), (qkv, qkv_out), (lse, lse_out), (mixed, mixed_out), (resid, resid_out),
            (lq, lq_out), (lk, lk_out), (lv, lv_out), (lwo, lwo_out),
        ],
    )
    own = sq.shape[2]
    block, width = cot.shape
    pairs_n = own // 128
    slots_n = ne * cap_pad
    n_gain, n_bias = gain_attn.shape[1], position_bias.shape[1]
    line_of = jnp.concatenate(
        [
            gain_attn[...].astype(F32), gain_moe[...].astype(F32), position_bias[...].astype(F32),
            jnp.zeros((1, own - 2 * n_gain - n_bias), F32),
        ],
        axis=1,
    )
    extra[...] = jnp.broadcast_to(line_of, (16, own)).astype(BF16)
    loads.wait(0)
    meet(n, ne)
    chain = Chain(n, dp, ex, x, x_all, chain_send, chain_recv)
    cots = Chain(n, dp, ex, cot, cot_all, c_send, c_recv)
    twos = Chain(n, dp, ex, two_own, two_all, t_send, t_recv)

    def column(ref, t):
        return ref.at[:, pl.ds(pl.multiple_of(t * own, 128), own)]

    def line(kind, d):
        t = lax.rem(dp + d, n)
        src, dst = [
            (column(wq, t), sq.at[dp]), (column(wk, t), sk.at[dp]), (column(wv, t), sv.at[dp]),
            (extra, sext.at[dp]), (wo, swo.at[dp]), (smeta, meta_all.at[dp]),
        ][kind]
        return remote(src, dst, line_send.at[kind, d], line_recv.at[kind, d], (t, ex))

    for d in range(1, n):
        for kind in range(4):
            line(kind, d).start()
    chain.start()
    for d in range(1, n):
        line(4, d).start()
    here = pl.ds(pl.multiple_of(dp * own, 128), own)
    sq[dp] = wq[:, here]
    sk[dp] = wk[:, here]
    sv[dp] = wv[:, here]
    sext[dp] = extra[...]
    swo[dp] = wo[...]
    x_all[dp] = x[...]

    tok = meta_in.shape[1]
    routes = meta_in[...]
    ids = lax.broadcasted_iota(jnp.int32, (ne, tok), 0)
    first = (ids == routes[0:1, :]).astype(F32)
    second = (ids == routes[1:2, :]).astype(F32)
    before = (
        lax.broadcasted_iota(jnp.int32, (tok, tok), 0) < lax.broadcasted_iota(jnp.int32, (tok, tok), 1)
    ).astype(BF16)
    counts = mm((first + second).astype(BF16), before)
    slot_a = jnp.sum(counts * first, axis=0, keepdims=True)
    slot_b = jnp.sum((counts + first) * second, axis=0, keepdims=True)
    asked = routes.astype(F32)
    dest_a = jnp.where(slot_a < cap, asked[0:1, :] * cap_pad + slot_a, -1.0)
    dest_b = jnp.where(slot_b < cap, asked[1:2, :] * cap_pad + slot_b, -1.0)
    gate = asked[2:3, :] * (1.0 / 65536.0)
    smeta[...] = jnp.concatenate([dest_a, dest_b, gate, jnp.zeros((5, tok), F32)], axis=0)
    meta_all[dp] = smeta[...]
    for d in range(1, n):
        line(5, d).start()

    pairs = [(sq, lq), (sk, lk), (sv, lv), (sext, lext), (swo, lwo)]
    partner = ex + 1 - 2 * lax.rem(ex, 2)

    def plane(kind, k):
        src, dst = pairs[kind]
        return remote(
            src, dst.at[:, ex], plane_send.at[kind, k], plane_recv.at[kind, k],
            (dp, lax.rem(ex + 2 * k, ne)),
        )

    def core(kind, k):
        src, dst = pairs[kind]
        at = lax.rem(ex + ne - 2 * k, ne)
        return remote(
            src if k == 0 else dst.at[:, at], dst.at[:, at],
            core_send.at[kind, k], core_recv.at[kind, k], (dp, partner),
        )

    def keep_own(kind):
        return pltpu.make_async_copy(pairs[kind][0], pairs[kind][1].at[:, ex], own_sem.at[kind])

    def spread(kind):
        for d in range(1, n):
            line(kind, d).wait_recv()
        for k in range(1, ne // 2):
            plane(kind, k).start()
        core(kind, 0).start()
        keep_own(kind).start()

    def pass_on(kind):
        for k in range(1, ne // 2):
            plane(kind, k).wait_recv()
            core(kind, k).start()

    def settle(kind):
        keep_own(kind).wait()
        for k in range(ne // 2):
            core(kind, k).wait()
        for k in range(1, ne // 2):
            plane(kind, k).wait_send()

    for kind in range(4):
        spread(kind)

    def to_plane(rows, land, send, recv, group, k):
        peer = lax.rem(ex + k, ne)
        return remote(
            rows.at[group, pl.ds(pl.multiple_of(peer * cap_pad, 16), cap_pad)], land.at[group, ex],
            send.at[group, k], recv.at[group, k], (dp, peer),
        )

    def kept(rows, land, group, sem):
        return pltpu.make_async_copy(
            rows.at[group, pl.ds(pl.multiple_of(ex * cap_pad, 16), cap_pad)], land.at[group, ex], sem.at[group, 0]
        )

    def dispatch(group, tokens, rows, land, send, recv, weigh):
        meta = meta_all[group]
        slot_ids = lax.broadcasted_iota(jnp.int32, (slots_n, block), 0).astype(F32)
        hit_a, hit_b = slot_ids == meta[0:1, :], slot_ids == meta[1:2, :]
        chosen = jnp.where(hit_a | hit_b, 1.0, 0.0).astype(BF16)
        found = mm(chosen, tokens)
        if weigh:
            share = meta[2:3, :]
            factor = jnp.sum(
                jnp.where(hit_a, share, 0.0) + jnp.where(hit_b, 1.0 - share, 0.0), axis=1, keepdims=True
            )
            found = found * factor
        rows[group] = found.astype(BF16)
        for k in range(1, ne):
            to_plane(rows, land, send, recv, group, k).start()
        kept(rows, land, group, send).start()

    def send_cot(group, tokens):
        dispatch(group, tokens, cot_rows, d_outs, pc_send, pc_recv, True)

    def send_two(group, tokens):
        dispatch(group, tokens, two_rows, slots, pt_send, pt_recv, False)

    loads.wait(1)
    send_cot(dp, cot[...])

    def weights(d):
        t = lax.rem(dp + d, n)
        return remote(packed.at[t], wgu.at[dp], w_send.at[d], w_recv.at[d], (t, ex))

    keep_w = pltpu.make_async_copy(packed.at[dp], wgu.at[dp], own_sem.at[5])

    def hop(line_chain, h, then):
        for side in range(2):
            @pl.when(line_chain.held(h, side))
            def _():
                then(line_chain.arrive(h, side))

    def x_hop(h):
        hop(chain, h, lambda at: None)

    def send_weights(early):
        for d in range(1, n):
            t = lax.rem(dp + d, n)
            inside = (t > 0) & (t < n - 1) & ((t == dp + 1) | (t + 1 == dp))

            @pl.when(inside if early else jnp.logical_not(inside))
            def _():
                weights(d).start()

    main = piece // 128 * 128
    step = min(wg.shape[0], 64)

    def pack(i):
        rows = pl.ds(pl.multiple_of(i * step, step), step)
        gate_w, up_w = wg[rows, :], wu[rows, :]
        for j in range(n):
            g = gate_w[:, j * piece : (j + 1) * piece]
            u = up_w[:, j * piece : (j + 1) * piece]
            packed[j, rows, :] = jnp.concatenate([g[:, :main], u[:, :main], g[:, main:], u[:, main:]], axis=1)

    loads.wait(2, 3)
    pl.loop(0, wg.shape[0] // step)(pack)
    x_hop(0)
    spread(4)
    for kind in range(4):
        pass_on(kind)
    if n > 2:
        x_hop(1)
    send_weights(True)
    for kind in range(4):
        settle(kind)
    stores.start(5, 6, 7)

    devices = n * ne
    shared = jnp.max(lext[...].astype(F32), axis=2).reshape(devices, own).astype(BF16)

    def laid_out(first_lane, count, total):
        lanes = lax.broadcasted_iota(jnp.int32, (own, total), 1)
        rows = lax.broadcasted_iota(jnp.int32, (own, total), 0)
        spreading = jnp.where(lax.rem(lanes, count) + first_lane == rows, 1.0, 0.0).astype(BF16)
        everywhere = mm(shared, spreading)
        owner = lax.broadcasted_iota(jnp.int32, (devices, total), 0)
        lane_owner = lax.broadcasted_iota(jnp.int32, (devices, total), 1) // count
        return jnp.sum(jnp.where(owner == lane_owner, everywhere, 0.0), axis=0, keepdims=True)

    gain_one = laid_out(0, n_gain, width)
    gain_two = laid_out(n_gain, n_gain, width)
    gains[...] = jnp.concatenate([gain_one, gain_two, jnp.zeros((6, width), F32)], axis=0)
    entries = HEADS * BUCKETS
    flat = laid_out(2 * n_gain, n_bias, entries)
    lanes = lax.broadcasted_iota(jnp.int32, (8, entries), 1)
    head_of = lax.broadcasted_iota(jnp.int32, (8, entries), 0) + dp * (HEADS // n)
    by_head = jnp.where(lax.rem(lanes, HEADS) == head_of, jnp.broadcast_to(flat, (8, entries)), 0.0).astype(BF16)
    bucket_rows = lax.broadcasted_iota(jnp.int32, (entries, 128), 0) // HEADS
    to_bucket = jnp.where(
        bucket_rows == lax.broadcasted_iota(jnp.int32, (entries, 128), 1), 1.0, 0.0
    ).astype(BF16)
    table = mm(by_head, to_bucket).astype(BF16)
    wide = vectors.shape[1]
    vectors[...] = mm(table, bucket_hot(wide, 0, wide // 2), NT)

    def project(j):
        at = pl.ds(pl.multiple_of(j * block, block), block)
        xf = x_all[j].astype(F32)
        inverse = lax.rsqrt(jnp.mean(xf * xf, axis=-1, keepdims=True) + EPSILON)
        low = (xf * inverse * gains[0:1, :]).astype(BF16)
        normed[at, :] = low
        for w, ref in enumerate((lq, lk, lv)):
            qkv[at, w * own : (w + 1) * own] = mm(low, rows_flat(ref)).astype(BF16)

    project(dp)

    def project_hop(h):
        @pl.loop(0, 2)
        def _(side):
            @pl.when(((side == 0) & (dp > h)) | ((side == 1) & (dp + 1 + h < n)))
            def _():
                project(chain.block(h + 1, side))

    for h in range(n - 2):
        project_hop(h)
    pass_on(4)
    x_hop(n - 2)
    cots.start()
    keep_w.start()
    project_hop(n - 2)
    stores.start(0, 1)

    def attend(pair):
        for side in range(2):
            bias_tile(vectors, 2 * pair + side, tiles.at[side])
        lane = lax.broadcasted_iota(jnp.int32, (block, 128), 1)
        low_half = lane < HEAD_DIM
        k_pair = qkv[:, own + pair * 128 : own + (pair + 1) * 128]
        v_pair = qkv[:, 2 * own + pair * 128 : 2 * own + (pair + 1) * 128]

        @pl.loop(0, n)
        def _(i):
            at = pl.ds(pl.multiple_of(i * block, block), block)
            q_pair = qkv[at, pair * 128 : (pair + 1) * 128]
            outs, logs = [], []
            for side in range(2):
                mask = low_half if side == 0 else jnp.logical_not(low_half)
                logits = logits_of(n, block, i, q_pair, k_pair, mask, tiles.at[side])
                row_max = jnp.max(logits, axis=-1, keepdims=True)
                exponent = jnp.exp(logits - row_max)
                total = jnp.sum(exponent, axis=-1, keepdims=True)
                probs_low = (exponent * (1.0 / total)).astype(BF16)
                outs.append(mm(probs_low, v_pair))
                logs.append(jnp.broadcast_to(row_max + jnp.log(total), (block, 128)))
            heads[at, pair * 128 : (pair + 1) * 128] = jnp.where(low_half, outs[0], outs[1]).astype(BF16)
            lse[at, pair * 128 : (pair + 1) * 128] = jnp.where(low_half, logs[0], logs[1])

    def cot_hop(h):
        hop(cots, h, lambda group: send_cot(group, cot_all[group]))

    for d in range(1, n):
        line(5, d).wait_recv()
    def give(d):
        t = lax.rem(dp + d, n)
        return remote(
            heads.at[pl.ds(pl.multiple_of(t * block, block), block)], mixed_in.at[dp], m_send.at[d], m_recv.at[d],
            (t, ex),
        )

    for pair in range(pairs_n):
        attend(pair)
        if pair == pairs_n - 1:
            for d in range(1, n):
                give(d).start()
    mixed_in[dp] = heads[pl.ds(pl.multiple_of(dp * block, block), block), :]
    settle(4)
    stores.start(8, 2)
    cot_hop(0)
    for d in range(1, n):
        give(d).wait()
    mixed[...] = jnp.concatenate([mixed_in[j] for j in range(n)], axis=1)
    total = x[...].astype(F32) + mm(mixed[...], rows_flat(lwo))
    resid[...] = total
    inverse = lax.rsqrt(jnp.mean(total * total, axis=-1, keepdims=True) + EPSILON)
    two_own[...] = (total * inverse * gains[1:2, :]).astype(BF16)
    twos.start()
    stores.start(3, 4)

    send_two(dp, two_own[...])
    for h in range(1, n - 1):
        cot_hop(h)
    for h in range(n - 1):
        if h == n - 2:
            for to_end in (True, False):
                for d in range(1, n):
                    t = lax.rem(dp + d, n)
                    inside = (t > 0) & (t < n - 1) & ((t == dp + 1) | (t + 1 == dp))
                    end = (t == 0) | (t == n - 1)

                    @pl.when(jnp.logical_not(inside) & (end if to_end else jnp.logical_not(end)))
                    def _():
                        weights(d).start()

        hop(twos, h, lambda group: send_two(group, two_all[group]))
    stores.wait(*range(9))
    chain.finish()
    cots.finish()
    twos.finish()
    for d in range(1, n):
        for kind in range(6):
            line(kind, d).wait_send()
    keep_w.wait()
    for d in range(1, n):
        weights(d).wait()
    for rows, land, send, recv in (
        (two_rows, slots, pt_send, pt_recv), (cot_rows, d_outs, pc_send, pc_recv),
    ):
        @pl.loop(0, n)
        def _(group):
            kept(rows, land, group, send).wait()
            for k in range(1, ne):
                to_plane(rows, land, send, recv, group, k).wait()


def front(n, ne, cap, cap_pad, x, wq, wk, wv, wo, gain_attn, gain_moe, position_bias, meta_in, wg, wu, cot):
    tok, width = x.shape
    wrows = wq.shape[0]
    own = width // n
    piece = wg.shape[1] // n
    wide = 2 * n * tok
    slots_n = ne * cap_pad
    sem = pltpu.SemaphoreType.DMA
    shape = jax.ShapeDtypeStruct
    return pl.pallas_call(
        functools.partial(front_kernel, n, ne, cap, cap_pad, piece),
        in_specs=[ANY] + [VM] * 8 + [ANY] * 3,
        out_specs=[ANY] * 9 + [VM] * 3 + [ANY] * 3,
        out_shape=[
            shape((n * tok, width), BF16),
            shape((n * tok, 3 * own), BF16),
            shape((n * tok, own), F32),
            shape((tok, width), BF16),
            shape((tok, width), F32),
            shape((n, ne, wrows, own), BF16),
            shape((n, ne, wrows, own), BF16),
            shape((n, ne, wrows, own), BF16),
            shape((n, ne, wrows, width), BF16),
            shape((n, 8, tok), F32),
            shape((8, wide), F32),
            shape((8, width), F32),
            shape((n, ne, cap_pad, width), BF16),
            shape((n, ne, cap_pad, width), BF16),
            shape((n, tok, 2 * piece), BF16),
        ],
        scratch_shapes=[
            pltpu.VMEM((tok, width), BF16),
            pltpu.VMEM(wg.shape, BF16),
            pltpu.VMEM(wu.shape, BF16),
            pltpu.VMEM((tok, width), BF16),
            pltpu.VMEM((n * tok, width), BF16),
            pltpu.VMEM((n * tok, 3 * own), BF16),
            pltpu.VMEM((n * tok, own), F32),
            pltpu.VMEM((tok, width), BF16),
            pltpu.VMEM((tok, width), F32),
            pltpu.VMEM((n, ne, wrows, own), BF16),
            pltpu.VMEM((n, ne, wrows, own), BF16),
            pltpu.VMEM((n, ne, wrows, own), BF16),
            pltpu.VMEM((n, ne, wrows, width), BF16),
            pltpu.VMEM((16, own), BF16),
            pltpu.VMEM((n, wrows, own), BF16),
            pltpu.VMEM((n, wrows, own), BF16),
            pltpu.VMEM((n, wrows, own), BF16),
            pltpu.VMEM((n, 16, own), BF16),
            pltpu.VMEM((n, wrows, width), BF16),
            pltpu.VMEM((8, tok), F32),
            pltpu.VMEM((n, ne, 16, own), BF16),
            pltpu.VMEM((n, tok, 2 * piece), BF16),
            pltpu.VMEM((n, tok, width), BF16),
            pltpu.VMEM((n * tok, own), BF16),
            pltpu.VMEM((n, tok, own), BF16),
            pltpu.VMEM((2, tok, wide), F32),
            pltpu.VMEM((n, tok, width), BF16),
            pltpu.VMEM((n, tok, width), BF16),
            pltpu.VMEM((tok, width), BF16),
            pltpu.VMEM((n, slots_n, width), BF16),
            pltpu.VMEM((n, slots_n, width), BF16),
            sem((6, n)), sem((6, n)),
            sem((5, ne // 2)), sem((5, ne // 2)), sem((5, ne // 2)), sem((5, ne // 2)),
            sem((n, 2)), sem((n, 2)), sem((6,)),
            sem((n,)), sem((n,)), sem((n,)), sem((n,)),
            sem((n, 2)), sem((n, 2)), sem((n, 2)), sem((n, 2)),
            sem((n, ne)), sem((n, ne)), sem((n, ne)), sem((n, ne)), sem((4,)), sem((9,)),
        ],
        compiler_params=pltpu.CompilerParams(
            collective_id=1, has_side_effects=True, vmem_limit_bytes=60 * 1024 * 1024
        ),
        name="front",
    )(x, wq, wk, wv, wo, gain_attn, gain_moe, position_bias, meta_in, wg, wu, cot)


def experts_kernel(
    n, ne, cap_pad, deep, main,
    slots, d_outs, wgu_in, wd_in, meta_all,
    out_rows, d_two, gwgu_out, gwd_out,
    wgu_ref, gwgu, gwd, wd_ref, s_buf, d_buf, back, part, landed, gwgu_acc,
    load_sem, keep_sem, p_send, p_recv, z_send, z_recv, wd_sem,
):
    dp, ex = lax.axis_index("dp"), lax.axis_index("expert")
    slots_n, width = s_buf.shape[1:]
    tok = d_two.shape[0]
    greet(n, ne, dp, ex)
    toward = 2 * ((2 * dp) // n) - 1

    def group_at(step):
        return lax.rem(dp + n + toward * (1 + step), n)

    def load(step, kind):
        at = group_at(step)
        src, dst = ((slots, s_buf), (d_outs, d_buf))[kind]
        return pltpu.make_async_copy(src.at[at], dst.at[at], load_sem.at[kind, step])

    whole = Copies(
        wd_sem,
        [(wgu_in, wgu_ref), (wd_in, wd_ref.at[pl.ds(0, deep)]), (gwgu, gwgu_out), (gwd, gwd_out)],
    )
    whole.start(0, 1)
    for step in range(n):
        for kind in range(2):
            load(step, kind).start()
    wd_ref[deep:, :] = jnp.zeros((wd_ref.shape[0] - deep, width), BF16)
    gwgu_acc[...] = jnp.zeros_like(gwgu_acc)
    gwd[...] = jnp.zeros_like(gwd)
    whole.wait(0, 1)
    meet(n, ne)

    def rows_of(peer):
        return pl.ds(pl.multiple_of(peer * cap_pad, 16), cap_pad)

    def give(at, k):
        peer = lax.rem(ex + k, ne)
        return remote(
            d_buf.at[at, rows_of(peer)], back.at[at, rows_of(ex)], p_send.at[at, k], p_recv.at[at, k], (dp, peer)
        )

    def take(at, k):
        peer = lax.rem(ex + ne - k, ne)
        return remote(
            d_buf.at[at, rows_of(ex)], back.at[at, rows_of(peer)], p_send.at[at, k], p_recv.at[at, k], (dp, peer)
        )

    def keep(at):
        return pltpu.make_async_copy(s_buf.at[at], out_rows.at[at], keep_sem.at[at])

    def owed(at):
        return remote(part.at[at], landed.at[dp], z_send.at[at], z_recv.at[dp], (at, ex))

    def combine(at):
        for k in range(1, ne):
            take(at, k).wait_recv()
        meta = meta_all[at]
        ids = lax.broadcasted_iota(jnp.int32, (slots_n, tok), 0).astype(F32)
        hit = (ids == meta[0:1, :]) | (ids == meta[1:2, :])
        return mm(jnp.where(hit, 1.0, 0.0).astype(BF16), back[at], TN)

    @pl.loop(0, n)
    def _(step):
        at = group_at(step)
        for kind in range(2):
            load(step, kind).wait()
        wgu, wd = wgu_ref[...], wd_ref[...]
        parts = -(-slots_n // 640)
        size = slots_n // parts
        low_lane = lax.broadcasted_iota(jnp.int32, (size, 128), 1) < 64
        for p in range(parts):
            here = slice(p * size, (p + 1) * size)
            rows, d_out = s_buf[at, here, :], d_buf[at, here, :]
            pre = mm(rows, wgu)
            d_hidden = mm(d_out, wd, NT)
            gate, up, tail = pre[:, :main], pre[:, main : 2 * main], pre[:, 2 * main :]
            tail_up = pltpu.roll(tail, 64, 1)
            act, slope = gelu_pair(gate)
            act_t, slope_t = gelu_pair(tail)
            hidden_t = jnp.where(low_lane, act_t * tail_up, 0.0)
            hidden = jnp.concatenate([(act * up).astype(BF16), hidden_t.astype(BF16)], axis=1)
            dh, dh_t = d_hidden[:, :main], d_hidden[:, main:]
            d_gate = dh * up * slope
            d_up = dh * act
            d_tail = jnp.where(low_lane, dh_t * tail_up * slope_t, pltpu.roll(dh_t * act_t, 64, 1))
            d_pre = jnp.concatenate([d_gate.astype(BF16), d_up.astype(BF16), d_tail.astype(BF16)], axis=1)
            d_rows = mm(d_pre, wgu, NT).astype(BF16)
            gwd[...] += mm(hidden, d_out, TN)[:deep]
            d_buf[at, here, :] = d_rows
            if p == parts - 1:
                for k in range(1, ne):
                    give(at, k).start()
                back[at, rows_of(ex), :] = d_buf[at, rows_of(ex), :]
            gwgu_acc[...] += mm(rows, d_pre, TN)
            s_buf[at, here, :] = mm(hidden, wd).astype(BF16)
        keep(at).start()

        @pl.when(step > 0)
        def _():
            past = group_at(step - 1)
            part[past] = combine(past).astype(BF16)
            owed(past).start()

    gwgu[...] = gwgu_acc[...].astype(BF16)
    whole.start(2, 3)
    total = combine(dp)
    for d in range(1, n):
        src = lax.rem(dp + d, n)
        remote(part.at[src], landed.at[src], z_send.at[src], z_recv.at[src], (src, ex)).wait_recv()
        total = total + landed[src].astype(F32)
    d_two[...] = total
    whole.wait(2, 3)
    for d in range(1, n):
        owed(lax.rem(dp + d, n)).wait_send()

    @pl.loop(0, n)
    def _(at):
        keep(at).wait()
        for k in range(1, ne):
            give(at, k).wait_send()


def experts(n, ne, cap_pad, deep, slots, d_outs, wgu, wd, meta_all):
    width, columns = wgu.shape
    tok = meta_all.shape[2]
    main = (columns - 128) // 2
    slots_n = ne * cap_pad
    slots = slots.reshape(n, slots_n, width)
    d_outs = d_outs.reshape(n, slots_n, width)
    sem = pltpu.SemaphoreType.DMA
    return pl.pallas_call(
        functools.partial(experts_kernel, n, ne, cap_pad, deep, main),
        in_specs=[ANY, ANY, ANY, ANY, VM],
        out_specs=[ANY, VM, ANY, ANY],
        out_shape=[
            jax.ShapeDtypeStruct((n, slots_n, width), BF16),
            jax.ShapeDtypeStruct((tok, width), F32),
            jax.ShapeDtypeStruct((width, columns), BF16),
            jax.ShapeDtypeStruct((deep, width), F32),
        ],
        scratch_shapes=[
            pltpu.VMEM((width, columns), BF16),
            pltpu.VMEM((width, columns), BF16),
            pltpu.VMEM((deep, width), F32),
            pltpu.VMEM((-(-deep // 128) * 128, width), BF16),
            pltpu.VMEM((n, slots_n, width), BF16),
            pltpu.VMEM((n, slots_n, width), BF16),
            pltpu.VMEM((n, slots_n, width), BF16),
            pltpu.VMEM((n, tok, width), BF16),
            pltpu.VMEM((n, tok, width), BF16),
            pltpu.VMEM((width, columns), F32),
            sem((2, n)), sem((n,)), sem((n, ne)), sem((n, ne)), sem((n,)), sem((n,)), sem((4,)),
        ],
        compiler_params=pltpu.CompilerParams(
            collective_id=3, has_side_effects=True, vmem_limit_bytes=60 * 1024 * 1024
        ),
        name="experts",
    )(slots, d_outs, wgu, wd, meta_all)


def backward_kernel(
    n, ne, cap_pad,
    gains, vectors, meta_all,
    d_two_in, resid_in, cot_in, wo_in, x_in, mixed_in, qkv_in, lse_in, normed_in, wq_in, wk_in, wv_in,
    gwgu, out_rows,
    block_out, grad_in, g_all, small_all, gw_in, out_in,
    d_two, resid, cot, wo, x, mixed, qkv, lse, normed, wq, wk, wv,
    dm, dm_in, tiles, sums, dq_s, dk_s, dv_s, dk_acc, dv_acc, diag, d_res,
    dn_part, dn_land, moe_part, moe_land, out_one,
    g_send, g_land, g2_send, g2_land, o_send, o_land, o2_send, o2_land,
    small_own, small_land, small_sum,
    out_s, out_r, w_s, w_r, dm_s, dm_r, dn_s, dn_r, moe_s, moe_r, g_s, g_r, o_s, o_r, g2_s, g2_r, o2_s, o2_r,
    sp_s, sp_r, sz_s, sz_r, keep_sem, in_sem,
):
    dp, ex = lax.axis_index("dp"), lax.axis_index("expert")
    tok, width = cot.shape
    own = dq_s.shape[1]
    pairs_n = own // 128
    slots_n = ne * cap_pad
    wrows = g_all.shape[1]
    greet(n, ne, dp, ex)
    loads = Copies(
        in_sem,
        [
            (d_two_in, d_two), (resid_in, resid), (cot_in, cot), (wo_in, wo), (x_in, x), (mixed_in, mixed),
            (qkv_in, qkv), (lse_in, lse), (normed_in, normed), (wq_in, wq), (wk_in, wk), (wv_in, wv),
        ],
    )
    loads.start(0, 1, 2, 3, 5, 6, 7, 9, 10, 11, 8, 4)
    toward = 2 * ((2 * dp) // n) - 1

    def group_at(step):
        return lax.rem(dp + n + toward * (1 + step), n)

    def rows_of(peer):
        return pl.ds(pl.multiple_of(peer * cap_pad, 16), cap_pad)

    def to_line(src, dst, send, recv, t):
        return remote(src.at[t], dst.at[dp], send.at[t], recv.at[dp], (t, ex))

    def from_line(src, dst, send, recv, t):
        return remote(src.at[t], dst.at[t], send.at[t], recv.at[t], (t, ex))

    def to_plane(src, dst, send, recv, k):
        return remote(src, dst.at[ex], send.at[k], recv.at[k], (dp, lax.rem(ex + k, ne)))

    def from_plane(src, dst, send, recv, k):
        peer = lax.rem(ex + ne - k, ne)
        return remote(src, dst.at[peer], send.at[k], recv.at[k], (dp, peer))

    def out_give(at, k):
        peer = lax.rem(ex + k, ne)
        return remote(
            out_rows.at[at, rows_of(peer)], out_in.at[at, rows_of(ex)], out_s.at[at, k], out_r.at[at, k], (dp, peer)
        )

    def out_take(at, k):
        peer = lax.rem(ex + ne - k, ne)
        return remote(
            out_rows.at[at, rows_of(ex)], out_in.at[at, rows_of(peer)], out_s.at[at, k], out_r.at[at, k], (dp, peer)
        )

    def out_keep(at):
        return pltpu.make_async_copy(out_rows.at[at, rows_of(ex)], out_in.at[at, rows_of(ex)], out_s.at[at, 0])

    loads.wait(0, 1, 2)
    values = resid[...]
    d_normed = d_two[...]
    inverse = lax.rsqrt(jnp.mean(values * values, axis=-1, keepdims=True) + EPSILON)
    scaled = gains[1:2, :] * d_normed
    gain_rows_two = jnp.sum(d_normed * values * inverse, axis=0, keepdims=True)
    mean = jnp.mean(scaled * values, axis=-1, keepdims=True)
    d_resid = cot[...].astype(F32) + inverse * scaled - values * (inverse * inverse * inverse * mean)
    d_res[...] = d_resid
    d_attn = d_resid.astype(BF16)
    loads.wait(3)
    d_mixed = mm(d_attn, wo[...], NT).astype(BF16)
    meet(n, ne)
    for j in range(n):
        dm[j] = d_mixed[:, j * own : (j + 1) * own]
    for d in range(1, n):
        to_line(dm, dm_in, dm_s, dm_r, lax.rem(dp + d, n)).start()
    dm_in[dp] = dm[dp]
    for d in range(1, n):
        to_line(gwgu, gw_in, w_s, w_r, lax.rem(dp + d, n)).start()
    keep_w = pltpu.make_async_copy(gwgu.at[dp], gw_in.at[dp], keep_sem.at[0])
    keep_w.start()

    @pl.loop(0, n)
    def _(step):
        at = group_at(step)
        for k in range(1, ne):
            out_give(at, k).start()
        out_keep(at).start()

    loads.wait(5)
    o_send[...] = mm(mixed[...], d_attn, TN).reshape(n, ne, wrows, width).astype(BF16)
    for k in range(1, ne):
        to_plane(o_send.at[:, lax.rem(ex + k, ne)], o_land, o_s, o_r, k).start()
    o_land[ex] = o_send[:, ex]
    for i in range(width // 128):
        small_own[8 + i : 9 + i, :] = gain_rows_two[:, i * 128 : (i + 1) * 128]
    for d in range(1, n):
        from_line(dm, dm_in, dm_s, dm_r, lax.rem(dp + d, n)).wait_recv()

    def sum_copy(part, land, send, recv, r, side):
        t = lax.rem(dp + n + (n - r) * (1 - 2 * side), n)
        target = lax.rem(dp + n + 1 - 2 * side, n)
        return t, remote(part.at[t], land.at[r - 1, side], send.at[r - 1, side], recv.at[r - 1, side], (target, ex))

    def takes_part(r, side):
        return ((side == 0) & (dp < r) & (dp + 1 < n)) | ((side == 1) & (dp + r >= n) & (dp > 0))

    def is_fed(r, side):
        return ((side == 0) & (dp > 0) & (r > 1)) | ((side == 1) & (dp + 1 < n) & (r > 1))

    def fed(part, land, send, recv, r, side):
        remote(
            part.at[dp], land.at[r - 1, side], send.at[r - 1, side], recv.at[r - 1, side], (dp, ex)
        ).wait_recv()

    def sum_round(part, land, send, recv, term, r):
        @pl.loop(0, 2)
        def _(side):
            @pl.when(takes_part(r, side))
            def _():
                t, copy = sum_copy(part, land, send, recv, r, side)
                mine = term(t)

                @pl.when(is_fed(r, side))
                def _():
                    fed(part, land, send, recv, r - 1, side)
                    part[t] = (mine + land[max(r - 2, 0), side].astype(F32)).astype(BF16)

                @pl.when(jnp.logical_not(is_fed(r, side)))
                def _():
                    part[t] = mine.astype(BF16)

                copy.start()

    def sum_end(part, land, send, recv, mine):
        @pl.when(dp > 0)
        def _():
            fed(part, land, send, recv, n - 1, 0)

        @pl.when(dp + 1 < n)
        def _():
            fed(part, land, send, recv, n - 1, 1)

        left = jnp.where(dp > 0, land[n - 2, 0].astype(F32), 0.0)
        right = jnp.where(dp + 1 < n, land[n - 2, 1].astype(F32), 0.0)
        return mine + left + right

    def sum_sent(part, land, send, recv):
        for r in range(1, n):
            for side in range(2):
                @pl.when(takes_part(r, side))
                def _():
                    sum_copy(part, land, send, recv, r, side)[1].wait_send()

    dn = (dn_part, dn_land, dn_s, dn_r)
    moes = (moe_part, moe_land, moe_s, moe_r)
    def moe(at):
        for k in range(1, ne):
            out_take(at, k).wait_recv()
        out_keep(at).wait()
        load = pltpu.make_async_copy(out_in.at[at], out_one, keep_sem.at[1])
        load.start()
        meta = meta_all[at]
        ids = lax.broadcasted_iota(jnp.int32, (slots_n, tok), 0).astype(F32)
        gate = meta[2:3, :]
        weight = jnp.where(ids == meta[0:1, :], gate, 0.0) + jnp.where(ids == meta[1:2, :], 1.0 - gate, 0.0)
        load.wait()
        return mm(weight.astype(BF16), out_one[...], TN)

    loads.wait(6, 7, 9, 10, 11)
    lane = lax.broadcasted_iota(jnp.int32, (tok, 128), 1)
    low_half = lane < HEAD_DIM
    key_low = lax.broadcasted_iota(jnp.int32, (n * tok, 128), 1) < HEAD_DIM
    diag[...] = jnp.zeros_like(diag)
    for pair in range(pairs_n):
        cols = slice(pair * 128, (pair + 1) * 128)
        for side in range(2):
            bias_tile(vectors, 2 * pair + side, tiles.at[side])
        sums[...] = jnp.zeros_like(sums)
        dk_acc[...] = jnp.zeros_like(dk_acc)
        dv_acc[...] = jnp.zeros_like(dv_acc)
        k_pair = qkv[:, own + pair * 128 : own + (pair + 1) * 128]
        v_pair = qkv[:, 2 * own + pair * 128 : 2 * own + (pair + 1) * 128]

        @pl.loop(0, n)
        def _(i):
            at = pl.ds(pl.multiple_of(i * tok, tok), tok)
            q_pair = qkv[at, cols]
            dm_pair = dm_in[i, :, cols]
            dqs, dks, dvs = [], [], []
            for side in range(2):
                mask = low_half if side == 0 else jnp.logical_not(low_half)
                logits = logits_of(n, tok, i, q_pair, k_pair, mask, tiles.at[side])
                first = pair * 128 + side * HEAD_DIM
                probs = jnp.exp(logits - lse[at, first : first + 1])
                d_probs = mm(jnp.where(mask, dm_pair, jnp.zeros_like(dm_pair)), v_pair, NT)
                inner = jnp.sum(probs * d_probs, axis=-1, keepdims=True)
                d_logits = (probs * (d_probs - inner)).astype(BF16)
                dvs.append(mm(probs.astype(BF16), dm_pair, TN))
                dqs.append(mm(d_logits, k_pair))
                dks.append(mm(d_logits, q_pair, TN))
                wide = d_logits.astype(F32)
                for j in range(n):
                    here = pl.ds(tile_offset(n, tok, i, j), tok)
                    sums[side, :, here] += wide[:, j * tok : (j + 1) * tok]
            dq_s[at, cols] = (jnp.where(low_half, dqs[0], dqs[1]) * SCALE).astype(BF16)
            dk_acc[...] += jnp.where(key_low, dks[0], dks[1])
            dv_acc[...] += jnp.where(key_low, dvs[0], dvs[1])

        dk_s[:, cols] = (dk_acc[...] * SCALE).astype(BF16)
        dv_s[:, cols] = dv_acc[...].astype(BF16)
        for side in range(2):
            diag[2 * pair + side : 2 * pair + side + 1, :] = diagonal_sum(sums[side])

    def d_norm(t):
        at = pl.ds(pl.multiple_of(t * tok, tok), tok)
        return mm(dq_s[at, :], wq[...], NT) + mm(dk_s[at, :], wk[...], NT) + mm(dv_s[at, :], wv[...], NT)

    sum_round(*dn, d_norm, 1)
    sum_round(*moes, moe, 1)

    loads.wait(8, 4)
    for w, ref in enumerate((dq_s, dk_s, dv_s)):
        g_send[:, :, w] = mm(normed[...], ref[...], TN).reshape(n, ne, wrows, own).astype(BF16)
    for k in range(1, ne):
        to_plane(g_send.at[:, lax.rem(ex + k, ne)], g_land, g_s, g_r, k).start()
    g_land[ex] = g_send[:, ex]

    for r in range(2, n):
        sum_round(*dn, d_norm, r)
        sum_round(*moes, moe, r)

    rest = diag[...]
    table = jnp.zeros((8, 128), F32)
    wide = vectors.shape[1]
    hot = bucket_hot(wide, tok, wide // 2)
    for _ in range(3):
        piece = rest.astype(BF16)
        table = table + mm(piece, hot)
        rest = rest - piece.astype(F32)
    small_own[16:24, :] = table

    for k in range(1, ne):
        from_plane(o_send.at[:, ex], o_land, o_s, o_r, k).wait_recv()
    total = o_land[0].astype(F32)
    for e in range(1, ne):
        total = total + o_land[e].astype(F32)
    o2_send[...] = total.astype(BF16)
    for d in range(1, n):
        to_line(o2_send, o2_land, o2_s, o2_r, lax.rem(dp + d, n)).start()
    o2_land[dp] = o2_send[dp]

    for k in range(1, ne):
        from_plane(g_send.at[:, ex], g_land, g_s, g_r, k).wait_recv()
    total = g_land[0].astype(F32)
    for e in range(1, ne):
        total = total + g_land[e].astype(F32)
    g2_send[...] = total.astype(BF16)
    for d in range(1, n):
        to_line(g2_send, g2_land, g2_s, g2_r, lax.rem(dp + d, n)).start()
    g2_land[dp] = g2_send[dp]

    total = sum_end(*dn, d_norm(dp))
    values = x[...].astype(F32)
    inverse = lax.rsqrt(jnp.mean(values * values, axis=-1, keepdims=True) + EPSILON)
    scaled = gains[0:1, :] * total
    gain_rows_one = jnp.sum(total * values * inverse, axis=0, keepdims=True)
    mean = jnp.mean(scaled * values, axis=-1, keepdims=True)
    grad_in[...] = (d_res[...] + inverse * scaled - values * (inverse * inverse * inverse * mean)).astype(BF16)
    for i in range(width // 128):
        small_own[i : i + 1, :] = gain_rows_one[:, i * 128 : (i + 1) * 128]
    for k in range(1, ne):
        to_plane(small_own, small_land, sp_s, sp_r, k).start()
    small_land[ex] = small_own[...]
    for k in range(1, ne):
        from_plane(small_own, small_land, sp_s, sp_r, k).wait_recv()
    total = small_land[0]
    for e in range(1, ne):
        total = total + small_land[e]
    small_sum[...] = total
    for d in range(1, n):
        t = lax.rem(dp + d, n)
        remote(small_sum, small_all.at[dp], sz_s.at[t], sz_r.at[dp], (t, ex)).start()
    small_all[dp] = total

    block_out[...] = sum_end(*moes, resid[...] + moe(dp)).astype(BF16)

    for d in range(1, n):
        t = lax.rem(dp + d, n)
        from_line(o2_send, o2_land, o2_s, o2_r, t).wait_recv()
        from_line(g2_send, g2_land, g2_s, g2_r, t).wait_recv()
        remote(small_sum, small_all.at[t], sz_s.at[t], sz_r.at[t], (t, ex)).wait_recv()
    total = o2_land[0].astype(F32)
    for j in range(1, n):
        total = total + o2_land[j].astype(F32)
    g_all[3] = total
    for w in range(3):
        g_all[w] = jnp.concatenate([g2_land[j, w] for j in range(n)], axis=1).astype(F32)
    for d in range(1, n):
        t = lax.rem(dp + d, n)
        from_line(gwgu, gw_in, w_s, w_r, t).wait_recv()
        for src, dst, send, recv in (
            (gwgu, gw_in, w_s, w_r), (dm, dm_in, dm_s, dm_r),
            (o2_send, o2_land, o2_s, o2_r), (g2_send, g2_land, g2_s, g2_r),
        ):
            to_line(src, dst, send, recv, t).wait_send()
        remote(small_sum, small_all.at[dp], sz_s.at[t], sz_r.at[dp], (t, ex)).wait_send()
    keep_w.wait()
    sum_sent(*dn)
    sum_sent(*moes)
    for k in range(1, ne):
        to_plane(o_send.at[:, ex], o_land, o_s, o_r, k).wait_send()
        to_plane(g_send.at[:, ex], g_land, g_s, g_r, k).wait_send()
        to_plane(small_own, small_land, sp_s, sp_r, k).wait_send()

    @pl.loop(0, n)
    def _(at):
        for k in range(1, ne):
            out_give(at, k).wait_send()


def backward(
    n, ne, cap_pad, wrows, d_two, resid, cot, x, gains, mixed, wo, qkv, lse, normed, vectors,
    wq, wk, wv, meta_all, gwgu, out_rows,
):
    tok, width = cot.shape
    own = wq.shape[1]
    wide = vectors.shape[1]
    both = gwgu.shape[2]
    slots_n = ne * cap_pad
    length = n * tok
    sem = pltpu.SemaphoreType.DMA
    shape = jax.ShapeDtypeStruct
    return pl.pallas_call(
        functools.partial(backward_kernel, n, ne, cap_pad),
        in_specs=[VM] * 3 + [ANY] * 14,
        out_specs=[VM] * 4 + [ANY] * 2,
        out_shape=[
            shape((tok, width), BF16),
            shape((tok, width), BF16),
            shape((4, wrows, width), F32),
            shape((n, 24, 128), F32),
            shape((n, tok, both), BF16),
            shape((n, slots_n, width), BF16),
        ],
        scratch_shapes=[
            pltpu.VMEM((tok, width), F32),
            pltpu.VMEM((tok, width), F32),
            pltpu.VMEM((tok, width), BF16),
            pltpu.VMEM((width, width), BF16),
            pltpu.VMEM((tok, width), BF16),
            pltpu.VMEM((tok, width), BF16),
            pltpu.VMEM((length, 3 * own), BF16),
            pltpu.VMEM((length, own), F32),
            pltpu.VMEM((length, width), BF16),
            pltpu.VMEM((width, own), BF16),
            pltpu.VMEM((width, own), BF16),
            pltpu.VMEM((width, own), BF16),
            pltpu.VMEM((n, tok, own), BF16),
            pltpu.VMEM((n, tok, own), BF16),
            pltpu.VMEM((2, tok, wide), F32),
            pltpu.VMEM((2, tok, wide), F32),
            pltpu.VMEM((length, own), BF16),
            pltpu.VMEM((length, own), BF16),
            pltpu.VMEM((length, own), BF16),
            pltpu.VMEM((length, 128), F32),
            pltpu.VMEM((length, 128), F32),
            pltpu.VMEM((8, wide), F32),
            pltpu.VMEM((tok, width), F32),
            pltpu.VMEM((n, tok, width), BF16),
            pltpu.VMEM((n - 1, 2, tok, width), BF16),
            pltpu.VMEM((n, tok, width), BF16),
            pltpu.VMEM((n - 1, 2, tok, width), BF16),
            pltpu.VMEM((slots_n, width), BF16),
            pltpu.VMEM((n, ne, 3, wrows, own), BF16),
            pltpu.VMEM((ne, n, 3, wrows, own), BF16),
            pltpu.VMEM((n, 3, wrows, own), BF16),
            pltpu.VMEM((n, 3, wrows, own), BF16),
            pltpu.VMEM((n, ne, wrows, width), BF16),
            pltpu.VMEM((ne, n, wrows, width), BF16),
            pltpu.VMEM((n, wrows, width), BF16),
            pltpu.VMEM((n, wrows, width), BF16),
            pltpu.VMEM((24, 128), F32),
            pltpu.VMEM((ne, 24, 128), F32),
            pltpu.VMEM((24, 128), F32),
            sem((n, ne)), sem((n, ne)), sem((n,)), sem((n,)), sem((n,)), sem((n,)), sem((n, 2)), sem((n, 2)),
            sem((n, 2)), sem((n, 2)), sem((ne,)), sem((ne,)), sem((ne,)), sem((ne,)), sem((n,)), sem((n,)),
            sem((n,)), sem((n,)), sem((ne,)), sem((ne,)), sem((n,)), sem((n,)), sem((2,)), sem((12,)),
        ],
        compiler_params=pltpu.CompilerParams(
            collective_id=4, has_side_effects=True, vmem_limit_bytes=60 * 1024 * 1024
        ),
        name="backward",
    )(
        gains, vectors, meta_all, d_two, resid, cot, wo, x, mixed, qkv, lse, normed, wq, wk, wv, gwgu, out_rows
    )


def split_pieces(value):
    pieces = []
    for _ in range(3):
        piece = value.astype(BF16)
        pieces.append(piece)
        value = value - piece.astype(F32)
    return pieces


def finish_kernel(
    n, ne, heads_own, piece, blocks, g_all, small, out_in, grad_in, gwd_in,
    gate_ref, up_ref, gq, gk, gv, go, gain_one, gain_two, bias, block_out, grad_out, gwd,
):
    main = piece // 128 * 128
    rest = piece - main
    gates, ups = [], []
    for j in range(n):
        block = blocks[j].astype(F32)
        gates += [block[:, :main], block[:, 2 * main : 2 * main + rest]]
        ups += [block[:, main : 2 * main], block[:, 2 * main + rest :]]
    gate_ref[...] = jnp.concatenate(gates, axis=1)
    up_ref[...] = jnp.concatenate(ups, axis=1)
    block_out[...] = out_in[...]
    grad_out[...] = grad_in[...]
    gwd[...] = gwd_in[...]

    @pl.when(pl.program_id(0) == 0)
    def _():
        for i, ref in enumerate((gq, gk, gv, go)):
            ref[...] = g_all[i]
        me = lax.axis_index("dp") * ne + lax.axis_index("expert")
        total = small[0, :16]
        for j in range(1, n):
            total = total + small[j, :16]
        rows = lax.broadcasted_iota(jnp.int32, (8, 128), 0)
        lanes = lax.broadcasted_iota(jnp.int32, (8, 128), 1)
        for i, ref in enumerate((gain_one, gain_two)):
            count = ref.shape[1]
            at = me * count
            row = jnp.sum(jnp.where(rows == at // 128, total[8 * i : 8 * i + 8], 0.0), axis=0, keepdims=True)
            row = jnp.broadcast_to(row, (8, 128))
            ref[...] = pltpu.roll(row, lax.rem(128 - lax.rem(at, 128), 128), 1)[:1, :count]
        table = jnp.concatenate([small[j, 16 : 16 + heads_own] for j in range(n)], axis=0)
        heads = n * heads_own
        count = bias.shape[1]
        at = me * count
        table = jnp.concatenate([table, jnp.zeros((128 - heads, 128), F32)], axis=0)
        hot = jnp.where(lanes == at // heads, 1.0, 0.0).astype(BF16)
        row = sum(mm(hot, part, NT) for part in split_pieces(table))
        bias[...] = pltpu.roll(row, lax.rem(128 - lax.rem(at, heads), 128), 1)[:1, :count]


def finish(n, ne, heads_own, n_gain, n_bias, blocks, g_all, small, block_out, grad_in, gwd):
    tok, both = blocks.shape[1:]
    wrows, width = g_all.shape[1:]
    deep = gwd.shape[0]
    piece = both // 2
    steps = 4
    step, part = tok // steps, deep // steps
    total = n * piece
    shape = jax.ShapeDtypeStruct
    fixed2 = lambda i: (0, 0)
    fixed3 = lambda i: (0, 0, 0)
    move = lambda i: (i, 0)
    return pl.pallas_call(
        functools.partial(finish_kernel, n, ne, heads_own, piece),
        grid=(steps,),
        in_specs=[
            pl.BlockSpec((n, step, both), lambda i: (0, i, 0)),
            pl.BlockSpec((4, wrows, width), fixed3),
            pl.BlockSpec(small.shape, fixed3),
            pl.BlockSpec((step, width), move),
            pl.BlockSpec((step, width), move),
            pl.BlockSpec((part, width), move),
        ],
        out_specs=[pl.BlockSpec((step, total), move)] * 2
        + [pl.BlockSpec((wrows, width), fixed2)] * 4
        + [pl.BlockSpec((1, n_gain), fixed2)] * 2
        + [pl.BlockSpec((1, n_bias), fixed2)]
        + [pl.BlockSpec((step, width), move)] * 2
        + [pl.BlockSpec((part, width), move)],
        out_shape=[shape((tok, total), F32)] * 2
        + [shape((wrows, width), F32)] * 4
        + [shape((1, n_gain), F32)] * 2
        + [shape((1, n_bias), F32)]
        + [shape((tok, width), BF16)] * 2
        + [shape((deep, width), F32)],
        compiler_params=pltpu.CompilerParams(vmem_limit_bytes=VMEM_LIMIT),
        name="finish",
    )(blocks, g_all, small, block_out, grad_in, gwd)


def local(
    inputs, cotangent, gain_attn, w_query, w_key, w_value, w_out, position_bias,
    gain_moe, w_gate, w_up, w_down, routes, gate_fixed,
):
    n = lax.axis_size("dp")
    experts_n = lax.axis_size("expert")
    dp = lax.axis_index("dp")
    ex = lax.axis_index("expert")
    tok, width = inputs.shape[1:]
    length = n * tok
    own = HEADS * HEAD_DIM // n
    heads_own = HEADS // n
    wrows = w_query.shape[0]
    capacity = 5 * tok // (2 * experts_n)
    cap_pad = -(-capacity // 16) * 16
    slots_n = experts_n * cap_pad

    n_gain, n_bias = gain_attn.shape[0], position_bias.shape[0]
    meta_in = jnp.concatenate([routes[0].T, gate_fixed], axis=0)
    normed, qkv, lse, mixed, resid, wq, wk, wv, wo, meta_all, vectors, gains, slots, d_outs, wgu = front(
        n, experts_n, capacity, cap_pad, inputs[0], w_query, w_key, w_value, w_out,
        gain_attn.reshape(1, -1), gain_moe.reshape(1, -1), position_bias.reshape(1, -1),
        meta_in, w_gate[0], w_up[0], cotangent[0],
    )
    wq, wk, wv = (w.reshape(width, own) for w in (wq, wk, wv))
    wo = wo.reshape(width, width)
    wgu = wgu.reshape(width, -1)
    deep = w_down.shape[1]
    out_rows, grad_normed_two, gwgu, grad_w_down = experts(
        n, experts_n, cap_pad, deep, slots, d_outs, wgu, w_down[0], meta_all
    )

    block_out, grad_inputs, g_all, small, got, _ = backward(
        n, experts_n, cap_pad, wrows, grad_normed_two, resid, cotangent[0], inputs[0], gains, mixed, wo,
        qkv, lse, normed, vectors, wq, wk, wv, meta_all, gwgu.reshape(n, width // n, -1), out_rows,
    )
    (
        grad_w_gate, grad_w_up, gq, gk, gv, go, grad_gain_one, grad_gain_two, grad_bias, block_out, grad_inputs,
        grad_w_down,
    ) = finish(n, experts_n, heads_own, n_gain, n_bias, got, g_all, small, block_out, grad_inputs, grad_w_down)

    return (
        block_out[None],
        grad_inputs[None],
        grad_gain_one[0],
        gq,
        gk,
        gv,
        go,
        grad_bias[0],
        grad_gain_two[0],
        grad_w_gate[None],
        grad_w_up[None],
        grad_w_down[None],
    )


def solution(mesh):
    vector = P(("dp", "expert"))
    matrix = P(("dp", "expert"), None)
    split = P("expert", "dp", None)
    return jax.shard_map(
        local,
        mesh=mesh,
        in_specs=(
            split, split, vector, matrix, matrix, matrix, matrix, vector, vector,
            split, split, split, split, P("expert", "dp"),
        ),
        out_specs=(
            split, split, vector, matrix, matrix, matrix, matrix, vector, vector,
            split, split, split,
        ),
        check_vma=False,
    )
```
